32 devices in a mesh: grp: 4 (over x, core), fsdp: 8 (over z, y).
Axes of the slice: x: 2, y: 2, z: 4, core: 2. Of those that a mesh axis runs over, the one named last changes fastest.
Arguments:
- hidden_in: bfloat16 [8192, 2048], P(('grp', 'fsdp')), may hold values from -6 to 6
- query_weight: bfloat16 [2048, 2048], P(('grp', 'fsdp')), may hold values from -0.125 to 0.125
- key_matrix: bfloat16 [2048, 1024], P(('grp', 'fsdp')), may hold values from -0.125 to 0.125
- value_matrix: bfloat16 [2048, 1024], P(('grp', 'fsdp')), may hold values from -0.125 to 0.125
- gate_weight: bfloat16 [2048, 2048], P(('grp', 'fsdp')), may hold values from -0.125 to 0.125
- out_weight: bfloat16 [2048, 2048], P(('grp', 'fsdp')), may hold values from -2 to 2
- norm_attn: bfloat16 [2048], P(('grp', 'fsdp')), may hold values from 0.25 to 1.75
- query_gain: bfloat16 [128], P(('grp', 'fsdp')), may hold values from 0.25 to 1.75
- key_gain: bfloat16 [128], P(('grp', 'fsdp')), may hold values from 0.25 to 1.75
- norm_ffn: bfloat16 [2048], P(('grp', 'fsdp')), may hold values from 0.25 to 1.75
- ffn_gate: bfloat16 [2048, 6144], P(('grp', 'fsdp')), may hold values from -0.125 to 0.125
- ffn_up: bfloat16 [2048, 6144], P(('grp', 'fsdp')), may hold values from -0.125 to 0.125
- ffn_down: bfloat16 [6144, 2048], P(('grp', 'fsdp')), may hold values from -0.078125 to 0.078125
- cotangent: bfloat16 [8192, 2048], P(('grp', 'fsdp')), may hold values from -6 to 6
- sequence_numbers: int32 [8192], P('grp'), may hold values from 0 to 8, as said below
- positions: int32 [8192], P('grp'), may hold values from 0 to 1151, as said below
Outputs:
- output: bfloat16 [8192, 2048], P(('grp', 'fsdp'))
- input_grad: float32 [8192, 2048], P(('grp', 'fsdp'))
- grad_query: float32 [2048, 2048], P(('grp', 'fsdp'))
- grad_key: float32 [2048, 1024], P(('grp', 'fsdp'))
- grad_value: float32 [2048, 1024], P(('grp', 'fsdp'))
- grad_gate: float32 [2048, 2048], P(('grp', 'fsdp'))
- grad_out: float32 [2048, 2048], P(('grp', 'fsdp'))
- grad_norm_attn: float32 [2048], P(('grp', 'fsdp'))
- grad_query_gain: float32 [128], P(('grp', 'fsdp'))
- grad_key_gain: float32 [128], P(('grp', 'fsdp'))
- grad_norm_ffn: float32 [2048], P(('grp', 'fsdp'))
- grad_ffn_gate: float32 [2048, 6144], P(('grp', 'fsdp'))
- grad_ffn_up: float32 [2048, 6144], P(('grp', 'fsdp'))
- grad_ffn_down: float32 [6144, 2048], P(('grp', 'fsdp'))
The draws below stay inside these ranges and needn't reach their ends.
Inputs may be any that keep to these rules, and one draw needn't show every extreme that they name: `sequence_numbers`: every aligned run of 2048 rows is one prompt group: 8 prompt blocks and 8 continuations, as blocks of 128 consecutive rows in a drawn order. A prompt block has sequence number 0; continuation c (1 to 8) has c on all its 128 tokens. Prompt tokens have positions 0 to 1023 in order within their blocks; the tokens of every continuation have positions 1024 to 1151 in order.
All inputs are finite; a program needn't handle non-finite values.
Results may differ from the reference program's by a relative error of at most 0.024.
Values may be sent and summed in bfloat16 or wider, within the bound.
A program may use at most 448 MiB of HBM per device.

```python
import math
import jax
import jax.numpy as jnp
from jax import lax

MODEL_WIDTH = 2048
QUERY_HEADS = 16
KEY_VALUE_HEADS = 8
HEAD_SIZE = 128
FF = 6144
PROMPT = 1024
CONT = 128
GROUP_TOKENS = 2048
TOKEN_ROWS = 8192
GROUP_COUNT = 4


def placement_tables(key):
    group_total = TOKEN_ROWS // GROUP_TOKENS
    per_group = GROUP_TOKENS // CONT
    prompt_blocks = PROMPT // CONT
    block_key = jax.random.fold_in(key, 23)
    block_scores = jax.random.randint(block_key, (group_total, per_group), 0, 1 << 14) * per_group + jnp.arange(per_group, dtype=jnp.int32)[None, :]
    block_order = jnp.argsort(block_scores, axis=-1, stable=True).astype(jnp.int32)
    offsets = jnp.arange(CONT, dtype=jnp.int32)[None, None, :]
    full_shape = (group_total, per_group, CONT)
    is_cont = (block_order >= prompt_blocks)[..., None]
    seq_numbers = jnp.broadcast_to(jnp.where(is_cont, block_order[..., None] - prompt_blocks + 1, 0), full_shape)
    place_pos = jnp.where(is_cont, PROMPT + offsets, block_order[..., None] * CONT + offsets)
    place_pos = jnp.broadcast_to(place_pos, full_shape)
    return (seq_numbers.reshape(TOKEN_ROWS).astype(jnp.int32), place_pos.reshape(TOKEN_ROWS).astype(jnp.int32))


def draw_sequence_numbers(key, part):
    return placement_tables(key)[0]


def draw_positions(key, part):
    return placement_tables(key)[1]


def block_levels(stream_key, extent, pieces, low, largest):
    level = 1.0
    for axis_at, blocks in pieces:
        heights = jax.random.uniform(jax.random.fold_in(jax.random.fold_in(stream_key, 6), axis_at), (blocks,), jnp.float32, low / len(pieces), largest / len(pieces))
        level = level * jnp.repeat(jnp.exp(heights), extent[axis_at] // blocks).reshape((-1,) + (1,) * (len(extent) - 1 - axis_at))
    return level


def noise(rng, extent, spread, bound, cuts=(), kind=jnp.bfloat16):
    factor_of = block_levels(rng, extent, cuts, -0.22, 0.18) if cuts else 1.0
    values = jax.random.normal(rng, extent, jnp.float32) * spread * factor_of
    return jnp.minimum(jnp.maximum(values, -bound), bound).astype(kind)


def setup_inputs(seed: int = 0) -> dict:
    keys = jax.random.split(jax.random.key(seed), 17)
    hidden_in = noise(keys[0], (TOKEN_ROWS, MODEL_WIDTH), 1.0, 6.0, ((0, 32),))
    query_weight = noise(keys[1], (MODEL_WIDTH, QUERY_HEADS * HEAD_SIZE), MODEL_WIDTH ** -0.5, 0.125, ((0, 32),))
    key_matrix = noise(keys[2], (MODEL_WIDTH, KEY_VALUE_HEADS * HEAD_SIZE), MODEL_WIDTH ** -0.5, 0.125, ((0, 32),))
    value_matrix = noise(keys[3], (MODEL_WIDTH, KEY_VALUE_HEADS * HEAD_SIZE), MODEL_WIDTH ** -0.5, 0.125, ((0, 32),))
    gate_weight = noise(keys[4], (MODEL_WIDTH, QUERY_HEADS * HEAD_SIZE), MODEL_WIDTH ** -0.5, 0.125, ((0, 32),))
    out_weight = noise(keys[5], (QUERY_HEADS * HEAD_SIZE, MODEL_WIDTH), (QUERY_HEADS * HEAD_SIZE // 256) ** -0.5, 2.0, ((0, 32),))
    norm_attn = jnp.clip(1.0 + 0.15 * jax.random.normal(keys[6], (MODEL_WIDTH,), jnp.float32), 0.25, 1.75).astype(jnp.bfloat16)
    query_gain = jnp.clip(1.0 + 0.15 * jax.random.normal(keys[7], (HEAD_SIZE,), jnp.float32), 0.25, 1.75).astype(jnp.bfloat16)
    key_gain = jnp.clip(1.0 + 0.15 * jax.random.normal(keys[8], (HEAD_SIZE,), jnp.float32), 0.25, 1.75).astype(jnp.bfloat16)
    norm_ffn = jnp.clip(1.0 + 0.15 * jax.random.normal(keys[9], (MODEL_WIDTH,), jnp.float32), 0.25, 1.75).astype(jnp.bfloat16)
    ffn_gate = noise(keys[10], (MODEL_WIDTH, FF), MODEL_WIDTH ** -0.5, 0.125, ((0, 32),))
    ffn_up = noise(keys[11], (MODEL_WIDTH, FF), MODEL_WIDTH ** -0.5, 0.125, ((0, 32),))
    ffn_down = noise(keys[12], (FF, MODEL_WIDTH), FF ** -0.5, 0.078125, ((0, 32),))
    cotangent = noise(keys[13], (TOKEN_ROWS, MODEL_WIDTH), 1.0, 6.0, ((0, 32),))
    sequence_numbers = draw_sequence_numbers(jax.random.fold_in(keys[16], 71), 0)
    positions = draw_positions(jax.random.fold_in(keys[16], 71), 0)
    return dict(hidden_in=hidden_in, query_weight=query_weight, key_matrix=key_matrix, value_matrix=value_matrix, gate_weight=gate_weight, out_weight=out_weight, norm_attn=norm_attn, query_gain=query_gain, key_gain=key_gain, norm_ffn=norm_ffn, ffn_gate=ffn_gate, ffn_up=ffn_up, ffn_down=ffn_down, cotangent=cotangent, sequence_numbers=sequence_numbers, positions=positions)


@jax.custom_vjp
def low(v):
    return lax.optimization_barrier(v.astype(jnp.bfloat16)).astype(jnp.float32)

@jax.custom_vjp
def low_back(v):
    return v

def low_keep(v):
    return (low(v), None)

def low_pass(kept, grad):
    return (grad,)

def back_keep(v):
    return (v, None)

def back_low(kept, grad):
    return (low(grad),)
low.defvjp(low_keep, low_pass)
low_back.defvjp(back_keep, back_low)

def matrix_product(left, right):
    return jnp.dot(left, right, precision=lax.Precision.HIGHEST)

def root_mean_scale(values, gains):
    return values * lax.rsqrt(lax.optimization_barrier(jnp.mean(values * values, axis=-1, keepdims=True)) + 1e-06) * gains

def rope_tables(positions):
    steps_half = jnp.arange(HEAD_SIZE // 2).astype(jnp.float32)
    inverse = jnp.power(1000000.0, steps_half * (-2.0 / HEAD_SIZE))
    angles = positions.astype(jnp.float32)[:, None] * inverse[None, :]
    angles = jnp.concatenate([angles, angles], axis=-1)
    return (jnp.cos(angles)[:, None, :], jnp.sin(angles)[:, None, :])

def rotary_apply(values, cosine_factor, sine_factor):
    half_dim = values.shape[-1] // 2
    turned = jnp.concatenate([-values[..., half_dim:], values[..., :half_dim]], axis=-1)
    return values * cosine_factor + turned * sine_factor

def attend_window(slice_items):
    query_rows, keys_all, values_all, row_sequence, row_position = slice_items
    every_row = query_rows.shape[0]
    block_row_span = min(1024, every_row)
    block_total = every_row // block_row_span
    scale_qk = 1.0 / math.sqrt(HEAD_SIZE)

    def block_attend(block_items):
        query_blk, seq_blk, pos_blk = block_items
        scores = jnp.einsum('qgrd,kgd->grqk', query_blk, keys_all, precision=lax.Precision.HIGHEST) * scale_qk
        scores = low_back(scores)
        allowed = (row_position[None, :] <= pos_blk[:, None]) & ((row_sequence[None, :] == 0) | (row_sequence[None, :] == seq_blk[:, None]))
        masked = jnp.where(allowed, scores, -1e+30)
        row_peak = lax.optimization_barrier(jnp.max(masked, axis=-1, keepdims=True))
        exponent = jnp.exp(masked - row_peak)
        softmax_w = low(exponent / lax.optimization_barrier(jnp.sum(exponent, axis=-1, keepdims=True)))
        return jnp.einsum('grqk,kgd->qgrd', softmax_w, values_all, precision=lax.Precision.HIGHEST)
    reshaped_heads = (query_rows.reshape(block_total, block_row_span, KEY_VALUE_HEADS, QUERY_HEADS // KEY_VALUE_HEADS, HEAD_SIZE), row_sequence.reshape(block_total, block_row_span), row_position.reshape(block_total, block_row_span))
    output_list = lax.map(jax.checkpoint(block_attend), reshaped_heads)
    return output_list.reshape(every_row, KEY_VALUE_HEADS, QUERY_HEADS // KEY_VALUE_HEADS, HEAD_SIZE)

def reference(hidden_in, query_weight, key_matrix, value_matrix, gate_weight, out_weight, norm_attn, query_gain, key_gain, norm_ffn, ffn_gate, ffn_up, ffn_down, cotangent, sequence_numbers, positions):
    cosine_factor, sine_factor = rope_tables(positions)

    def forward(hidden, w_query, key_projection, value_projection, w_gate, w_out, gain_attn, gain_query, key_norm_gain, gain_ffn, w_ffn_gate, w_ffn_up, w_ffn_down):
        normed_input = low(root_mean_scale(hidden, gain_attn))
        query_raw = low_back(matrix_product(normed_input, w_query))
        key_unrotated = low_back(matrix_product(normed_input, key_projection))
        value_projected = low(low_back(matrix_product(normed_input, value_projection)))
        gate_raw = low_back(matrix_product(normed_input, w_gate))
        query_rotated = low(rotary_apply(root_mean_scale(query_raw.reshape(TOKEN_ROWS, QUERY_HEADS, HEAD_SIZE), gain_query), cosine_factor, sine_factor))
        key_rotated = low(rotary_apply(root_mean_scale(key_unrotated.reshape(TOKEN_ROWS, KEY_VALUE_HEADS, HEAD_SIZE), key_norm_gain), cosine_factor, sine_factor))
        attended_rows = lax.map(attend_window, (query_rotated.reshape(GROUP_COUNT, GROUP_TOKENS, KEY_VALUE_HEADS, QUERY_HEADS // KEY_VALUE_HEADS, HEAD_SIZE), key_rotated.reshape(GROUP_COUNT, GROUP_TOKENS, KEY_VALUE_HEADS, HEAD_SIZE), value_projected.reshape(GROUP_COUNT, GROUP_TOKENS, KEY_VALUE_HEADS, HEAD_SIZE), sequence_numbers.reshape(GROUP_COUNT, GROUP_TOKENS), positions.reshape(GROUP_COUNT, GROUP_TOKENS)))
        attended_rows = low_back(attended_rows.reshape(TOKEN_ROWS, QUERY_HEADS * HEAD_SIZE))
        gated = low(attended_rows * jax.nn.sigmoid(gate_raw))
        middle = hidden + low_back(matrix_product(gated, w_out))
        normed_two = low(root_mean_scale(middle, gain_ffn))
        gate_ffn = low_back(matrix_product(normed_two, w_ffn_gate))
        up_ffn = low_back(matrix_product(normed_two, w_ffn_up))
        mixed_low = low(jax.nn.silu(gate_ffn) * up_ffn)
        return middle + low_back(matrix_product(mixed_low, w_ffn_down))
    result, pullback = jax.vjp(forward, hidden_in.astype(jnp.float32), query_weight.astype(jnp.float32), key_matrix.astype(jnp.float32), value_matrix.astype(jnp.float32), gate_weight.astype(jnp.float32), out_weight.astype(jnp.float32), norm_attn.astype(jnp.float32), query_gain.astype(jnp.float32), key_gain.astype(jnp.float32), norm_ffn.astype(jnp.float32), ffn_gate.astype(jnp.float32), ffn_up.astype(jnp.float32), ffn_down.astype(jnp.float32))
    grads = pullback(cotangent.astype(jnp.float32))
    return (result.astype(jnp.bfloat16), grads[0], grads[1], grads[2], grads[3], grads[4], grads[5], grads[6], grads[7], grads[8], grads[9], grads[10], grads[11], grads[12])
```

```python
import math

import jax
import jax.numpy as jnp
from jax import lax
from jax.sharding import Mesh
from jax.sharding import PartitionSpec as P

QUERY_HEADS = 16
KEY_VALUE_HEADS = 8
HEAD_SIZE = 128
GROUP_TOKENS = 2048
CORNERS = 2
PLANES = 4
ALL = ("x", "core", "cell", "z", "y")
TENSOR = ("x", "core", "y")
DATA = ("cell", "z")
RANKS = CORNERS**3


def root_mean_scale(values, gains):
    return values * lax.rsqrt(jnp.mean(values * values, axis=-1, keepdims=True) + 1e-06) * gains


def rope_tables(positions):
    steps_half = jnp.arange(HEAD_SIZE // 2).astype(jnp.float32)
    inverse = jnp.power(1000000.0, steps_half * (-2.0 / HEAD_SIZE))
    angles = positions.astype(jnp.float32)[..., None] * inverse
    angles = jnp.concatenate([angles, angles], axis=-1)
    return (jnp.cos(angles)[..., None, :], jnp.sin(angles)[..., None, :])


def rotary_apply(values, cosine_factor, sine_factor):
    half_dim = values.shape[-1] // 2
    turned = jnp.concatenate([-values[..., half_dim:], values[..., :half_dim]], axis=-1)
    return values * cosine_factor + turned * sine_factor


def matrix_product(left, right):
    return jnp.dot(left, right, preferred_element_type=jnp.float32)


def contract_last(left, right):
    return lax.dot_general(
        left, right, (((1,), (1,)), ((), ())), preferred_element_type=jnp.float32
    )


def contract_first(left, right):
    return lax.dot_general(
        left, right, (((0,), (0,)), ((), ())), preferred_element_type=jnp.float32
    )


def low(values):
    return values.astype(jnp.bfloat16)


def make_shards(cells):
    data_total = cells * PLANES

    def gather_tokens(rows):
        return lax.all_gather(rows, TENSOR, axis=0, tiled=True)

    def scatter_tokens(terms):
        return lax.psum_scatter(low(terms), TENSOR, scatter_dimension=0, tiled=True).astype(
            jnp.float32
        )

    def split_units(weight):
        rows, units = weight.shape
        piece = units // (RANKS * data_total)
        split = weight.reshape(rows, CORNERS**2, data_total, CORNERS, piece)
        return jnp.transpose(split, (0, 1, 3, 2, 4)).reshape(rows, RANKS, units // RANKS)

    def join_units(parts):
        ranks, rows, units = parts.shape
        split = parts.reshape(CORNERS**2, CORNERS, rows, data_total, units // data_total)
        return jnp.transpose(split, (2, 0, 3, 1, 4)).reshape(rows, ranks * units)

    def split_columns(weight):
        return weight.reshape(weight.shape[0], RANKS, -1)

    def join_columns(parts):
        return jnp.transpose(parts, (1, 0, 2)).reshape(parts.shape[1], -1)

    def gather_columns(pieces):
        sent = jnp.transpose(jnp.concatenate(pieces, axis=-1), (1, 0, 2))
        mine = lax.all_to_all(sent, TENSOR, split_axis=0, concat_axis=0, tiled=True)
        rows, columns = mine.shape[1:]
        every = lax.all_gather(mine, DATA, axis=0, tiled=False)
        every = every.reshape(data_total, CORNERS**2, CORNERS, rows, columns)
        return jnp.transpose(every, (1, 0, 2, 3, 4)).reshape(-1, columns)

    def scatter_columns(term):
        rows = term.shape[0] // (RANKS * data_total)
        split = low(term).reshape(CORNERS**2, data_total, CORNERS, rows, -1)
        split = jnp.transpose(split, (1, 0, 2, 3, 4)).reshape(data_total * RANKS, rows, -1)
        mine = lax.psum_scatter(split, DATA, scatter_dimension=0, tiled=True)
        return lax.all_to_all(mine, TENSOR, split_axis=0, concat_axis=0, tiled=True).astype(
            jnp.float32
        )

    inner = CORNERS * data_total
    to_rank = []
    for source in range(inner):
        rank_y, place = divmod(source, data_total)
        to_rank.append((source, place * CORNERS + rank_y))
    from_rank = [(b, a) for a, b in to_rank]
    INNER = ("cell", "z", "y")

    def shards(
        hidden_in,
        query_weight,
        key_matrix,
        value_matrix,
        gate_weight,
        out_weight,
        norm_attn,
        query_gain,
        key_gain,
        norm_ffn,
        ffn_gate,
        ffn_up,
        ffn_down,
        cotangent,
        sequence_numbers,
        positions,
    ):
        rows = hidden_in.shape[0]
        tokens = rows * RANKS
        groups = CORNERS**2
        window = GROUP_TOKENS // PLANES
        repeat = QUERY_HEADS // KEY_VALUE_HEADS
        query_columns = QUERY_HEADS * HEAD_SIZE // RANKS
        key_columns = KEY_VALUE_HEADS * HEAD_SIZE // RANKS
        scale_qk = 1.0 / math.sqrt(HEAD_SIZE)

        sizes = [norm_attn.shape[0], norm_ffn.shape[0], query_gain.shape[0], key_gain.shape[0]]
        gains = lax.all_gather(
            jnp.concatenate([norm_attn, norm_ffn, query_gain, key_gain]), ALL, axis=0, tiled=False
        ).astype(jnp.float32)
        cuts = [0]
        for size in sizes:
            cuts.append(cuts[-1] + size)
        gain_attn, gain_ffn, gain_query, gain_key = (
            gains[:, a:b].reshape(-1) for a, b in zip(cuts[:-1], cuts[1:])
        )

        w_attn = gather_columns(
            [
                split_columns(query_weight),
                split_columns(key_matrix),
                split_columns(value_matrix),
                split_columns(gate_weight),
            ]
        )
        w_out = lax.all_gather(
            lax.ppermute(out_weight, INNER, to_rank), DATA, axis=0, tiled=True
        )
        w_ffn = gather_columns([split_units(ffn_gate), split_units(ffn_up)])
        w_down = lax.all_gather(ffn_down, DATA, axis=0, tiled=True)

        plane = lax.axis_index("z")
        group_start = lax.axis_index("cell") * GROUP_TOKENS
        marks = jnp.stack(
            [
                lax.dynamic_slice_in_dim(sequence_numbers, group_start, GROUP_TOKENS),
                lax.dynamic_slice_in_dim(positions, group_start, GROUP_TOKENS),
            ]
        )
        marks = lax.all_gather(marks, ("x", "core"), axis=0, tiled=False)
        key_seq, key_pos = marks[:, 0], marks[:, 1]
        own = lax.dynamic_slice_in_dim(marks, plane * window, window, axis=2)
        own_seq, own_pos = own[:, 0], own[:, 1]
        cosine_factor, sine_factor = rope_tables(own_pos)
        allowed = (key_pos[:, None, :] <= own_pos[:, :, None]) & (
            (key_seq[:, None, :] == 0) | (key_seq[:, None, :] == own_seq[:, :, None])
        )

        def prepare_heads(raw_values, gain_values):
            return rotary_apply(
                root_mean_scale(raw_values, gain_values), cosine_factor, sine_factor
            )

        hidden = hidden_in.astype(jnp.float32)
        normed_input = gather_tokens(low(root_mean_scale(hidden, gain_attn)))
        raw = matrix_product(normed_input, w_attn)
        a, b, c = query_columns, query_columns + key_columns, query_columns + 2 * key_columns
        query_raw = raw[:, :a].reshape(groups, window, repeat, HEAD_SIZE)
        key_raw = raw[:, a:b].reshape(groups, window, 1, HEAD_SIZE)
        value_low = low(raw[:, b:c]).reshape(groups, window, HEAD_SIZE)
        gate_sig = jax.nn.sigmoid(raw[:, c:])
        query_low = low(prepare_heads(query_raw, gain_query))
        key_low = low(prepare_heads(key_raw, gain_key)).reshape(groups, window, HEAD_SIZE)
        pair = lax.all_gather(
            jnp.concatenate([key_low, value_low], axis=-1), "z", axis=0, tiled=False
        )
        pair = jnp.transpose(pair, (1, 0, 2, 3)).reshape(groups, GROUP_TOKENS, 2 * HEAD_SIZE)
        keys_all, values_all = pair[..., :HEAD_SIZE], pair[..., HEAD_SIZE:]

        scores = (
            jnp.einsum("gqrd,gkd->grqk", query_low, keys_all, preferred_element_type=jnp.float32)
            * scale_qk
        )
        masked = jnp.where(allowed[:, None], scores, -1e30)
        peak = jnp.max(masked, axis=-1, keepdims=True)
        exponent = jnp.exp(masked - peak)
        probs = exponent / jnp.sum(exponent, axis=-1, keepdims=True)
        probs_low = low(probs)
        attended = jnp.einsum(
            "grqk,gkd->gqrd", probs_low, values_all, preferred_element_type=jnp.float32
        )
        attended_rows = attended.reshape(tokens, query_columns)
        gated_low = low(attended_rows * gate_sig)
        middle = hidden + scatter_tokens(matrix_product(gated_low, w_out))

        normed_two = gather_tokens(low(root_mean_scale(middle, gain_ffn)))
        both = matrix_product(normed_two, w_ffn)
        units = both.shape[1] // 2
        gate_ffn, up_ffn = both[:, :units], both[:, units:]
        ffn_sig = jax.nn.sigmoid(gate_ffn)
        mixed_low = low(gate_ffn * ffn_sig * up_ffn)
        output = low(middle + scatter_tokens(matrix_product(mixed_low, w_down)))

        cotangent_all = gather_tokens(cotangent)
        d_mixed = contract_last(cotangent_all, w_down)
        d_up_low = low(d_mixed * gate_ffn * ffn_sig)
        d_gate_ffn_low = low(d_mixed * up_ffn * ffn_sig * (1.0 + gate_ffn * (1.0 - ffn_sig)))
        d_both = jnp.concatenate([d_gate_ffn_low, d_up_low], axis=-1)
        d_normed_two = scatter_tokens(contract_last(d_both, w_ffn))
        grad_down = lax.psum_scatter(
            low(contract_first(mixed_low, cotangent_all)), DATA, scatter_dimension=0, tiled=True
        ).astype(jnp.float32)
        grad_both = scatter_columns(contract_first(normed_two, d_both))
        grad_gate = join_units(grad_both[..., :units])
        grad_up = join_units(grad_both[..., units:])
        unused_two, norm_two_back = jax.vjp(root_mean_scale, middle, gain_ffn)
        d_middle_norm, grad_norm_two_term = norm_two_back(d_normed_two)
        d_middle = cotangent.astype(jnp.float32) + d_middle_norm

        branch_all = gather_tokens(low(d_middle))
        d_gated = contract_last(branch_all, w_out)
        grad_out = lax.psum_scatter(
            low(contract_first(gated_low, branch_all)), DATA, scatter_dimension=0, tiled=True
        )
        grad_out = lax.ppermute(grad_out, INNER, from_rank).astype(jnp.float32)
        d_attended = low(d_gated * gate_sig)
        d_gate_low = low(d_gated * attended_rows * gate_sig * (1.0 - gate_sig))
        d_heads = d_attended.reshape(groups, window, repeat, HEAD_SIZE)
        row_delta = jnp.transpose(
            jnp.sum(d_heads.astype(jnp.float32) * attended, axis=-1), (0, 2, 1)
        )
        d_probs = jnp.einsum(
            "gqrd,gkd->grqk", d_heads, values_all, preferred_element_type=jnp.float32
        )
        d_scores = low(probs * (d_probs - row_delta[..., None]))
        d_query_rot = (
            jnp.einsum("grqk,gkd->gqrd", d_scores, keys_all, preferred_element_type=jnp.float32)
            * scale_qk
        )
        d_keys = (
            jnp.einsum("grqk,gqrd->gkd", d_scores, query_low, preferred_element_type=jnp.float32)
            * scale_qk
        )
        d_values = jnp.einsum(
            "grqk,gqrd->gkd", probs_low, d_heads, preferred_element_type=jnp.float32
        )
        d_pair = low(jnp.concatenate([d_keys, d_values], axis=-1))
        d_pair = jnp.transpose(
            d_pair.reshape(groups, PLANES, window, 2 * HEAD_SIZE), (1, 0, 2, 3)
        )
        d_pair = lax.psum_scatter(d_pair, "z", scatter_dimension=0, tiled=True)
        d_pair = d_pair.reshape(groups, window, 2 * HEAD_SIZE).astype(jnp.float32)
        d_key_rot, d_value = d_pair[..., :HEAD_SIZE], d_pair[..., HEAD_SIZE:]
        unused_query, query_back = jax.vjp(prepare_heads, query_raw, gain_query)
        d_query_raw, grad_query_gain_term = query_back(d_query_rot)
        unused_key, key_back = jax.vjp(prepare_heads, key_raw, gain_key)
        d_key_raw, grad_key_gain_term = key_back(d_key_rot[:, :, None, :])
        d_raw = jnp.concatenate(
            [
                low(d_query_raw.reshape(tokens, query_columns)),
                low(d_key_raw.reshape(tokens, key_columns)),
                low(d_value.reshape(tokens, key_columns)),
                d_gate_low,
            ],
            axis=-1,
        )
        d_normed = scatter_tokens(contract_last(d_raw, w_attn))
        grad_attn = scatter_columns(contract_first(normed_input, d_raw))
        grad_query = join_columns(grad_attn[..., :a])
        grad_key = join_columns(grad_attn[..., a:b])
        grad_value = join_columns(grad_attn[..., b:c])
        grad_gatew = join_columns(grad_attn[..., c:])
        unused_one, norm_one_back = jax.vjp(root_mean_scale, hidden, gain_attn)
        d_hidden_norm, grad_norm_one_term = norm_one_back(d_normed)
        input_grad = d_middle + d_hidden_norm

        terms = jnp.concatenate(
            [
                t.reshape(RANKS * data_total, -1)
                for t in (
                    grad_norm_one_term,
                    grad_norm_two_term,
                    grad_query_gain_term,
                    grad_key_gain_term,
                )
            ],
            axis=-1,
        )
        small = lax.psum_scatter(terms, ALL, scatter_dimension=0, tiled=True).reshape(-1)
        grad_norm_attn, grad_norm_ffn, grad_query_gain, grad_key_gain = (
            small[s:e] for s, e in zip(cuts[:-1], cuts[1:])
        )
        return (
            output,
            input_grad,
            grad_query,
            grad_key,
            grad_value,
            grad_gatew,
            grad_out,
            grad_norm_attn,
            grad_query_gain,
            grad_key_gain,
            grad_norm_ffn,
            grad_gate,
            grad_up,
            grad_down,
        )

    return shards


def solution(mesh):
    cells = mesh.shape["fsdp"] // (PLANES * CORNERS)
    split = Mesh(
        mesh.devices.reshape(CORNERS, CORNERS, cells, PLANES, CORNERS),
        ALL,
    )
    rows, flat, group = P(ALL, None), P(ALL), P(("x", "core"))
    return jax.shard_map(
        make_shards(cells),
        mesh=split,
        in_specs=(rows,) * 6 + (flat,) * 4 + (rows,) * 4 + (group,) * 2,
        out_specs=(rows,) * 7 + (flat,) * 4 + (rows,) * 3,
        check_vma=False,
    )
```

```python
import functools
import math

import jax
import jax.numpy as jnp
from jax import lax
from jax.experimental import pallas as pl
from jax.experimental.pallas import tpu as pltpu
from jax.sharding import Mesh
from jax.sharding import PartitionSpec as P

QUERY_HEADS = 16
KEY_VALUE_HEADS = 8
HEAD_SIZE = 128
GROUP_TOKENS = 2048
CORNERS = 2
PLANES = 4
ALL = ("x", "core", "cell", "z", "y")
TENSOR = ("x", "core", "y")
DATA = ("cell", "z")
RANKS = CORNERS**3
CHUNKS = 4
MESH_ID = pl.DeviceIdType.MESH


def remote(source, target, send, receive, device):
    return pltpu.make_async_remote_copy(src_ref=source, dst_ref=target, send_sem=send, recv_sem=receive,
        device_id=device, device_id_type=MESH_ID)

def greet(devices):
    barrier = pltpu.get_barrier_semaphore()
    for device in devices:
        pl.semaphore_signal(barrier, inc=1, device_id=device, device_id_type=MESH_ID)
    pl.semaphore_wait(barrier, len(devices))

def corner():
    x, c, y = lax.axis_index("x"), lax.axis_index("core"), lax.axis_index("y")
    return x, c, y, {"x": 1 - x}, {"y": 1 - y}, {"core": 1 - c}

def slot(x, c, y):
    return (x * 2 + c) * 2 + y

def gather_kernel(rows, in_ref, out_ref, send_x, send_y, send_c, recv_x, recv_y, recv_c, local):
    x, c, y, dev_x, dev_y, dev_c = corner()
    chunk = rows // CHUNKS
    def at(index, k):
        return out_ref.at[pl.ds(pl.multiple_of(index * rows + k * chunk, chunk), chunk), :]
    own, beside_x, beside_y = slot(x, c, y), slot(1 - x, c, y), slot(x, c, 1 - y)
    across = slot(1 - x, c, 1 - y)
    mirror = [slot(x, 1 - c, y), slot(1 - x, 1 - c, y), slot(x, 1 - c, 1 - y), slot(1 - x, 1 - c, 1 - y)]
    greet([dev_x, dev_y, dev_c])
    keep = pltpu.make_async_copy(in_ref, out_ref.at[pl.ds(pl.multiple_of(own * rows, rows), rows), :], local)
    keep.start()
    sent = []
    def go(copy):
        copy.start(); sent.append(copy)
    half = CHUNKS // 2
    order_x = list(range(CHUNKS)); order_y = order_x[half:] + order_x[:half]
    def mine(k):
        return in_ref.at[pl.ds(k * chunk, chunk), :]
    for i in range(CHUNKS):
        k = order_x[i]; go(remote(mine(k), at(own, k), send_x.at[k], recv_x.at[k], dev_x))
        k = order_y[i]; go(remote(mine(k), at(own, k), send_y.at[k], recv_y.at[k], dev_y))
    for k in range(CHUNKS):
        go(remote(mine(k), at(own, k), send_c.at[k], recv_c.at[k], dev_c))
    def landed(index, k, sem, device):
        remote(at(index, k), at(index, k), sem, sem, device).wait_recv()
    for i in range(CHUNKS):
        k = order_x[i]
        landed(beside_x, k, recv_x.at[k], dev_x)
        if k < half:
            go(remote(at(beside_x, k), at(beside_x, k), send_y.at[CHUNKS + k], recv_y.at[CHUNKS + k], dev_y))
        go(remote(at(beside_x, k), at(beside_x, k), send_c.at[CHUNKS + k], recv_c.at[CHUNKS + k], dev_c))
        k = order_y[i]
        landed(beside_y, k, recv_y.at[k], dev_y)
        if k >= half:
            go(remote(at(beside_y, k), at(beside_y, k), send_x.at[half + k], recv_x.at[half + k], dev_x))
        go(remote(at(beside_y, k), at(beside_y, k), send_c.at[2 * CHUNKS + k], recv_c.at[2 * CHUNKS + k], dev_c))
    for i in range(half):
        k = i
        landed(across, k, recv_y.at[CHUNKS + k], dev_y)
        go(remote(at(across, k), at(across, k), send_c.at[3 * CHUNKS + k], recv_c.at[3 * CHUNKS + k], dev_c))
        k = half + i
        landed(across, k, recv_x.at[half + k], dev_x)
        go(remote(at(across, k), at(across, k), send_c.at[3 * CHUNKS + k], recv_c.at[3 * CHUNKS + k], dev_c))
    for b in range(4):
        for k in range(CHUNKS):
            landed(mirror[b], k, recv_c.at[b * CHUNKS + k], dev_c)
    for copy in sent:
        copy.wait_send()
    keep.wait()

def gather_tokens(block):
    rows, columns = block.shape
    dma = pltpu.SemaphoreType.DMA
    n = CHUNKS
    return pl.pallas_call(
        functools.partial(gather_kernel, rows),
        out_shape=jax.ShapeDtypeStruct((8 * rows, columns), block.dtype),
        in_specs=[pl.BlockSpec(memory_space=pltpu.VMEM)],
        out_specs=pl.BlockSpec(memory_space=pl.ANY),
        scratch_shapes=[dma((n + n // 2,)), dma((n + n // 2,)), dma((4 * n,)), dma((n + n // 2,)), dma((n + n // 2,)), dma((4 * n,)), dma(())],
        compiler_params=pltpu.CompilerParams(collective_id=0, has_side_effects=True),
    )(block)

def scatter_kernel(rows, part_ref, out_ref, core_buf, x_buf, y_buf, x_diag, y_diag, d_sum, x_sum, y_sum,
                   send_c, recv_c, send_x, recv_x, send_y, recv_y):
    x, c, y, dev_x, dev_y, dev_c = corner()
    chunk = rows // CHUNKS
    half = CHUNKS // 2
    D, X, Y, O = range(4)
    place = [(1 - x, 1 - y), (1 - x, y), (x, 1 - y), (x, y)]
    mine = [slot(px, c, py) for px, py in place]
    theirs = [slot(px, 1 - c, py) for px, py in place]
    f32 = jnp.float32
    columns = out_ref.shape[1]
    def piece(k):
        return pl.ds(k * chunk, chunk)
    greet([dev_x, dev_y, dev_c])
    sent = []
    def go(copy):
        copy.start(); sent.append(copy)
    orders = {D: [0, 2, 1, 3], X: [0, 1, 2, 3], Y: [2, 3, 0, 1], O: [0, 1, 2, 3]}
    orders = orders if CHUNKS == 4 else {b: list(range(CHUNKS)) for b in range(4)}
    for b in (D, X, Y, O):
        for k in orders[b]:
            go(remote(part_ref.at[theirs[b], piece(k), :], core_buf.at[b, piece(k), :], send_c.at[b * CHUNKS + k], recv_c.at[b * CHUNKS + k], dev_c))
    def got(ref, sem, device):
        remote(ref, ref, sem, sem, device).wait_recv()
    step = 16
    def total(target, k, *sources, dtype):
        def body(i, carry):
            r = pl.multiple_of(k * chunk + i * step, step)
            acc = None
            for source in sources:
                v = source(r).astype(f32)
                acc = v if acc is None else acc + v
            target[pl.ds(r, step), :] = acc.astype(dtype)
            return carry
        lax.fori_loop(0, chunk // step, body, 0)
    def own_part(b):
        return lambda r: part_ref[mine[b], pl.ds(r, step), :]
    def core_part(b):
        return lambda r: core_buf[b, pl.ds(r, step), :]
    def from_(ref, shift=0):
        return lambda r: ref[pl.ds(r - shift if shift else r, step), :]
    bf = jnp.bfloat16
    for k in orders[D]:
        got(core_buf.at[D, piece(k), :], recv_c.at[D * CHUNKS + k], dev_c)
        total(d_sum, k, own_part(D), core_part(D), dtype=bf)
        if k < half:
            go(remote(d_sum.at[piece(k), :], x_diag.at[pl.ds(k * chunk, chunk), :], send_x.at[CHUNKS + k], recv_x.at[CHUNKS + k], dev_x))
        else:
            go(remote(d_sum.at[piece(k), :], y_diag.at[pl.ds((k - half) * chunk, chunk), :], send_y.at[half + k], recv_y.at[half + k], dev_y))
    for i in range(half):
        k = i
        got(core_buf.at[X, piece(k), :], recv_c.at[X * CHUNKS + k], dev_c)
        total(x_sum, k, own_part(X), core_part(X), dtype=bf)
        go(remote(x_sum.at[piece(k), :], x_buf.at[piece(k), :], send_x.at[k], recv_x.at[k], dev_x))
        k = half + i
        got(core_buf.at[Y, piece(k), :], recv_c.at[Y * CHUNKS + k], dev_c)
        total(y_sum, k, own_part(Y), core_part(Y), dtype=bf)
        go(remote(y_sum.at[piece(k), :], y_buf.at[piece(k), :], send_y.at[k], recv_y.at[k], dev_y))
    for i in range(half):
        k = half + i
        got(core_buf.at[X, piece(k), :], recv_c.at[X * CHUNKS + k], dev_c)
        got(y_diag.at[pl.ds(i * chunk, chunk), :], recv_y.at[half + k], dev_y)
        total(x_sum, k, own_part(X), core_part(X), from_(y_diag, half * chunk), dtype=bf)
        go(remote(x_sum.at[piece(k), :], x_buf.at[piece(k), :], send_x.at[k], recv_x.at[k], dev_x))
        k = i
        got(core_buf.at[Y, piece(k), :], recv_c.at[Y * CHUNKS + k], dev_c)
        got(x_diag.at[pl.ds(i * chunk, chunk), :], recv_x.at[CHUNKS + k], dev_x)
        total(y_sum, k, own_part(Y), core_part(Y), from_(x_diag), dtype=bf)
        go(remote(y_sum.at[piece(k), :], y_buf.at[piece(k), :], send_y.at[k], recv_y.at[k], dev_y))
    for k in range(CHUNKS):
        got(core_buf.at[O, piece(k), :], recv_c.at[O * CHUNKS + k], dev_c)
        got(x_buf.at[piece(k), :], recv_x.at[k], dev_x)
        got(y_buf.at[piece(k), :], recv_y.at[k], dev_y)
        total(out_ref, k, own_part(O), core_part(O), from_(x_buf), from_(y_buf), dtype=out_ref.dtype)
    for copy in sent:
        copy.wait_send()

def scatter_blocks(terms):
    ranks, rows, columns = terms.shape
    dma = pltpu.SemaphoreType.DMA
    n = CHUNKS
    vm = lambda *s: pltpu.VMEM(s, jnp.bfloat16)
    return pl.pallas_call(
        functools.partial(scatter_kernel, rows),
        out_shape=jax.ShapeDtypeStruct((rows, columns), jnp.float32),
        in_specs=[pl.BlockSpec(memory_space=pltpu.VMEM)],
        out_specs=pl.BlockSpec(memory_space=pltpu.VMEM),
        scratch_shapes=[vm(4, rows, columns), vm(rows, columns), vm(rows, columns), vm(rows // 2, columns), vm(rows // 2, columns),
            vm(rows, columns), vm(rows, columns), vm(rows, columns),
            dma((4 * n,)), dma((4 * n,)), dma((n + n // 2,)), dma((n + n // 2,)), dma((n + n // 2,)), dma((n + n // 2,))],
        compiler_params=pltpu.CompilerParams(collective_id=1, has_side_effects=True, vmem_limit_bytes=40 << 20),
    )(terms)

OTHERS = [(dx, dc, dy) for dx in (0, 1) for dc in (0, 1) for dy in (0, 1) if dx + dc + dy]

def flip(value, bit):
    return 1 - value if bit else value

def hello_kernel(total, gains_ref, marks_ref, weight_ref, gains_out, marks_out, weight_out,
                 gain_send, gain_recv, mark_send, mark_recv, weight_send, weight_recv, local):
    x, c, y, dev_x, dev_y, dev_c = corner()
    me, device = everyone(total)
    own = slot(x, c, y)
    group = x * 2 + c
    keeps = [
        pltpu.make_async_copy(gains_ref, gains_out.at[me], local.at[0]),
        pltpu.make_async_copy(marks_ref, marks_out.at[group], local.at[1]),
        pltpu.make_async_copy(weight_ref.at[own], weight_out.at[own], local.at[2]),
    ]
    for keep in keeps:
        keep.start()
    sent = []
    for i, (dx, dc, dy) in enumerate(OTHERS):
        there = {"x": flip(x, dx), "core": flip(c, dc), "y": flip(y, dy)}
        other = slot(flip(x, dx), flip(c, dc), flip(y, dy))
        copy = remote(weight_ref.at[other], weight_out.at[own], weight_send.at[i], weight_recv.at[i], there)
        copy.start(); sent.append(copy)
        if not dy:
            copy = remote(marks_ref, marks_out.at[group], mark_send.at[i], mark_recv.at[i], there)
            copy.start(); sent.append(copy)
    def send_gain(d, carry):
        remote(gains_ref, gains_out.at[me], gain_send.at[d], gain_recv.at[d], device(lax.rem(me + d, total))).start()
        return carry
    lax.fori_loop(1, total, send_gain, 0)
    def take_gain(d, carry):
        source = lax.rem(me + total - d, total)
        remote(gains_out.at[source], gains_out.at[source], gain_recv.at[d], gain_recv.at[d], device(source)).wait_recv()
        remote(gains_ref, gains_out.at[me], gain_send.at[d], gain_recv.at[d], device(lax.rem(me + d, total))).wait_send()
        return carry
    lax.fori_loop(1, total, take_gain, 0)
    for i, (dx, dc, dy) in enumerate(OTHERS):
        there = {"x": flip(x, dx), "core": flip(c, dc), "y": flip(y, dy)}
        other = slot(flip(x, dx), flip(c, dc), flip(y, dy))
        remote(weight_out.at[other], weight_out.at[other], weight_recv.at[i], weight_recv.at[i], there).wait_recv()
        if not dy:
            theirs = flip(x, dx) * 2 + flip(c, dc)
            remote(marks_out.at[theirs], marks_out.at[theirs], mark_recv.at[i], mark_recv.at[i], there).wait_recv()
    for copy in sent:
        copy.wait_send()
    for keep in keeps:
        keep.wait()

def hello(total, gains, marks, weight, collective_id):
    dma = pltpu.SemaphoreType.DMA
    vmem, anyspace = pl.BlockSpec(memory_space=pltpu.VMEM), pl.BlockSpec(memory_space=pl.ANY)
    n = len(OTHERS)
    return pl.pallas_call(
        functools.partial(hello_kernel, total),
        out_shape=[jax.ShapeDtypeStruct((total,) + gains.shape, gains.dtype),
                   jax.ShapeDtypeStruct((4,) + marks.shape, marks.dtype),
                   jax.ShapeDtypeStruct(weight.shape, weight.dtype)],
        in_specs=[vmem, vmem, vmem], out_specs=[vmem, vmem, anyspace],
        scratch_shapes=[dma((total,)), dma((total,)), dma((n,)), dma((n,)), dma((n,)), dma((n,)), dma((3,))],
        compiler_params=pltpu.CompilerParams(collective_id=collective_id, has_side_effects=True),
    )(gains, marks, weight)

def swap_kernel(in_ref, out_ref, send, recv, local):
    x, c, y, dev_x, dev_y, dev_c = corner()
    own = slot(x, c, y)
    places = [({"x": flip(x, dx), "core": flip(c, dc), "y": flip(y, dy)}, slot(flip(x, dx), flip(c, dc), flip(y, dy))) for dx, dc, dy in OTHERS]
    greet([p for p, _ in places])
    keep = pltpu.make_async_copy(in_ref.at[own], out_ref.at[own], local)
    keep.start()
    sent = []
    for i, (there, other) in enumerate(places):
        copy = remote(in_ref.at[other], out_ref.at[own], send.at[i], recv.at[i], there)
        copy.start(); sent.append(copy)
    for i, (there, other) in enumerate(places):
        remote(out_ref.at[other], out_ref.at[other], recv.at[i], recv.at[i], there).wait_recv()
    for copy in sent:
        copy.wait_send()
    keep.wait()

def swap(blocks, collective_id):
    dma = pltpu.SemaphoreType.DMA
    n = len(OTHERS)
    return pl.pallas_call(
        swap_kernel, out_shape=jax.ShapeDtypeStruct(blocks.shape, blocks.dtype),
        in_specs=[pl.BlockSpec(memory_space=pltpu.VMEM)], out_specs=pl.BlockSpec(memory_space=pl.ANY),
        scratch_shapes=[dma((n,)), dma((n,)), dma(())],
        compiler_params=pltpu.CompilerParams(collective_id=collective_id, has_side_effects=True),
    )(blocks)

LINE = 4
def line_greet(z):
    barrier = pltpu.get_barrier_semaphore()
    @pl.when(z > 0)
    def _():
        pl.semaphore_signal(barrier, inc=1, device_id={"z": z - 1}, device_id_type=MESH_ID)
    @pl.when(z < LINE - 1)
    def _():
        pl.semaphore_signal(barrier, inc=1, device_id={"z": z + 1}, device_id_type=MESH_ID)
    @pl.when((z == 0) | (z == LINE - 1))
    def _():
        pl.semaphore_wait(barrier, 1)
    @pl.when((z > 0) & (z < LINE - 1))
    def _():
        pl.semaphore_wait(barrier, 2)

def line_gather_kernel(pieces, in_ref, out_ref, up_send, up_recv, down_send, down_recv, local):
    z = lax.axis_index("z")
    rows = in_ref.shape[0] // pieces
    line_greet(z)
    keep = pltpu.make_async_copy(in_ref, out_ref.at[z], local)
    keep.start()
    def at(block, k):
        return out_ref.at[block, pl.ds(k * rows, rows), :]
    def up(t, k, source=None):
        s = at(z - t, k) if source is None else source
        return remote(s, at(z - t, k), up_send.at[t * pieces + k], up_recv.at[t * pieces + k], {"z": z + 1})
    def down(t, k, source=None):
        s = at(z + t, k) if source is None else source
        return remote(s, at(z + t, k), down_send.at[t * pieces + k], down_recv.at[t * pieces + k], {"z": z - 1})
    for k in range(pieces):
        mine = in_ref.at[pl.ds(k * rows, rows), :]
        @pl.when(z < LINE - 1)
        def _():
            up(0, k, mine).start()
        @pl.when(z > 0)
        def _():
            down(0, k, mine).start()
    for t in range(LINE - 1):
        for k in range(pieces):
            @pl.when(z - 1 - t >= 0)
            def _():
                i = t * pieces + k
                remote(at(z - 1 - t, k), at(z - 1 - t, k), up_recv.at[i], up_recv.at[i], {"z": z - 1}).wait_recv()
                @pl.when(z < LINE - 1)
                def _():
                    if t + 1 < LINE - 1:
                        up(t + 1, k).start()
            @pl.when(z + 1 + t < LINE)
            def _():
                i = t * pieces + k
                remote(at(z + 1 + t, k), at(z + 1 + t, k), down_recv.at[i], down_recv.at[i], {"z": z + 1}).wait_recv()
                @pl.when(z > 0)
                def _():
                    if t + 1 < LINE - 1:
                        down(t + 1, k).start()
    for t in range(LINE - 1):
        for k in range(pieces):
            @pl.when((z < LINE - 1) & (z - t >= 0))
            def _():
                up(t, k).wait_send()
            @pl.when((z > 0) & (z + t < LINE))
            def _():
                down(t, k).wait_send()
    keep.wait()

def line_gather(block, collective_id, pieces=4):
    dma = pltpu.SemaphoreType.DMA
    n = (LINE - 1) * pieces
    return pl.pallas_call(
        functools.partial(line_gather_kernel, pieces), out_shape=jax.ShapeDtypeStruct((LINE,) + block.shape, block.dtype),
        in_specs=[pl.BlockSpec(memory_space=pltpu.VMEM)], out_specs=pl.BlockSpec(memory_space=pl.ANY),
        scratch_shapes=[dma((n,)), dma((n,)), dma((n,)), dma((n,)), dma(())],
        compiler_params=pltpu.CompilerParams(collective_id=collective_id, has_side_effects=True),
    )(block)

def line_scatter_kernel(pieces, in_ref, out_ref, up_buf, down_buf, up_stage, down_stage, up_send, up_recv, down_send, down_recv):
    z = lax.axis_index("z")
    rows = in_ref.shape[1] // pieces
    step = 32
    f32, bf = jnp.float32, jnp.bfloat16
    line_greet(z)
    def cut(k):
        return pl.ds(k * rows, rows)
    def add(target, index, a, b, k):
        def body(i, carry):
            r = pl.ds(pl.multiple_of(k * rows + i * step, step), step)
            target[index, r, :] = (a(r).astype(f32) + b(r).astype(f32)).astype(target.dtype)
            return carry
        lax.fori_loop(0, rows // step, body, 0)
    for d in range(LINE - 1, 0, -1):
        for k in range(pieces):
            i = (d - 1) * pieces + k
            @pl.when(z + d < LINE)
            def _():
                @pl.when(z == 0)
                def _():
                    remote(in_ref.at[z + d, cut(k), :], up_buf.at[d - 1, cut(k), :], up_send.at[i], up_recv.at[i], {"z": z + 1}).start()
                @pl.when(z > 0)
                def _():
                    if d + 1 < LINE:
                        j = d * pieces + k
                        remote(up_buf.at[d, cut(k), :], up_buf.at[d, cut(k), :], up_recv.at[j], up_recv.at[j], {"z": z - 1}).wait_recv()
                        add(up_stage, d - 1, lambda r: in_ref[z + d, r, :], lambda r: up_buf[d, r, :], k)
                        remote(up_stage.at[d - 1, cut(k), :], up_buf.at[d - 1, cut(k), :], up_send.at[i], up_recv.at[i], {"z": z + 1}).start()
            @pl.when(z - d >= 0)
            def _():
                @pl.when(z == LINE - 1)
                def _():
                    remote(in_ref.at[z - d, cut(k), :], down_buf.at[d - 1, cut(k), :], down_send.at[i], down_recv.at[i], {"z": z - 1}).start()
                @pl.when(z < LINE - 1)
                def _():
                    if d + 1 < LINE:
                        j = d * pieces + k
                        remote(down_buf.at[d, cut(k), :], down_buf.at[d, cut(k), :], down_recv.at[j], down_recv.at[j], {"z": z + 1}).wait_recv()
                        add(down_stage, d - 1, lambda r: in_ref[z - d, r, :], lambda r: down_buf[d, r, :], k)
                        remote(down_stage.at[d - 1, cut(k), :], down_buf.at[d - 1, cut(k), :], down_send.at[i], down_recv.at[i], {"z": z - 1}).start()
    for k in range(pieces):
        @pl.when(z > 0)
        def _():
            remote(up_buf.at[0, cut(k), :], up_buf.at[0, cut(k), :], up_recv.at[k], up_recv.at[k], {"z": z - 1}).wait_recv()
        @pl.when(z < LINE - 1)
        def _():
            remote(down_buf.at[0, cut(k), :], down_buf.at[0, cut(k), :], down_recv.at[k], down_recv.at[k], {"z": z + 1}).wait_recv()
        def body(i, carry):
            r = pl.ds(pl.multiple_of(k * rows + i * step, step), step)
            own = in_ref[z, r, :].astype(f32)
            @pl.when(z == 0)
            def _():
                out_ref[r, :] = own + down_buf[0, r, :].astype(f32)
            @pl.when(z == LINE - 1)
            def _():
                out_ref[r, :] = own + up_buf[0, r, :].astype(f32)
            @pl.when((z > 0) & (z < LINE - 1))
            def _():
                out_ref[r, :] = own + up_buf[0, r, :].astype(f32) + down_buf[0, r, :].astype(f32)
            return carry
        lax.fori_loop(0, rows // step, body, 0)
    for d in range(LINE - 1, 0, -1):
        for k in range(pieces):
            i = (d - 1) * pieces + k
            @pl.when(z + d < LINE)
            def _():
                remote(up_stage.at[d - 1, cut(k), :], up_buf.at[d - 1, cut(k), :], up_send.at[i], up_recv.at[i], {"z": z + 1}).wait_send()
            @pl.when(z - d >= 0)
            def _():
                remote(down_stage.at[d - 1, cut(k), :], down_buf.at[d - 1, cut(k), :], down_send.at[i], down_recv.at[i], {"z": z - 1}).wait_send()

def line_scatter(terms, collective_id, pieces=4):
    dma = pltpu.SemaphoreType.DMA
    line, rows, columns = terms.shape
    n = (LINE - 1) * pieces
    vm = pltpu.VMEM((LINE - 1, rows, columns), jnp.bfloat16)
    return pl.pallas_call(
        functools.partial(line_scatter_kernel, pieces), out_shape=jax.ShapeDtypeStruct((rows, columns), jnp.float32),
        in_specs=[pl.BlockSpec(memory_space=pltpu.VMEM)], out_specs=pl.BlockSpec(memory_space=pltpu.VMEM),
        scratch_shapes=[vm, vm, vm, vm, dma((n,)), dma((n,)), dma((n,)), dma((n,))],
        compiler_params=pltpu.CompilerParams(collective_id=collective_id, has_side_effects=True, vmem_limit_bytes=40 << 20),
    )(terms)


def everyone(total):
    names = ALL
    sizes = [lax.axis_size(n) for n in names]
    me = 0
    for n, size in zip(names, sizes):
        me = me * size + lax.axis_index(n)

    def device(index):
        where = {}
        for n, size in reversed(list(zip(names, sizes))):
            where[n] = lax.rem(index, size)
            index = index // size
        return where

    barrier = pltpu.get_barrier_semaphore()

    def greet_one(d, carry):
        pl.semaphore_signal(barrier, inc=1, device_id=device(lax.rem(me + d, total)), device_id_type=MESH_ID)
        return carry

    lax.fori_loop(1, total, greet_one, 0)
    pl.semaphore_wait(barrier, total - 1)
    return me, device


def spread_kernel(total, in_ref, out_ref, buffer, send, recv):
    me, device = everyone(total)

    def put(d, carry):
        other = lax.rem(me + d, total)
        remote(in_ref.at[other], buffer.at[me], send.at[d], recv.at[d], device(other)).start()
        return carry

    lax.fori_loop(1, total, put, 0)

    def take(d, carry):
        source = lax.rem(me + total - d, total)
        other = lax.rem(me + d, total)
        remote(buffer.at[source], buffer.at[source], recv.at[d], recv.at[d], device(source)).wait_recv()
        remote(in_ref.at[other], buffer.at[me], send.at[d], recv.at[d], device(other)).wait_send()
        return carry

    lax.fori_loop(1, total, take, 0)
    out_ref[...] = in_ref[me]

    def add(d, carry):
        out_ref[...] += buffer[lax.rem(me + d, total)]
        return carry

    lax.fori_loop(1, total, add, 0)


def spread_sum(tiles, collective_id):
    dma = pltpu.SemaphoreType.DMA
    total = tiles.shape[0]
    vmem = pl.BlockSpec(memory_space=pltpu.VMEM)
    return pl.pallas_call(
        functools.partial(spread_kernel, total),
        out_shape=jax.ShapeDtypeStruct(tiles.shape[1:], tiles.dtype),
        in_specs=[vmem],
        out_specs=vmem,
        scratch_shapes=[pltpu.VMEM(tiles.shape, tiles.dtype), dma((total,)), dma((total,))],
        compiler_params=pltpu.CompilerParams(collective_id=collective_id, has_side_effects=True),
    )(tiles)


def root_mean_scale(values, gains):
    return values * lax.rsqrt(jnp.mean(values * values, axis=-1, keepdims=True) + 1e-06) * gains


def rope_tables(positions):
    steps_half = jnp.arange(HEAD_SIZE // 2).astype(jnp.float32)
    inverse = jnp.power(1000000.0, steps_half * (-2.0 / HEAD_SIZE))
    angles = positions.astype(jnp.float32)[..., None] * inverse
    angles = jnp.concatenate([angles, angles], axis=-1)
    return (jnp.cos(angles)[..., None, :], jnp.sin(angles)[..., None, :])


def rotary_apply(values, cosine_factor, sine_factor):
    half_dim = values.shape[-1] // 2
    turned = jnp.concatenate([-values[..., half_dim:], values[..., :half_dim]], axis=-1)
    return values * cosine_factor + turned * sine_factor


def matrix_product(left, right):
    return jnp.dot(left, right, preferred_element_type=jnp.float32)


def contract_last(left, right):
    return lax.dot_general(
        left, right, (((1,), (1,)), ((), ())), preferred_element_type=jnp.float32
    )


def contract_first(left, right):
    return lax.dot_general(
        left, right, (((0,), (0,)), ((), ())), preferred_element_type=jnp.float32
    )


def low(values):
    return values.astype(jnp.bfloat16)


def make_shards(cells):
    data_total = cells * PLANES

    def scatter_tokens(terms):
        return scatter_blocks(low(terms).reshape(RANKS, -1, terms.shape[1]))

    def split_units(weight):
        rows, units = weight.shape
        piece = units // (RANKS * data_total)
        split = weight.reshape(rows, CORNERS**2, data_total, CORNERS, piece)
        return jnp.transpose(split, (0, 1, 3, 2, 4)).reshape(rows, RANKS, units // RANKS)

    def join_units(parts):
        ranks, rows, units = parts.shape
        split = parts.reshape(CORNERS**2, CORNERS, rows, data_total, units // data_total)
        return jnp.transpose(split, (2, 0, 3, 1, 4)).reshape(rows, ranks * units)

    def split_columns(weight):
        return weight.reshape(weight.shape[0], RANKS, -1)

    def join_columns(parts):
        return jnp.transpose(parts, (1, 0, 2)).reshape(parts.shape[1], -1)

    def send_columns(pieces):
        return jnp.transpose(jnp.concatenate(pieces, axis=-1), (1, 0, 2))

    def gather_columns(mine):
        rows, columns = mine.shape[1:]
        every = lax.all_gather(mine, DATA, axis=0, tiled=False)
        every = every.reshape(data_total, CORNERS**2, CORNERS, rows, columns)
        return jnp.transpose(every, (1, 0, 2, 3, 4)).reshape(-1, columns)

    def scatter_columns(term, collective_id):
        rows = term.shape[0] // (RANKS * data_total)
        split = low(term).reshape(CORNERS**2, data_total, CORNERS, rows, -1)
        split = jnp.transpose(split, (1, 0, 2, 3, 4)).reshape(data_total * RANKS, rows, -1)
        mine = lax.psum_scatter(split, DATA, scatter_dimension=0, tiled=True)
        return swap(mine, collective_id).astype(jnp.float32)

    inner = CORNERS * data_total
    to_rank = []
    for source in range(inner):
        rank_y, place = divmod(source, data_total)
        to_rank.append((source, place * CORNERS + rank_y))
    from_rank = [(b, a) for a, b in to_rank]
    INNER = ("cell", "z", "y")

    def shards(
        hidden_in,
        query_weight,
        key_matrix,
        value_matrix,
        gate_weight,
        out_weight,
        norm_attn,
        query_gain,
        key_gain,
        norm_ffn,
        ffn_gate,
        ffn_up,
        ffn_down,
        cotangent,
        sequence_numbers,
        positions,
    ):
        rows = hidden_in.shape[0]
        tokens = rows * RANKS
        groups = CORNERS**2
        window = GROUP_TOKENS // PLANES
        repeat = QUERY_HEADS // KEY_VALUE_HEADS
        query_columns = QUERY_HEADS * HEAD_SIZE // RANKS
        key_columns = KEY_VALUE_HEADS * HEAD_SIZE // RANKS
        scale_qk = 1.0 / math.sqrt(HEAD_SIZE)

        sizes = [norm_attn.shape[0], norm_ffn.shape[0], query_gain.shape[0], key_gain.shape[0]]
        cuts = [0]
        for size in sizes:
            cuts.append(cuts[-1] + size)
        tile = (8, HEAD_SIZE)
        pad = tile[0] * tile[1] - cuts[-1]
        own_gains = jnp.concatenate([norm_attn, norm_ffn, query_gain, key_gain]).astype(jnp.float32)
        own_gains = jnp.pad(own_gains, (0, pad)).reshape(tile)
        plane = lax.axis_index("z")
        group_start = lax.axis_index("cell") * GROUP_TOKENS
        marks = jnp.concatenate(
            [
                lax.dynamic_slice_in_dim(sequence_numbers, group_start, GROUP_TOKENS),
                lax.dynamic_slice_in_dim(positions, group_start, GROUP_TOKENS),
            ]
        ).reshape(-1, HEAD_SIZE)
        gains, marks, attn_columns = hello(
            RANKS * data_total,
            own_gains,
            marks,
            send_columns(
                [
                    split_columns(query_weight),
                    split_columns(key_matrix),
                    split_columns(value_matrix),
                    split_columns(gate_weight),
                ]
            ),
            2,
        )
        gains = gains.reshape(RANKS * data_total, -1)
        gain_attn, gain_ffn, gain_query, gain_key = (
            gains[:, a:b].reshape(-1) for a, b in zip(cuts[:-1], cuts[1:])
        )
        w_attn = gather_columns(attn_columns)
        w_out = lax.all_gather(
            lax.ppermute(out_weight, INNER, to_rank), DATA, axis=0, tiled=True
        )
        w_down = lax.all_gather(ffn_down, DATA, axis=0, tiled=True)

        marks = marks.reshape(groups, 2, GROUP_TOKENS)
        key_seq, key_pos = marks[:, 0], marks[:, 1]
        own = lax.dynamic_slice_in_dim(marks, plane * window, window, axis=2)
        own_seq, own_pos = own[:, 0], own[:, 1]
        cosine_factor, sine_factor = rope_tables(own_pos)
        allowed = (key_pos[:, None, :] <= own_pos[:, :, None]) & (
            (key_seq[:, None, :] == 0) | (key_seq[:, None, :] == own_seq[:, :, None])
        )

        def prepare_heads(raw_values, gain_values):
            return rotary_apply(
                root_mean_scale(raw_values, gain_values), cosine_factor, sine_factor
            )

        hidden = hidden_in.astype(jnp.float32)
        normed_input = gather_tokens(low(root_mean_scale(hidden, gain_attn)))
        w_ffn = gather_columns(swap(send_columns([split_units(ffn_gate), split_units(ffn_up)]), 3))
        raw = matrix_product(normed_input, w_attn)
        a, b, c = query_columns, query_columns + key_columns, query_columns + 2 * key_columns
        query_raw = raw[:, :a].reshape(groups, window, repeat, HEAD_SIZE)
        key_raw = raw[:, a:b].reshape(groups, window, 1, HEAD_SIZE)
        value_low = low(raw[:, b:c]).reshape(groups, window, HEAD_SIZE)
        gate_sig = jax.nn.sigmoid(raw[:, c:])
        query_low = low(prepare_heads(query_raw, gain_query))
        key_low = low(prepare_heads(key_raw, gain_key)).reshape(groups, window, HEAD_SIZE)
        pair = line_gather(
            jnp.concatenate([key_low, value_low], axis=-1).reshape(tokens, 2 * HEAD_SIZE), 5
        )
        pair = pair.reshape(PLANES, groups, window, 2 * HEAD_SIZE)
        pair = jnp.transpose(pair, (1, 0, 2, 3)).reshape(groups, GROUP_TOKENS, 2 * HEAD_SIZE)
        keys_all, values_all = pair[..., :HEAD_SIZE], pair[..., HEAD_SIZE:]

        scores = (
            jnp.einsum("gqrd,gkd->grqk", query_low, keys_all, preferred_element_type=jnp.float32)
            * scale_qk
        )
        masked = jnp.where(allowed[:, None], scores, -1e30)
        peak = jnp.max(masked, axis=-1, keepdims=True)
        exponent = jnp.exp(masked - peak)
        probs = exponent / jnp.sum(exponent, axis=-1, keepdims=True)
        probs_low = low(probs)
        attended = jnp.einsum(
            "grqk,gkd->gqrd", probs_low, values_all, preferred_element_type=jnp.float32
        )
        attended_rows = attended.reshape(tokens, query_columns)
        gated_low = low(attended_rows * gate_sig)
        middle = hidden + scatter_tokens(matrix_product(gated_low, w_out))

        normed_two = gather_tokens(low(root_mean_scale(middle, gain_ffn)))
        both = matrix_product(normed_two, w_ffn)
        units = both.shape[1] // 2
        gate_ffn, up_ffn = both[:, :units], both[:, units:]
        ffn_sig = jax.nn.sigmoid(gate_ffn)
        mixed_low = low(gate_ffn * ffn_sig * up_ffn)
        output = low(middle + scatter_tokens(matrix_product(mixed_low, w_down)))

        cotangent_all = gather_tokens(cotangent)
        d_mixed = contract_last(cotangent_all, w_down)
        d_up_low = low(d_mixed * gate_ffn * ffn_sig)
        d_gate_ffn_low = low(d_mixed * up_ffn * ffn_sig * (1.0 + gate_ffn * (1.0 - ffn_sig)))
        d_both = jnp.concatenate([d_gate_ffn_low, d_up_low], axis=-1)
        d_normed_two = scatter_tokens(contract_last(d_both, w_ffn))
        grad_down = lax.psum_scatter(
            low(contract_first(mixed_low, cotangent_all)), DATA, scatter_dimension=0, tiled=True
        ).astype(jnp.float32)
        grad_both = scatter_columns(contract_first(normed_two, d_both), 3)
        grad_gate = join_units(grad_both[..., :units])
        grad_up = join_units(grad_both[..., units:])
        unused_two, norm_two_back = jax.vjp(root_mean_scale, middle, gain_ffn)
        d_middle_norm, grad_norm_two_term = norm_two_back(d_normed_two)
        d_middle = cotangent.astype(jnp.float32) + d_middle_norm

        branch_all = gather_tokens(low(d_middle))
        d_gated = contract_last(branch_all, w_out)
        grad_out = lax.psum_scatter(
            low(contract_first(gated_low, branch_all)), DATA, scatter_dimension=0, tiled=True
        )
        grad_out = lax.ppermute(grad_out, INNER, from_rank).astype(jnp.float32)
        d_attended = low(d_gated * gate_sig)
        d_gate_low = low(d_gated * attended_rows * gate_sig * (1.0 - gate_sig))
        d_heads = d_attended.reshape(groups, window, repeat, HEAD_SIZE)
        row_delta = jnp.transpose(
            jnp.sum(d_heads.astype(jnp.float32) * attended, axis=-1), (0, 2, 1)
        )
        d_probs = jnp.einsum(
            "gqrd,gkd->grqk", d_heads, values_all, preferred_element_type=jnp.float32
        )
        d_scores = low(probs * (d_probs - row_delta[..., None]))
        d_query_rot = (
            jnp.einsum("grqk,gkd->gqrd", d_scores, keys_all, preferred_element_type=jnp.float32)
            * scale_qk
        )
        d_keys = (
            jnp.einsum("grqk,gqrd->gkd", d_scores, query_low, preferred_element_type=jnp.float32)
            * scale_qk
        )
        d_values = jnp.einsum(
            "grqk,gqrd->gkd", probs_low, d_heads, preferred_element_type=jnp.float32
        )
        d_pair = low(jnp.concatenate([d_keys, d_values], axis=-1))
        d_pair = jnp.transpose(
            d_pair.reshape(groups, PLANES, window, 2 * HEAD_SIZE), (1, 0, 2, 3)
        )
        d_pair = line_scatter(d_pair.reshape(PLANES, tokens, 2 * HEAD_SIZE), 6)
        d_pair = d_pair.reshape(groups, window, 2 * HEAD_SIZE)
        d_key_rot, d_value = d_pair[..., :HEAD_SIZE], d_pair[..., HEAD_SIZE:]
        unused_query, query_back = jax.vjp(prepare_heads, query_raw, gain_query)
        d_query_raw, grad_query_gain_term = query_back(d_query_rot)
        unused_key, key_back = jax.vjp(prepare_heads, key_raw, gain_key)
        d_key_raw, grad_key_gain_term = key_back(d_key_rot[:, :, None, :])
        d_raw = jnp.concatenate(
            [
                low(d_query_raw.reshape(tokens, query_columns)),
                low(d_key_raw.reshape(tokens, key_columns)),
                low(d_value.reshape(tokens, key_columns)),
                d_gate_low,
            ],
            axis=-1,
        )
        d_normed = scatter_tokens(contract_last(d_raw, w_attn))
        grad_attn = scatter_columns(contract_first(normed_input, d_raw), 4)
        grad_query = join_columns(grad_attn[..., :a])
        grad_key = join_columns(grad_attn[..., a:b])
        grad_value = join_columns(grad_attn[..., b:c])
        grad_gatew = join_columns(grad_attn[..., c:])
        unused_one, norm_one_back = jax.vjp(root_mean_scale, hidden, gain_attn)
        d_hidden_norm, grad_norm_one_term = norm_one_back(d_normed)
        input_grad = d_middle + d_hidden_norm

        terms = jnp.concatenate(
            [
                t.reshape(RANKS * data_total, -1)
                for t in (
                    grad_norm_one_term,
                    grad_norm_two_term,
                    grad_query_gain_term,
                    grad_key_gain_term,
                )
            ],
            axis=-1,
        )
        terms = jnp.pad(terms, ((0, 0), (0, pad))).reshape((-1,) + tile)
        small = spread_sum(terms, 7).reshape(-1)
        grad_norm_attn, grad_norm_ffn, grad_query_gain, grad_key_gain = (
            small[s:e] for s, e in zip(cuts[:-1], cuts[1:])
        )
        return (
            output,
            input_grad,
            grad_query,
            grad_key,
            grad_value,
            grad_gatew,
            grad_out,
            grad_norm_attn,
            grad_query_gain,
            grad_key_gain,
            grad_norm_ffn,
            grad_gate,
            grad_up,
            grad_down,
        )

    return shards


def solution(mesh):
    cells = mesh.shape["fsdp"] // (PLANES * CORNERS)
    split = Mesh(
        mesh.devices.reshape(CORNERS, CORNERS, cells, PLANES, CORNERS),
        ALL,
    )
    rows, flat, group = P(ALL, None), P(ALL), P(("x", "core"))
    return jax.shard_map(
        make_shards(cells),
        mesh=split,
        in_specs=(rows,) * 6 + (flat,) * 4 + (rows,) * 4 + (group,) * 2,
        out_specs=(rows,) * 7 + (flat,) * 4 + (rows,) * 3,
        check_vma=False,
    )
```

```python
import functools
import math

import jax
import jax.numpy as jnp
from jax import lax
from jax.experimental import pallas as pl
from jax.experimental.pallas import tpu as pltpu
from jax.sharding import Mesh
from jax.sharding import PartitionSpec as P

QUERY_HEADS = 16
KEY_VALUE_HEADS = 8
HEAD_SIZE = 128
GROUP_TOKENS = 2048
CORNERS = 2
PLANES = 4
ALL = ("x", "core", "cell", "z", "y")
TENSOR = ("x", "core", "y")
DATA = ("cell", "z")
RANKS = CORNERS**3
CHUNKS = 4
MESH_ID = pl.DeviceIdType.MESH
OTHERS = [(dx, dc, dy) for dx in (0, 1) for dc in (0, 1) for dy in (0, 1) if dx + dc + dy]
DMA = pltpu.SemaphoreType.DMA
VMEM = pl.BlockSpec(memory_space=pltpu.VMEM)
ANYWHERE = pl.BlockSpec(memory_space=pl.ANY)


def remote(source, target, send, receive, device):
    return pltpu.make_async_remote_copy(
        src_ref=source,
        dst_ref=target,
        send_sem=send,
        recv_sem=receive,
        device_id=device,
        device_id_type=MESH_ID,
    )


def landed(ref, sem, device):
    remote(ref, ref, sem, sem, device).wait_recv()


def corner():
    return lax.axis_index("x"), lax.axis_index("core"), lax.axis_index("y")


def slot(x, c, y):
    return (x * CORNERS + c) * CORNERS + y


def flip(value, bit):
    return 1 - value if bit else value


def neighbours():
    x, c, y = corner()
    return {"x": 1 - x}, {"y": 1 - y}, {"core": 1 - c}


def plane_peers():
    x, c, y = corner()
    peers = []
    for dx, dc, dy in OTHERS:
        px, pc, py = flip(x, dx), flip(c, dc), flip(y, dy)
        peers.append(({"x": px, "core": pc, "y": py}, slot(px, pc, py)))
    return peers


def greet(plane, line):
    barrier = pltpu.get_barrier_semaphore()
    near = {"near": neighbours(), "all": [p for p, _ in plane_peers()], None: []}[plane]
    for device in near:
        pl.semaphore_signal(barrier, inc=1, device_id=device, device_id_type=MESH_ID)
    if not line:
        pl.semaphore_wait(barrier, len(near))
        return
    z = lax.axis_index("z")

    @pl.when(z > 0)
    def _():
        pl.semaphore_signal(barrier, inc=1, device_id={"z": z - 1}, device_id_type=MESH_ID)

    @pl.when(z < PLANES - 1)
    def _():
        pl.semaphore_signal(barrier, inc=1, device_id={"z": z + 1}, device_id_type=MESH_ID)

    edge = (z == 0) | (z == PLANES - 1)

    @pl.when(edge)
    def _():
        pl.semaphore_wait(barrier, len(near) + 1)

    @pl.when(jnp.logical_not(edge))
    def _():
        pl.semaphore_wait(barrier, len(near) + 2)


class Part:
    def __init__(self, inputs, outs, scratch, steps, plane=None, line=False):
        self.inputs = inputs
        self.outs = outs
        self.scratch = scratch
        self.steps = steps
        self.plane, self.line = plane, line


def run_kernel(parts, kept, *refs):
    refs = list(refs)

    def take(counts):
        groups = []
        for count in counts:
            groups.append(refs[:count])
            del refs[:count]
        return groups

    ins = take([len(p.inputs) for p in parts])
    outs = take([len(p.outs) for p in parts])
    scratch = take([len(p.scratch) for p in parts])
    ranks = [None, "near", "all"]
    plane = ranks[max(ranks.index(p.plane) for p in parts)]
    greet(plane, any(p.line for p in parts))
    plans = [p.steps(i, o, s) for p, i, o, s in zip(parts, ins, outs, scratch)]
    for first, _, _ in plans:
        first()
    ordered = []
    for _, middle, _ in plans:
        ordered += [((n + 0.5) / len(middle), step) for n, step in enumerate(middle)]
    for _, step in sorted(ordered, key=lambda pair: pair[0]):
        step()
    for _, _, last in plans:
        last()


def run(parts, collective_id, vmem=None):
    inputs = [pair for p in parts for pair in p.inputs]
    outs = [pair for p in parts for pair in p.outs]
    return pl.pallas_call(
        functools.partial(run_kernel, parts, None),
        out_shape=[shape for shape, _ in outs],
        in_specs=[spec for _, spec in inputs],
        out_specs=[spec for _, spec in outs],
        scratch_shapes=[s for p in parts for s in p.scratch],
        compiler_params=pltpu.CompilerParams(
            collective_id=collective_id,
            has_side_effects=True,
            vmem_limit_bytes=None if vmem is None else vmem << 20,
        ),
    )(*[array for array, _ in inputs])


def gather_part(block):
    rows, columns = block.shape
    n, half = CHUNKS, CHUNKS // 2
    chunk = rows // n

    def steps(ins, outs, scratch):
        (in_ref,), (out_ref,) = ins, outs
        send_x, send_y, send_c, recv_x, recv_y, recv_c, local = scratch
        x, c, y = corner()
        dev_x, dev_y, dev_c = neighbours()

        def at(index, k):
            start = pl.multiple_of(index * rows + k * chunk, chunk)
            return out_ref.at[pl.ds(start, chunk), :]

        own, beside_x, beside_y = slot(x, c, y), slot(1 - x, c, y), slot(x, c, 1 - y)
        across = slot(1 - x, c, 1 - y)
        mirror = [
            slot(x, 1 - c, y),
            slot(1 - x, 1 - c, y),
            slot(x, 1 - c, 1 - y),
            slot(1 - x, 1 - c, 1 - y),
        ]
        start = pl.multiple_of(own * rows, rows)
        keep = pltpu.make_async_copy(in_ref, out_ref.at[pl.ds(start, rows), :], local)
        sent = []

        def go(copy):
            copy.start()
            sent.append(copy)

        def share(index, k, b):
            go(remote(at(index, k), at(index, k), send_c.at[b * n + k], recv_c.at[b * n + k], dev_c))

        order_x = list(range(n))
        order_y = order_x[half:] + order_x[:half]

        def first():
            keep.start()

            def mine(k):
                return in_ref.at[pl.ds(k * chunk, chunk), :]

            for k, j in zip(order_x, order_y):
                go(remote(mine(k), at(own, k), send_x.at[k], recv_x.at[k], dev_x))
                go(remote(mine(j), at(own, j), send_y.at[j], recv_y.at[j], dev_y))
            for k in range(n):
                go(remote(mine(k), at(own, k), send_c.at[k], recv_c.at[k], dev_c))

        def straight(k, j):
            landed(at(beside_x, k), recv_x.at[k], dev_x)
            if k < half:
                to = at(beside_x, k)
                go(remote(to, to, send_y.at[n + k], recv_y.at[n + k], dev_y))
            share(beside_x, k, 1)
            landed(at(beside_y, j), recv_y.at[j], dev_y)
            if j >= half:
                to = at(beside_y, j)
                go(remote(to, to, send_x.at[half + j], recv_x.at[half + j], dev_x))
            share(beside_y, j, 2)

        def diagonal(k):
            landed(at(across, k), recv_y.at[n + k], dev_y)
            share(across, k, 3)
            landed(at(across, half + k), recv_x.at[n + k], dev_x)
            share(across, half + k, 3)

        def last():
            for b in range(4):
                for k in range(n):
                    landed(at(mirror[b], k), recv_c.at[b * n + k], dev_c)
            for copy in sent:
                copy.wait_send()
            keep.wait()

        middle = [functools.partial(straight, k, j) for k, j in zip(order_x, order_y)]
        middle += [functools.partial(diagonal, k) for k in range(half)]
        return first, middle, last

    link = DMA((n + half,))
    core = DMA((4 * n,))
    return Part(
        [(block, VMEM)],
        [(jax.ShapeDtypeStruct((RANKS * rows, columns), block.dtype), ANYWHERE)],
        [link, link, core, link, link, core, DMA(())],
        steps,
        plane="near",
    )


def add_rows(target, start, count, sources, step=16):
    def body(i, carry):
        r = pl.multiple_of(start + i * step, step)
        total = None
        for ref, shift in sources:
            value = ref[pl.ds(r - shift if shift else r, step), :].astype(jnp.float32)
            total = value if total is None else total + value
        target[pl.ds(r, step), :] = total.astype(target.dtype)
        return carry

    lax.fori_loop(0, count // step, body, 0)


def scatter_part(terms):
    ranks, rows, columns = terms.shape
    n, half = CHUNKS, CHUNKS // 2
    chunk = rows // n
    middle_row = half * chunk

    def steps(ins, outs, scratch):
        (part_ref,), (out_ref,) = ins, outs
        core_buf, x_buf, y_buf, x_diag, y_diag, d_sum, x_sum, y_sum = scratch[:8]
        send_c, recv_c, send_x, recv_x, send_y, recv_y = scratch[8:]
        x, c, y = corner()
        dev_x, dev_y, dev_c = neighbours()
        D, X, Y, O = range(4)
        place = [(1 - x, 1 - y), (1 - x, y), (x, 1 - y), (x, y)]
        mine = [slot(px, c, py) for px, py in place]
        theirs = [slot(px, 1 - c, py) for px, py in place]
        orders = {D: [], X: list(range(n)), O: list(range(n))}
        for k in range(half):
            orders[D] += [k, half + k]
        orders[Y] = orders[X][half:] + orders[X][:half]
        sent = []

        def go(copy):
            copy.start()
            sent.append(copy)

        def piece(k):
            return pl.ds(k * chunk, chunk)

        def first():
            for b in (D, X, Y, O):
                for k in orders[b]:
                    source = part_ref.at[theirs[b], piece(k), :]
                    i = b * n + k
                    go(remote(source, core_buf.at[b, piece(k), :], send_c.at[i], recv_c.at[i], dev_c))

        def chip(target, b, k, *more):
            landed(core_buf.at[b, piece(k), :], recv_c.at[b * n + k], dev_c)
            sources = [(part_ref.at[mine[b]], 0), (core_buf.at[b], 0), *more]
            add_rows(target, k * chunk, chunk, sources)

        def to_x(k):
            go(remote(x_sum.at[piece(k), :], x_buf.at[piece(k), :], send_x.at[k], recv_x.at[k], dev_x))

        def to_y(k):
            go(remote(y_sum.at[piece(k), :], y_buf.at[piece(k), :], send_y.at[k], recv_y.at[k], dev_y))

        def diagonal(k):
            chip(d_sum, D, k)
            source = d_sum.at[piece(k), :]
            if k < half:
                go(remote(source, x_diag.at[piece(k), :], send_x.at[n + k], recv_x.at[n + k], dev_x))
            else:
                to = y_diag.at[piece(k - half), :]
                go(remote(source, to, send_y.at[half + k], recv_y.at[half + k], dev_y))

        def direct(k):
            chip(x_sum, X, k)
            to_x(k)
            chip(y_sum, Y, half + k)
            to_y(half + k)

        def relayed(k):
            landed(y_diag.at[piece(k), :], recv_y.at[n + k], dev_y)
            chip(x_sum, X, half + k, (y_diag, middle_row))
            to_x(half + k)
            landed(x_diag.at[piece(k), :], recv_x.at[n + k], dev_x)
            chip(y_sum, Y, k, (x_diag, 0))
            to_y(k)

        def own(k):
            landed(x_buf.at[piece(k), :], recv_x.at[k], dev_x)
            landed(y_buf.at[piece(k), :], recv_y.at[k], dev_y)
            chip(out_ref, O, k, (x_buf, 0), (y_buf, 0))

        def last():
            for copy in sent:
                copy.wait_send()

        middle = [functools.partial(diagonal, k) for k in orders[D]]
        middle += [functools.partial(direct, k) for k in range(half)]
        middle += [functools.partial(relayed, k) for k in range(half)]
        middle += [functools.partial(own, k) for k in range(n)]
        return first, middle, last

    def low_vmem(*shape):
        return pltpu.VMEM(shape, jnp.bfloat16)

    whole, part = low_vmem(rows, columns), low_vmem(rows // 2, columns)
    link = DMA((n + half,))
    core = DMA((4 * n,))
    return Part(
        [(terms, VMEM)],
        [(jax.ShapeDtypeStruct((rows, columns), jnp.float32), VMEM)],
        [low_vmem(4, rows, columns), whole, whole, part, part, whole, whole, whole]
        + [core, core, link, link, link, link],
        steps,
        plane="near",
    )


def swap_part(blocks):
    def steps(ins, outs, scratch):
        (in_ref,), (out_ref,) = ins, outs
        send, recv, local = scratch
        own = slot(*corner())
        keep = pltpu.make_async_copy(in_ref.at[own], out_ref.at[own], local)
        peers = plane_peers()
        sent = []

        def first():
            keep.start()
            for i, (there, other) in enumerate(peers):
                copy = remote(in_ref.at[other], out_ref.at[own], send.at[i], recv.at[i], there)
                copy.start()
                sent.append(copy)

        def last():
            for i, (there, other) in enumerate(peers):
                landed(out_ref.at[other], recv.at[i], there)
            for copy in sent:
                copy.wait_send()
            keep.wait()

        return first, [], last

    n = len(OTHERS)
    return Part(
        [(blocks, VMEM)],
        [(jax.ShapeDtypeStruct(blocks.shape, blocks.dtype), ANYWHERE)],
        [DMA((n,)), DMA((n,)), DMA(())],
        steps,
        plane="all",
    )


def line_gather_part(block, pieces=4):
    rows = block.shape[0] // pieces

    def steps(ins, outs, scratch):
        (in_ref,), (out_ref,) = ins, outs
        up_send, up_recv, down_send, down_recv, local = scratch
        z = lax.axis_index("z")
        keep = pltpu.make_async_copy(in_ref, out_ref.at[z], local)

        def at(block, k):
            return out_ref.at[block, pl.ds(k * rows, rows), :]

        def up(t, k, source=None):
            s = at(z - t, k) if source is None else source
            i = t * pieces + k
            return remote(s, at(z - t, k), up_send.at[i], up_recv.at[i], {"z": z + 1})

        def down(t, k, source=None):
            s = at(z + t, k) if source is None else source
            i = t * pieces + k
            return remote(s, at(z + t, k), down_send.at[i], down_recv.at[i], {"z": z - 1})

        def first():
            keep.start()
            for k in range(pieces):
                mine = in_ref.at[pl.ds(k * rows, rows), :]

                @pl.when(z < PLANES - 1)
                def _():
                    up(0, k, mine).start()

                @pl.when(z > 0)
                def _():
                    down(0, k, mine).start()

        def arrive(t, k):
            i = t * pieces + k
            on = t + 1 < PLANES - 1

            @pl.when(z - 1 - t >= 0)
            def _():
                landed(at(z - 1 - t, k), up_recv.at[i], {"z": z - 1})
                if on:

                    @pl.when(z < PLANES - 1)
                    def _():
                        up(t + 1, k).start()

            @pl.when(z + 1 + t < PLANES)
            def _():
                landed(at(z + 1 + t, k), down_recv.at[i], {"z": z + 1})
                if on:

                    @pl.when(z > 0)
                    def _():
                        down(t + 1, k).start()

        def last():
            for t in range(PLANES - 1):
                for k in range(pieces):

                    @pl.when((z < PLANES - 1) & (z - t >= 0))
                    def _():
                        up(t, k).wait_send()

                    @pl.when((z > 0) & (z + t < PLANES))
                    def _():
                        down(t, k).wait_send()

            keep.wait()

        middle = [
            functools.partial(arrive, t, k) for t in range(PLANES - 1) for k in range(pieces)
        ]
        return first, middle, last

    sems = DMA(((PLANES - 1) * pieces,))
    return Part(
        [(block, VMEM)],
        [(jax.ShapeDtypeStruct((PLANES,) + block.shape, block.dtype), ANYWHERE)],
        [sems, sems, sems, sems, DMA(())],
        steps,
        line=True,
    )


def line_scatter_part(terms, pieces=4):
    line, all_rows, columns = terms.shape
    rows = all_rows // pieces
    step = 32

    def steps(ins, outs, scratch):
        (in_ref,), (out_ref,) = ins, outs
        up_buf, down_buf, up_stage, down_stage, up_send, up_recv, down_send, down_recv = scratch
        z = lax.axis_index("z")
        f32 = jnp.float32

        def cut(k):
            return pl.ds(k * rows, rows)

        def send_up(source, d, k):
            i = (d - 1) * pieces + k
            return remote(source, up_buf.at[d - 1, cut(k), :], up_send.at[i], up_recv.at[i], {"z": z + 1})

        def send_down(source, d, k):
            i = (d - 1) * pieces + k
            to = down_buf.at[d - 1, cut(k), :]
            return remote(source, to, down_send.at[i], down_recv.at[i], {"z": z - 1})

        def first():
            pass

        def pass_on(d, k):
            @pl.when(z + d < line)
            def _():
                @pl.when(z == 0)
                def _():
                    send_up(in_ref.at[z + d, cut(k), :], d, k).start()

                if d + 1 < line:

                    @pl.when(z > 0)
                    def _():
                        landed(up_buf.at[d, cut(k), :], up_recv.at[d * pieces + k], {"z": z - 1})
                        sources = [(in_ref.at[z + d], 0), (up_buf.at[d], 0)]
                        add_rows(up_stage.at[d - 1], k * rows, rows, sources, step)
                        send_up(up_stage.at[d - 1, cut(k), :], d, k).start()

            @pl.when(z - d >= 0)
            def _():
                @pl.when(z == line - 1)
                def _():
                    send_down(in_ref.at[z - d, cut(k), :], d, k).start()

                if d + 1 < line:

                    @pl.when(z < line - 1)
                    def _():
                        landed(down_buf.at[d, cut(k), :], down_recv.at[d * pieces + k], {"z": z + 1})
                        sources = [(in_ref.at[z - d], 0), (down_buf.at[d], 0)]
                        add_rows(down_stage.at[d - 1], k * rows, rows, sources, step)
                        send_down(down_stage.at[d - 1, cut(k), :], d, k).start()

        def own(k):
            @pl.when(z > 0)
            def _():
                landed(up_buf.at[0, cut(k), :], up_recv.at[k], {"z": z - 1})

            @pl.when(z < line - 1)
            def _():
                landed(down_buf.at[0, cut(k), :], down_recv.at[k], {"z": z + 1})

            mine, below, above = (in_ref.at[z], 0), (up_buf.at[0], 0), (down_buf.at[0], 0)

            @pl.when(z == 0)
            def _():
                add_rows(out_ref, k * rows, rows, [mine, above], step)

            @pl.when(z == line - 1)
            def _():
                add_rows(out_ref, k * rows, rows, [mine, below], step)

            @pl.when((z > 0) & (z < line - 1))
            def _():
                add_rows(out_ref, k * rows, rows, [mine, below, above], step)

        def last():
            for d in range(line - 1, 0, -1):
                for k in range(pieces):

                    @pl.when(z + d < line)
                    def _():
                        send_up(up_stage.at[d - 1, cut(k), :], d, k).wait_send()

                    @pl.when(z - d >= 0)
                    def _():
                        send_down(down_stage.at[d - 1, cut(k), :], d, k).wait_send()

        middle = [
            functools.partial(pass_on, d, k) for d in range(line - 1, 0, -1) for k in range(pieces)
        ]
        middle += [functools.partial(own, k) for k in range(pieces)]
        return first, middle, last

    sems = DMA(((line - 1) * pieces,))
    buffer = pltpu.VMEM((line - 1, all_rows, columns), jnp.bfloat16)
    return Part(
        [(terms, VMEM)],
        [(jax.ShapeDtypeStruct((all_rows, columns), jnp.float32), VMEM)],
        [buffer, buffer, buffer, buffer, sems, sems, sems, sems],
        steps,
        line=True,
    )


def everyone(total):
    sizes = [lax.axis_size(n) for n in ALL]
    me = 0
    for n, size in zip(ALL, sizes):
        me = me * size + lax.axis_index(n)

    def device(index):
        where = {}
        for n, size in reversed(list(zip(ALL, sizes))):
            where[n] = lax.rem(index, size)
            index = index // size
        return where

    barrier = pltpu.get_barrier_semaphore()

    def greet_one(d, carry):
        other = device(lax.rem(me + d, total))
        pl.semaphore_signal(barrier, inc=1, device_id=other, device_id_type=MESH_ID)
        return carry

    lax.fori_loop(1, total, greet_one, 0)
    pl.semaphore_wait(barrier, total - 1)
    return me, device


def hello_kernel(total, gains_ref, marks_ref, gains_out, marks_out, g_send, g_recv, m_send, m_recv, local):
    me, device = everyone(total)
    x, c, y = corner()
    group = x * CORNERS + c
    keeps = [
        pltpu.make_async_copy(gains_ref, gains_out.at[me], local.at[0]),
        pltpu.make_async_copy(marks_ref, marks_out.at[group], local.at[1]),
    ]
    for keep in keeps:
        keep.start()
    sent = []
    near = [(i, dx, dc) for i, (dx, dc) in enumerate([(0, 1), (1, 0), (1, 1)])]
    for i, dx, dc in near:
        there = {"x": flip(x, dx), "core": flip(c, dc)}
        copy = remote(marks_ref, marks_out.at[group], m_send.at[i], m_recv.at[i], there)
        copy.start()
        sent.append(copy)

    def give(d):
        other = device(lax.rem(me + d, total))
        return remote(gains_ref, gains_out.at[me], g_send.at[d], g_recv.at[d], other)

    def put(d, carry):
        give(d).start()
        return carry

    lax.fori_loop(1, total, put, 0)

    def take(d, carry):
        source = lax.rem(me + total - d, total)
        landed(gains_out.at[source], g_recv.at[d], device(source))
        give(d).wait_send()
        return carry

    lax.fori_loop(1, total, take, 0)
    for i, dx, dc in near:
        there = {"x": flip(x, dx), "core": flip(c, dc)}
        landed(marks_out.at[flip(x, dx) * CORNERS + flip(c, dc)], m_recv.at[i], there)
    for copy in sent:
        copy.wait_send()
    for keep in keeps:
        keep.wait()


def hello(total, gains, marks, collective_id):
    return pl.pallas_call(
        functools.partial(hello_kernel, total),
        out_shape=[
            jax.ShapeDtypeStruct((total,) + gains.shape, gains.dtype),
            jax.ShapeDtypeStruct((CORNERS**2,) + marks.shape, marks.dtype),
        ],
        in_specs=[VMEM, VMEM],
        out_specs=[VMEM, VMEM],
        scratch_shapes=[DMA((total,)), DMA((total,)), DMA((3,)), DMA((3,)), DMA((2,))],
        compiler_params=pltpu.CompilerParams(collective_id=collective_id, has_side_effects=True),
    )(gains, marks)


def spread_kernel(total, in_ref, out_ref, buffer, send, recv):
    me, device = everyone(total)

    def give(d):
        other = lax.rem(me + d, total)
        return remote(in_ref.at[other], buffer.at[me], send.at[d], recv.at[d], device(other))

    def put(d, carry):
        give(d).start()
        return carry

    lax.fori_loop(1, total, put, 0)

    def take(d, carry):
        source = lax.rem(me + total - d, total)
        landed(buffer.at[source], recv.at[d], device(source))
        give(d).wait_send()
        return carry

    lax.fori_loop(1, total, take, 0)
    out_ref[...] = in_ref[me]

    def add(d, carry):
        out_ref[...] += buffer[lax.rem(me + d, total)]
        return carry

    lax.fori_loop(1, total, add, 0)


def spread_sum(tiles, collective_id):
    total = tiles.shape[0]
    return pl.pallas_call(
        functools.partial(spread_kernel, total),
        out_shape=jax.ShapeDtypeStruct(tiles.shape[1:], tiles.dtype),
        in_specs=[VMEM],
        out_specs=VMEM,
        scratch_shapes=[pltpu.VMEM(tiles.shape, tiles.dtype), DMA((total,)), DMA((total,))],
        compiler_params=pltpu.CompilerParams(collective_id=collective_id, has_side_effects=True),
    )(tiles)


def root_mean_scale(values, gains):
    return values * lax.rsqrt(jnp.mean(values * values, axis=-1, keepdims=True) + 1e-06) * gains


def rope_tables(positions):
    steps_half = jnp.arange(HEAD_SIZE // 2).astype(jnp.float32)
    inverse = jnp.power(1000000.0, steps_half * (-2.0 / HEAD_SIZE))
    angles = positions.astype(jnp.float32)[..., None] * inverse
    angles = jnp.concatenate([angles, angles], axis=-1)
    return (jnp.cos(angles)[..., None, :], jnp.sin(angles)[..., None, :])


def rotary_apply(values, cosine_factor, sine_factor):
    half_dim = values.shape[-1] // 2
    turned = jnp.concatenate([-values[..., half_dim:], values[..., :half_dim]], axis=-1)
    return values * cosine_factor + turned * sine_factor


def matrix_product(left, right):
    return jnp.dot(left, right, preferred_element_type=jnp.float32)


def contract_last(left, right):
    return lax.dot_general(
        left, right, (((1,), (1,)), ((), ())), preferred_element_type=jnp.float32
    )


def contract_first(left, right):
    return lax.dot_general(
        left, right, (((0,), (0,)), ((), ())), preferred_element_type=jnp.float32
    )


def low(values):
    return values.astype(jnp.bfloat16)


def make_shards(cells):
    data_total = cells * PLANES

    def blocks(terms):
        return low(terms).reshape(RANKS, -1, terms.shape[1])

    def gather_tokens(rows):
        return run([gather_part(rows)], 0)[0]

    def scatter_tokens(terms):
        return run([scatter_part(blocks(terms))], 1, 40)[0]

    def split_units(weight):
        rows, units = weight.shape
        piece = units // (RANKS * data_total)
        split = weight.reshape(rows, CORNERS**2, data_total, CORNERS, piece)
        return jnp.transpose(split, (0, 1, 3, 2, 4)).reshape(rows, RANKS, units // RANKS)

    def join_units(parts):
        ranks, rows, units = parts.shape
        split = parts.reshape(CORNERS**2, CORNERS, rows, data_total, units // data_total)
        return jnp.transpose(split, (2, 0, 3, 1, 4)).reshape(rows, ranks * units)

    def split_columns(weight):
        return weight.reshape(weight.shape[0], RANKS, -1)

    def join_columns(parts):
        return jnp.transpose(parts, (1, 0, 2)).reshape(parts.shape[1], -1)

    def send_columns(pieces):
        return jnp.transpose(jnp.concatenate(pieces, axis=-1), (1, 0, 2))

    def gather_columns(mine):
        rows, columns = mine.shape[1:]
        every = lax.all_gather(mine, DATA, axis=0, tiled=False)
        every = every.reshape(data_total, CORNERS**2, CORNERS, rows, columns)
        return jnp.transpose(every, (1, 0, 2, 3, 4)).reshape(-1, columns)

    def sum_columns(term):
        rows = term.shape[0] // (RANKS * data_total)
        split = low(term).reshape(CORNERS**2, data_total, CORNERS, rows, -1)
        split = jnp.transpose(split, (1, 0, 2, 3, 4)).reshape(data_total * RANKS, rows, -1)
        return lax.psum_scatter(split, DATA, scatter_dimension=0, tiled=True)

    inner = CORNERS * data_total
    to_rank = []
    for source in range(inner):
        rank_y, place = divmod(source, data_total)
        to_rank.append((source, place * CORNERS + rank_y))
    from_rank = [(b, a) for a, b in to_rank]
    INNER = ("cell", "z", "y")

    def shards(
        hidden_in,
        query_weight,
        key_matrix,
        value_matrix,
        gate_weight,
        out_weight,
        norm_attn,
        query_gain,
        key_gain,
        norm_ffn,
        ffn_gate,
        ffn_up,
        ffn_down,
        cotangent,
        sequence_numbers,
        positions,
    ):
        rows = hidden_in.shape[0]
        tokens = rows * RANKS
        groups = CORNERS**2
        window = GROUP_TOKENS // PLANES
        repeat = QUERY_HEADS // KEY_VALUE_HEADS
        query_columns = QUERY_HEADS * HEAD_SIZE // RANKS
        key_columns = KEY_VALUE_HEADS * HEAD_SIZE // RANKS
        scale_qk = 1.0 / math.sqrt(HEAD_SIZE)

        sizes = [norm_attn.shape[0], norm_ffn.shape[0], query_gain.shape[0], key_gain.shape[0]]
        cuts = [0]
        for size in sizes:
            cuts.append(cuts[-1] + size)
        tile = (8, HEAD_SIZE)
        pad = tile[0] * tile[1] - cuts[-1]
        own_gains = jnp.concatenate([norm_attn, norm_ffn, query_gain, key_gain]).astype(jnp.float32)
        own_gains = jnp.pad(own_gains, (0, pad)).reshape(tile)
        plane = lax.axis_index("z")
        group_start = lax.axis_index("cell") * GROUP_TOKENS
        marks = jnp.concatenate(
            [
                lax.dynamic_slice_in_dim(sequence_numbers, group_start, GROUP_TOKENS),
                lax.dynamic_slice_in_dim(positions, group_start, GROUP_TOKENS),
            ]
        ).reshape(-1, HEAD_SIZE)
        attn_columns = send_columns(
            [
                split_columns(query_weight),
                split_columns(key_matrix),
                split_columns(value_matrix),
                split_columns(gate_weight),
            ]
        )
        (attn_columns,) = run([swap_part(attn_columns)], 4)
        attn_columns, own_gains = lax.optimization_barrier((attn_columns, own_gains))
        gains, marks = hello(RANKS * data_total, own_gains, marks, 2)
        gains = gains.reshape(RANKS * data_total, -1)
        gain_attn, gain_ffn, gain_query, gain_key = (
            gains[:, a:b].reshape(-1) for a, b in zip(cuts[:-1], cuts[1:])
        )
        w_attn = gather_columns(attn_columns)
        w_out = lax.all_gather(
            lax.ppermute(out_weight, INNER, to_rank), DATA, axis=0, tiled=True
        )

        marks = marks.reshape(groups, 2, GROUP_TOKENS)
        key_seq, key_pos = marks[:, 0], marks[:, 1]
        own = lax.dynamic_slice_in_dim(marks, plane * window, window, axis=2)
        own_seq, own_pos = own[:, 0], own[:, 1]
        cosine_factor, sine_factor = rope_tables(own_pos)
        allowed = (key_pos[:, None, :] <= own_pos[:, :, None]) & (
            (key_seq[:, None, :] == 0) | (key_seq[:, None, :] == own_seq[:, :, None])
        )

        def prepare_heads(raw_values, gain_values):
            return rotary_apply(
                root_mean_scale(raw_values, gain_values), cosine_factor, sine_factor
            )

        hidden = hidden_in.astype(jnp.float32)
        normed_input = gather_tokens(low(root_mean_scale(hidden, gain_attn)))
        raw = matrix_product(normed_input, w_attn)
        a, b, c = query_columns, query_columns + key_columns, query_columns + 2 * key_columns
        query_raw = raw[:, :a].reshape(groups, window, repeat, HEAD_SIZE)
        key_raw = raw[:, a:b].reshape(groups, window, 1, HEAD_SIZE)
        value_low = low(raw[:, b:c]).reshape(groups, window, HEAD_SIZE)
        gate_sig = jax.nn.sigmoid(raw[:, c:])
        query_low = low(prepare_heads(query_raw, gain_query))
        key_low = low(prepare_heads(key_raw, gain_key)).reshape(groups, window, HEAD_SIZE)
        pair = jnp.concatenate([key_low, value_low], axis=-1).reshape(tokens, 2 * HEAD_SIZE)
        ffn_columns = send_columns([split_units(ffn_gate), split_units(ffn_up)])
        pair, cotangent_all, ffn_columns = run(
            [line_gather_part(pair), gather_part(cotangent), swap_part(ffn_columns)], 3
        )
        w_ffn = gather_columns(ffn_columns)
        own_down, pair = lax.optimization_barrier((ffn_down, pair))
        w_down = lax.all_gather(own_down, DATA, axis=0, tiled=True)
        pair = pair.reshape(PLANES, groups, window, 2 * HEAD_SIZE)
        pair = jnp.transpose(pair, (1, 0, 2, 3)).reshape(groups, GROUP_TOKENS, 2 * HEAD_SIZE)
        keys_all, values_all = pair[..., :HEAD_SIZE], pair[..., HEAD_SIZE:]

        scores = (
            jnp.einsum("gqrd,gkd->grqk", query_low, keys_all, preferred_element_type=jnp.float32)
            * scale_qk
        )
        masked = jnp.where(allowed[:, None], scores, -1e30)
        peak = jnp.max(masked, axis=-1, keepdims=True)
        exponent = jnp.exp(masked - peak)
        probs = exponent / jnp.sum(exponent, axis=-1, keepdims=True)
        probs_low = low(probs)
        attended = jnp.einsum(
            "grqk,gkd->gqrd", probs_low, values_all, preferred_element_type=jnp.float32
        )
        attended_rows = attended.reshape(tokens, query_columns)
        gated_low = low(attended_rows * gate_sig)
        middle = hidden + scatter_tokens(matrix_product(gated_low, w_out))

        normed_two = gather_tokens(low(root_mean_scale(middle, gain_ffn)))
        both = matrix_product(normed_two, w_ffn)
        units = both.shape[1] // 2
        gate_ffn, up_ffn = both[:, :units], both[:, units:]
        ffn_sig = jax.nn.sigmoid(gate_ffn)
        mixed_low = low(gate_ffn * ffn_sig * up_ffn)
        down_terms = blocks(matrix_product(mixed_low, w_down))

        d_mixed = contract_last(cotangent_all, w_down)
        d_up_low = low(d_mixed * gate_ffn * ffn_sig)
        d_gate_ffn_low = low(d_mixed * up_ffn * ffn_sig * (1.0 + gate_ffn * (1.0 - ffn_sig)))
        d_both = jnp.concatenate([d_gate_ffn_low, d_up_low], axis=-1)
        both_term = low(contract_first(normed_two, d_both))
        down_term = low(contract_first(mixed_low, cotangent_all))
        two_terms = blocks(contract_last(d_both, w_ffn))
        two_terms, both_term, down_term = lax.optimization_barrier(
            (two_terms, both_term, down_term)
        )
        grad_both = sum_columns(both_term)
        grad_down = lax.psum_scatter(down_term, DATA, scatter_dimension=0, tiled=True).astype(
            jnp.float32
        )
        (d_normed_two,) = run([scatter_part(two_terms)], 1, 40)
        unused_two, norm_two_back = jax.vjp(root_mean_scale, middle, gain_ffn)
        d_middle_norm, grad_norm_two_term = norm_two_back(d_normed_two)
        d_middle = cotangent.astype(jnp.float32) + d_middle_norm

        branch_all = gather_tokens(low(d_middle))
        d_gated = contract_last(branch_all, w_out)
        grad_out = lax.psum_scatter(
            low(contract_first(gated_low, branch_all)), DATA, scatter_dimension=0, tiled=True
        )
        grad_out = lax.ppermute(grad_out, INNER, from_rank).astype(jnp.float32)
        d_attended = low(d_gated * gate_sig)
        d_gate_low = low(d_gated * attended_rows * gate_sig * (1.0 - gate_sig))
        d_heads = d_attended.reshape(groups, window, repeat, HEAD_SIZE)
        row_delta = jnp.transpose(
            jnp.sum(d_heads.astype(jnp.float32) * attended, axis=-1), (0, 2, 1)
        )
        d_probs = jnp.einsum(
            "gqrd,gkd->grqk", d_heads, values_all, preferred_element_type=jnp.float32
        )
        d_scores = low(probs * (d_probs - row_delta[..., None]))
        d_query_rot = (
            jnp.einsum("grqk,gkd->gqrd", d_scores, keys_all, preferred_element_type=jnp.float32)
            * scale_qk
        )
        d_keys = (
            jnp.einsum("grqk,gqrd->gkd", d_scores, query_low, preferred_element_type=jnp.float32)
            * scale_qk
        )
        d_values = jnp.einsum(
            "grqk,gqrd->gkd", probs_low, d_heads, preferred_element_type=jnp.float32
        )
        d_pair = low(jnp.concatenate([d_keys, d_values], axis=-1))
        d_pair = jnp.transpose(
            d_pair.reshape(groups, PLANES, window, 2 * HEAD_SIZE), (1, 0, 2, 3)
        )
        d_pair, result, grad_both = run(
            [
                line_scatter_part(d_pair.reshape(PLANES, tokens, 2 * HEAD_SIZE)),
                scatter_part(down_terms),
                swap_part(grad_both),
            ],
            5,
            56,
        )
        output = low(middle + result)
        grad_both = grad_both.astype(jnp.float32)
        grad_gate = join_units(grad_both[..., :units])
        grad_up = join_units(grad_both[..., units:])
        d_pair = d_pair.reshape(groups, window, 2 * HEAD_SIZE)
        d_key_rot, d_value = d_pair[..., :HEAD_SIZE], d_pair[..., HEAD_SIZE:]
        unused_query, query_back = jax.vjp(prepare_heads, query_raw, gain_query)
        d_query_raw, grad_query_gain_term = query_back(d_query_rot)
        unused_key, key_back = jax.vjp(prepare_heads, key_raw, gain_key)
        d_key_raw, grad_key_gain_term = key_back(d_key_rot[:, :, None, :])
        d_raw = jnp.concatenate(
            [
                low(d_query_raw.reshape(tokens, query_columns)),
                low(d_key_raw.reshape(tokens, key_columns)),
                low(d_value.reshape(tokens, key_columns)),
                d_gate_low,
            ],
            axis=-1,
        )
        attn_term = low(contract_first(normed_input, d_raw))
        one_terms = blocks(contract_last(d_raw, w_attn))
        one_terms, attn_term = lax.optimization_barrier((one_terms, attn_term))
        grad_attn = sum_columns(attn_term)
        (d_normed,) = run([scatter_part(one_terms)], 1, 40)
        (grad_attn,) = run([swap_part(grad_attn)], 4)
        grad_attn = grad_attn.astype(jnp.float32)
        grad_query = join_columns(grad_attn[..., :a])
        grad_key = join_columns(grad_attn[..., a:b])
        grad_value = join_columns(grad_attn[..., b:c])
        grad_gatew = join_columns(grad_attn[..., c:])
        unused_one, norm_one_back = jax.vjp(root_mean_scale, hidden, gain_attn)
        d_hidden_norm, grad_norm_one_term = norm_one_back(d_normed)
        input_grad = d_middle + d_hidden_norm

        terms = jnp.concatenate(
            [
                t.reshape(RANKS * data_total, -1)
                for t in (
                    grad_norm_one_term,
                    grad_norm_two_term,
                    grad_query_gain_term,
                    grad_key_gain_term,
                )
            ],
            axis=-1,
        )
        terms = jnp.pad(terms, ((0, 0), (0, pad))).reshape((-1,) + tile)
        small = spread_sum(terms, 7).reshape(-1)
        grad_norm_attn, grad_norm_ffn, grad_query_gain, grad_key_gain = (
            small[s:e] for s, e in zip(cuts[:-1], cuts[1:])
        )
        return (
            output,
            input_grad,
            grad_query,
            grad_key,
            grad_value,
            grad_gatew,
            grad_out,
            grad_norm_attn,
            grad_query_gain,
            grad_key_gain,
            grad_norm_ffn,
            grad_gate,
            grad_up,
            grad_down,
        )

    return shards


def solution(mesh):
    cells = mesh.shape["fsdp"] // (PLANES * CORNERS)
    split = Mesh(
        mesh.devices.reshape(CORNERS, CORNERS, cells, PLANES, CORNERS),
        ALL,
    )
    rows, flat, group = P(ALL, None), P(ALL), P(("x", "core"))
    return jax.shard_map(
        make_shards(cells),
        mesh=split,
        in_specs=(rows,) * 6 + (flat,) * 4 + (rows,) * 4 + (group,) * 2,
        out_specs=(rows,) * 7 + (flat,) * 4 + (rows,) * 3,
        check_vma=False,
    )
```

```python
import functools
import math

import jax
import jax.numpy as jnp
from jax import lax
from jax.experimental import pallas as pl
from jax.experimental.pallas import tpu as pltpu
from jax.sharding import Mesh
from jax.sharding import PartitionSpec as P

QUERY_HEADS = 16
KEY_VALUE_HEADS = 8
HEAD_SIZE = 128
REPEAT = QUERY_HEADS // KEY_VALUE_HEADS
GROUP_TOKENS = 2048
CORNERS = 2
PLANES = 4
ALL = ("x", "core", "cell", "z", "y")
TENSOR = ("x", "core", "y")
DATA = ("cell", "z")
RANKS = CORNERS**3
CHUNKS = 4
MESH_ID = pl.DeviceIdType.MESH
OTHERS = [(dx, dc, dy) for dx in (0, 1) for dc in (0, 1) for dy in (0, 1) if dx + dc + dy]
DMA = pltpu.SemaphoreType.DMA
VMEM = pl.BlockSpec(memory_space=pltpu.VMEM)
ANYWHERE = pl.BlockSpec(memory_space=pl.ANY)


def remote(source, target, send, receive, device):
    return pltpu.make_async_remote_copy(
        src_ref=source,
        dst_ref=target,
        send_sem=send,
        recv_sem=receive,
        device_id=device,
        device_id_type=MESH_ID,
    )


def landed(ref, sem, device):
    remote(ref, ref, sem, sem, device).wait_recv()


def corner():
    return lax.axis_index("x"), lax.axis_index("core"), lax.axis_index("y")


def slot(x, c, y):
    return (x * CORNERS + c) * CORNERS + y


def flip(value, bit):
    return 1 - value if bit else value


def neighbours():
    x, c, y = corner()
    return {"x": 1 - x}, {"y": 1 - y}, {"core": 1 - c}


def plane_peers():
    x, c, y = corner()
    peers = []
    for dx, dc, dy in OTHERS:
        px, pc, py = flip(x, dx), flip(c, dc), flip(y, dy)
        peers.append(({"x": px, "core": pc, "y": py}, slot(px, pc, py)))
    return peers


def greet(plane, line):
    if plane == "world":
        everyone(math.prod(lax.axis_size(n) for n in ALL))
        return
    barrier = pltpu.get_barrier_semaphore()
    near = {"near": neighbours(), "all": [p for p, _ in plane_peers()], None: []}[plane]
    for device in near:
        pl.semaphore_signal(barrier, inc=1, device_id=device, device_id_type=MESH_ID)
    if not line:
        pl.semaphore_wait(barrier, len(near))
        return
    z = lax.axis_index("z")

    @pl.when(z > 0)
    def _():
        pl.semaphore_signal(barrier, inc=1, device_id={"z": z - 1}, device_id_type=MESH_ID)

    @pl.when(z < PLANES - 1)
    def _():
        pl.semaphore_signal(barrier, inc=1, device_id={"z": z + 1}, device_id_type=MESH_ID)

    edge = (z == 0) | (z == PLANES - 1)

    @pl.when(edge)
    def _():
        pl.semaphore_wait(barrier, len(near) + 1)

    @pl.when(jnp.logical_not(edge))
    def _():
        pl.semaphore_wait(barrier, len(near) + 2)


class Part:
    def __init__(self, inputs, outs, scratch, steps, plane=None, line=False):
        self.inputs = inputs
        self.outs = outs
        self.scratch = scratch
        self.steps = steps
        self.plane, self.line = plane, line


def run_kernel(parts, *refs):
    refs = list(refs)

    def take(counts):
        groups = []
        for count in counts:
            groups.append(refs[:count])
            del refs[:count]
        return groups

    ins = take([len(p.inputs) for p in parts])
    outs = take([len(p.outs) for p in parts])
    scratch = take([len(p.scratch) for p in parts])
    ranks = [None, "near", "all", "world"]
    plane = ranks[max(ranks.index(p.plane) for p in parts)]
    greet(plane, any(p.line for p in parts))
    plans = [p.steps(i, o, s) for p, i, o, s in zip(parts, ins, outs, scratch)]
    for first, _, _ in plans:
        first()
    ordered = []
    for _, middle, _ in plans:
        ordered += [((n + 0.5) / len(middle), step) for n, step in enumerate(middle)]
    for _, step in sorted(ordered, key=lambda pair: pair[0]):
        step()
    for _, _, last in plans:
        last()


def expected(micros):
    return pl.CostEstimate(flops=0, bytes_accessed=int(micros * 3.5e6), transcendentals=0)


def run(parts, collective_id, vmem=None, micros=40):
    inputs = [pair for p in parts for pair in p.inputs]
    outs = [pair for p in parts for pair in p.outs]
    return pl.pallas_call(
        functools.partial(run_kernel, parts),
        out_shape=[shape for shape, _ in outs],
        in_specs=[spec for _, spec in inputs],
        out_specs=[spec for _, spec in outs],
        scratch_shapes=[s for p in parts for s in p.scratch],
        compiler_params=pltpu.CompilerParams(
            collective_id=collective_id,
            has_side_effects=True,
            vmem_limit_bytes=None if vmem is None else vmem << 20,
        ),
        cost_estimate=expected(micros),
    )(*[array for array, _ in inputs])


def gather_part(block):
    rows, columns = block.shape
    n, half = CHUNKS, CHUNKS // 2
    chunk = rows // n

    def steps(ins, outs, scratch):
        (in_ref,), (out_ref,) = ins, outs
        send_x, send_y, send_c, recv_x, recv_y, recv_c, local = scratch
        x, c, y = corner()
        dev_x, dev_y, dev_c = neighbours()

        def at(index, k):
            start = pl.multiple_of(index * rows + k * chunk, chunk)
            return out_ref.at[pl.ds(start, chunk), :]

        own, beside_x, beside_y = slot(x, c, y), slot(1 - x, c, y), slot(x, c, 1 - y)
        across = slot(1 - x, c, 1 - y)
        mirror = [
            slot(x, 1 - c, y),
            slot(1 - x, 1 - c, y),
            slot(x, 1 - c, 1 - y),
            slot(1 - x, 1 - c, 1 - y),
        ]
        start = pl.multiple_of(own * rows, rows)
        keep = pltpu.make_async_copy(in_ref, out_ref.at[pl.ds(start, rows), :], local)
        sent = []

        def go(copy):
            copy.start()
            sent.append(copy)

        def share(index, k, b):
            go(remote(at(index, k), at(index, k), send_c.at[b * n + k], recv_c.at[b * n + k], dev_c))

        order_x = list(range(n))
        order_y = order_x[half:] + order_x[:half]

        def first():
            keep.start()

            def mine(k):
                return in_ref.at[pl.ds(k * chunk, chunk), :]

            for k, j in zip(order_x, order_y):
                go(remote(mine(k), at(own, k), send_x.at[k], recv_x.at[k], dev_x))
                go(remote(mine(j), at(own, j), send_y.at[j], recv_y.at[j], dev_y))
            for k in range(n):
                go(remote(mine(k), at(own, k), send_c.at[k], recv_c.at[k], dev_c))

        def straight(k, j):
            landed(at(beside_x, k), recv_x.at[k], dev_x)
            if k < half:
                to = at(beside_x, k)
                go(remote(to, to, send_y.at[n + k], recv_y.at[n + k], dev_y))
            share(beside_x, k, 1)
            landed(at(beside_y, j), recv_y.at[j], dev_y)
            if j >= half:
                to = at(beside_y, j)
                go(remote(to, to, send_x.at[half + j], recv_x.at[half + j], dev_x))
            share(beside_y, j, 2)

        def diagonal(k):
            landed(at(across, k), recv_y.at[n + k], dev_y)
            share(across, k, 3)
            landed(at(across, half + k), recv_x.at[n + k], dev_x)
            share(across, half + k, 3)

        def last():
            for b in range(4):
                for k in range(n):
                    landed(at(mirror[b], k), recv_c.at[b * n + k], dev_c)
            for copy in sent:
                copy.wait_send()
            keep.wait()

        middle = [functools.partial(straight, k, j) for k, j in zip(order_x, order_y)]
        middle += [functools.partial(diagonal, k) for k in range(half)]
        return first, middle, last

    link = DMA((n + half,))
    core = DMA((4 * n,))
    return Part(
        [(block, VMEM)],
        [(jax.ShapeDtypeStruct((RANKS * rows, columns), block.dtype), ANYWHERE)],
        [link, link, core, link, link, core, DMA(())],
        steps,
        plane="near",
    )


def add_rows(target, start, count, sources, step=16):
    def body(i, carry):
        r = pl.multiple_of(start + i * step, step)
        total = None
        for ref, shift in sources:
            value = ref[pl.ds(r - shift if shift else r, step), :].astype(jnp.float32)
            total = value if total is None else total + value
        target[pl.ds(r, step), :] = total.astype(target.dtype)
        return carry

    lax.fori_loop(0, count // step, body, 0)


def scatter_part(terms):
    ranks, rows, columns = terms.shape
    n, half = CHUNKS, CHUNKS // 2
    chunk = rows // n
    middle_row = half * chunk

    def steps(ins, outs, scratch):
        (part_ref,), (out_ref,) = ins, outs
        core_buf, x_buf, y_buf, x_diag, y_diag, d_sum, x_sum, y_sum = scratch[:8]
        send_c, recv_c, send_x, recv_x, send_y, recv_y = scratch[8:]
        x, c, y = corner()
        dev_x, dev_y, dev_c = neighbours()
        D, X, Y, O = range(4)
        place = [(1 - x, 1 - y), (1 - x, y), (x, 1 - y), (x, y)]
        mine = [slot(px, c, py) for px, py in place]
        theirs = [slot(px, 1 - c, py) for px, py in place]
        orders = {D: [], X: list(range(n)), O: list(range(n))}
        for k in range(half):
            orders[D] += [k, half + k]
        orders[Y] = orders[X][half:] + orders[X][:half]
        sent = []

        def go(copy):
            copy.start()
            sent.append(copy)

        def piece(k):
            return pl.ds(k * chunk, chunk)

        def first():
            for b in (D, X, Y, O):
                for k in orders[b]:
                    source = part_ref.at[theirs[b], piece(k), :]
                    i = b * n + k
                    go(remote(source, core_buf.at[b, piece(k), :], send_c.at[i], recv_c.at[i], dev_c))

        def chip(target, b, k, *more):
            landed(core_buf.at[b, piece(k), :], recv_c.at[b * n + k], dev_c)
            sources = [(part_ref.at[mine[b]], 0), (core_buf.at[b], 0), *more]
            add_rows(target, k * chunk, chunk, sources)

        def to_x(k):
            go(remote(x_sum.at[piece(k), :], x_buf.at[piece(k), :], send_x.at[k], recv_x.at[k], dev_x))

        def to_y(k):
            go(remote(y_sum.at[piece(k), :], y_buf.at[piece(k), :], send_y.at[k], recv_y.at[k], dev_y))

        def diagonal(k):
            chip(d_sum, D, k)
            source = d_sum.at[piece(k), :]
            if k < half:
                go(remote(source, x_diag.at[piece(k), :], send_x.at[n + k], recv_x.at[n + k], dev_x))
            else:
                to = y_diag.at[piece(k - half), :]
                go(remote(source, to, send_y.at[half + k], recv_y.at[half + k], dev_y))

        def direct(k):
            chip(x_sum, X, k)
            to_x(k)
            chip(y_sum, Y, half + k)
            to_y(half + k)

        def relayed(k):
            landed(y_diag.at[piece(k), :], recv_y.at[n + k], dev_y)
            chip(x_sum, X, half + k, (y_diag, middle_row))
            to_x(half + k)
            landed(x_diag.at[piece(k), :], recv_x.at[n + k], dev_x)
            chip(y_sum, Y, k, (x_diag, 0))
            to_y(k)

        def own(k):
            landed(x_buf.at[piece(k), :], recv_x.at[k], dev_x)
            landed(y_buf.at[piece(k), :], recv_y.at[k], dev_y)
            chip(out_ref, O, k, (x_buf, 0), (y_buf, 0))

        def last():
            for copy in sent:
                copy.wait_send()

        middle = [functools.partial(diagonal, k) for k in orders[D]]
        middle += [functools.partial(direct, k) for k in range(half)]
        middle += [functools.partial(relayed, k) for k in range(half)]
        middle += [functools.partial(own, k) for k in range(n)]
        return first, middle, last

    def low_vmem(*shape):
        return pltpu.VMEM(shape, jnp.bfloat16)

    whole, part = low_vmem(rows, columns), low_vmem(rows // 2, columns)
    link = DMA((n + half,))
    core = DMA((4 * n,))
    return Part(
        [(terms, VMEM)],
        [(jax.ShapeDtypeStruct((rows, columns), jnp.float32), VMEM)],
        [low_vmem(4, rows, columns), whole, whole, part, part, whole, whole, whole]
        + [core, core, link, link, link, link],
        steps,
        plane="near",
    )


def swap_part(blocks):
    def steps(ins, outs, scratch):
        (in_ref,), (out_ref,) = ins, outs
        send, recv, local = scratch
        own = slot(*corner())
        keep = pltpu.make_async_copy(in_ref.at[own], out_ref.at[own], local)
        peers = plane_peers()
        sent = []

        def first():
            keep.start()
            for i, (there, other) in enumerate(peers):
                copy = remote(in_ref.at[other], out_ref.at[own], send.at[i], recv.at[i], there)
                copy.start()
                sent.append(copy)

        def last():
            for i, (there, other) in enumerate(peers):
                landed(out_ref.at[other], recv.at[i], there)
            for copy in sent:
                copy.wait_send()
            keep.wait()

        return first, [], last

    n = len(OTHERS)
    return Part(
        [(blocks, VMEM)],
        [(jax.ShapeDtypeStruct(blocks.shape, blocks.dtype), ANYWHERE)],
        [DMA((n,)), DMA((n,)), DMA(())],
        steps,
        plane="all",
    )


def line_gather_part(block, pieces=4):
    rows = block.shape[0] // pieces

    def steps(ins, outs, scratch):
        (in_ref,), (out_ref,) = ins, outs
        up_send, up_recv, down_send, down_recv, local = scratch
        z = lax.axis_index("z")
        keep = pltpu.make_async_copy(in_ref, out_ref.at[z], local)

        def at(block, k):
            return out_ref.at[block, pl.ds(k * rows, rows), :]

        def up(t, k, source=None):
            s = at(z - t, k) if source is None else source
            i = t * pieces + k
            return remote(s, at(z - t, k), up_send.at[i], up_recv.at[i], {"z": z + 1})

        def down(t, k, source=None):
            s = at(z + t, k) if source is None else source
            i = t * pieces + k
            return remote(s, at(z + t, k), down_send.at[i], down_recv.at[i], {"z": z - 1})

        def first():
            keep.start()
            for k in range(pieces):
                mine = in_ref.at[pl.ds(k * rows, rows), :]

                @pl.when(z < PLANES - 1)
                def _():
                    up(0, k, mine).start()

                @pl.when(z > 0)
                def _():
                    down(0, k, mine).start()

        def arrive(t, k):
            i = t * pieces + k
            on = t + 1 < PLANES - 1

            @pl.when(z - 1 - t >= 0)
            def _():
                landed(at(z - 1 - t, k), up_recv.at[i], {"z": z - 1})
                if on:

                    @pl.when(z < PLANES - 1)
                    def _():
                        up(t + 1, k).start()

            @pl.when(z + 1 + t < PLANES)
            def _():
                landed(at(z + 1 + t, k), down_recv.at[i], {"z": z + 1})
                if on:

                    @pl.when(z > 0)
                    def _():
                        down(t + 1, k).start()

        def last():
            for t in range(PLANES - 1):
                for k in range(pieces):

                    @pl.when((z < PLANES - 1) & (z - t >= 0))
                    def _():
                        up(t, k).wait_send()

                    @pl.when((z > 0) & (z + t < PLANES))
                    def _():
                        down(t, k).wait_send()

            keep.wait()

        middle = [
            functools.partial(arrive, t, k) for t in range(PLANES - 1) for k in range(pieces)
        ]
        return first, middle, last

    sems = DMA(((PLANES - 1) * pieces,))
    return Part(
        [(block, VMEM)],
        [(jax.ShapeDtypeStruct((PLANES,) + block.shape, block.dtype), ANYWHERE)],
        [sems, sems, sems, sems, DMA(())],
        steps,
        line=True,
    )


def line_scatter_part(terms, pieces=4):
    line, all_rows, columns = terms.shape
    rows = all_rows // pieces
    step = 32

    def steps(ins, outs, scratch):
        (in_ref,), (out_ref,) = ins, outs
        up_buf, down_buf, up_stage, down_stage, up_send, up_recv, down_send, down_recv = scratch
        z = lax.axis_index("z")
        f32 = jnp.float32

        def cut(k):
            return pl.ds(k * rows, rows)

        def send_up(source, d, k):
            i = (d - 1) * pieces + k
            return remote(source, up_buf.at[d - 1, cut(k), :], up_send.at[i], up_recv.at[i], {"z": z + 1})

        def send_down(source, d, k):
            i = (d - 1) * pieces + k
            to = down_buf.at[d - 1, cut(k), :]
            return remote(source, to, down_send.at[i], down_recv.at[i], {"z": z - 1})

        def first():
            pass

        def pass_on(d, k):
            @pl.when(z + d < line)
            def _():
                @pl.when(z == 0)
                def _():
                    send_up(in_ref.at[z + d, cut(k), :], d, k).start()

                if d + 1 < line:

                    @pl.when(z > 0)
                    def _():
                        landed(up_buf.at[d, cut(k), :], up_recv.at[d * pieces + k], {"z": z - 1})
                        sources = [(in_ref.at[z + d], 0), (up_buf.at[d], 0)]
                        add_rows(up_stage.at[d - 1], k * rows, rows, sources, step)
                        send_up(up_stage.at[d - 1, cut(k), :], d, k).start()

            @pl.when(z - d >= 0)
            def _():
                @pl.when(z == line - 1)
                def _():
                    send_down(in_ref.at[z - d, cut(k), :], d, k).start()

                if d + 1 < line:

                    @pl.when(z < line - 1)
                    def _():
                        landed(down_buf.at[d, cut(k), :], down_recv.at[d * pieces + k], {"z": z + 1})
                        sources = [(in_ref.at[z - d], 0), (down_buf.at[d], 0)]
                        add_rows(down_stage.at[d - 1], k * rows, rows, sources, step)
                        send_down(down_stage.at[d - 1, cut(k), :], d, k).start()

        def own(k):
            @pl.when(z > 0)
            def _():
                landed(up_buf.at[0, cut(k), :], up_recv.at[k], {"z": z - 1})

            @pl.when(z < line - 1)
            def _():
                landed(down_buf.at[0, cut(k), :], down_recv.at[k], {"z": z + 1})

            mine, below, above = (in_ref.at[z], 0), (up_buf.at[0], 0), (down_buf.at[0], 0)

            @pl.when(z == 0)
            def _():
                add_rows(out_ref, k * rows, rows, [mine, above], step)

            @pl.when(z == line - 1)
            def _():
                add_rows(out_ref, k * rows, rows, [mine, below], step)

            @pl.when((z > 0) & (z < line - 1))
            def _():
                add_rows(out_ref, k * rows, rows, [mine, below, above], step)

        def last():
            for d in range(line - 1, 0, -1):
                for k in range(pieces):

                    @pl.when(z + d < line)
                    def _():
                        send_up(up_stage.at[d - 1, cut(k), :], d, k).wait_send()

                    @pl.when(z - d >= 0)
                    def _():
                        send_down(down_stage.at[d - 1, cut(k), :], d, k).wait_send()

        middle = [
            functools.partial(pass_on, d, k) for d in range(line - 1, 0, -1) for k in range(pieces)
        ]
        middle += [functools.partial(own, k) for k in range(pieces)]
        return first, middle, last

    sems = DMA(((line - 1) * pieces,))
    buffer = pltpu.VMEM((line - 1, all_rows, columns), jnp.bfloat16)
    return Part(
        [(terms, VMEM)],
        [(jax.ShapeDtypeStruct((all_rows, columns), jnp.float32), VMEM)],
        [buffer, buffer, buffer, buffer, sems, sems, sems, sems],
        steps,
        line=True,
    )


def places():
    sizes = [lax.axis_size(n) for n in ALL]
    me = 0
    for n, size in zip(ALL, sizes):
        me = me * size + lax.axis_index(n)

    def device(index):
        where = {}
        for n, size in reversed(list(zip(ALL, sizes))):
            where[n] = lax.rem(index, size)
            index = index // size
        return where

    return me, device


def everyone(total):
    me, device = places()
    barrier = pltpu.get_barrier_semaphore()

    def greet_one(d, carry):
        other = device(lax.rem(me + d, total))
        pl.semaphore_signal(barrier, inc=1, device_id=other, device_id_type=MESH_ID)
        return carry

    lax.fori_loop(1, total, greet_one, 0)
    pl.semaphore_wait(barrier, total - 1)
    return me, device


def hello_part(total, gains, marks):
    def steps(ins, outs, scratch):
        gains_ref, marks_ref = ins
        gains_out, marks_out = outs
        g_send, g_recv, m_send, m_recv, local = scratch
        me, device = places()
        x, c, y = corner()
        group = x * CORNERS + c
        keeps = [
            pltpu.make_async_copy(gains_ref, gains_out.at[me], local.at[0]),
            pltpu.make_async_copy(marks_ref, marks_out.at[group], local.at[1]),
        ]
        near = [(i, dx, dc) for i, (dx, dc) in enumerate([(0, 1), (1, 0), (1, 1)])]
        sent = []

        def give(d):
            other = device(lax.rem(me + d, total))
            return remote(gains_ref, gains_out.at[me], g_send.at[d], g_recv.at[d], other)

        def first():
            for keep in keeps:
                keep.start()
            for i, dx, dc in near:
                there = {"x": flip(x, dx), "core": flip(c, dc)}
                copy = remote(marks_ref, marks_out.at[group], m_send.at[i], m_recv.at[i], there)
                copy.start()
                sent.append(copy)

            def put(d, carry):
                give(d).start()
                return carry

            lax.fori_loop(1, total, put, 0)

        def last():
            def take(d, carry):
                source = lax.rem(me + total - d, total)
                landed(gains_out.at[source], g_recv.at[d], device(source))
                give(d).wait_send()
                return carry

            lax.fori_loop(1, total, take, 0)
            for i, dx, dc in near:
                there = {"x": flip(x, dx), "core": flip(c, dc)}
                theirs = flip(x, dx) * CORNERS + flip(c, dc)
                landed(marks_out.at[theirs], m_recv.at[i], there)
            for copy in sent:
                copy.wait_send()
            for keep in keeps:
                keep.wait()

        return first, [], last

    return Part(
        [(gains, VMEM), (marks, VMEM)],
        [
            (jax.ShapeDtypeStruct((total,) + gains.shape, gains.dtype), VMEM),
            (jax.ShapeDtypeStruct((CORNERS**2,) + marks.shape, marks.dtype), VMEM),
        ],
        [DMA((total,)), DMA((total,)), DMA((3,)), DMA((3,)), DMA((2,))],
        steps,
        plane="world",
    )


def columns_part(blocks):
    ranks, rows, columns = blocks.shape

    def steps(ins, outs, scratch):
        (in_ref,), (out_ref,) = ins, outs
        send, recv, up_send, up_recv, down_send, down_recv, local = scratch
        x, c, y = corner()
        z = lax.axis_index("z")
        own = slot(x, c, y)
        peers = plane_peers()
        spots = [(x * CORNERS + c, y)]
        spots += [(flip(x, dx) * CORNERS + flip(c, dc), flip(y, dy)) for dx, dc, dy in OTHERS]

        def at(i, plane):
            return out_ref.at[spots[i][0], plane, spots[i][1]]

        keep = pltpu.make_async_copy(in_ref.at[own], at(0, z), local)
        sent = []

        def up(t, i, source=None):
            s = at(i, z - t) if source is None else source
            n = t * RANKS + i
            return remote(s, at(i, z - t), up_send.at[n], up_recv.at[n], {"z": z + 1})

        def down(t, i, source=None):
            s = at(i, z + t) if source is None else source
            n = t * RANKS + i
            return remote(s, at(i, z + t), down_send.at[n], down_recv.at[n], {"z": z - 1})

        def begin(i, source=None):
            @pl.when(z < PLANES - 1)
            def _():
                up(0, i, source).start()

            @pl.when(z > 0)
            def _():
                down(0, i, source).start()

        def first():
            keep.start()
            for i, (there, other) in enumerate(peers):
                copy = remote(in_ref.at[other], at(0, z), send.at[i], recv.at[i], there)
                copy.start()
                sent.append(copy)
            begin(0, in_ref.at[own])

        def swapped(i):
            landed(at(i, z), recv.at[i - 1], peers[i - 1][0])
            begin(i)

        def arrive(t, i):
            n = t * RANKS + i
            on = t + 1 < PLANES - 1

            @pl.when(z - 1 - t >= 0)
            def _():
                landed(at(i, z - 1 - t), up_recv.at[n], {"z": z - 1})
                if on:

                    @pl.when(z < PLANES - 1)
                    def _():
                        up(t + 1, i).start()

            @pl.when(z + 1 + t < PLANES)
            def _():
                landed(at(i, z + 1 + t), down_recv.at[n], {"z": z + 1})
                if on:

                    @pl.when(z > 0)
                    def _():
                        down(t + 1, i).start()

        def last():
            for copy in sent:
                copy.wait_send()
            for t in range(PLANES - 1):
                for i in range(RANKS):

                    @pl.when((z < PLANES - 1) & (z - t >= 0))
                    def _():
                        up(t, i).wait_send()

                    @pl.when((z > 0) & (z + t < PLANES))
                    def _():
                        down(t, i).wait_send()

            keep.wait()

        middle = [functools.partial(swapped, i) for i in range(1, RANKS)]
        middle += [
            functools.partial(arrive, t, i) for t in range(PLANES - 1) for i in range(RANKS)
        ]
        return first, middle, last

    n = len(OTHERS)
    sems = DMA(((PLANES - 1) * RANKS,))
    shape = (CORNERS**2, PLANES, CORNERS, rows, columns)
    return Part(
        [(blocks, VMEM)],
        [(jax.ShapeDtypeStruct(shape, blocks.dtype), ANYWHERE)],
        [DMA((n,)), DMA((n,)), sems, sems, sems, sems, DMA(())],
        steps,
        plane="all",
        line=True,
    )


def spread_part(tiles):
    total = tiles.shape[0]

    def steps(ins, outs, scratch):
        (in_ref,), (out_ref,) = ins, outs
        buffer, send, recv = scratch
        me, device = places()

        def give(d):
            other = lax.rem(me + d, total)
            return remote(in_ref.at[other], buffer.at[me], send.at[d], recv.at[d], device(other))

        def first():
            def put(d, carry):
                give(d).start()
                return carry

            lax.fori_loop(1, total, put, 0)

        def last():
            def take(d, carry):
                source = lax.rem(me + total - d, total)
                landed(buffer.at[source], recv.at[d], device(source))
                give(d).wait_send()
                return carry

            lax.fori_loop(1, total, take, 0)
            out_ref[...] = in_ref[me]

            def add(d, carry):
                out_ref[...] += buffer[lax.rem(me + d, total)]
                return carry

            lax.fori_loop(1, total, add, 0)

        return first, [], last

    return Part(
        [(tiles, VMEM)],
        [(jax.ShapeDtypeStruct(tiles.shape[1:], tiles.dtype), VMEM)],
        [pltpu.VMEM(tiles.shape, tiles.dtype), DMA((total,)), DMA((total,))],
        steps,
        plane="world",
    )


def root_mean_scale(values, gains):
    return values * lax.rsqrt(jnp.mean(values * values, axis=-1, keepdims=True) + 1e-06) * gains


def rope_tables(positions):
    half = HEAD_SIZE // 2
    steps_half = jnp.arange(half).astype(jnp.float32)
    inverse = jnp.power(1000000.0, steps_half * (-2.0 / HEAD_SIZE))
    angles = positions.astype(jnp.float32)[:, None] * inverse[None, :]
    cosine, sine = jnp.cos(angles), jnp.sin(angles)
    return jnp.concatenate([cosine, cosine], axis=-1), jnp.concatenate([-sine, sine], axis=-1)


def matrix_product(left, right):
    return jnp.dot(left, right, preferred_element_type=jnp.float32)


def contract_last(left, right):
    return lax.dot_general(
        left, right, (((1,), (1,)), ((), ())), preferred_element_type=jnp.float32
    )


def contract_first(left, right):
    return lax.dot_general(
        left, right, (((0,), (0,)), ((), ())), preferred_element_type=jnp.float32
    )


def low(values):
    return values.astype(jnp.bfloat16)

def turn(values, cosine, sine):
    return values * cosine + pltpu.roll(values, HEAD_SIZE // 2, 1) * sine


def turn_back(grads, cosine, sine):
    return grads * cosine + pltpu.roll(grads * sine, HEAD_SIZE // 2, 1)


def unit_scale(values):
    return lax.rsqrt(jnp.mean(values * values, axis=-1, keepdims=True) + 1e-06)


def norm_back(raw, gain, grads):
    scale = unit_scale(raw)
    unit = raw * scale
    inner = grads * gain
    d_raw = scale * (inner - unit * jnp.mean(inner * unit, axis=-1, keepdims=True))
    return d_raw, grads * unit


def head(index):
    return slice(index * HEAD_SIZE, (index + 1) * HEAD_SIZE)


def dot(left, right):
    return jnp.dot(left, right, preferred_element_type=jnp.float32)


def dot_rows(left, right):
    return lax.dot_general(
        left, right, (((1,), (1,)), ((), ())), preferred_element_type=jnp.float32
    )


def prepare_kernel(
    x_ref, gain_ref, w_ref, cos_ref, sin_ref, qg_ref, kg_ref, x_out, q_ref, kv_ref, raw_ref, gate_ref
):
    hidden = x_ref[...].astype(jnp.float32)
    x_out[...] = low(hidden * unit_scale(hidden) * gain_ref[...])
    raw = dot(x_out[...], w_ref[...])
    cosine, sine = cos_ref[...], sin_ref[...]

    def prepare(values, gain):
        return low(turn(values * unit_scale(values) * gain, cosine, sine))

    for h in range(REPEAT):
        q_ref[:, head(h)] = prepare(raw[:, head(h)], qg_ref[...])
    kv_ref[:, head(0)] = prepare(raw[:, head(REPEAT)], kg_ref[...])
    kv_ref[:, head(1)] = low(raw[:, head(REPEAT + 1)])
    raw_ref[...] = raw[:, : (REPEAT + 1) * HEAD_SIZE]
    gate_ref[...] = raw[:, (REPEAT + 2) * HEAD_SIZE :]


def rows_spec(rows, columns):
    return pl.BlockSpec((rows, columns), lambda i: (i, 0))


def fixed_spec(*shape):
    return pl.BlockSpec(shape, lambda i: (0,) * len(shape))


def kernel_params(vmem):
    return pltpu.CompilerParams(vmem_limit_bytes=vmem << 20)


def prepare_attention(hidden, gain_attn, w_attn, cosine, sine, gain_query, gain_key):
    tokens, width = hidden.shape
    columns = w_attn.shape[1]
    q_columns = REPEAT * HEAD_SIZE
    rows = tokens // RANKS
    shape = jax.ShapeDtypeStruct
    return pl.pallas_call(
        prepare_kernel,
        grid=(RANKS,),
        out_shape=[
            shape((tokens, width), jnp.bfloat16),
            shape((tokens, q_columns), jnp.bfloat16),
            shape((tokens, 2 * HEAD_SIZE), jnp.bfloat16),
            shape((tokens, q_columns + HEAD_SIZE), jnp.float32),
            shape((tokens, q_columns), jnp.float32),
        ],
        in_specs=[
            rows_spec(rows, width),
            fixed_spec(1, width),
            fixed_spec(width, columns),
            rows_spec(rows, HEAD_SIZE),
            rows_spec(rows, HEAD_SIZE),
            fixed_spec(1, HEAD_SIZE),
            fixed_spec(1, HEAD_SIZE),
        ],
        out_specs=[
            rows_spec(rows, width),
            rows_spec(rows, q_columns),
            rows_spec(rows, 2 * HEAD_SIZE),
            rows_spec(rows, q_columns + HEAD_SIZE),
            rows_spec(rows, q_columns),
        ],
        compiler_params=kernel_params(32),
        cost_estimate=expected(12),
    )(hidden, gain_attn[None], w_attn, cosine, sine, gain_query[None], gain_key[None])


EXPONENT = math.log2(math.e) / math.sqrt(HEAD_SIZE)


def allowed_keys(own_ref, keys_ref, z, window):
    seq, pos = own_ref[0, :, 0:1], own_ref[0, :, 1:2]
    key_seq = keys_ref[0, 0:1, z * window : (z + 1) * window]
    key_pos = keys_ref[0, 1:2, z * window : (z + 1) * window]
    return (key_pos <= pos) & ((key_seq == 0) | (key_seq == seq))


def attend_kernel(q_ref, kv_ref, gate_ref, own_ref, keys_ref, wo_ref, terms_ref, att_ref, log_ref, gated_ref):
    planes, window = kv_ref.shape[0], kv_ref.shape[1]
    totals = [None] * REPEAT
    ones = jnp.ones((window, HEAD_SIZE), jnp.bfloat16)
    for z in range(planes):
        allowed = allowed_keys(own_ref, keys_ref, z, window)
        keys = kv_ref[z, :, head(0)]
        values = jnp.concatenate([kv_ref[z, :, head(1)], ones], axis=1)
        for h in range(REPEAT):
            scores = dot_rows(q_ref[:, head(h)], keys) * EXPONENT
            exponent = low(jnp.where(allowed, jnp.exp2(scores), 0.0))
            part = dot(exponent, values)
            totals[h] = part if totals[h] is None else totals[h] + part
    for h in range(REPEAT):
        weight = totals[h][:, head(1)]
        attended = totals[h][:, head(0)] / weight
        att_ref[:, head(h)] = attended
        log_ref[:, head(h)] = jnp.log2(weight)
        gated_ref[:, head(h)] = low(attended * jax.nn.sigmoid(gate_ref[:, head(h)]))
    terms_ref[...] = low(dot(gated_ref[...], wo_ref[...]))


def group_specs(window):
    return [
        pl.BlockSpec((PLANES, window, 2 * HEAD_SIZE), lambda i: (0, i, 0)),
        pl.BlockSpec((1, window, 2), lambda i: (i, 0, 0)),
        pl.BlockSpec((1, 2, PLANES * window), lambda i: (i, 0, 0)),
    ]


def attend(query, pair, gate, own, keys, w_out):
    tokens, q_columns = query.shape
    groups = own.shape[0]
    window = tokens // groups
    width = w_out.shape[1]
    kv, mine, marks = group_specs(window)
    shape = jax.ShapeDtypeStruct
    columns = rows_spec(window, q_columns)
    return pl.pallas_call(
        attend_kernel,
        grid=(groups,),
        out_shape=[
            shape((tokens, width), jnp.bfloat16),
            shape((tokens, q_columns), jnp.float32),
            shape((tokens, q_columns), jnp.float32),
            shape((tokens, q_columns), jnp.bfloat16),
        ],
        in_specs=[columns, kv, columns, mine, marks, fixed_spec(q_columns, width)],
        out_specs=[rows_spec(window, width), columns, columns, columns],
        compiler_params=kernel_params(48),
        cost_estimate=expected(18),
    )(query, pair, gate, own, keys, w_out)


def attend_back_kernel(
    branch_ref, wo_ref, q_ref, kv_ref, gate_ref, own_ref, keys_ref, att_ref, log_ref, raw_ref,
    cos_ref, sin_ref, qg_ref, dq_ref, dgate_ref, dkv_ref, gain_ref,
):
    planes, window = kv_ref.shape[0], kv_ref.shape[1]
    scale = 1.0 / math.sqrt(HEAD_SIZE)
    d_gated = dot_rows(branch_ref[...], wo_ref[...])
    gate = jax.nn.sigmoid(gate_ref[...])
    attended = att_ref[...]
    d_attended = low(d_gated * gate)
    dgate_ref[...] = low(d_gated * attended * gate * (1.0 - gate))
    product = d_attended.astype(jnp.float32) * attended
    delta = [jnp.sum(product[:, head(h)], axis=-1, keepdims=True) for h in range(REPEAT)]
    turned_q = [jnp.transpose(q_ref[:, head(h)]) for h in range(REPEAT)]
    turned_d = [jnp.transpose(d_attended[:, head(h)]) for h in range(REPEAT)]
    d_query = [None] * REPEAT
    for z in range(planes):
        allowed = allowed_keys(own_ref, keys_ref, z, window)
        keys, values = kv_ref[z, :, head(0)], kv_ref[z, :, head(1)]
        d_keys, d_values = None, None
        for h in range(REPEAT):
            scores = dot_rows(q_ref[:, head(h)], keys) * EXPONENT - log_ref[:, h * HEAD_SIZE : h * HEAD_SIZE + 1]
            probs = jnp.where(allowed, jnp.exp2(scores), 0.0)
            d_probs = dot_rows(d_attended[:, head(h)], values)
            d_scores = low(probs * (d_probs - delta[h]))
            part = dot(d_scores, keys)
            d_query[h] = part if d_query[h] is None else d_query[h] + part
            part = dot(turned_q[h], d_scores)
            d_keys = part if d_keys is None else d_keys + part
            part = dot(turned_d[h], low(probs))
            d_values = part if d_values is None else d_values + part
        dkv_ref[z, :, head(0)] = low(jnp.transpose(d_keys * scale))
        dkv_ref[z, :, head(1)] = low(jnp.transpose(d_values))
    cosine, sine = cos_ref[...], sin_ref[...]
    total = jnp.zeros((1, HEAD_SIZE), jnp.float32)
    for h in range(REPEAT):
        grads = turn_back(d_query[h] * scale, cosine, sine)
        d_raw, by_row = norm_back(raw_ref[:, head(h)], qg_ref[...], grads)
        dq_ref[:, head(h)] = low(d_raw)
        total += jnp.sum(by_row, axis=0, keepdims=True)
    gain_ref[0] = jnp.broadcast_to(total, gain_ref.shape[1:])


def attend_back(branch, w_out, query, pair, gate, own, keys, attended, log, raw, cosine, sine, gain):
    tokens, q_columns = query.shape
    groups = own.shape[0]
    window = tokens // groups
    width = w_out.shape[1]
    kv, mine, marks = group_specs(window)
    shape = jax.ShapeDtypeStruct
    columns = rows_spec(window, q_columns)
    table = rows_spec(window, HEAD_SIZE)
    return pl.pallas_call(
        attend_back_kernel,
        grid=(groups,),
        out_shape=[
            shape((tokens, q_columns), jnp.bfloat16),
            shape((tokens, q_columns), jnp.bfloat16),
            shape(pair.shape, jnp.bfloat16),
            shape((groups, 8, HEAD_SIZE), jnp.float32),
        ],
        in_specs=[
            rows_spec(window, width), fixed_spec(q_columns, width), columns, kv, columns, mine, marks,
            columns, columns, rows_spec(window, raw.shape[1]), table, table, fixed_spec(1, HEAD_SIZE),
        ],
        out_specs=[columns, columns, kv, pl.BlockSpec((1, 8, HEAD_SIZE), lambda i: (i, 0, 0))],
        compiler_params=kernel_params(56),
        cost_estimate=expected(35),
    )(branch, w_out, query, pair, gate, own, keys, attended, log, raw, cosine, sine, gain[None])


def finish_kernel(dkv_ref, raw_ref, cos_ref, sin_ref, kg_ref, dq_ref, dgate_ref, out_ref, gain_ref):
    grads = turn_back(dkv_ref[:, head(0)], cos_ref[...], sin_ref[...])
    d_raw, by_row = norm_back(raw_ref[:, head(REPEAT)], kg_ref[...], grads)
    out_ref[:, : REPEAT * HEAD_SIZE] = dq_ref[...]
    out_ref[:, head(REPEAT)] = low(d_raw)
    out_ref[:, head(REPEAT + 1)] = low(dkv_ref[:, head(1)])
    out_ref[:, (REPEAT + 2) * HEAD_SIZE :] = dgate_ref[...]
    gain_ref[0] = jnp.broadcast_to(jnp.sum(by_row, axis=0, keepdims=True), gain_ref.shape[1:])


def finish_attention(d_pair, raw, cosine, sine, gain, d_query, d_gate, steps=4):
    tokens, q_columns = d_query.shape
    rows = tokens // steps
    shape = jax.ShapeDtypeStruct
    table = rows_spec(rows, HEAD_SIZE)
    columns = 2 * q_columns + 2 * HEAD_SIZE
    return pl.pallas_call(
        finish_kernel,
        grid=(steps,),
        out_shape=[shape((tokens, columns), jnp.bfloat16), shape((steps, 8, HEAD_SIZE), jnp.float32)],
        in_specs=[
            rows_spec(rows, 2 * HEAD_SIZE), rows_spec(rows, raw.shape[1]), table, table,
            fixed_spec(1, HEAD_SIZE), rows_spec(rows, q_columns), rows_spec(rows, q_columns),
        ],
        out_specs=[rows_spec(rows, columns), pl.BlockSpec((1, 8, HEAD_SIZE), lambda i: (i, 0, 0))],
        compiler_params=kernel_params(32),
        cost_estimate=expected(5),
    )(d_pair, raw, cosine, sine, gain[None], d_query, d_gate)


def split_kernel(pieces, gate_ref, up_ref, out_ref):
    units = gate_ref.shape[1] // CORNERS
    piece = units // pieces
    for y in range(CORNERS):
        for at, ref in ((0, gate_ref), (units, up_ref)):
            starts = [(d * CORNERS + y) * piece for d in range(pieces)]
            parts = [ref[:, start : start + piece] for start in starts]
            out_ref[y, :, at : at + units] = jnp.concatenate(parts, axis=1)


def split_units(gate, up, pieces):
    rows, units = gate.shape
    width = units // CORNERS**2
    narrow = pl.BlockSpec((rows, width), lambda i: (0, i))
    return pl.pallas_call(
        functools.partial(split_kernel, pieces),
        grid=(CORNERS**2,),
        out_shape=jax.ShapeDtypeStruct((RANKS, rows, width), gate.dtype),
        in_specs=[narrow, narrow],
        out_specs=pl.BlockSpec((CORNERS, rows, width), lambda i: (i, 0, 0)),
        cost_estimate=expected(3),
    )(gate, up)


def join_kernel(pieces, in_ref, gate_ref, up_ref):
    units = gate_ref.shape[1] // CORNERS
    piece = units // pieces
    for at, ref in ((0, gate_ref), (units, up_ref)):
        parts = []
        for d in range(pieces):
            for y in range(CORNERS):
                parts.append(in_ref[y, :, at + d * piece : at + (d + 1) * piece].astype(jnp.float32))
        ref[...] = jnp.concatenate(parts, axis=1)


def join_units(parts, pieces):
    ranks, rows, width = parts.shape
    narrow = pl.BlockSpec((rows, width), lambda i: (0, i))
    shape = jax.ShapeDtypeStruct((rows, width * CORNERS**2), jnp.float32)
    return pl.pallas_call(
        functools.partial(join_kernel, pieces),
        grid=(CORNERS**2,),
        out_shape=[shape, shape],
        in_specs=[pl.BlockSpec((CORNERS, rows, width), lambda i: (i, 0, 0))],
        out_specs=[narrow, narrow],
        cost_estimate=expected(4),
    )(parts)


def widen_kernel(in_ref, *out_refs):
    start = 0
    for ref in out_refs:
        width = ref.shape[1]
        ref[...] = in_ref[0, :, start : start + width].astype(jnp.float32)
        start += width


def widen_columns(parts, widths):
    ranks, rows, columns = parts.shape
    return pl.pallas_call(
        widen_kernel,
        grid=(ranks,),
        out_shape=[jax.ShapeDtypeStruct((rows, ranks * w), jnp.float32) for w in widths],
        in_specs=[pl.BlockSpec((1, rows, columns), lambda i: (i, 0, 0))],
        out_specs=[pl.BlockSpec((rows, w), lambda i: (0, i)) for w in widths],
        cost_estimate=expected(3),
    )(parts)


def make_shards(cells):
    data_total = cells * PLANES

    def blocks(terms):
        return low(terms).reshape(RANKS, -1, terms.shape[1])

    def gather_tokens(rows):
        return run([gather_part(rows)], 0)[0]

    def scatter_tokens(terms):
        return run([scatter_part(blocks(terms))], 1, 40)[0]

    def split_columns(weight):
        return weight.reshape(weight.shape[0], RANKS, -1)

    def send_columns(pieces):
        return jnp.transpose(jnp.concatenate(pieces, axis=-1), (1, 0, 2))

    def join_cells(rows):
        if cells > 1:
            rows = lax.all_gather(rows, "cell", axis=0, tiled=False)
            rows = jnp.transpose(rows, (1, 0, 2, 3, 4, 5))
        return rows.reshape(-1, rows.shape[-1])

    def gather_columns(mine):
        rows, columns = mine.shape[1:]
        every = lax.all_gather(mine, DATA, axis=0, tiled=False)
        every = every.reshape(data_total, CORNERS**2, CORNERS, rows, columns)
        return jnp.transpose(every, (1, 0, 2, 3, 4)).reshape(-1, columns)

    def sum_columns(term):
        rows = term.shape[0] // (RANKS * data_total)
        split = low(term).reshape(CORNERS**2, data_total, CORNERS, rows, -1)
        split = jnp.transpose(split, (1, 0, 2, 3, 4)).reshape(data_total * RANKS, rows, -1)
        return lax.psum_scatter(split, DATA, scatter_dimension=0, tiled=True)

    inner = CORNERS * data_total
    to_rank = []
    for source in range(inner):
        rank_y, place = divmod(source, data_total)
        to_rank.append((source, place * CORNERS + rank_y))
    from_rank = [(b, a) for a, b in to_rank]
    INNER = ("cell", "z", "y")

    def shards(
        hidden_in,
        query_weight,
        key_matrix,
        value_matrix,
        gate_weight,
        out_weight,
        norm_attn,
        query_gain,
        key_gain,
        norm_ffn,
        ffn_gate,
        ffn_up,
        ffn_down,
        cotangent,
        sequence_numbers,
        positions,
    ):
        rows = hidden_in.shape[0]
        tokens = rows * RANKS
        groups = CORNERS**2
        window = GROUP_TOKENS // PLANES

        sizes = [norm_attn.shape[0], norm_ffn.shape[0], query_gain.shape[0], key_gain.shape[0]]
        cuts = [0]
        for size in sizes:
            cuts.append(cuts[-1] + size)
        tile = (8, HEAD_SIZE)
        pad = tile[0] * tile[1] - cuts[-1]
        own_gains = jnp.concatenate([norm_attn, norm_ffn, query_gain, key_gain]).astype(jnp.float32)
        own_gains = jnp.pad(own_gains, (0, pad)).reshape(tile)
        plane = lax.axis_index("z")
        group_start = lax.axis_index("cell") * GROUP_TOKENS
        marks = jnp.concatenate(
            [
                lax.dynamic_slice_in_dim(sequence_numbers, group_start, GROUP_TOKENS),
                lax.dynamic_slice_in_dim(positions, group_start, GROUP_TOKENS),
            ]
        ).reshape(-1, HEAD_SIZE)
        attn_columns = send_columns(
            [
                split_columns(query_weight),
                split_columns(key_matrix),
                split_columns(value_matrix),
                split_columns(gate_weight),
            ]
        )
        attn_rows, hidden_all, gains, marks = run(
            [
                columns_part(attn_columns),
                gather_part(hidden_in),
                hello_part(RANKS * data_total, own_gains, marks),
            ],
            2,
            micros=70,
        )
        attn_rows, out_rows, down_rows = lax.optimization_barrier(
            (attn_rows, lax.ppermute(out_weight, INNER, to_rank), ffn_down)
        )
        w_attn = join_cells(attn_rows)
        gains = gains.reshape(RANKS * data_total, -1)
        gain_attn, gain_ffn, gain_query, gain_key = (
            gains[:, a:b].reshape(-1) for a, b in zip(cuts[:-1], cuts[1:])
        )
        w_out = lax.all_gather(out_rows, DATA, axis=0, tiled=True)
        w_down = lax.all_gather(down_rows, DATA, axis=0, tiled=True)

        marks = marks.reshape(groups, 2, GROUP_TOKENS)
        own_marks = lax.dynamic_slice_in_dim(marks, plane * window, window, axis=2)
        cosine, sine = rope_tables(own_marks[:, 1].reshape(tokens))
        own_marks = jnp.transpose(own_marks, (0, 2, 1))

        hidden = hidden_in.astype(jnp.float32)
        normed_input, query_low, pair, raw, gate_raw = prepare_attention(
            hidden_all, gain_attn, w_attn, cosine, sine, gain_query, gain_key
        )
        ffn_columns = split_units(ffn_gate, ffn_up, data_total)
        pair, cotangent_all, ffn_columns = run(
            [line_gather_part(pair), gather_part(cotangent), swap_part(ffn_columns)], 3, micros=75
        )
        w_ffn = gather_columns(ffn_columns)
        out_terms, attended, log_weight, gated_low = attend(
            query_low, pair, gate_raw, own_marks, marks, w_out
        )
        out_terms = out_terms.reshape(RANKS, rows, -1)
        middle = hidden + run([scatter_part(out_terms)], 1, 40)[0]

        normed_two = gather_tokens(low(root_mean_scale(middle, gain_ffn)))
        both = matrix_product(normed_two, w_ffn)
        units = both.shape[1] // 2
        gate_ffn, up_ffn = both[:, :units], both[:, units:]
        ffn_sig = jax.nn.sigmoid(gate_ffn)
        mixed_low = low(gate_ffn * ffn_sig * up_ffn)
        down_terms = blocks(matrix_product(mixed_low, w_down))

        down_term = low(contract_first(mixed_low, cotangent_all))
        down_term, cotangent_all = lax.optimization_barrier((down_term, cotangent_all))
        grad_down = lax.psum_scatter(down_term, DATA, scatter_dimension=0, tiled=True).astype(
            jnp.float32
        )
        d_mixed = contract_last(cotangent_all, w_down)
        d_up_low = low(d_mixed * gate_ffn * ffn_sig)
        d_gate_ffn_low = low(d_mixed * up_ffn * ffn_sig * (1.0 + gate_ffn * (1.0 - ffn_sig)))
        d_both = jnp.concatenate([d_gate_ffn_low, d_up_low], axis=-1)
        both_term = low(contract_first(normed_two, d_both))
        both_term, d_both = lax.optimization_barrier((both_term, d_both))
        two_terms = blocks(contract_last(d_both, w_ffn))
        grad_both = sum_columns(both_term)
        two_terms, grad_down = lax.optimization_barrier((two_terms, grad_down))
        (d_normed_two,) = run([scatter_part(two_terms)], 1, 40)
        unused_two, norm_two_back = jax.vjp(root_mean_scale, middle, gain_ffn)
        d_middle_norm, grad_norm_two_term = norm_two_back(d_normed_two)
        d_middle = cotangent.astype(jnp.float32) + d_middle_norm

        branch_all = gather_tokens(low(d_middle))
        grad_out = lax.psum_scatter(
            low(contract_first(gated_low, branch_all)), DATA, scatter_dimension=0, tiled=True
        )
        grad_out = lax.ppermute(grad_out, INNER, from_rank).astype(jnp.float32)
        d_query, d_gate, d_pair, query_gain_terms = attend_back(
            branch_all, w_out, query_low, pair, gate_raw, own_marks, marks,
            attended, log_weight, raw, cosine, sine, gain_query,
        )
        d_pair, result, grad_both = run(
            [
                line_scatter_part(d_pair),
                scatter_part(down_terms),
                swap_part(grad_both),
            ],
            5,
            56,
            75,
        )
        output = low(middle + result)
        d_raw, key_gain_terms = finish_attention(
            d_pair, raw, cosine, sine, gain_key, d_query, d_gate
        )
        grad_query_gain_term = jnp.sum(query_gain_terms[:, 0], axis=0)
        grad_key_gain_term = jnp.sum(key_gain_terms[:, 0], axis=0)
        a = REPEAT * HEAD_SIZE
        b, c = a + HEAD_SIZE, a + 2 * HEAD_SIZE
        attn_term = low(contract_first(normed_input, d_raw))
        attn_term, d_raw = lax.optimization_barrier((attn_term, d_raw))
        one_terms = blocks(contract_last(d_raw, w_attn))
        grad_attn = sum_columns(attn_term)
        (d_normed,) = run([scatter_part(one_terms)], 1, 40)
        unused_one, norm_one_back = jax.vjp(root_mean_scale, hidden, gain_attn)
        d_hidden_norm, grad_norm_one_term = norm_one_back(d_normed)
        input_grad = d_middle + d_hidden_norm

        terms = jnp.concatenate(
            [
                t.reshape(RANKS * data_total, -1)
                for t in (
                    grad_norm_one_term,
                    grad_norm_two_term,
                    grad_query_gain_term,
                    grad_key_gain_term,
                )
            ],
            axis=-1,
        )
        terms = jnp.pad(terms, ((0, 0), (0, pad))).reshape((-1,) + tile)
        grad_attn, small = run([swap_part(grad_attn), spread_part(terms)], 4, micros=15)
        small = small.reshape(-1)
        grad_query, grad_key, grad_value, grad_gatew = widen_columns(grad_attn, (a, b - a, c - b, a))
        grad_both, d_normed = lax.optimization_barrier((grad_both, d_normed))
        grad_gate, grad_up = join_units(grad_both, data_total)
        grad_norm_attn, grad_norm_ffn, grad_query_gain, grad_key_gain = (
            small[s:e] for s, e in zip(cuts[:-1], cuts[1:])
        )
        return (
            output,
            input_grad,
            grad_query,
            grad_key,
            grad_value,
            grad_gatew,
            grad_out,
            grad_norm_attn,
            grad_query_gain,
            grad_key_gain,
            grad_norm_ffn,
            grad_gate,
            grad_up,
            grad_down,
        )

    return shards


def solution(mesh):
    cells = mesh.shape["fsdp"] // (PLANES * CORNERS)
    split = Mesh(
        mesh.devices.reshape(CORNERS, CORNERS, cells, PLANES, CORNERS),
        ALL,
    )
    rows, flat, group = P(ALL, None), P(ALL), P(("x", "core"))
    return jax.shard_map(
        make_shards(cells),
        mesh=split,
        in_specs=(rows,) * 6 + (flat,) * 4 + (rows,) * 4 + (group,) * 2,
        out_specs=(rows,) * 7 + (flat,) * 4 + (rows,) * 3,
        check_vma=False,
    )
```

```python
import functools
import math

import jax
import jax.numpy as jnp
from jax import lax
from jax.experimental import pallas as pl
from jax.experimental.pallas import tpu as pltpu
from jax.sharding import Mesh
from jax.sharding import PartitionSpec as P

QUERY_HEADS = 16
KEY_VALUE_HEADS = 8
HEAD_SIZE = 128
REPEAT = QUERY_HEADS // KEY_VALUE_HEADS
GROUP_TOKENS = 2048
CORNERS = 2
PLANES = 4
ALL = ("x", "core", "cell", "z", "y")
TENSOR = ("x", "core", "y")
DATA = ("cell", "z")
RANKS = CORNERS**3
CHUNKS = 4
MESH_ID = pl.DeviceIdType.MESH
OTHERS = [(dx, dc, dy) for dx in (0, 1) for dc in (0, 1) for dy in (0, 1) if dx + dc + dy]
DMA = pltpu.SemaphoreType.DMA
VMEM = pl.BlockSpec(memory_space=pltpu.VMEM)
ANYWHERE = pl.BlockSpec(memory_space=pl.ANY)


def remote(source, target, send, receive, device):
    return pltpu.make_async_remote_copy(
        src_ref=source,
        dst_ref=target,
        send_sem=send,
        recv_sem=receive,
        device_id=device,
        device_id_type=MESH_ID,
    )


def landed(ref, sem, device):
    remote(ref, ref, sem, sem, device).wait_recv()


def corner():
    return lax.axis_index("x"), lax.axis_index("core"), lax.axis_index("y")


def slot(x, c, y):
    return (x * CORNERS + c) * CORNERS + y


def flip(value, bit):
    return 1 - value if bit else value


def neighbours():
    x, c, y = corner()
    return {"x": 1 - x}, {"y": 1 - y}, {"core": 1 - c}


def plane_peers():
    x, c, y = corner()
    peers = []
    for dx, dc, dy in OTHERS:
        px, pc, py = flip(x, dx), flip(c, dc), flip(y, dy)
        peers.append(({"x": px, "core": pc, "y": py}, slot(px, pc, py)))
    return peers


def greet(plane, line):
    if plane == "world":
        everyone(math.prod(lax.axis_size(n) for n in ALL))
        return
    barrier = pltpu.get_barrier_semaphore()
    near = {"near": neighbours(), "all": [p for p, _ in plane_peers()], None: []}[plane]
    for device in near:
        pl.semaphore_signal(barrier, inc=1, device_id=device, device_id_type=MESH_ID)
    if not line:
        pl.semaphore_wait(barrier, len(near))
        return
    z = lax.axis_index("z")

    @pl.when(z > 0)
    def _():
        pl.semaphore_signal(barrier, inc=1, device_id={"z": z - 1}, device_id_type=MESH_ID)

    @pl.when(z < PLANES - 1)
    def _():
        pl.semaphore_signal(barrier, inc=1, device_id={"z": z + 1}, device_id_type=MESH_ID)

    edge = (z == 0) | (z == PLANES - 1)

    @pl.when(edge)
    def _():
        pl.semaphore_wait(barrier, len(near) + 1)

    @pl.when(jnp.logical_not(edge))
    def _():
        pl.semaphore_wait(barrier, len(near) + 2)


class Part:
    def __init__(self, inputs, outs, scratch, steps, plane=None, line=False):
        self.begin = 0.0
        self.inputs = inputs
        self.outs = outs
        self.scratch = scratch
        self.steps = steps
        self.plane, self.line = plane, line


def run_kernel(parts, *refs):
    refs = list(refs)

    def take(counts):
        groups = []
        for count in counts:
            groups.append(refs[:count])
            del refs[:count]
        return groups

    ins = take([len(p.inputs) for p in parts])
    outs = take([len(p.outs) for p in parts])
    scratch = take([len(p.scratch) for p in parts])
    ranks = [None, "near", "all", "world"]
    plane = ranks[max(ranks.index(p.plane) for p in parts)]
    greet(plane, any(p.line for p in parts))
    plans = [p.steps(i, o, s) for p, i, o, s in zip(parts, ins, outs, scratch)]
    ordered = []
    for p, (first, middle, _) in zip(parts, plans):
        ordered.append((p.begin - 1.0 if p.begin == 0 else p.begin, first))
        for n, step in enumerate(middle):
            ordered.append((p.begin + (1.0 - p.begin) * (n + 0.5) / len(middle), step))
    for _, step in sorted(ordered, key=lambda pair: pair[0]):
        step()
    for _, _, last in plans:
        last()


def expected(micros):
    return pl.CostEstimate(flops=0, bytes_accessed=int(micros * 3.5e6), transcendentals=0)


def run(parts, collective_id, vmem=None, micros=40):
    inputs = [pair for p in parts for pair in p.inputs]
    outs = [pair for p in parts for pair in p.outs]
    return pl.pallas_call(
        functools.partial(run_kernel, parts),
        out_shape=[shape for shape, _ in outs],
        in_specs=[spec for _, spec in inputs],
        out_specs=[spec for _, spec in outs],
        scratch_shapes=[s for p in parts for s in p.scratch],
        compiler_params=pltpu.CompilerParams(
            collective_id=collective_id,
            has_side_effects=True,
            vmem_limit_bytes=None if vmem is None else vmem << 20,
        ),
        cost_estimate=expected(micros),
    )(*[array for array, _ in inputs])


def later(part, begin):
    part.begin = begin
    return part


def gather_part(block):
    rows, columns = block.shape
    n, half = CHUNKS, CHUNKS // 2
    chunk = rows // n

    def steps(ins, outs, scratch):
        (in_ref,), (out_ref,) = ins, outs
        send_x, send_y, send_c, recv_x, recv_y, recv_c, local = scratch
        x, c, y = corner()
        dev_x, dev_y, dev_c = neighbours()

        def at(index, k):
            start = pl.multiple_of(index * rows + k * chunk, chunk)
            return out_ref.at[pl.ds(start, chunk), :]

        own, beside_x, beside_y = slot(x, c, y), slot(1 - x, c, y), slot(x, c, 1 - y)
        across = slot(1 - x, c, 1 - y)
        mirror = [
            slot(x, 1 - c, y),
            slot(1 - x, 1 - c, y),
            slot(x, 1 - c, 1 - y),
            slot(1 - x, 1 - c, 1 - y),
        ]
        start = pl.multiple_of(own * rows, rows)
        keep = pltpu.make_async_copy(in_ref, out_ref.at[pl.ds(start, rows), :], local)
        sent = []

        def go(copy):
            copy.start()
            sent.append(copy)

        def share(index, k, b):
            go(remote(at(index, k), at(index, k), send_c.at[b * n + k], recv_c.at[b * n + k], dev_c))

        order_x = list(range(n))
        order_y = order_x[half:] + order_x[:half]

        def first():
            keep.start()

            def mine(k):
                return in_ref.at[pl.ds(k * chunk, chunk), :]

            for k, j in zip(order_x, order_y):
                go(remote(mine(k), at(own, k), send_x.at[k], recv_x.at[k], dev_x))
                go(remote(mine(j), at(own, j), send_y.at[j], recv_y.at[j], dev_y))
            for k in range(n):
                go(remote(mine(k), at(own, k), send_c.at[k], recv_c.at[k], dev_c))

        def straight(k, j):
            landed(at(beside_x, k), recv_x.at[k], dev_x)
            if k < half:
                to = at(beside_x, k)
                go(remote(to, to, send_y.at[n + k], recv_y.at[n + k], dev_y))
            share(beside_x, k, 1)
            landed(at(beside_y, j), recv_y.at[j], dev_y)
            if j >= half:
                to = at(beside_y, j)
                go(remote(to, to, send_x.at[half + j], recv_x.at[half + j], dev_x))
            share(beside_y, j, 2)

        def diagonal(k):
            landed(at(across, k), recv_y.at[n + k], dev_y)
            share(across, k, 3)
            landed(at(across, half + k), recv_x.at[n + k], dev_x)
            share(across, half + k, 3)

        def last():
            for b in range(4):
                for k in range(n):
                    landed(at(mirror[b], k), recv_c.at[b * n + k], dev_c)
            for copy in sent:
                copy.wait_send()
            keep.wait()

        middle = [functools.partial(straight, k, j) for k, j in zip(order_x, order_y)]
        middle += [functools.partial(diagonal, k) for k in range(half)]
        return first, middle, last

    link = DMA((n + half,))
    core = DMA((4 * n,))
    return Part(
        [(block, VMEM)],
        [(jax.ShapeDtypeStruct((RANKS * rows, columns), block.dtype), ANYWHERE)],
        [link, link, core, link, link, core, DMA(())],
        steps,
        plane="near",
    )


def add_rows(target, start, count, sources, step=16):
    def body(i, carry):
        r = pl.multiple_of(start + i * step, step)
        total = None
        for ref, shift in sources:
            value = ref[pl.ds(r - shift if shift else r, step), :].astype(jnp.float32)
            total = value if total is None else total + value
        target[pl.ds(r, step), :] = total.astype(target.dtype)
        return carry

    lax.fori_loop(0, count // step, body, 0)


def scatter_part(terms=None, product=None, transposed=False, tile=512):
    if product is None:
        ranks, rows, columns = terms.shape
    else:
        left, right = product
        rows, columns = left.shape[0] // RANKS, right.shape[0 if transposed else 1]
    n, half = CHUNKS, CHUNKS // 2
    chunk = rows // n
    middle_row = half * chunk

    def steps(ins, outs, scratch):
        (out_ref,) = outs
        if product is None:
            (part_ref,) = ins
        else:
            left_ref, right_ref = ins
            part_ref, scratch = scratch[-1], scratch[:-1]
        core_buf, x_buf, y_buf, x_diag, y_diag, d_sum, x_sum, y_sum = scratch[:8]
        send_c, recv_c, send_x, recv_x, send_y, recv_y = scratch[8:]
        x, c, y = corner()
        dev_x, dev_y, dev_c = neighbours()
        D, X, Y, O = range(4)
        place = [(1 - x, 1 - y), (1 - x, y), (x, 1 - y), (x, y)]
        mine = [slot(px, c, py) for px, py in place]
        theirs = [slot(px, 1 - c, py) for px, py in place]
        orders = {D: [], X: list(range(n)), O: list(range(n))}
        for k in range(half):
            orders[D] += [k, half + k]
        orders[Y] = orders[X][half:] + orders[X][:half]
        sent = []

        def go(copy):
            copy.start()
            sent.append(copy)

        def piece(k):
            return pl.ds(k * chunk, chunk)

        def make(index):
            def body(j, carry):
                at = pl.ds(pl.multiple_of(j * tile, tile), tile)
                some = left_ref[pl.ds(pl.multiple_of(index * rows, rows), rows), :]
                if transposed:
                    value = dot_rows(some, right_ref[at, :])
                else:
                    value = dot(some, right_ref[:, at])
                part_ref[index, :, at] = low(value)
                return carry

            lax.fori_loop(0, columns // tile, body, 0)

        def to_core(b):
            for k in orders[b]:
                source = part_ref.at[theirs[b], piece(k), :]
                i = b * n + k
                go(remote(source, core_buf.at[b, piece(k), :], send_c.at[i], recv_c.at[i], dev_c))

        def made_for_core(b):
            make(theirs[b])
            to_core(b)

        def first():
            if product is None:
                for b in (D, X, Y, O):
                    to_core(b)
            else:
                made_for_core(D)
                make(mine[D])

        def chip(target, b, k, *more):
            landed(core_buf.at[b, piece(k), :], recv_c.at[b * n + k], dev_c)
            sources = [(part_ref.at[mine[b]], 0), (core_buf.at[b], 0), *more]
            add_rows(target, k * chunk, chunk, sources)

        def to_x(k):
            go(remote(x_sum.at[piece(k), :], x_buf.at[piece(k), :], send_x.at[k], recv_x.at[k], dev_x))

        def to_y(k):
            go(remote(y_sum.at[piece(k), :], y_buf.at[piece(k), :], send_y.at[k], recv_y.at[k], dev_y))

        def diagonal(k):
            chip(d_sum, D, k)
            source = d_sum.at[piece(k), :]
            if k < half:
                go(remote(source, x_diag.at[piece(k), :], send_x.at[n + k], recv_x.at[n + k], dev_x))
            else:
                to = y_diag.at[piece(k - half), :]
                go(remote(source, to, send_y.at[half + k], recv_y.at[half + k], dev_y))

        def direct(k):
            chip(x_sum, X, k)
            to_x(k)
            chip(y_sum, Y, half + k)
            to_y(half + k)

        def relayed(k):
            landed(y_diag.at[piece(k), :], recv_y.at[n + k], dev_y)
            chip(x_sum, X, half + k, (y_diag, middle_row))
            to_x(half + k)
            landed(x_diag.at[piece(k), :], recv_x.at[n + k], dev_x)
            chip(y_sum, Y, k, (x_diag, 0))
            to_y(k)

        def own(k):
            landed(x_buf.at[piece(k), :], recv_x.at[k], dev_x)
            landed(y_buf.at[piece(k), :], recv_y.at[k], dev_y)
            chip(out_ref, O, k, (x_buf, 0), (y_buf, 0))

        def last():
            for copy in sent:
                copy.wait_send()

        def makes(b):
            if product is None:
                return []
            return [functools.partial(made_for_core, b), functools.partial(make, mine[b])]

        middle = [functools.partial(diagonal, k) for k in orders[D]]
        middle += makes(X) + makes(Y)
        middle += [functools.partial(direct, k) for k in range(half)]
        middle += makes(O)
        middle += [functools.partial(relayed, k) for k in range(half)]
        middle += [functools.partial(own, k) for k in range(n)]
        return first, middle, last

    def low_vmem(*shape):
        return pltpu.VMEM(shape, jnp.bfloat16)

    whole, part = low_vmem(rows, columns), low_vmem(rows // 2, columns)
    link = DMA((n + half,))
    core = DMA((4 * n,))
    made = [] if product is None else [low_vmem(RANKS, rows, columns)]
    return Part(
        [(terms, VMEM)] if product is None else [(left, VMEM), (right, VMEM)],
        [(jax.ShapeDtypeStruct((rows, columns), jnp.float32), VMEM)],
        [low_vmem(4, rows, columns), whole, whole, part, part, whole, whole, whole]
        + [core, core, link, link, link, link]
        + made,
        steps,
        plane="near",
    )


def swap_part(blocks):
    def steps(ins, outs, scratch):
        (in_ref,), (out_ref,) = ins, outs
        send, recv, local = scratch
        own = slot(*corner())
        keep = pltpu.make_async_copy(in_ref.at[own], out_ref.at[own], local)
        peers = plane_peers()
        sent = []

        def first():
            keep.start()
            for i, (there, other) in enumerate(peers):
                copy = remote(in_ref.at[other], out_ref.at[own], send.at[i], recv.at[i], there)
                copy.start()
                sent.append(copy)

        def last():
            for i, (there, other) in enumerate(peers):
                landed(out_ref.at[other], recv.at[i], there)
            for copy in sent:
                copy.wait_send()
            keep.wait()

        return first, [], last

    n = len(OTHERS)
    return Part(
        [(blocks, VMEM)],
        [(jax.ShapeDtypeStruct(blocks.shape, blocks.dtype), ANYWHERE)],
        [DMA((n,)), DMA((n,)), DMA(())],
        steps,
        plane="all",
    )


def owners_part(block):
    def steps(ins, outs, scratch):
        (in_ref,), (out_ref,) = ins, outs
        send, recv, local = scratch
        cells = lax.axis_size("cell")
        total = cells * PLANES
        y, place = lax.axis_index("y"), lax.axis_index("cell") * PLANES + lax.axis_index("z")
        here = place * CORNERS + y
        to = y * total + place
        whence = lax.rem(here, total) * CORNERS + here // total

        def device(index):
            planes = index // CORNERS
            return {"cell": planes // PLANES, "z": lax.rem(planes, PLANES), "y": lax.rem(index, CORNERS)}

        def first():
            @pl.when(to == here)
            def _():
                pltpu.make_async_copy(in_ref, out_ref, local).start()

            @pl.when(to != here)
            def _():
                remote(in_ref, out_ref, send, recv, device(to)).start()

        def last():
            @pl.when(to == here)
            def _():
                pltpu.make_async_copy(in_ref, out_ref, local).wait()

            @pl.when(to != here)
            def _():
                landed(out_ref, recv, device(whence))
                remote(in_ref, out_ref, send, recv, device(to)).wait_send()

        return first, [], last

    return Part(
        [(block, VMEM)],
        [(jax.ShapeDtypeStruct(block.shape, block.dtype), VMEM)],
        [DMA(()), DMA(()), DMA(())],
        steps,
        plane="world",
    )


def line_gather_part(block, pieces=4):
    rows = block.shape[0] // pieces

    def steps(ins, outs, scratch):
        (in_ref,), (out_ref,) = ins, outs
        up_send, up_recv, down_send, down_recv, local = scratch
        z = lax.axis_index("z")
        keep = pltpu.make_async_copy(in_ref, out_ref.at[z], local)

        def at(block, k):
            return out_ref.at[block, pl.ds(k * rows, rows), :]

        def up(t, k, source=None):
            s = at(z - t, k) if source is None else source
            i = t * pieces + k
            return remote(s, at(z - t, k), up_send.at[i], up_recv.at[i], {"z": z + 1})

        def down(t, k, source=None):
            s = at(z + t, k) if source is None else source
            i = t * pieces + k
            return remote(s, at(z + t, k), down_send.at[i], down_recv.at[i], {"z": z - 1})

        def first():
            keep.start()
            for k in range(pieces):
                mine = in_ref.at[pl.ds(k * rows, rows), :]

                @pl.when(z < PLANES - 1)
                def _():
                    up(0, k, mine).start()

                @pl.when(z > 0)
                def _():
                    down(0, k, mine).start()

        def arrive(t, k):
            i = t * pieces + k
            on = t + 1 < PLANES - 1

            @pl.when(z - 1 - t >= 0)
            def _():
                landed(at(z - 1 - t, k), up_recv.at[i], {"z": z - 1})
                if on:

                    @pl.when(z < PLANES - 1)
                    def _():
                        up(t + 1, k).start()

            @pl.when(z + 1 + t < PLANES)
            def _():
                landed(at(z + 1 + t, k), down_recv.at[i], {"z": z + 1})
                if on:

                    @pl.when(z > 0)
                    def _():
                        down(t + 1, k).start()

        def last():
            for t in range(PLANES - 1):
                for k in range(pieces):

                    @pl.when((z < PLANES - 1) & (z - t >= 0))
                    def _():
                        up(t, k).wait_send()

                    @pl.when((z > 0) & (z + t < PLANES))
                    def _():
                        down(t, k).wait_send()

            keep.wait()

        middle = [
            functools.partial(arrive, t, k) for t in range(PLANES - 1) for k in range(pieces)
        ]
        return first, middle, last

    sems = DMA(((PLANES - 1) * pieces,))
    return Part(
        [(block, VMEM)],
        [(jax.ShapeDtypeStruct((PLANES,) + block.shape, block.dtype), ANYWHERE)],
        [sems, sems, sems, sems, DMA(())],
        steps,
        line=True,
    )


def line_scatter_part(terms, pieces=4):
    line, all_rows, columns = terms.shape
    rows = all_rows // pieces
    step = 32

    def steps(ins, outs, scratch):
        (in_ref,), (out_ref,) = ins, outs
        up_buf, down_buf, up_stage, down_stage, up_send, up_recv, down_send, down_recv = scratch
        z = lax.axis_index("z")
        f32 = jnp.float32

        def cut(k):
            return pl.ds(k * rows, rows)

        def send_up(source, d, k):
            i = (d - 1) * pieces + k
            return remote(source, up_buf.at[d - 1, cut(k), :], up_send.at[i], up_recv.at[i], {"z": z + 1})

        def send_down(source, d, k):
            i = (d - 1) * pieces + k
            to = down_buf.at[d - 1, cut(k), :]
            return remote(source, to, down_send.at[i], down_recv.at[i], {"z": z - 1})

        def first():
            pass

        def pass_on(d, k):
            @pl.when(z + d < line)
            def _():
                @pl.when(z == 0)
                def _():
                    send_up(in_ref.at[z + d, cut(k), :], d, k).start()

                if d + 1 < line:

                    @pl.when(z > 0)
                    def _():
                        landed(up_buf.at[d, cut(k), :], up_recv.at[d * pieces + k], {"z": z - 1})
                        sources = [(in_ref.at[z + d], 0), (up_buf.at[d], 0)]
                        add_rows(up_stage.at[d - 1], k * rows, rows, sources, step)
                        send_up(up_stage.at[d - 1, cut(k), :], d, k).start()

            @pl.when(z - d >= 0)
            def _():
                @pl.when(z == line - 1)
                def _():
                    send_down(in_ref.at[z - d, cut(k), :], d, k).start()

                if d + 1 < line:

                    @pl.when(z < line - 1)
                    def _():
                        landed(down_buf.at[d, cut(k), :], down_recv.at[d * pieces + k], {"z": z + 1})
                        sources = [(in_ref.at[z - d], 0), (down_buf.at[d], 0)]
                        add_rows(down_stage.at[d - 1], k * rows, rows, sources, step)
                        send_down(down_stage.at[d - 1, cut(k), :], d, k).start()

        def own(k):
            @pl.when(z > 0)
            def _():
                landed(up_buf.at[0, cut(k), :], up_recv.at[k], {"z": z - 1})

            @pl.when(z < line - 1)
            def _():
                landed(down_buf.at[0, cut(k), :], down_recv.at[k], {"z": z + 1})

            mine, below, above = (in_ref.at[z], 0), (up_buf.at[0], 0), (down_buf.at[0], 0)

            @pl.when(z == 0)
            def _():
                add_rows(out_ref, k * rows, rows, [mine, above], step)

            @pl.when(z == line - 1)
            def _():
                add_rows(out_ref, k * rows, rows, [mine, below], step)

            @pl.when((z > 0) & (z < line - 1))
            def _():
                add_rows(out_ref, k * rows, rows, [mine, below, above], step)

        def last():
            for d in range(line - 1, 0, -1):
                for k in range(pieces):

                    @pl.when(z + d < line)
                    def _():
                        send_up(up_stage.at[d - 1, cut(k), :], d, k).wait_send()

                    @pl.when(z - d >= 0)
                    def _():
                        send_down(down_stage.at[d - 1, cut(k), :], d, k).wait_send()

        middle = [
            functools.partial(pass_on, d, k) for d in range(line - 1, 0, -1) for k in range(pieces)
        ]
        middle += [functools.partial(own, k) for k in range(pieces)]
        return first, middle, last

    sems = DMA(((line - 1) * pieces,))
    buffer = pltpu.VMEM((line - 1, all_rows, columns), jnp.bfloat16)
    return Part(
        [(terms, VMEM)],
        [(jax.ShapeDtypeStruct((all_rows, columns), jnp.float32), VMEM)],
        [buffer, buffer, buffer, buffer, sems, sems, sems, sems],
        steps,
        line=True,
    )


def places():
    sizes = [lax.axis_size(n) for n in ALL]
    me = 0
    for n, size in zip(ALL, sizes):
        me = me * size + lax.axis_index(n)

    def device(index):
        where = {}
        for n, size in reversed(list(zip(ALL, sizes))):
            where[n] = lax.rem(index, size)
            index = index // size
        return where

    return me, device


def everyone(total):
    me, device = places()
    barrier = pltpu.get_barrier_semaphore()

    def greet_one(d, carry):
        other = device(lax.rem(me + d, total))
        pl.semaphore_signal(barrier, inc=1, device_id=other, device_id_type=MESH_ID)
        return carry

    lax.fori_loop(1, total, greet_one, 0)
    pl.semaphore_wait(barrier, total - 1)
    return me, device


def hello_part(total, gains, marks):
    def steps(ins, outs, scratch):
        gains_ref, marks_ref = ins
        gains_out, marks_out = outs
        g_send, g_recv, m_send, m_recv, local = scratch
        me, device = places()
        x, c, y = corner()
        group = x * CORNERS + c
        keeps = [
            pltpu.make_async_copy(gains_ref, gains_out.at[me], local.at[0]),
            pltpu.make_async_copy(marks_ref, marks_out.at[group], local.at[1]),
        ]
        near = [(i, dx, dc) for i, (dx, dc) in enumerate([(0, 1), (1, 0), (1, 1)])]
        sent = []

        def give(d):
            other = device(lax.rem(me + d, total))
            return remote(gains_ref, gains_out.at[me], g_send.at[d], g_recv.at[d], other)

        def first():
            for keep in keeps:
                keep.start()
            for i, dx, dc in near:
                there = {"x": flip(x, dx), "core": flip(c, dc)}
                copy = remote(marks_ref, marks_out.at[group], m_send.at[i], m_recv.at[i], there)
                copy.start()
                sent.append(copy)

            def put(d, carry):
                give(d).start()
                return carry

            lax.fori_loop(1, total, put, 0)

        def last():
            def take(d, carry):
                source = lax.rem(me + total - d, total)
                landed(gains_out.at[source], g_recv.at[d], device(source))
                give(d).wait_send()
                return carry

            lax.fori_loop(1, total, take, 0)
            for i, dx, dc in near:
                there = {"x": flip(x, dx), "core": flip(c, dc)}
                theirs = flip(x, dx) * CORNERS + flip(c, dc)
                landed(marks_out.at[theirs], m_recv.at[i], there)
            for copy in sent:
                copy.wait_send()
            for keep in keeps:
                keep.wait()

        return first, [], last

    return Part(
        [(gains, VMEM), (marks, VMEM)],
        [
            (jax.ShapeDtypeStruct((total,) + gains.shape, gains.dtype), VMEM),
            (jax.ShapeDtypeStruct((CORNERS**2,) + marks.shape, marks.dtype), VMEM),
        ],
        [DMA((total,)), DMA((total,)), DMA((3,)), DMA((3,)), DMA((2,))],
        steps,
        plane="world",
    )


def columns_part(blocks):
    ranks, rows, columns = blocks.shape

    def steps(ins, outs, scratch):
        (in_ref,), (out_ref,) = ins, outs
        send, recv, up_send, up_recv, down_send, down_recv, local = scratch
        x, c, y = corner()
        z = lax.axis_index("z")
        own = slot(x, c, y)
        peers = plane_peers()
        spots = [(x * CORNERS + c, y)]
        spots += [(flip(x, dx) * CORNERS + flip(c, dc), flip(y, dy)) for dx, dc, dy in OTHERS]

        def at(i, plane):
            return out_ref.at[spots[i][0], plane, spots[i][1]]

        keep = pltpu.make_async_copy(in_ref.at[own], at(0, z), local)
        sent = []

        def up(t, i, source=None):
            s = at(i, z - t) if source is None else source
            n = t * RANKS + i
            return remote(s, at(i, z - t), up_send.at[n], up_recv.at[n], {"z": z + 1})

        def down(t, i, source=None):
            s = at(i, z + t) if source is None else source
            n = t * RANKS + i
            return remote(s, at(i, z + t), down_send.at[n], down_recv.at[n], {"z": z - 1})

        def begin(i, source=None):
            @pl.when(z < PLANES - 1)
            def _():
                up(0, i, source).start()

            @pl.when(z > 0)
            def _():
                down(0, i, source).start()

        def first():
            keep.start()
            for i, (there, other) in enumerate(peers):
                copy = remote(in_ref.at[other], at(0, z), send.at[i], recv.at[i], there)
                copy.start()
                sent.append(copy)
            begin(0, in_ref.at[own])

        def swapped(i):
            landed(at(i, z), recv.at[i - 1], peers[i - 1][0])
            begin(i)

        def arrive(t, i):
            n = t * RANKS + i
            on = t + 1 < PLANES - 1

            @pl.when(z - 1 - t >= 0)
            def _():
                landed(at(i, z - 1 - t), up_recv.at[n], {"z": z - 1})
                if on:

                    @pl.when(z < PLANES - 1)
                    def _():
                        up(t + 1, i).start()

            @pl.when(z + 1 + t < PLANES)
            def _():
                landed(at(i, z + 1 + t), down_recv.at[n], {"z": z + 1})
                if on:

                    @pl.when(z > 0)
                    def _():
                        down(t + 1, i).start()

        def last():
            for copy in sent:
                copy.wait_send()
            for t in range(PLANES - 1):
                for i in range(RANKS):

                    @pl.when((z < PLANES - 1) & (z - t >= 0))
                    def _():
                        up(t, i).wait_send()

                    @pl.when((z > 0) & (z + t < PLANES))
                    def _():
                        down(t, i).wait_send()

            keep.wait()

        middle = [functools.partial(swapped, i) for i in range(1, RANKS)]
        middle += [
            functools.partial(arrive, t, i) for t in range(PLANES - 1) for i in range(RANKS)
        ]
        return first, middle, last

    n = len(OTHERS)
    sems = DMA(((PLANES - 1) * RANKS,))
    shape = (CORNERS**2, PLANES, CORNERS, rows, columns)
    return Part(
        [(blocks, VMEM)],
        [(jax.ShapeDtypeStruct(shape, blocks.dtype), ANYWHERE)],
        [DMA((n,)), DMA((n,)), sems, sems, sems, sems, DMA(())],
        steps,
        plane="all",
        line=True,
    )


def spread_part(tiles):
    total = tiles.shape[0]

    def steps(ins, outs, scratch):
        (in_ref,), (out_ref,) = ins, outs
        buffer, send, recv = scratch
        me, device = places()

        def give(d):
            other = lax.rem(me + d, total)
            return remote(in_ref.at[other], buffer.at[me], send.at[d], recv.at[d], device(other))

        def first():
            def put(d, carry):
                give(d).start()
                return carry

            lax.fori_loop(1, total, put, 0)

        def last():
            def take(d, carry):
                source = lax.rem(me + total - d, total)
                landed(buffer.at[source], recv.at[d], device(source))
                give(d).wait_send()
                return carry

            lax.fori_loop(1, total, take, 0)
            out_ref[...] = in_ref[me]

            def add(d, carry):
                out_ref[...] += buffer[lax.rem(me + d, total)]
                return carry

            lax.fori_loop(1, total, add, 0)

        return first, [], last

    return Part(
        [(tiles, VMEM)],
        [(jax.ShapeDtypeStruct(tiles.shape[1:], tiles.dtype), VMEM)],
        [pltpu.VMEM(tiles.shape, tiles.dtype), DMA((total,)), DMA((total,))],
        steps,
        plane="world",
    )


def root_mean_scale(values, gains):
    return values * lax.rsqrt(jnp.mean(values * values, axis=-1, keepdims=True) + 1e-06) * gains


def rope_tables(positions):
    half = HEAD_SIZE // 2
    steps_half = jnp.arange(half).astype(jnp.float32)
    inverse = jnp.power(1000000.0, steps_half * (-2.0 / HEAD_SIZE))
    angles = positions.astype(jnp.float32)[:, None] * inverse[None, :]
    cosine, sine = jnp.cos(angles), jnp.sin(angles)
    return jnp.concatenate([cosine, cosine], axis=-1), jnp.concatenate([-sine, sine], axis=-1)


def matrix_product(left, right):
    return jnp.dot(left, right, preferred_element_type=jnp.float32)


def contract_last(left, right):
    return lax.dot_general(
        left, right, (((1,), (1,)), ((), ())), preferred_element_type=jnp.float32
    )


def contract_first(left, right):
    return lax.dot_general(
        left, right, (((0,), (0,)), ((), ())), preferred_element_type=jnp.float32
    )


def low(values):
    return values.astype(jnp.bfloat16)

def turn(values, cosine, sine):
    return values * cosine + pltpu.roll(values, HEAD_SIZE // 2, 1) * sine


def turn_back(grads, cosine, sine):
    return grads * cosine + pltpu.roll(grads * sine, HEAD_SIZE // 2, 1)


def unit_scale(values):
    return lax.rsqrt(jnp.mean(values * values, axis=-1, keepdims=True) + 1e-06)


def norm_back(raw, gain, grads):
    scale = unit_scale(raw)
    unit = raw * scale
    inner = grads * gain
    d_raw = scale * (inner - unit * jnp.mean(inner * unit, axis=-1, keepdims=True))
    return d_raw, grads * unit


def head(index):
    return slice(index * HEAD_SIZE, (index + 1) * HEAD_SIZE)


def dot(left, right):
    return jnp.dot(left, right, preferred_element_type=jnp.float32)


def dot_rows(left, right):
    return lax.dot_general(
        left, right, (((1,), (1,)), ((), ())), preferred_element_type=jnp.float32
    )


def prepare_kernel(
    x_ref, gain_ref, w_ref, cos_ref, sin_ref, qg_ref, kg_ref, x_out, q_ref, kv_ref, raw_ref, gate_ref
):
    hidden = x_ref[...].astype(jnp.float32)
    x_out[...] = low(hidden * unit_scale(hidden) * gain_ref[...])
    raw = dot(x_out[...], w_ref[...])
    cosine, sine = cos_ref[...], sin_ref[...]

    def prepare(values, gain):
        return low(turn(values * unit_scale(values) * gain, cosine, sine))

    for h in range(REPEAT):
        q_ref[:, head(h)] = prepare(raw[:, head(h)], qg_ref[...])
    kv_ref[:, head(0)] = prepare(raw[:, head(REPEAT)], kg_ref[...])
    kv_ref[:, head(1)] = low(raw[:, head(REPEAT + 1)])
    raw_ref[...] = raw[:, : (REPEAT + 1) * HEAD_SIZE]
    gate_ref[...] = raw[:, (REPEAT + 2) * HEAD_SIZE :]


def rows_spec(rows, columns):
    return pl.BlockSpec((rows, columns), lambda i: (i, 0))


def fixed_spec(*shape):
    return pl.BlockSpec(shape, lambda i: (0,) * len(shape))


def kernel_params(vmem):
    return pltpu.CompilerParams(vmem_limit_bytes=vmem << 20)


def prepare_attention(hidden, gain_attn, w_attn, cosine, sine, gain_query, gain_key):
    tokens, width = hidden.shape
    columns = w_attn.shape[1]
    q_columns = REPEAT * HEAD_SIZE
    rows = tokens // RANKS
    shape = jax.ShapeDtypeStruct
    return pl.pallas_call(
        prepare_kernel,
        grid=(RANKS,),
        out_shape=[
            shape((tokens, width), jnp.bfloat16),
            shape((tokens, q_columns), jnp.bfloat16),
            shape((tokens, 2 * HEAD_SIZE), jnp.bfloat16),
            shape((tokens, q_columns + HEAD_SIZE), jnp.float32),
            shape((tokens, q_columns), jnp.float32),
        ],
        in_specs=[
            rows_spec(rows, width),
            fixed_spec(1, width),
            fixed_spec(width, columns),
            rows_spec(rows, HEAD_SIZE),
            rows_spec(rows, HEAD_SIZE),
            fixed_spec(1, HEAD_SIZE),
            fixed_spec(1, HEAD_SIZE),
        ],
        out_specs=[
            rows_spec(rows, width),
            rows_spec(rows, q_columns),
            rows_spec(rows, 2 * HEAD_SIZE),
            rows_spec(rows, q_columns + HEAD_SIZE),
            rows_spec(rows, q_columns),
        ],
        compiler_params=kernel_params(32),
        cost_estimate=expected(12),
    )(hidden, gain_attn[None], w_attn, cosine, sine, gain_query[None], gain_key[None])


EXPONENT = math.log2(math.e) / math.sqrt(HEAD_SIZE)


def allowed_keys(own_ref, keys_ref, z, window):
    seq, pos = own_ref[0, :, 0:1], own_ref[0, :, 1:2]
    key_seq = keys_ref[0, 0:1, z * window : (z + 1) * window]
    key_pos = keys_ref[0, 1:2, z * window : (z + 1) * window]
    return (key_pos <= pos) & ((key_seq == 0) | (key_seq == seq))


def attend_kernel(q_ref, kv_ref, gate_ref, own_ref, keys_ref, wo_ref, terms_ref, att_ref, log_ref, gated_ref):
    planes, window = kv_ref.shape[0], kv_ref.shape[1]
    totals = [None] * REPEAT
    ones = jnp.ones((window, HEAD_SIZE), jnp.bfloat16)
    for z in range(planes):
        allowed = allowed_keys(own_ref, keys_ref, z, window)
        keys = kv_ref[z, :, head(0)]
        values = jnp.concatenate([kv_ref[z, :, head(1)], ones], axis=1)
        for h in range(REPEAT):
            scores = dot_rows(q_ref[:, head(h)], keys) * EXPONENT
            exponent = low(jnp.where(allowed, jnp.exp2(scores), 0.0))
            part = dot(exponent, values)
            totals[h] = part if totals[h] is None else totals[h] + part
    for h in range(REPEAT):
        weight = totals[h][:, head(1)]
        attended = totals[h][:, head(0)] / weight
        att_ref[:, head(h)] = attended
        log_ref[:, head(h)] = jnp.log2(weight)
        gated_ref[:, head(h)] = low(attended * jax.nn.sigmoid(gate_ref[:, head(h)]))
    terms_ref[...] = low(dot(gated_ref[...], wo_ref[...]))


def group_specs(window):
    return [
        pl.BlockSpec((PLANES, window, 2 * HEAD_SIZE), lambda i: (0, i, 0)),
        pl.BlockSpec((1, window, 2), lambda i: (i, 0, 0)),
        pl.BlockSpec((1, 2, PLANES * window), lambda i: (i, 0, 0)),
    ]


def attend(query, pair, gate, own, keys, w_out):
    tokens, q_columns = query.shape
    groups = own.shape[0]
    window = tokens // groups
    width = w_out.shape[1]
    kv, mine, marks = group_specs(window)
    shape = jax.ShapeDtypeStruct
    columns = rows_spec(window, q_columns)
    return pl.pallas_call(
        attend_kernel,
        grid=(groups,),
        out_shape=[
            shape((tokens, width), jnp.bfloat16),
            shape((tokens, q_columns), jnp.float32),
            shape((tokens, q_columns), jnp.float32),
            shape((tokens, q_columns), jnp.bfloat16),
        ],
        in_specs=[columns, kv, columns, mine, marks, fixed_spec(q_columns, width)],
        out_specs=[rows_spec(window, width), columns, columns, columns],
        compiler_params=kernel_params(48),
        cost_estimate=expected(18),
    )(query, pair, gate, own, keys, w_out)


def attend_back_kernel(
    branch_ref, wo_ref, q_ref, kv_ref, gate_ref, own_ref, keys_ref, att_ref, log_ref, raw_ref,
    cos_ref, sin_ref, qg_ref, dq_ref, dgate_ref, dkv_ref, gain_ref,
):
    planes, window = kv_ref.shape[0], kv_ref.shape[1]
    scale = 1.0 / math.sqrt(HEAD_SIZE)
    d_gated = dot_rows(branch_ref[...], wo_ref[...])
    gate = jax.nn.sigmoid(gate_ref[...])
    attended = att_ref[...]
    d_attended = low(d_gated * gate)
    dgate_ref[...] = low(d_gated * attended * gate * (1.0 - gate))
    product = d_attended.astype(jnp.float32) * attended
    delta = [jnp.sum(product[:, head(h)], axis=-1, keepdims=True) for h in range(REPEAT)]
    turned_q = [jnp.transpose(q_ref[:, head(h)]) for h in range(REPEAT)]
    turned_d = [jnp.transpose(d_attended[:, head(h)]) for h in range(REPEAT)]
    d_query = [None] * REPEAT
    for z in range(planes):
        allowed = allowed_keys(own_ref, keys_ref, z, window)
        keys, values = kv_ref[z, :, head(0)], kv_ref[z, :, head(1)]
        d_keys, d_values = None, None
        for h in range(REPEAT):
            scores = dot_rows(q_ref[:, head(h)], keys) * EXPONENT - log_ref[:, h * HEAD_SIZE : h * HEAD_SIZE + 1]
            probs = jnp.where(allowed, jnp.exp2(scores), 0.0)
            d_probs = dot_rows(d_attended[:, head(h)], values)
            d_scores = low(probs * (d_probs - delta[h]))
            part = dot(d_scores, keys)
            d_query[h] = part if d_query[h] is None else d_query[h] + part
            part = dot(turned_q[h], d_scores)
            d_keys = part if d_keys is None else d_keys + part
            part = dot(turned_d[h], low(probs))
            d_values = part if d_values is None else d_values + part
        dkv_ref[z, :, head(0)] = low(jnp.transpose(d_keys * scale))
        dkv_ref[z, :, head(1)] = low(jnp.transpose(d_values))
    cosine, sine = cos_ref[...], sin_ref[...]
    total = jnp.zeros((1, HEAD_SIZE), jnp.float32)
    for h in range(REPEAT):
        grads = turn_back(d_query[h] * scale, cosine, sine)
        d_raw, by_row = norm_back(raw_ref[:, head(h)], qg_ref[...], grads)
        dq_ref[:, head(h)] = low(d_raw)
        total += jnp.sum(by_row, axis=0, keepdims=True)
    gain_ref[0] = jnp.broadcast_to(total, gain_ref.shape[1:])


def attend_back(branch, w_out, query, pair, gate, own, keys, attended, log, raw, cosine, sine, gain):
    tokens, q_columns = query.shape
    groups = own.shape[0]
    window = tokens // groups
    width = w_out.shape[1]
    kv, mine, marks = group_specs(window)
    shape = jax.ShapeDtypeStruct
    columns = rows_spec(window, q_columns)
    table = rows_spec(window, HEAD_SIZE)
    return pl.pallas_call(
        attend_back_kernel,
        grid=(groups,),
        out_shape=[
            shape((tokens, q_columns), jnp.bfloat16),
            shape((tokens, q_columns), jnp.bfloat16),
            shape(pair.shape, jnp.bfloat16),
            shape((groups, 8, HEAD_SIZE), jnp.float32),
        ],
        in_specs=[
            rows_spec(window, width), fixed_spec(q_columns, width), columns, kv, columns, mine, marks,
            columns, columns, rows_spec(window, raw.shape[1]), table, table, fixed_spec(1, HEAD_SIZE),
        ],
        out_specs=[columns, columns, kv, pl.BlockSpec((1, 8, HEAD_SIZE), lambda i: (i, 0, 0))],
        compiler_params=kernel_params(56),
        cost_estimate=expected(35),
    )(branch, w_out, query, pair, gate, own, keys, attended, log, raw, cosine, sine, gain[None])


def finish_kernel(dkv_ref, raw_ref, cos_ref, sin_ref, kg_ref, dq_ref, dgate_ref, out_ref, gain_ref):
    grads = turn_back(dkv_ref[:, head(0)], cos_ref[...], sin_ref[...])
    d_raw, by_row = norm_back(raw_ref[:, head(REPEAT)], kg_ref[...], grads)
    out_ref[:, : REPEAT * HEAD_SIZE] = dq_ref[...]
    out_ref[:, head(REPEAT)] = low(d_raw)
    out_ref[:, head(REPEAT + 1)] = low(dkv_ref[:, head(1)])
    out_ref[:, (REPEAT + 2) * HEAD_SIZE :] = dgate_ref[...]
    gain_ref[0] = jnp.broadcast_to(jnp.sum(by_row, axis=0, keepdims=True), gain_ref.shape[1:])


def finish_attention(d_pair, raw, cosine, sine, gain, d_query, d_gate, steps=4):
    tokens, q_columns = d_query.shape
    rows = tokens // steps
    shape = jax.ShapeDtypeStruct
    table = rows_spec(rows, HEAD_SIZE)
    columns = 2 * q_columns + 2 * HEAD_SIZE
    return pl.pallas_call(
        finish_kernel,
        grid=(steps,),
        out_shape=[shape((tokens, columns), jnp.bfloat16), shape((steps, 8, HEAD_SIZE), jnp.float32)],
        in_specs=[
            rows_spec(rows, 2 * HEAD_SIZE), rows_spec(rows, raw.shape[1]), table, table,
            fixed_spec(1, HEAD_SIZE), rows_spec(rows, q_columns), rows_spec(rows, q_columns),
        ],
        out_specs=[rows_spec(rows, columns), pl.BlockSpec((1, 8, HEAD_SIZE), lambda i: (i, 0, 0))],
        compiler_params=kernel_params(32),
        cost_estimate=expected(5),
    )(d_pair, raw, cosine, sine, gain[None], d_query, d_gate)


def split_part(gate, up, pieces):
    rows, every = gate.shape
    units = every // RANKS
    piece = units // pieces

    def steps(ins, outs, scratch):
        (out_ref,) = outs

        def some(corner_at):
            for y in range(CORNERS):
                for at, ref in ((0, ins[0]), (units, ins[1])):
                    starts = [((corner_at * pieces + d) * CORNERS + y) * piece for d in range(pieces)]
                    parts = [ref[:, start : start + piece] for start in starts]
                    out_ref[corner_at * CORNERS + y, :, at : at + units] = jnp.concatenate(parts, axis=1)

        return (lambda: None), [functools.partial(some, i) for i in range(CORNERS**2)], (lambda: None)

    return Part(
        [(gate, VMEM), (up, VMEM)],
        [(jax.ShapeDtypeStruct((RANKS, rows, 2 * units), gate.dtype), VMEM)],
        [],
        steps,
    )


def join_part(blocks, pieces):
    ranks, rows, width = blocks.shape
    units = width // 2
    piece = units // pieces

    def steps(ins, outs, scratch):
        (in_ref,) = ins

        def some(corner_at):
            for at, ref in ((0, outs[0]), (units, outs[1])):
                parts = []
                for d in range(pieces):
                    for y in range(CORNERS):
                        here = slice(at + d * piece, at + (d + 1) * piece)
                        parts.append(in_ref[corner_at * CORNERS + y, :, here].astype(jnp.float32))
                wide = CORNERS * units
                ref[:, corner_at * wide : (corner_at + 1) * wide] = jnp.concatenate(parts, axis=1)

        return (lambda: None), [functools.partial(some, i) for i in range(CORNERS**2)], (lambda: None)

    out = (jax.ShapeDtypeStruct((rows, ranks * units), jnp.float32), VMEM)
    return Part([(blocks, VMEM)], [out, out], [], steps)


def norm_rows_kernel(x_ref, gain_ref, grads_ref, more_ref, out_ref, term_ref):
    values = x_ref[...].astype(jnp.float32)
    d_values, by_row = norm_back(values, gain_ref[...], grads_ref[...])
    out_ref[...] = more_ref[...].astype(jnp.float32) + d_values

    @pl.when(pl.program_id(0) == 0)
    def _():
        term_ref[...] = jnp.zeros_like(term_ref)

    term_ref[...] += jnp.sum(by_row.reshape(-1, *term_ref.shape), axis=0)


def norm_rows_back(values, gain, grads, more, steps=4):
    rows, width = values.shape
    some = rows_spec(rows // steps, width)
    d_values, term = pl.pallas_call(
        norm_rows_kernel,
        grid=(steps,),
        out_shape=[jax.ShapeDtypeStruct(values.shape, jnp.float32), jax.ShapeDtypeStruct((8, width), jnp.float32)],
        in_specs=[some, fixed_spec(1, width), some, some],
        out_specs=[some, fixed_spec(8, width)],
        compiler_params=kernel_params(32),
        cost_estimate=expected(3),
    )(values, gain[None], grads, more)
    return d_values, jnp.sum(term, axis=0)


def widen_kernel(in_ref, *out_refs):
    start = 0
    for ref in out_refs:
        width = ref.shape[1]
        ref[...] = in_ref[0, :, start : start + width].astype(jnp.float32)
        start += width


def widen_columns(parts, widths):
    ranks, rows, columns = parts.shape
    return pl.pallas_call(
        widen_kernel,
        grid=(ranks,),
        out_shape=[jax.ShapeDtypeStruct((rows, ranks * w), jnp.float32) for w in widths],
        in_specs=[pl.BlockSpec((1, rows, columns), lambda i: (i, 0, 0))],
        out_specs=[pl.BlockSpec((rows, w), lambda i: (0, i)) for w in widths],
        cost_estimate=expected(3),
    )(parts)


def make_shards(cells):
    data_total = cells * PLANES

    def blocks(terms):
        return low(terms).reshape(RANKS, -1, terms.shape[1])

    def gather_tokens(rows):
        return run([gather_part(rows)], 0)[0]

    def scatter_tokens(terms):
        return run([scatter_part(blocks(terms))], 1, 40)[0]

    def split_columns(weight):
        return weight.reshape(weight.shape[0], RANKS, -1)

    def send_columns(pieces):
        return jnp.transpose(jnp.concatenate(pieces, axis=-1), (1, 0, 2))

    def join_cells(rows):
        if cells > 1:
            rows = lax.all_gather(rows, "cell", axis=0, tiled=False)
            rows = jnp.transpose(rows, (1, 0, 2, 3, 4, 5))
        return rows.reshape(-1, rows.shape[-1])

    def gather_columns(mine):
        rows, columns = mine.shape[1:]
        every = lax.all_gather(mine, DATA, axis=0, tiled=False)
        every = every.reshape(data_total, CORNERS**2, CORNERS, rows, columns)
        return jnp.transpose(every, (1, 0, 2, 3, 4)).reshape(-1, columns)

    def sum_columns(term):
        rows = term.shape[0] // (RANKS * data_total)
        split = low(term).reshape(CORNERS**2, data_total, CORNERS, rows, -1)
        split = jnp.transpose(split, (1, 0, 2, 3, 4)).reshape(data_total * RANKS, rows, -1)
        return lax.psum_scatter(split, DATA, scatter_dimension=0, tiled=True)

    inner = CORNERS * data_total
    to_rank = []
    for source in range(inner):
        rank_y, place = divmod(source, data_total)
        to_rank.append((source, place * CORNERS + rank_y))
    INNER = ("cell", "z", "y")

    def shards(
        hidden_in,
        query_weight,
        key_matrix,
        value_matrix,
        gate_weight,
        out_weight,
        norm_attn,
        query_gain,
        key_gain,
        norm_ffn,
        ffn_gate,
        ffn_up,
        ffn_down,
        cotangent,
        sequence_numbers,
        positions,
    ):
        rows = hidden_in.shape[0]
        tokens = rows * RANKS
        groups = CORNERS**2
        window = GROUP_TOKENS // PLANES

        sizes = [norm_attn.shape[0], norm_ffn.shape[0], query_gain.shape[0], key_gain.shape[0]]
        cuts = [0]
        for size in sizes:
            cuts.append(cuts[-1] + size)
        tile = (8, HEAD_SIZE)
        pad = tile[0] * tile[1] - cuts[-1]
        own_gains = jnp.concatenate([norm_attn, norm_ffn, query_gain, key_gain]).astype(jnp.float32)
        own_gains = jnp.pad(own_gains, (0, pad)).reshape(tile)
        plane = lax.axis_index("z")
        group_start = lax.axis_index("cell") * GROUP_TOKENS
        marks = jnp.concatenate(
            [
                lax.dynamic_slice_in_dim(sequence_numbers, group_start, GROUP_TOKENS),
                lax.dynamic_slice_in_dim(positions, group_start, GROUP_TOKENS),
            ]
        ).reshape(-1, HEAD_SIZE)
        attn_columns = send_columns(
            [
                split_columns(query_weight),
                split_columns(key_matrix),
                split_columns(value_matrix),
                split_columns(gate_weight),
            ]
        )
        attn_rows, hidden_all, gains, marks, ffn_columns = run(
            [
                columns_part(attn_columns),
                later(gather_part(hidden_in), 0.22),
                hello_part(RANKS * data_total, own_gains, marks),
                split_part(ffn_gate, ffn_up, data_total),
            ],
            2,
            micros=70,
        )
        attn_rows, out_rows, down_rows = lax.optimization_barrier(
            (attn_rows, lax.ppermute(out_weight, INNER, to_rank), ffn_down)
        )
        w_attn = join_cells(attn_rows)
        gains = gains.reshape(RANKS * data_total, -1)
        gain_attn, gain_ffn, gain_query, gain_key = (
            gains[:, a:b].reshape(-1) for a, b in zip(cuts[:-1], cuts[1:])
        )
        w_out = lax.all_gather(out_rows, DATA, axis=0, tiled=True)
        w_down = lax.all_gather(down_rows, DATA, axis=0, tiled=True)

        marks = marks.reshape(groups, 2, GROUP_TOKENS)
        own_marks = lax.dynamic_slice_in_dim(marks, plane * window, window, axis=2)
        cosine, sine = rope_tables(own_marks[:, 1].reshape(tokens))
        own_marks = jnp.transpose(own_marks, (0, 2, 1))

        hidden = hidden_in.astype(jnp.float32)
        normed_input, query_low, pair, raw, gate_raw = prepare_attention(
            hidden_all, gain_attn, w_attn, cosine, sine, gain_query, gain_key
        )
        pair, cotangent_all, ffn_columns = run(
            [line_gather_part(pair), gather_part(cotangent), swap_part(ffn_columns)], 3, micros=75
        )
        w_ffn = gather_columns(ffn_columns)
        out_terms, attended, log_weight, gated_low = attend(
            query_low, pair, gate_raw, own_marks, marks, w_out
        )
        out_terms = out_terms.reshape(RANKS, rows, -1)
        middle = hidden + run([scatter_part(out_terms)], 1, 40)[0]

        normed_two = gather_tokens(low(root_mean_scale(middle, gain_ffn)))
        both = matrix_product(normed_two, w_ffn)
        units = both.shape[1] // 2
        gate_ffn, up_ffn = both[:, :units], both[:, units:]
        ffn_sig = jax.nn.sigmoid(gate_ffn)
        mixed_low = low(gate_ffn * ffn_sig * up_ffn)

        down_term = low(contract_first(mixed_low, cotangent_all))
        down_term, cotangent_all = lax.optimization_barrier((down_term, cotangent_all))
        grad_down = lax.psum_scatter(down_term, DATA, scatter_dimension=0, tiled=True).astype(
            jnp.float32
        )
        d_mixed = contract_last(cotangent_all, w_down)
        d_up_low = low(d_mixed * gate_ffn * ffn_sig)
        d_gate_ffn_low = low(d_mixed * up_ffn * ffn_sig * (1.0 + gate_ffn * (1.0 - ffn_sig)))
        d_both = jnp.concatenate([d_gate_ffn_low, d_up_low], axis=-1)
        both_term = low(contract_first(normed_two, d_both))
        both_term, d_both = lax.optimization_barrier((both_term, d_both))
        grad_both = sum_columns(both_term)
        (d_normed_two,) = run([scatter_part(product=(d_both, w_ffn), transposed=True)], 6, 48, 45)
        d_middle, grad_norm_two_term = norm_rows_back(middle, gain_ffn, d_normed_two, cotangent)

        branch_all = gather_tokens(low(d_middle))
        branch_all, grad_down = lax.optimization_barrier((branch_all, grad_down))
        d_query, d_gate, d_pair, query_gain_terms = attend_back(
            branch_all, w_out, query_low, pair, gate_raw, own_marks, marks,
            attended, log_weight, raw, cosine, sine, gain_query,
        )
        d_pair, result, grad_both = run(
            [
                line_scatter_part(d_pair),
                scatter_part(product=(mixed_low, w_down)),
                swap_part(grad_both),
            ],
            5,
            56,
            75,
        )
        branch_all, d_pair = lax.optimization_barrier((branch_all, d_pair))
        out_term = low(contract_first(gated_low, branch_all))
        grad_out = lax.psum_scatter(out_term, DATA, scatter_dimension=0, tiled=True)
        output = low(middle + result)
        d_raw, key_gain_terms = finish_attention(
            d_pair, raw, cosine, sine, gain_key, d_query, d_gate
        )
        grad_query_gain_term = jnp.sum(query_gain_terms[:, 0], axis=0)
        grad_key_gain_term = jnp.sum(key_gain_terms[:, 0], axis=0)
        a = REPEAT * HEAD_SIZE
        b, c = a + HEAD_SIZE, a + 2 * HEAD_SIZE
        attn_term = low(contract_first(normed_input, d_raw))
        attn_term, d_raw = lax.optimization_barrier((attn_term, d_raw))
        split = attn_term.reshape(CORNERS**2, cells, PLANES, CORNERS, -1, attn_term.shape[1])
        split = jnp.transpose(split, (2, 1, 0, 3, 4, 5)).reshape(PLANES, -1, attn_term.shape[1])
        d_normed, grad_attn, grad_gate, grad_up = run(
            [
                scatter_part(product=(d_raw, w_attn), transposed=True),
                line_scatter_part(split),
                join_part(grad_both, data_total),
            ],
            7,
            56,
            60,
        )
        grad_attn = low(grad_attn)
        if cells > 1:
            grad_attn = lax.psum_scatter(grad_attn, "cell", scatter_dimension=0, tiled=True)
        grad_attn = grad_attn.reshape(RANKS, -1, attn_term.shape[1])
        input_grad, grad_norm_one_term = norm_rows_back(hidden_in, gain_attn, d_normed, d_middle)

        terms = jnp.concatenate(
            [
                t.reshape(RANKS * data_total, -1)
                for t in (
                    grad_norm_one_term,
                    grad_norm_two_term,
                    grad_query_gain_term,
                    grad_key_gain_term,
                )
            ],
            axis=-1,
        )
        terms = jnp.pad(terms, ((0, 0), (0, pad))).reshape((-1,) + tile)
        grad_attn, small, grad_out = run(
            [swap_part(grad_attn), spread_part(terms), owners_part(grad_out)], 4, micros=18
        )
        grad_out = grad_out.astype(jnp.float32)
        small = small.reshape(-1)
        grad_query, grad_key, grad_value, grad_gatew = widen_columns(grad_attn, (a, b - a, c - b, a))
        grad_norm_attn, grad_norm_ffn, grad_query_gain, grad_key_gain = (
            small[s:e] for s, e in zip(cuts[:-1], cuts[1:])
        )
        return (
            output,
            input_grad,
            grad_query,
            grad_key,
            grad_value,
            grad_gatew,
            grad_out,
            grad_norm_attn,
            grad_query_gain,
            grad_key_gain,
            grad_norm_ffn,
            grad_gate,
            grad_up,
            grad_down,
        )

    return shards


def solution(mesh):
    cells = mesh.shape["fsdp"] // (PLANES * CORNERS)
    split = Mesh(
        mesh.devices.reshape(CORNERS, CORNERS, cells, PLANES, CORNERS),
        ALL,
    )
    rows, flat, group = P(ALL, None), P(ALL), P(("x", "core"))
    return jax.shard_map(
        make_shards(cells),
        mesh=split,
        in_specs=(rows,) * 6 + (flat,) * 4 + (rows,) * 4 + (group,) * 2,
        out_specs=(rows,) * 7 + (flat,) * 4 + (rows,) * 3,
        check_vma=False,
    )
```

```python
import functools
import math

import jax
import jax.numpy as jnp
from jax import lax
from jax.experimental import pallas as pl
from jax.experimental.pallas import tpu as pltpu
from jax.sharding import Mesh
from jax.sharding import PartitionSpec as P

QUERY_HEADS = 16
KEY_VALUE_HEADS = 8
HEAD_SIZE = 128
REPEAT = QUERY_HEADS // KEY_VALUE_HEADS
GROUP_TOKENS = 2048
CORNERS = 2
PLANES = 4
ALL = ("x", "core", "cell", "z", "y")
TENSOR = ("x", "core", "y")
DATA = ("cell", "z")
RANKS = CORNERS**3
CHUNKS = 4
MESH_ID = pl.DeviceIdType.MESH
OTHERS = [(dx, dc, dy) for dx in (0, 1) for dc in (0, 1) for dy in (0, 1) if dx + dc + dy]
DMA = pltpu.SemaphoreType.DMA
VMEM = pl.BlockSpec(memory_space=pltpu.VMEM)
ANYWHERE = pl.BlockSpec(memory_space=pl.ANY)


def remote(source, target, send, receive, device):
    return pltpu.make_async_remote_copy(
        src_ref=source,
        dst_ref=target,
        send_sem=send,
        recv_sem=receive,
        device_id=device,
        device_id_type=MESH_ID,
    )


def landed(ref, sem, device):
    remote(ref, ref, sem, sem, device).wait_recv()


def corner():
    return lax.axis_index("x"), lax.axis_index("core"), lax.axis_index("y")


def slot(x, c, y):
    return (x * CORNERS + c) * CORNERS + y


def flip(value, bit):
    return 1 - value if bit else value


def neighbours():
    x, c, y = corner()
    return {"x": 1 - x}, {"y": 1 - y}, {"core": 1 - c}


def plane_peers():
    x, c, y = corner()
    peers = []
    for dx, dc, dy in OTHERS:
        px, pc, py = flip(x, dx), flip(c, dc), flip(y, dy)
        peers.append(({"x": px, "core": pc, "y": py}, slot(px, pc, py)))
    return peers


def greet(plane, line):
    if plane == "world":
        everyone(math.prod(lax.axis_size(n) for n in ALL))
        return
    barrier = pltpu.get_barrier_semaphore()
    near = {"near": neighbours(), "all": [p for p, _ in plane_peers()], None: []}[plane]
    for device in near:
        pl.semaphore_signal(barrier, inc=1, device_id=device, device_id_type=MESH_ID)
    if not line:
        pl.semaphore_wait(barrier, len(near))
        return
    z = lax.axis_index("z")

    @pl.when(z > 0)
    def _():
        pl.semaphore_signal(barrier, inc=1, device_id={"z": z - 1}, device_id_type=MESH_ID)

    @pl.when(z < PLANES - 1)
    def _():
        pl.semaphore_signal(barrier, inc=1, device_id={"z": z + 1}, device_id_type=MESH_ID)

    edge = (z == 0) | (z == PLANES - 1)

    @pl.when(edge)
    def _():
        pl.semaphore_wait(barrier, len(near) + 1)

    @pl.when(jnp.logical_not(edge))
    def _():
        pl.semaphore_wait(barrier, len(near) + 2)


class Part:
    def __init__(self, inputs, outs, scratch, steps, plane=None, line=False):
        self.begin, self.end = 0.0, 1.0
        self.inputs = inputs
        self.outs = outs
        self.scratch = scratch
        self.steps = steps
        self.plane, self.line = plane, line


def run_kernel(parts, *refs):
    refs = list(refs)

    def take(counts):
        groups = []
        for count in counts:
            groups.append(refs[:count])
            del refs[:count]
        return groups

    ins = take([len(p.inputs) for p in parts])
    outs = take([len(p.outs) for p in parts])
    scratch = take([len(p.scratch) for p in parts])
    ranks = [None, "near", "all", "world"]
    plane = ranks[max(ranks.index(p.plane) for p in parts)]
    greet(plane, any(p.line for p in parts))
    plans = [p.steps(i, o, s) for p, i, o, s in zip(parts, ins, outs, scratch)]
    ordered = []
    for p, (first, middle, _) in zip(parts, plans):
        ordered.append((p.begin - 1.0 if p.begin == 0 else p.begin, first))
        for n, step in enumerate(middle):
            ordered.append((p.begin + (p.end - p.begin) * (n + 0.5) / len(middle), step))
    for _, step in sorted(ordered, key=lambda pair: pair[0]):
        step()
    for _, _, last in plans:
        last()


def expected(micros):
    return pl.CostEstimate(flops=0, bytes_accessed=int(micros * 3.5e6), transcendentals=0)


def run(parts, collective_id, vmem=None, micros=40):
    inputs = [pair for p in parts for pair in p.inputs]
    outs = [pair for p in parts for pair in p.outs]
    return pl.pallas_call(
        functools.partial(run_kernel, parts),
        out_shape=[shape for shape, _ in outs],
        in_specs=[spec for _, spec in inputs],
        out_specs=[spec for _, spec in outs],
        scratch_shapes=[s for p in parts for s in p.scratch],
        compiler_params=pltpu.CompilerParams(
            collective_id=collective_id,
            has_side_effects=True,
            vmem_limit_bytes=None if vmem is None else vmem << 20,
        ),
        cost_estimate=expected(micros),
    )(*[array for array, _ in inputs])


def between(part, begin, end):
    part.begin, part.end = begin, end
    return part


def gather_part(block):
    rows, columns = block.shape
    n, half = CHUNKS, CHUNKS // 2
    chunk = rows // n

    def steps(ins, outs, scratch):
        (in_ref,), (out_ref,) = ins, outs
        send_x, send_y, send_c, recv_x, recv_y, recv_c, local = scratch
        x, c, y = corner()
        dev_x, dev_y, dev_c = neighbours()

        def at(index, k):
            start = pl.multiple_of(index * rows + k * chunk, chunk)
            return out_ref.at[pl.ds(start, chunk), :]

        own, beside_x, beside_y = slot(x, c, y), slot(1 - x, c, y), slot(x, c, 1 - y)
        across = slot(1 - x, c, 1 - y)
        mirror = [
            slot(x, 1 - c, y),
            slot(1 - x, 1 - c, y),
            slot(x, 1 - c, 1 - y),
            slot(1 - x, 1 - c, 1 - y),
        ]
        start = pl.multiple_of(own * rows, rows)
        keep = pltpu.make_async_copy(in_ref, out_ref.at[pl.ds(start, rows), :], local)
        sent = []

        def go(copy):
            copy.start()
            sent.append(copy)

        def share(index, k, b):
            go(remote(at(index, k), at(index, k), send_c.at[b * n + k], recv_c.at[b * n + k], dev_c))

        order_x = list(range(n))
        order_y = order_x[half:] + order_x[:half]

        def first():
            keep.start()

            def mine(k):
                return in_ref.at[pl.ds(k * chunk, chunk), :]

            for k, j in zip(order_x, order_y):
                go(remote(mine(k), at(own, k), send_x.at[k], recv_x.at[k], dev_x))
                go(remote(mine(j), at(own, j), send_y.at[j], recv_y.at[j], dev_y))
            for k in range(n):
                go(remote(mine(k), at(own, k), send_c.at[k], recv_c.at[k], dev_c))

        def straight(k, j):
            landed(at(beside_x, k), recv_x.at[k], dev_x)
            if k < half:
                to = at(beside_x, k)
                go(remote(to, to, send_y.at[n + k], recv_y.at[n + k], dev_y))
            share(beside_x, k, 1)
            landed(at(beside_y, j), recv_y.at[j], dev_y)
            if j >= half:
                to = at(beside_y, j)
                go(remote(to, to, send_x.at[half + j], recv_x.at[half + j], dev_x))
            share(beside_y, j, 2)

        def diagonal(k):
            landed(at(across, k), recv_y.at[n + k], dev_y)
            share(across, k, 3)
            landed(at(across, half + k), recv_x.at[n + k], dev_x)
            share(across, half + k, 3)

        def last():
            for b in range(4):
                for k in range(n):
                    landed(at(mirror[b], k), recv_c.at[b * n + k], dev_c)
            for copy in sent:
                copy.wait_send()
            keep.wait()

        middle = [functools.partial(straight, k, j) for k, j in zip(order_x, order_y)]
        middle += [functools.partial(diagonal, k) for k in range(half)]
        return first, middle, last

    link = DMA((n + half,))
    core = DMA((4 * n,))
    return Part(
        [(block, VMEM)],
        [(jax.ShapeDtypeStruct((RANKS * rows, columns), block.dtype), ANYWHERE)],
        [link, link, core, link, link, core, DMA(())],
        steps,
        plane="near",
    )


def add_rows(target, start, count, sources, step=16):
    def body(i, carry):
        r = pl.multiple_of(start + i * step, step)
        total = None
        for ref, shift in sources:
            value = ref[pl.ds(r - shift if shift else r, step), :].astype(jnp.float32)
            total = value if total is None else total + value
        target[pl.ds(r, step), :] = total.astype(target.dtype)
        return carry

    lax.fori_loop(0, count // step, body, 0)


def scatter_part(terms=None, product=None, transposed=False, tile=512):
    if product is None:
        ranks, rows, columns = terms.shape
    else:
        left, right = product
        rows, columns = left.shape[0] // RANKS, right.shape[0 if transposed else 1]
    n, half = CHUNKS, CHUNKS // 2
    chunk = rows // n
    middle_row = half * chunk

    def steps(ins, outs, scratch):
        (out_ref,) = outs
        if product is None:
            (part_ref,) = ins
        else:
            left_ref, right_ref = ins
            part_ref, scratch = scratch[-1], scratch[:-1]
        core_buf, x_buf, y_buf, x_diag, y_diag, d_sum, x_sum, y_sum = scratch[:8]
        send_c, recv_c, send_x, recv_x, send_y, recv_y = scratch[8:]
        x, c, y = corner()
        dev_x, dev_y, dev_c = neighbours()
        D, X, Y, O = range(4)
        place = [(1 - x, 1 - y), (1 - x, y), (x, 1 - y), (x, y)]
        mine = [slot(px, c, py) for px, py in place]
        theirs = [slot(px, 1 - c, py) for px, py in place]
        orders = {D: [], X: list(range(n)), O: list(range(n))}
        for k in range(half):
            orders[D] += [k, half + k]
        orders[Y] = orders[X][half:] + orders[X][:half]
        sent = []

        def go(copy):
            copy.start()
            sent.append(copy)

        def piece(k):
            return pl.ds(k * chunk, chunk)

        def make(index):
            def body(j, carry):
                at = pl.ds(pl.multiple_of(j * tile, tile), tile)
                some = left_ref[pl.ds(pl.multiple_of(index * rows, rows), rows), :]
                if transposed:
                    value = dot_rows(some, right_ref[at, :])
                else:
                    value = dot(some, right_ref[:, at])
                part_ref[index, :, at] = low(value)
                return carry

            lax.fori_loop(0, columns // tile, body, 0)

        def to_core(b):
            for k in orders[b]:
                source = part_ref.at[theirs[b], piece(k), :]
                i = b * n + k
                go(remote(source, core_buf.at[b, piece(k), :], send_c.at[i], recv_c.at[i], dev_c))

        def made_for_core(b):
            make(theirs[b])
            to_core(b)

        def first():
            if product is None:
                for b in (D, X, Y, O):
                    to_core(b)
            else:
                made_for_core(D)
                make(mine[D])

        def chip(target, b, k, *more):
            landed(core_buf.at[b, piece(k), :], recv_c.at[b * n + k], dev_c)
            sources = [(part_ref.at[mine[b]], 0), (core_buf.at[b], 0), *more]
            add_rows(target, k * chunk, chunk, sources)

        def to_x(k):
            go(remote(x_sum.at[piece(k), :], x_buf.at[piece(k), :], send_x.at[k], recv_x.at[k], dev_x))

        def to_y(k):
            go(remote(y_sum.at[piece(k), :], y_buf.at[piece(k), :], send_y.at[k], recv_y.at[k], dev_y))

        def diagonal(k):
            chip(d_sum, D, k)
            source = d_sum.at[piece(k), :]
            if k < half:
                go(remote(source, x_diag.at[piece(k), :], send_x.at[n + k], recv_x.at[n + k], dev_x))
            else:
                to = y_diag.at[piece(k - half), :]
                go(remote(source, to, send_y.at[half + k], recv_y.at[half + k], dev_y))

        def direct(k):
            chip(x_sum, X, k)
            to_x(k)
            chip(y_sum, Y, half + k)
            to_y(half + k)

        def relayed(k):
            landed(y_diag.at[piece(k), :], recv_y.at[n + k], dev_y)
            chip(x_sum, X, half + k, (y_diag, middle_row))
            to_x(half + k)
            landed(x_diag.at[piece(k), :], recv_x.at[n + k], dev_x)
            chip(y_sum, Y, k, (x_diag, 0))
            to_y(k)

        def own(k):
            landed(x_buf.at[piece(k), :], recv_x.at[k], dev_x)
            landed(y_buf.at[piece(k), :], recv_y.at[k], dev_y)
            chip(out_ref, O, k, (x_buf, 0), (y_buf, 0))

        def last():
            for copy in sent:
                copy.wait_send()

        def makes(b):
            if product is None:
                return []
            return [functools.partial(made_for_core, b), functools.partial(make, mine[b])]

        middle = [functools.partial(diagonal, k) for k in orders[D]]
        middle += makes(X) + makes(Y)
        middle += [functools.partial(direct, k) for k in range(half)]
        middle += makes(O)
        middle += [functools.partial(relayed, k) for k in range(half)]
        middle += [functools.partial(own, k) for k in range(n)]
        return first, middle, last

    def low_vmem(*shape):
        return pltpu.VMEM(shape, jnp.bfloat16)

    whole, part = low_vmem(rows, columns), low_vmem(rows // 2, columns)
    link = DMA((n + half,))
    core = DMA((4 * n,))
    made = [] if product is None else [low_vmem(RANKS, rows, columns)]
    return Part(
        [(terms, VMEM)] if product is None else [(left, VMEM), (right, VMEM)],
        [(jax.ShapeDtypeStruct((rows, columns), jnp.float32), VMEM)],
        [low_vmem(4, rows, columns), whole, whole, part, part, whole, whole, whole]
        + [core, core, link, link, link, link]
        + made,
        steps,
        plane="near",
    )


def swap_part(blocks):
    def steps(ins, outs, scratch):
        (in_ref,), (out_ref,) = ins, outs
        send, recv, local = scratch
        own = slot(*corner())
        keep = pltpu.make_async_copy(in_ref.at[own], out_ref.at[own], local)
        peers = plane_peers()
        sent = []

        def first():
            keep.start()
            for i, (there, other) in enumerate(peers):
                copy = remote(in_ref.at[other], out_ref.at[own], send.at[i], recv.at[i], there)
                copy.start()
                sent.append(copy)

        def last():
            for i, (there, other) in enumerate(peers):
                landed(out_ref.at[other], recv.at[i], there)
            for copy in sent:
                copy.wait_send()
            keep.wait()

        return first, [], last

    n = len(OTHERS)
    return Part(
        [(blocks, VMEM)],
        [(jax.ShapeDtypeStruct(blocks.shape, blocks.dtype), ANYWHERE)],
        [DMA((n,)), DMA((n,)), DMA(())],
        steps,
        plane="all",
    )


def halves_part(term, owners):
    rows = term.shape[0] // owners
    half = owners // CORNERS

    def steps(ins, outs, scratch):
        (in_ref,), (out_ref,) = ins, outs
        send, recv, local = scratch
        y = lax.axis_index("y")
        dev_y = neighbours()[1]

        def rows_of(i, side):
            return in_ref.at[pl.ds(pl.multiple_of((i * CORNERS + side) * rows, rows), rows), :]

        def keep(i):
            return pltpu.make_async_copy(rows_of(i, y), out_ref.at[y * half + i], local.at[i])

        def give(i):
            return remote(rows_of(i, 1 - y), out_ref.at[y * half + i], send.at[i], recv.at[i], dev_y)

        def first():
            for i in range(half):
                keep(i).start()
                give(i).start()

        def last():
            for i in range(half):
                landed(out_ref.at[(1 - y) * half + i], recv.at[i], dev_y)
                give(i).wait_send()
                keep(i).wait()

        return first, [], last

    return Part(
        [(term, VMEM)],
        [(jax.ShapeDtypeStruct((owners, rows, term.shape[1]), term.dtype), VMEM)],
        [DMA((half,)), DMA((half,)), DMA((half,))],
        steps,
        plane="near",
    )


def line_gather_part(block, pieces=4):
    rows = block.shape[0] // pieces

    def steps(ins, outs, scratch):
        (in_ref,), (out_ref,) = ins, outs
        up_send, up_recv, down_send, down_recv, local = scratch
        z = lax.axis_index("z")
        keep = pltpu.make_async_copy(in_ref, out_ref.at[z], local)

        def at(block, k):
            return out_ref.at[block, pl.ds(k * rows, rows), :]

        def up(t, k, source=None):
            s = at(z - t, k) if source is None else source
            i = t * pieces + k
            return remote(s, at(z - t, k), up_send.at[i], up_recv.at[i], {"z": z + 1})

        def down(t, k, source=None):
            s = at(z + t, k) if source is None else source
            i = t * pieces + k
            return remote(s, at(z + t, k), down_send.at[i], down_recv.at[i], {"z": z - 1})

        def first():
            keep.start()
            for k in range(pieces):
                mine = in_ref.at[pl.ds(k * rows, rows), :]

                @pl.when(z < PLANES - 1)
                def _():
                    up(0, k, mine).start()

                @pl.when(z > 0)
                def _():
                    down(0, k, mine).start()

        def arrive(t, k):
            i = t * pieces + k
            on = t + 1 < PLANES - 1

            @pl.when(z - 1 - t >= 0)
            def _():
                landed(at(z - 1 - t, k), up_recv.at[i], {"z": z - 1})
                if on:

                    @pl.when(z < PLANES - 1)
                    def _():
                        up(t + 1, k).start()

            @pl.when(z + 1 + t < PLANES)
            def _():
                landed(at(z + 1 + t, k), down_recv.at[i], {"z": z + 1})
                if on:

                    @pl.when(z > 0)
                    def _():
                        down(t + 1, k).start()

        def last():
            for t in range(PLANES - 1):
                for k in range(pieces):

                    @pl.when((z < PLANES - 1) & (z - t >= 0))
                    def _():
                        up(t, k).wait_send()

                    @pl.when((z > 0) & (z + t < PLANES))
                    def _():
                        down(t, k).wait_send()

            keep.wait()

        middle = [
            functools.partial(arrive, t, k) for t in range(PLANES - 1) for k in range(pieces)
        ]
        return first, middle, last

    sems = DMA(((PLANES - 1) * pieces,))
    return Part(
        [(block, VMEM)],
        [(jax.ShapeDtypeStruct((PLANES,) + block.shape, block.dtype), ANYWHERE)],
        [sems, sems, sems, sems, DMA(())],
        steps,
        line=True,
    )


def line_scatter_part(terms, pieces=4, kind=jnp.float32):
    line, all_rows, columns = terms.shape
    rows = all_rows // pieces
    step = 32

    def steps(ins, outs, scratch):
        (in_ref,), (out_ref,) = ins, outs
        up_buf, down_buf, up_stage, down_stage, up_send, up_recv, down_send, down_recv = scratch
        z = lax.axis_index("z")
        f32 = jnp.float32

        def cut(k):
            return pl.ds(k * rows, rows)

        def send_up(source, d, k):
            i = (d - 1) * pieces + k
            return remote(source, up_buf.at[d - 1, cut(k), :], up_send.at[i], up_recv.at[i], {"z": z + 1})

        def send_down(source, d, k):
            i = (d - 1) * pieces + k
            to = down_buf.at[d - 1, cut(k), :]
            return remote(source, to, down_send.at[i], down_recv.at[i], {"z": z - 1})

        def first():
            for d in range(line - 1, 0, -1):
                for k in range(pieces):

                    @pl.when(z == 0)
                    def _():
                        send_up(in_ref.at[d, cut(k), :], d, k).start()

                    @pl.when(z == line - 1)
                    def _():
                        send_down(in_ref.at[line - 1 - d, cut(k), :], d, k).start()

        def pass_on(d, k):
            @pl.when(z + d < line)
            def _():
                if d + 1 < line:

                    @pl.when(z > 0)
                    def _():
                        landed(up_buf.at[d, cut(k), :], up_recv.at[d * pieces + k], {"z": z - 1})
                        sources = [(in_ref.at[z + d], 0), (up_buf.at[d], 0)]
                        add_rows(up_stage.at[d - 1], k * rows, rows, sources, step)
                        send_up(up_stage.at[d - 1, cut(k), :], d, k).start()

            @pl.when(z - d >= 0)
            def _():
                if d + 1 < line:

                    @pl.when(z < line - 1)
                    def _():
                        landed(down_buf.at[d, cut(k), :], down_recv.at[d * pieces + k], {"z": z + 1})
                        sources = [(in_ref.at[z - d], 0), (down_buf.at[d], 0)]
                        add_rows(down_stage.at[d - 1], k * rows, rows, sources, step)
                        send_down(down_stage.at[d - 1, cut(k), :], d, k).start()

        def own(k):
            @pl.when(z > 0)
            def _():
                landed(up_buf.at[0, cut(k), :], up_recv.at[k], {"z": z - 1})

            @pl.when(z < line - 1)
            def _():
                landed(down_buf.at[0, cut(k), :], down_recv.at[k], {"z": z + 1})

            mine, below, above = (in_ref.at[z], 0), (up_buf.at[0], 0), (down_buf.at[0], 0)

            @pl.when(z == 0)
            def _():
                add_rows(out_ref, k * rows, rows, [mine, above], step)

            @pl.when(z == line - 1)
            def _():
                add_rows(out_ref, k * rows, rows, [mine, below], step)

            @pl.when((z > 0) & (z < line - 1))
            def _():
                add_rows(out_ref, k * rows, rows, [mine, below, above], step)

        def last():
            for d in range(line - 1, 0, -1):
                for k in range(pieces):

                    @pl.when(z + d < line)
                    def _():
                        send_up(up_stage.at[d - 1, cut(k), :], d, k).wait_send()

                    @pl.when(z - d >= 0)
                    def _():
                        send_down(down_stage.at[d - 1, cut(k), :], d, k).wait_send()

        middle = [
            functools.partial(pass_on, d, k) for d in range(line - 2, 0, -1) for k in range(pieces)
        ]
        middle += [functools.partial(own, k) for k in range(pieces)]
        return first, middle, last

    sems = DMA(((line - 1) * pieces,))
    buffer = pltpu.VMEM((line - 1, all_rows, columns), jnp.bfloat16)
    return Part(
        [(terms, VMEM)],
        [(jax.ShapeDtypeStruct((all_rows, columns), kind), VMEM)],
        [buffer, buffer, buffer, buffer, sems, sems, sems, sems],
        steps,
        line=True,
    )


def places():
    sizes = [lax.axis_size(n) for n in ALL]
    me = 0
    for n, size in zip(ALL, sizes):
        me = me * size + lax.axis_index(n)

    def device(index):
        where = {}
        for n, size in reversed(list(zip(ALL, sizes))):
            where[n] = lax.rem(index, size)
            index = index // size
        return where

    return me, device


def everyone(total):
    me, device = places()
    barrier = pltpu.get_barrier_semaphore()

    def greet_one(d, carry):
        other = device(lax.rem(me + d, total))
        pl.semaphore_signal(barrier, inc=1, device_id=other, device_id_type=MESH_ID)
        return carry

    lax.fori_loop(1, total, greet_one, 0)
    pl.semaphore_wait(barrier, total - 1)
    return me, device


def hello_part(total, gains, marks):
    def steps(ins, outs, scratch):
        gains_ref, marks_ref = ins
        gains_out, marks_out = outs
        g_send, g_recv, m_send, m_recv, local = scratch
        me, device = places()
        x, c, y = corner()
        group = x * CORNERS + c
        keeps = [
            pltpu.make_async_copy(gains_ref, gains_out.at[me], local.at[0]),
            pltpu.make_async_copy(marks_ref, marks_out.at[group], local.at[1]),
        ]
        near = [(i, dx, dc) for i, (dx, dc) in enumerate([(0, 1), (1, 0), (1, 1)])]
        sent = []

        def give(d):
            other = device(lax.rem(me + d, total))
            return remote(gains_ref, gains_out.at[me], g_send.at[d], g_recv.at[d], other)

        def first():
            for keep in keeps:
                keep.start()
            for i, dx, dc in near:
                there = {"x": flip(x, dx), "core": flip(c, dc)}
                copy = remote(marks_ref, marks_out.at[group], m_send.at[i], m_recv.at[i], there)
                copy.start()
                sent.append(copy)

            def put(d, carry):
                give(d).start()
                return carry

            lax.fori_loop(1, total, put, 0)

        def last():
            def take(d, carry):
                source = lax.rem(me + total - d, total)
                landed(gains_out.at[source], g_recv.at[d], device(source))
                give(d).wait_send()
                return carry

            lax.fori_loop(1, total, take, 0)
            for i, dx, dc in near:
                there = {"x": flip(x, dx), "core": flip(c, dc)}
                theirs = flip(x, dx) * CORNERS + flip(c, dc)
                landed(marks_out.at[theirs], m_recv.at[i], there)
            for copy in sent:
                copy.wait_send()
            for keep in keeps:
                keep.wait()

        return first, [], last

    return Part(
        [(gains, VMEM), (marks, VMEM)],
        [
            (jax.ShapeDtypeStruct((total,) + gains.shape, gains.dtype), VMEM),
            (jax.ShapeDtypeStruct((CORNERS**2,) + marks.shape, marks.dtype), VMEM),
        ],
        [DMA((total,)), DMA((total,)), DMA((3,)), DMA((3,)), DMA((2,))],
        steps,
        plane="world",
    )


def columns_part(blocks):
    ranks, rows, columns = blocks.shape

    def steps(ins, outs, scratch):
        (in_ref,), (out_ref,) = ins, outs
        send, recv, up_send, up_recv, down_send, down_recv, local = scratch
        x, c, y = corner()
        z = lax.axis_index("z")
        own = slot(x, c, y)
        peers = plane_peers()
        spots = [(x * CORNERS + c, y)]
        spots += [(flip(x, dx) * CORNERS + flip(c, dc), flip(y, dy)) for dx, dc, dy in OTHERS]

        def at(i, plane):
            return out_ref.at[spots[i][0], plane, spots[i][1]]

        keep = pltpu.make_async_copy(in_ref.at[own], at(0, z), local)
        sent = []

        def up(t, i, source=None):
            s = at(i, z - t) if source is None else source
            n = t * RANKS + i
            return remote(s, at(i, z - t), up_send.at[n], up_recv.at[n], {"z": z + 1})

        def down(t, i, source=None):
            s = at(i, z + t) if source is None else source
            n = t * RANKS + i
            return remote(s, at(i, z + t), down_send.at[n], down_recv.at[n], {"z": z - 1})

        def begin(i, source=None):
            @pl.when(z < PLANES - 1)
            def _():
                up(0, i, source).start()

            @pl.when(z > 0)
            def _():
                down(0, i, source).start()

        def first():
            keep.start()
            for i, (there, other) in enumerate(peers):
                copy = remote(in_ref.at[other], at(0, z), send.at[i], recv.at[i], there)
                copy.start()
                sent.append(copy)
            begin(0, in_ref.at[own])

        def swapped(i):
            landed(at(i, z), recv.at[i - 1], peers[i - 1][0])
            begin(i)

        def arrive(t, i):
            n = t * RANKS + i
            on = t + 1 < PLANES - 1

            @pl.when(z - 1 - t >= 0)
            def _():
                landed(at(i, z - 1 - t), up_recv.at[n], {"z": z - 1})
                if on:

                    @pl.when(z < PLANES - 1)
                    def _():
                        up(t + 1, i).start()

            @pl.when(z + 1 + t < PLANES)
            def _():
                landed(at(i, z + 1 + t), down_recv.at[n], {"z": z + 1})
                if on:

                    @pl.when(z > 0)
                    def _():
                        down(t + 1, i).start()

        def last():
            for copy in sent:
                copy.wait_send()
            for t in range(PLANES - 1):
                for i in range(RANKS):

                    @pl.when((z < PLANES - 1) & (z - t >= 0))
                    def _():
                        up(t, i).wait_send()

                    @pl.when((z > 0) & (z + t < PLANES))
                    def _():
                        down(t, i).wait_send()

            keep.wait()

        middle = [functools.partial(swapped, i) for i in range(1, RANKS)]
        middle += [
            functools.partial(arrive, t, i) for t in range(PLANES - 1) for i in range(RANKS)
        ]
        return first, middle, last

    n = len(OTHERS)
    sems = DMA(((PLANES - 1) * RANKS,))
    shape = (CORNERS**2, PLANES, CORNERS, rows, columns)
    return Part(
        [(blocks, VMEM)],
        [(jax.ShapeDtypeStruct(shape, blocks.dtype), ANYWHERE)],
        [DMA((n,)), DMA((n,)), sems, sems, sems, sems, DMA(())],
        steps,
        plane="all",
        line=True,
    )


def spread_part(tiles):
    total = tiles.shape[0]

    def steps(ins, outs, scratch):
        (in_ref,), (out_ref,) = ins, outs
        buffer, send, recv = scratch
        me, device = places()

        def give(d):
            other = lax.rem(me + d, total)
            return remote(in_ref.at[other], buffer.at[me], send.at[d], recv.at[d], device(other))

        def first():
            def put(d, carry):
                give(d).start()
                return carry

            lax.fori_loop(1, total, put, 0)

        def last():
            def take(d, carry):
                source = lax.rem(me + total - d, total)
                landed(buffer.at[source], recv.at[d], device(source))
                give(d).wait_send()
                return carry

            lax.fori_loop(1, total, take, 0)
            out_ref[...] = in_ref[me]

            def add(d, carry):
                out_ref[...] += buffer[lax.rem(me + d, total)]
                return carry

            lax.fori_loop(1, total, add, 0)

        return first, [], last

    return Part(
        [(tiles, VMEM)],
        [(jax.ShapeDtypeStruct(tiles.shape[1:], tiles.dtype), VMEM)],
        [pltpu.VMEM(tiles.shape, tiles.dtype), DMA((total,)), DMA((total,))],
        steps,
        plane="world",
    )


def root_mean_scale(values, gains):
    return values * lax.rsqrt(jnp.mean(values * values, axis=-1, keepdims=True) + 1e-06) * gains


def rope_tables(positions):
    half = HEAD_SIZE // 2
    steps_half = jnp.arange(half).astype(jnp.float32)
    inverse = jnp.power(1000000.0, steps_half * (-2.0 / HEAD_SIZE))
    angles = positions.astype(jnp.float32)[:, None] * inverse[None, :]
    cosine, sine = jnp.cos(angles), jnp.sin(angles)
    return jnp.concatenate([cosine, cosine], axis=-1), jnp.concatenate([-sine, sine], axis=-1)


def matrix_product(left, right):
    return jnp.dot(left, right, preferred_element_type=jnp.float32)


def contract_last(left, right):
    return lax.dot_general(
        left, right, (((1,), (1,)), ((), ())), preferred_element_type=jnp.float32
    )


def contract_first(left, right):
    return lax.dot_general(
        left, right, (((0,), (0,)), ((), ())), preferred_element_type=jnp.float32
    )


def low(values):
    return values.astype(jnp.bfloat16)

def turn(values, cosine, sine):
    return values * cosine + pltpu.roll(values, HEAD_SIZE // 2, 1) * sine


def turn_back(grads, cosine, sine):
    return grads * cosine + pltpu.roll(grads * sine, HEAD_SIZE // 2, 1)


def unit_scale(values):
    return lax.rsqrt(jnp.mean(values * values, axis=-1, keepdims=True) + 1e-06)


def norm_back(raw, gain, grads):
    scale = unit_scale(raw)
    unit = raw * scale
    inner = grads * gain
    d_raw = scale * (inner - unit * jnp.mean(inner * unit, axis=-1, keepdims=True))
    return d_raw, grads * unit


def head(index):
    return slice(index * HEAD_SIZE, (index + 1) * HEAD_SIZE)


def dot(left, right):
    return jnp.dot(left, right, preferred_element_type=jnp.float32)


def dot_rows(left, right):
    return lax.dot_general(
        left, right, (((1,), (1,)), ((), ())), preferred_element_type=jnp.float32
    )


def prepare_kernel(
    x_ref, gain_ref, w_ref, cos_ref, sin_ref, qg_ref, kg_ref, x_out, q_ref, kv_ref, raw_ref, gate_ref
):
    hidden = x_ref[...].astype(jnp.float32)
    x_out[...] = low(hidden * unit_scale(hidden) * gain_ref[...])
    raw = dot(x_out[...], w_ref[...])
    cosine, sine = cos_ref[...], sin_ref[...]

    def prepare(values, gain):
        return low(turn(values * unit_scale(values) * gain, cosine, sine))

    for h in range(REPEAT):
        q_ref[:, head(h)] = prepare(raw[:, head(h)], qg_ref[...])
    kv_ref[:, head(0)] = prepare(raw[:, head(REPEAT)], kg_ref[...])
    kv_ref[:, head(1)] = low(raw[:, head(REPEAT + 1)])
    raw_ref[...] = raw[:, : (REPEAT + 1) * HEAD_SIZE]
    gate_ref[...] = raw[:, (REPEAT + 2) * HEAD_SIZE :]


def rows_spec(rows, columns):
    return pl.BlockSpec((rows, columns), lambda i: (i, 0))


def fixed_spec(*shape):
    return pl.BlockSpec(shape, lambda i: (0,) * len(shape))


def kernel_params(vmem):
    return pltpu.CompilerParams(vmem_limit_bytes=vmem << 20)


def prepare_attention(hidden, gain_attn, w_attn, cosine, sine, gain_query, gain_key):
    tokens, width = hidden.shape
    columns = w_attn.shape[1]
    q_columns = REPEAT * HEAD_SIZE
    rows = tokens // RANKS
    shape = jax.ShapeDtypeStruct
    return pl.pallas_call(
        prepare_kernel,
        grid=(RANKS,),
        out_shape=[
            shape((tokens, width), jnp.bfloat16),
            shape((tokens, q_columns), jnp.bfloat16),
            shape((tokens, 2 * HEAD_SIZE), jnp.bfloat16),
            shape((tokens, q_columns + HEAD_SIZE), jnp.float32),
            shape((tokens, q_columns), jnp.float32),
        ],
        in_specs=[
            rows_spec(rows, width),
            fixed_spec(1, width),
            fixed_spec(width, columns),
            rows_spec(rows, HEAD_SIZE),
            rows_spec(rows, HEAD_SIZE),
            fixed_spec(1, HEAD_SIZE),
            fixed_spec(1, HEAD_SIZE),
        ],
        out_specs=[
            rows_spec(rows, width),
            rows_spec(rows, q_columns),
            rows_spec(rows, 2 * HEAD_SIZE),
            rows_spec(rows, q_columns + HEAD_SIZE),
            rows_spec(rows, q_columns),
        ],
        compiler_params=kernel_params(60),
        cost_estimate=expected(12),
    )(hidden, gain_attn[None], w_attn, cosine, sine, gain_query[None], gain_key[None])


EXPONENT = math.log2(math.e) / math.sqrt(HEAD_SIZE)


def allowed_keys(own_ref, keys_ref, z, window):
    seq, pos = own_ref[0, :, 0:1], own_ref[0, :, 1:2]
    key_seq = keys_ref[0, 0:1, z * window : (z + 1) * window]
    key_pos = keys_ref[0, 1:2, z * window : (z + 1) * window]
    return (key_pos <= pos) & ((key_seq == 0) | (key_seq == seq))


def attend_kernel(q_ref, kv_ref, gate_ref, own_ref, keys_ref, wo_ref, terms_ref, att_ref, log_ref, gated_ref):
    planes, window = kv_ref.shape[0], kv_ref.shape[1]
    totals = [None] * REPEAT
    ones = jnp.ones((window, HEAD_SIZE), jnp.bfloat16)
    for z in range(planes):
        allowed = allowed_keys(own_ref, keys_ref, z, window)
        keys = kv_ref[z, :, head(0)]
        values = jnp.concatenate([kv_ref[z, :, head(1)], ones], axis=1)
        for h in range(REPEAT):
            scores = dot_rows(q_ref[:, head(h)], keys) * EXPONENT
            exponent = low(jnp.where(allowed, jnp.exp2(scores), 0.0))
            part = dot(exponent, values)
            totals[h] = part if totals[h] is None else totals[h] + part
    for h in range(REPEAT):
        weight = totals[h][:, head(1)]
        attended = totals[h][:, head(0)] / weight
        att_ref[:, head(h)] = attended
        log_ref[:, head(h)] = jnp.log2(weight)
        gated_ref[:, head(h)] = low(attended * jax.nn.sigmoid(gate_ref[:, head(h)]))
    terms_ref[...] = low(dot(gated_ref[...], wo_ref[...]))


def group_specs(window):
    return [
        pl.BlockSpec((PLANES, window, 2 * HEAD_SIZE), lambda i: (0, i, 0)),
        pl.BlockSpec((1, window, 2), lambda i: (i, 0, 0)),
        pl.BlockSpec((1, 2, PLANES * window), lambda i: (i, 0, 0)),
    ]


def attend(query, pair, gate, own, keys, w_out):
    tokens, q_columns = query.shape
    groups = own.shape[0]
    window = tokens // groups
    width = w_out.shape[1]
    kv, mine, marks = group_specs(window)
    shape = jax.ShapeDtypeStruct
    columns = rows_spec(window, q_columns)
    return pl.pallas_call(
        attend_kernel,
        grid=(groups,),
        out_shape=[
            shape((tokens, width), jnp.bfloat16),
            shape((tokens, q_columns), jnp.float32),
            shape((tokens, q_columns), jnp.float32),
            shape((tokens, q_columns), jnp.bfloat16),
        ],
        in_specs=[columns, kv, columns, mine, marks, fixed_spec(q_columns, width)],
        out_specs=[rows_spec(window, width), columns, columns, columns],
        compiler_params=kernel_params(48),
        cost_estimate=expected(18),
    )(query, pair, gate, own, keys, w_out)


def attend_back_kernel(
    branch_ref, wo_ref, q_ref, kv_ref, gate_ref, own_ref, keys_ref, att_ref, log_ref, raw_ref,
    cos_ref, sin_ref, qg_ref, dq_ref, dgate_ref, dkv_ref, gain_ref,
):
    planes, window = kv_ref.shape[0], kv_ref.shape[1]
    scale = 1.0 / math.sqrt(HEAD_SIZE)
    d_gated = dot_rows(branch_ref[...], wo_ref[...])
    gate = jax.nn.sigmoid(gate_ref[...])
    attended = att_ref[...]
    d_attended = low(d_gated * gate)
    dgate_ref[...] = low(d_gated * attended * gate * (1.0 - gate))
    product = d_attended.astype(jnp.float32) * attended
    delta = [jnp.sum(product[:, head(h)], axis=-1, keepdims=True) for h in range(REPEAT)]
    turned_q = [jnp.transpose(q_ref[:, head(h)]) for h in range(REPEAT)]
    turned_d = [jnp.transpose(d_attended[:, head(h)]) for h in range(REPEAT)]
    d_query = [None] * REPEAT
    for z in range(planes):
        allowed = allowed_keys(own_ref, keys_ref, z, window)
        keys, values = kv_ref[z, :, head(0)], kv_ref[z, :, head(1)]
        d_keys, d_values = None, None
        for h in range(REPEAT):
            scores = dot_rows(q_ref[:, head(h)], keys) * EXPONENT - log_ref[:, h * HEAD_SIZE : h * HEAD_SIZE + 1]
            probs = jnp.where(allowed, jnp.exp2(scores), 0.0)
            d_probs = dot_rows(d_attended[:, head(h)], values)
            d_scores = low(probs * (d_probs - delta[h]))
            part = dot(d_scores, keys)
            d_query[h] = part if d_query[h] is None else d_query[h] + part
            part = dot(turned_q[h], d_scores)
            d_keys = part if d_keys is None else d_keys + part
            part = dot(turned_d[h], low(probs))
            d_values = part if d_values is None else d_values + part
        dkv_ref[z, :, head(0)] = low(jnp.transpose(d_keys * scale))
        dkv_ref[z, :, head(1)] = low(jnp.transpose(d_values))
    cosine, sine = cos_ref[...], sin_ref[...]
    total = jnp.zeros((1, HEAD_SIZE), jnp.float32)
    for h in range(REPEAT):
        grads = turn_back(d_query[h] * scale, cosine, sine)
        d_raw, by_row = norm_back(raw_ref[:, head(h)], qg_ref[...], grads)
        dq_ref[:, head(h)] = low(d_raw)
        total += jnp.sum(by_row, axis=0, keepdims=True)
    gain_ref[0] = jnp.broadcast_to(total, gain_ref.shape[1:])


def attend_back(branch, w_out, query, pair, gate, own, keys, attended, log, raw, cosine, sine, gain):
    tokens, q_columns = query.shape
    groups = own.shape[0]
    window = tokens // groups
    width = w_out.shape[1]
    kv, mine, marks = group_specs(window)
    shape = jax.ShapeDtypeStruct
    columns = rows_spec(window, q_columns)
    table = rows_spec(window, HEAD_SIZE)
    return pl.pallas_call(
        attend_back_kernel,
        grid=(groups,),
        out_shape=[
            shape((tokens, q_columns), jnp.bfloat16),
            shape((tokens, q_columns), jnp.bfloat16),
            shape(pair.shape, jnp.bfloat16),
            shape((groups, 8, HEAD_SIZE), jnp.float32),
        ],
        in_specs=[
            rows_spec(window, width), fixed_spec(q_columns, width), columns, kv, columns, mine, marks,
            columns, columns, rows_spec(window, raw.shape[1]), table, table, fixed_spec(1, HEAD_SIZE),
        ],
        out_specs=[columns, columns, kv, pl.BlockSpec((1, 8, HEAD_SIZE), lambda i: (i, 0, 0))],
        compiler_params=kernel_params(56),
        cost_estimate=expected(35),
    )(branch, w_out, query, pair, gate, own, keys, attended, log, raw, cosine, sine, gain[None])


def finish_kernel(dkv_ref, raw_ref, cos_ref, sin_ref, kg_ref, dq_ref, dgate_ref, out_ref, gain_ref):
    grads = turn_back(dkv_ref[:, head(0)], cos_ref[...], sin_ref[...])
    d_raw, by_row = norm_back(raw_ref[:, head(REPEAT)], kg_ref[...], grads)
    out_ref[:, : REPEAT * HEAD_SIZE] = dq_ref[...]
    out_ref[:, head(REPEAT)] = low(d_raw)
    out_ref[:, head(REPEAT + 1)] = low(dkv_ref[:, head(1)])
    out_ref[:, (REPEAT + 2) * HEAD_SIZE :] = dgate_ref[...]
    gain_ref[0] = jnp.broadcast_to(jnp.sum(by_row, axis=0, keepdims=True), gain_ref.shape[1:])


def finish_attention(d_pair, raw, cosine, sine, gain, d_query, d_gate, steps=4):
    tokens, q_columns = d_query.shape
    rows = tokens // steps
    shape = jax.ShapeDtypeStruct
    table = rows_spec(rows, HEAD_SIZE)
    columns = 2 * q_columns + 2 * HEAD_SIZE
    return pl.pallas_call(
        finish_kernel,
        grid=(steps,),
        out_shape=[shape((tokens, columns), jnp.bfloat16), shape((steps, 8, HEAD_SIZE), jnp.float32)],
        in_specs=[
            rows_spec(rows, 2 * HEAD_SIZE), rows_spec(rows, raw.shape[1]), table, table,
            fixed_spec(1, HEAD_SIZE), rows_spec(rows, q_columns), rows_spec(rows, q_columns),
        ],
        out_specs=[rows_spec(rows, columns), pl.BlockSpec((1, 8, HEAD_SIZE), lambda i: (i, 0, 0))],
        compiler_params=kernel_params(60),
        cost_estimate=expected(5),
    )(d_pair, raw, cosine, sine, gain[None], d_query, d_gate)


def split_part(gate, up, pieces):
    rows, every = gate.shape
    units = every // RANKS
    piece = units // pieces

    def steps(ins, outs, scratch):
        (out_ref,) = outs

        def some(corner_at):
            for y in range(CORNERS):
                for at, ref in ((0, ins[0]), (units, ins[1])):
                    starts = [((corner_at * pieces + d) * CORNERS + y) * piece for d in range(pieces)]
                    parts = [ref[:, start : start + piece] for start in starts]
                    out_ref[corner_at * CORNERS + y, :, at : at + units] = jnp.concatenate(parts, axis=1)

        return (lambda: None), [functools.partial(some, i) for i in range(CORNERS**2)], (lambda: None)

    return Part(
        [(gate, VMEM), (up, VMEM)],
        [(jax.ShapeDtypeStruct((RANKS, rows, 2 * units), gate.dtype), VMEM)],
        [],
        steps,
    )


def join_part(blocks, pieces):
    ranks, rows, width = blocks.shape
    units = width // 2
    piece = units // pieces

    def steps(ins, outs, scratch):
        (in_ref,) = ins

        def some(corner_at):
            for at, ref in ((0, outs[0]), (units, outs[1])):
                parts = []
                for d in range(pieces):
                    for y in range(CORNERS):
                        here = slice(at + d * piece, at + (d + 1) * piece)
                        parts.append(in_ref[corner_at * CORNERS + y, :, here])
                wide = CORNERS * units
                ref[:, corner_at * wide : (corner_at + 1) * wide] = jnp.concatenate(parts, axis=1)

        return (lambda: None), [functools.partial(some, i) for i in range(CORNERS**2)], (lambda: None)

    out = (jax.ShapeDtypeStruct((rows, ranks * units), blocks.dtype), VMEM)
    return Part([(blocks, VMEM)], [out, out], [], steps)


def norm_rows_kernel(x_ref, gain_ref, grads_ref, more_ref, out_ref, term_ref):
    values = x_ref[...].astype(jnp.float32)
    d_values, by_row = norm_back(values, gain_ref[...], grads_ref[...])
    out_ref[...] = more_ref[...].astype(jnp.float32) + d_values

    @pl.when(pl.program_id(0) == 0)
    def _():
        term_ref[...] = jnp.zeros_like(term_ref)

    term_ref[...] += jnp.sum(by_row.reshape(-1, *term_ref.shape), axis=0)


def norm_rows_back(values, gain, grads, more, steps=4):
    rows, width = values.shape
    some = rows_spec(rows // steps, width)
    d_values, term = pl.pallas_call(
        norm_rows_kernel,
        grid=(steps,),
        out_shape=[jax.ShapeDtypeStruct(values.shape, jnp.float32), jax.ShapeDtypeStruct((8, width), jnp.float32)],
        in_specs=[some, fixed_spec(1, width), some, some],
        out_specs=[some, fixed_spec(8, width)],
        compiler_params=kernel_params(60),
        cost_estimate=expected(3),
    )(values, gain[None], grads, more)
    return d_values, jnp.sum(term, axis=0)


def widen_kernel(in_ref, *out_refs):
    for rank in range(RANKS):
        start = 0
        for ref in out_refs:
            width = ref.shape[1] // RANKS
            value = in_ref[rank, :, start : start + width].astype(jnp.float32)
            ref[:, rank * width : (rank + 1) * width] = value
            start += width


def widen_columns(parts, widths):
    ranks, rows, columns = parts.shape
    return pl.pallas_call(
        widen_kernel,
        out_shape=[jax.ShapeDtypeStruct((rows, ranks * w), jnp.float32) for w in widths],
        in_specs=[VMEM],
        out_specs=[VMEM] * len(widths),
        compiler_params=kernel_params(32),
        cost_estimate=expected(3),
    )(parts)


def make_shards(cells):
    data_total = cells * PLANES

    def blocks(terms):
        return low(terms).reshape(RANKS, -1, terms.shape[1])

    def gather_tokens(rows):
        return run([gather_part(rows)], 0)[0]

    def scatter_tokens(terms):
        return run([scatter_part(blocks(terms))], 1, 40)[0]

    def split_columns(weight):
        return weight.reshape(weight.shape[0], RANKS, -1)

    def send_columns(pieces):
        return jnp.transpose(jnp.concatenate(pieces, axis=-1), (1, 0, 2))

    def join_cells(rows):
        if cells > 1:
            rows = lax.all_gather(rows, "cell", axis=0, tiled=False)
            rows = jnp.transpose(rows, (1, 0, 2, 3, 4, 5))
        return rows.reshape(-1, rows.shape[-1])

    def gather_columns(mine):
        rows, columns = mine.shape[1:]
        every = lax.all_gather(mine, DATA, axis=0, tiled=False)
        every = every.reshape(data_total, CORNERS**2, CORNERS, rows, columns)
        return jnp.transpose(every, (1, 0, 2, 3, 4)).reshape(-1, columns)

    def sum_columns(term):
        rows = term.shape[0] // (RANKS * data_total)
        split = low(term).reshape(CORNERS**2, data_total, CORNERS, rows, -1)
        split = jnp.transpose(split, (1, 0, 2, 3, 4)).reshape(data_total * RANKS, rows, -1)
        return lax.psum_scatter(split, DATA, scatter_dimension=0, tiled=True)

    inner = CORNERS * data_total
    to_rank = []
    for source in range(inner):
        rank_y, place = divmod(source, data_total)
        to_rank.append((source, place * CORNERS + rank_y))
    INNER = ("cell", "z", "y")

    def shards(
        hidden_in,
        query_weight,
        key_matrix,
        value_matrix,
        gate_weight,
        out_weight,
        norm_attn,
        query_gain,
        key_gain,
        norm_ffn,
        ffn_gate,
        ffn_up,
        ffn_down,
        cotangent,
        sequence_numbers,
        positions,
    ):
        rows = hidden_in.shape[0]
        tokens = rows * RANKS
        groups = CORNERS**2
        window = GROUP_TOKENS // PLANES

        sizes = [norm_attn.shape[0], norm_ffn.shape[0], query_gain.shape[0], key_gain.shape[0]]
        cuts = [0]
        for size in sizes:
            cuts.append(cuts[-1] + size)
        tile = (8, HEAD_SIZE)
        pad = tile[0] * tile[1] - cuts[-1]
        own_gains = jnp.concatenate([norm_attn, norm_ffn, query_gain, key_gain]).astype(jnp.float32)
        own_gains = jnp.pad(own_gains, (0, pad)).reshape(tile)
        plane = lax.axis_index("z")
        group_start = lax.axis_index("cell") * GROUP_TOKENS
        marks = jnp.concatenate(
            [
                lax.dynamic_slice_in_dim(sequence_numbers, group_start, GROUP_TOKENS),
                lax.dynamic_slice_in_dim(positions, group_start, GROUP_TOKENS),
            ]
        ).reshape(-1, HEAD_SIZE)
        attn_columns = send_columns(
            [
                split_columns(query_weight),
                split_columns(key_matrix),
                split_columns(value_matrix),
                split_columns(gate_weight),
            ]
        )
        attn_rows, hidden_all, gains, marks, ffn_columns = run(
            [
                columns_part(attn_columns),
                between(gather_part(hidden_in), 0.22, 0.8),
                hello_part(RANKS * data_total, own_gains, marks),
                split_part(ffn_gate, ffn_up, data_total),
            ],
            2,
            micros=70,
        )
        attn_rows, out_rows, down_rows = lax.optimization_barrier(
            (attn_rows, lax.ppermute(out_weight, INNER, to_rank), ffn_down)
        )
        w_attn = join_cells(attn_rows)
        gains = gains.reshape(RANKS * data_total, -1)
        gain_attn, gain_ffn, gain_query, gain_key = (
            gains[:, a:b].reshape(-1) for a, b in zip(cuts[:-1], cuts[1:])
        )
        w_out = lax.all_gather(out_rows, DATA, axis=0, tiled=True)
        w_down = lax.all_gather(down_rows, DATA, axis=0, tiled=True)

        marks = marks.reshape(groups, 2, GROUP_TOKENS)
        own_marks = lax.dynamic_slice_in_dim(marks, plane * window, window, axis=2)
        cosine, sine = rope_tables(own_marks[:, 1].reshape(tokens))
        own_marks = jnp.transpose(own_marks, (0, 2, 1))

        hidden = hidden_in.astype(jnp.float32)
        normed_input, query_low, pair, raw, gate_raw = prepare_attention(
            hidden_all, gain_attn, w_attn, cosine, sine, gain_query, gain_key
        )
        pair, cotangent_all, ffn_columns = run(
            [line_gather_part(pair), gather_part(cotangent), swap_part(ffn_columns)], 3, micros=75
        )
        w_ffn = gather_columns(ffn_columns)
        out_terms, attended, log_weight, gated_low = attend(
            query_low, pair, gate_raw, own_marks, marks, w_out
        )
        out_terms = out_terms.reshape(RANKS, rows, -1)
        middle = hidden + run([scatter_part(out_terms)], 1, 40)[0]

        normed_two = gather_tokens(low(root_mean_scale(middle, gain_ffn)))
        both = matrix_product(normed_two, w_ffn)
        units = both.shape[1] // 2
        gate_ffn, up_ffn = both[:, :units], both[:, units:]
        ffn_sig = jax.nn.sigmoid(gate_ffn)
        mixed_low = low(gate_ffn * ffn_sig * up_ffn)

        down_term = low(contract_first(mixed_low, cotangent_all))
        down_term, cotangent_all = lax.optimization_barrier((down_term, cotangent_all))
        grad_down = lax.psum_scatter(down_term, DATA, scatter_dimension=0, tiled=True).astype(
            jnp.float32
        )
        d_mixed = contract_last(cotangent_all, w_down)
        d_up_low = low(d_mixed * gate_ffn * ffn_sig)
        d_gate_ffn_low = low(d_mixed * up_ffn * ffn_sig * (1.0 + gate_ffn * (1.0 - ffn_sig)))
        d_both = jnp.concatenate([d_gate_ffn_low, d_up_low], axis=-1)
        both_term = low(contract_first(normed_two, d_both))
        both_term, d_both = lax.optimization_barrier((both_term, d_both))
        grad_both = sum_columns(both_term)
        (d_normed_two,) = run([scatter_part(product=(d_both, w_ffn), transposed=True)], 6, 48, 45)
        d_middle, grad_norm_two_term = norm_rows_back(middle, gain_ffn, d_normed_two, cotangent)

        branch_all = gather_tokens(low(d_middle))
        branch_all, grad_down = lax.optimization_barrier((branch_all, grad_down))
        d_query, d_gate, d_pair, query_gain_terms = attend_back(
            branch_all, w_out, query_low, pair, gate_raw, own_marks, marks,
            attended, log_weight, raw, cosine, sine, gain_query,
        )
        out_term = low(contract_first(gated_low, branch_all))
        d_pair, result, grad_both, out_term = run(
            [
                line_scatter_part(d_pair),
                scatter_part(product=(mixed_low, w_down)),
                swap_part(grad_both),
                halves_part(out_term, data_total),
            ],
            5,
            58,
            75,
        )
        grad_out = lax.psum_scatter(
            out_term.reshape(-1, out_term.shape[-1]), DATA, scatter_dimension=0, tiled=True
        ).astype(jnp.float32)
        output = low(middle + result)
        d_raw, key_gain_terms = finish_attention(
            d_pair, raw, cosine, sine, gain_key, d_query, d_gate
        )
        grad_query_gain_term = jnp.sum(query_gain_terms[:, 0], axis=0)
        grad_key_gain_term = jnp.sum(key_gain_terms[:, 0], axis=0)
        a = REPEAT * HEAD_SIZE
        b, c = a + HEAD_SIZE, a + 2 * HEAD_SIZE
        attn_term = low(contract_first(normed_input, d_raw))
        attn_term, d_raw = lax.optimization_barrier((attn_term, d_raw))
        split = attn_term.reshape(CORNERS**2, cells, PLANES, CORNERS, -1, attn_term.shape[1])
        split = jnp.transpose(split, (2, 1, 0, 3, 4, 5)).reshape(PLANES, -1, attn_term.shape[1])
        grad_attn, d_normed, grad_gate, grad_up = run(
            [
                line_scatter_part(split, kind=jnp.bfloat16),
                scatter_part(product=(d_raw, w_attn), transposed=True),
                join_part(grad_both, data_total),
            ],
            7,
            56,
            60,
        )
        if cells > 1:
            grad_attn = lax.psum_scatter(grad_attn, "cell", scatter_dimension=0, tiled=True)
        grad_gate, grad_up = grad_gate.astype(jnp.float32), grad_up.astype(jnp.float32)
        grad_attn = grad_attn.reshape(RANKS, -1, attn_term.shape[1])
        input_grad, grad_norm_one_term = norm_rows_back(hidden_in, gain_attn, d_normed, d_middle)

        terms = jnp.concatenate(
            [
                t.reshape(RANKS * data_total, -1)
                for t in (
                    grad_norm_one_term,
                    grad_norm_two_term,
                    grad_query_gain_term,
                    grad_key_gain_term,
                )
            ],
            axis=-1,
        )
        terms = jnp.pad(terms, ((0, 0), (0, pad))).reshape((-1,) + tile)
        grad_attn, small = run([swap_part(grad_attn), spread_part(terms)], 4, micros=15)
        small = small.reshape(-1)
        grad_query, grad_key, grad_value, grad_gatew = widen_columns(grad_attn, (a, b - a, c - b, a))
        grad_norm_attn, grad_norm_ffn, grad_query_gain, grad_key_gain = (
            small[s:e] for s, e in zip(cuts[:-1], cuts[1:])
        )
        return (
            output,
            input_grad,
            grad_query,
            grad_key,
            grad_value,
            grad_gatew,
            grad_out,
            grad_norm_attn,
            grad_query_gain,
            grad_key_gain,
            grad_norm_ffn,
            grad_gate,
            grad_up,
            grad_down,
        )

    return shards


def solution(mesh):
    cells = mesh.shape["fsdp"] // (PLANES * CORNERS)
    split = Mesh(
        mesh.devices.reshape(CORNERS, CORNERS, cells, PLANES, CORNERS),
        ALL,
    )
    rows, flat, group = P(ALL, None), P(ALL), P(("x", "core"))
    return jax.shard_map(
        make_shards(cells),
        mesh=split,
        in_specs=(rows,) * 6 + (flat,) * 4 + (rows,) * 4 + (group,) * 2,
        out_specs=(rows,) * 7 + (flat,) * 4 + (rows,) * 3,
        check_vma=False,
    )
```

```python
import functools
import math

import jax
import jax.numpy as jnp
from jax import lax
from jax.experimental import pallas as pl
from jax.experimental.pallas import tpu as pltpu
from jax.sharding import Mesh
from jax.sharding import PartitionSpec as P

QUERY_HEADS = 16
KEY_VALUE_HEADS = 8
HEAD_SIZE = 128
REPEAT = QUERY_HEADS // KEY_VALUE_HEADS
GROUP_TOKENS = 2048
CORNERS = 2
PLANES = 4
ALL = ("x", "core", "cell", "z", "y")
TENSOR = ("x", "core", "y")
DATA = ("cell", "z")
RANKS = CORNERS**3
CHUNKS = 4
MESH_ID = pl.DeviceIdType.MESH
OTHERS = [(dx, dc, dy) for dx in (0, 1) for dc in (0, 1) for dy in (0, 1) if dx + dc + dy]
DMA = pltpu.SemaphoreType.DMA
VMEM = pl.BlockSpec(memory_space=pltpu.VMEM)
ANYWHERE = pl.BlockSpec(memory_space=pl.ANY)


def remote(source, target, send, receive, device):
    return pltpu.make_async_remote_copy(
        src_ref=source,
        dst_ref=target,
        send_sem=send,
        recv_sem=receive,
        device_id=device,
        device_id_type=MESH_ID,
    )


def landed(ref, sem, device):
    remote(ref, ref, sem, sem, device).wait_recv()


def corner():
    return lax.axis_index("x"), lax.axis_index("core"), lax.axis_index("y")


def slot(x, c, y):
    return (x * CORNERS + c) * CORNERS + y


def flip(value, bit):
    return 1 - value if bit else value


def neighbours():
    x, c, y = corner()
    return {"x": 1 - x}, {"y": 1 - y}, {"core": 1 - c}


def plane_peers():
    x, c, y = corner()
    peers = []
    for dx, dc, dy in OTHERS:
        px, pc, py = flip(x, dx), flip(c, dc), flip(y, dy)
        peers.append(({"x": px, "core": pc, "y": py}, slot(px, pc, py)))
    return peers


def greet(plane, line):
    barrier = pltpu.get_barrier_semaphore()
    near = {"near": neighbours(), "all": [p for p, _ in plane_peers()], None: []}[plane]
    for device in near:
        pl.semaphore_signal(barrier, inc=1, device_id=device, device_id_type=MESH_ID)
    if not line:
        pl.semaphore_wait(barrier, len(near))
        return
    z = lax.axis_index("z")

    @pl.when(z > 0)
    def _():
        pl.semaphore_signal(barrier, inc=1, device_id={"z": z - 1}, device_id_type=MESH_ID)

    @pl.when(z < PLANES - 1)
    def _():
        pl.semaphore_signal(barrier, inc=1, device_id={"z": z + 1}, device_id_type=MESH_ID)

    edge = (z == 0) | (z == PLANES - 1)

    @pl.when(edge)
    def _():
        pl.semaphore_wait(barrier, len(near) + 1)

    @pl.when(jnp.logical_not(edge))
    def _():
        pl.semaphore_wait(barrier, len(near) + 2)


class Part:
    def __init__(self, inputs, outs, scratch, steps, plane=None, line=False):
        self.begin, self.end = 0.0, 1.0
        self.inputs = inputs
        self.outs = outs
        self.scratch = scratch
        self.steps = steps
        self.plane, self.line = plane, line


def run_kernel(parts, *refs):
    refs = list(refs)

    def take(counts):
        groups = []
        for count in counts:
            groups.append(refs[:count])
            del refs[:count]
        return groups

    ins = take([len(p.inputs) for p in parts])
    outs = take([len(p.outs) for p in parts])
    scratch = take([len(p.scratch) for p in parts])
    ranks = [None, "near", "all"]
    plane = ranks[max(ranks.index(p.plane) for p in parts)]
    greet(plane, any(p.line for p in parts))
    plans = [p.steps(i, o, s) for p, i, o, s in zip(parts, ins, outs, scratch)]
    ordered = []
    for p, (first, middle, _) in zip(parts, plans):
        ordered.append((p.begin - 1.0 if p.begin == 0 else p.begin, first))
        for n, step in enumerate(middle):
            ordered.append((p.begin + (p.end - p.begin) * (n + 0.5) / len(middle), step))
    for _, step in sorted(ordered, key=lambda pair: pair[0]):
        step()
    for _, _, last in plans:
        last()


def expected(micros):
    return pl.CostEstimate(flops=0, bytes_accessed=int(micros * 3.5e6), transcendentals=0)


def run(parts, collective_id, vmem=None, micros=40):
    inputs = [pair for p in parts for pair in p.inputs]
    outs = [pair for p in parts for pair in p.outs]
    return pl.pallas_call(
        functools.partial(run_kernel, parts),
        out_shape=[shape for shape, _ in outs],
        in_specs=[spec for _, spec in inputs],
        out_specs=[spec for _, spec in outs],
        scratch_shapes=[s for p in parts for s in p.scratch],
        compiler_params=pltpu.CompilerParams(
            collective_id=collective_id,
            has_side_effects=True,
            vmem_limit_bytes=None if vmem is None else vmem << 20,
        ),
        cost_estimate=expected(micros),
    )(*[array for array, _ in inputs])


def between(part, begin, end):
    part.begin, part.end = begin, end
    return part


def gather_part(block):
    rows, columns = block.shape
    n, half = CHUNKS, CHUNKS // 2
    chunk = rows // n

    def steps(ins, outs, scratch):
        (in_ref,), (out_ref,) = ins, outs
        send_x, send_y, send_c, recv_x, recv_y, recv_c, local = scratch
        x, c, y = corner()
        dev_x, dev_y, dev_c = neighbours()

        def at(index, k):
            start = pl.multiple_of(index * rows + k * chunk, chunk)
            return out_ref.at[pl.ds(start, chunk), :]

        own, beside_x, beside_y = slot(x, c, y), slot(1 - x, c, y), slot(x, c, 1 - y)
        across = slot(1 - x, c, 1 - y)
        mirror = [
            slot(x, 1 - c, y),
            slot(1 - x, 1 - c, y),
            slot(x, 1 - c, 1 - y),
            slot(1 - x, 1 - c, 1 - y),
        ]
        start = pl.multiple_of(own * rows, rows)
        keep = pltpu.make_async_copy(in_ref, out_ref.at[pl.ds(start, rows), :], local)
        sent = []

        def go(copy):
            copy.start()
            sent.append(copy)

        def share(index, k, b):
            go(remote(at(index, k), at(index, k), send_c.at[b * n + k], recv_c.at[b * n + k], dev_c))

        order_x = list(range(n))
        order_y = order_x[half:] + order_x[:half]

        def first():
            keep.start()

            def mine(k):
                return in_ref.at[pl.ds(k * chunk, chunk), :]

            for k, j in zip(order_x, order_y):
                go(remote(mine(k), at(own, k), send_x.at[k], recv_x.at[k], dev_x))
                go(remote(mine(j), at(own, j), send_y.at[j], recv_y.at[j], dev_y))
            for k in range(n):
                go(remote(mine(k), at(own, k), send_c.at[k], recv_c.at[k], dev_c))

        def straight(k, j):
            landed(at(beside_x, k), recv_x.at[k], dev_x)
            if k < half:
                to = at(beside_x, k)
                go(remote(to, to, send_y.at[n + k], recv_y.at[n + k], dev_y))
            share(beside_x, k, 1)
            landed(at(beside_y, j), recv_y.at[j], dev_y)
            if j >= half:
                to = at(beside_y, j)
                go(remote(to, to, send_x.at[half + j], recv_x.at[half + j], dev_x))
            share(beside_y, j, 2)

        def diagonal(k):
            landed(at(across, k), recv_y.at[n + k], dev_y)
            share(across, k, 3)
            landed(at(across, half + k), recv_x.at[n + k], dev_x)
            share(across, half + k, 3)

        def last():
            for b in range(4):
                for k in range(n):
                    landed(at(mirror[b], k), recv_c.at[b * n + k], dev_c)
            for copy in sent:
                copy.wait_send()
            keep.wait()

        middle = [functools.partial(straight, k, j) for k, j in zip(order_x, order_y)]
        middle += [functools.partial(diagonal, k) for k in range(half)]
        return first, middle, last

    link = DMA((n + half,))
    core = DMA((4 * n,))
    return Part(
        [(block, VMEM)],
        [(jax.ShapeDtypeStruct((RANKS * rows, columns), block.dtype), ANYWHERE)],
        [link, link, core, link, link, core, DMA(())],
        steps,
        plane="near",
    )


def add_rows(target, start, count, sources, step=16):
    def body(i, carry):
        r = pl.multiple_of(start + i * step, step)
        total = None
        for ref, shift in sources:
            value = ref[pl.ds(r - shift if shift else r, step), :].astype(jnp.float32)
            total = value if total is None else total + value
        target[pl.ds(r, step), :] = total.astype(target.dtype)
        return carry

    lax.fori_loop(0, count // step, body, 0)


def scatter_part(terms=None, product=None, transposed=False, tile=512):
    if product is None:
        ranks, rows, columns = terms.shape
    else:
        left, right = product
        rows, columns = left.shape[0] // RANKS, right.shape[0 if transposed else 1]
    n, half = CHUNKS, CHUNKS // 2
    chunk = rows // n
    middle_row = half * chunk

    def steps(ins, outs, scratch):
        (out_ref,) = outs
        if product is None:
            (part_ref,) = ins
        else:
            left_ref, right_ref = ins
            part_ref, scratch = scratch[-1], scratch[:-1]
        core_buf, x_buf, y_buf, x_diag, y_diag, d_sum, x_sum, y_sum = scratch[:8]
        send_c, recv_c, send_x, recv_x, send_y, recv_y = scratch[8:]
        x, c, y = corner()
        dev_x, dev_y, dev_c = neighbours()
        D, X, Y, O = range(4)
        place = [(1 - x, 1 - y), (1 - x, y), (x, 1 - y), (x, y)]
        mine = [slot(px, c, py) for px, py in place]
        theirs = [slot(px, 1 - c, py) for px, py in place]
        orders = {D: [], X: list(range(n)), O: list(range(n))}
        for k in range(half):
            orders[D] += [k, half + k]
        orders[Y] = orders[X][half:] + orders[X][:half]
        sent = []

        def go(copy):
            copy.start()
            sent.append(copy)

        def piece(k):
            return pl.ds(k * chunk, chunk)

        def make(index):
            def body(j, carry):
                at = pl.ds(pl.multiple_of(j * tile, tile), tile)
                some = left_ref[pl.ds(pl.multiple_of(index * rows, rows), rows), :]
                if transposed:
                    value = dot_rows(some, right_ref[at, :])
                else:
                    value = dot(some, right_ref[:, at])
                part_ref[index, :, at] = low(value)
                return carry

            lax.fori_loop(0, columns // tile, body, 0)

        def to_core(b):
            for k in orders[b]:
                source = part_ref.at[theirs[b], piece(k), :]
                i = b * n + k
                go(remote(source, core_buf.at[b, piece(k), :], send_c.at[i], recv_c.at[i], dev_c))

        def made_for_core(b):
            make(theirs[b])
            to_core(b)

        def first():
            if product is None:
                for b in (D, X, Y, O):
                    to_core(b)
            else:
                made_for_core(D)
                make(mine[D])

        def chip(target, b, k, *more):
            landed(core_buf.at[b, piece(k), :], recv_c.at[b * n + k], dev_c)
            sources = [(part_ref.at[mine[b]], 0), (core_buf.at[b], 0), *more]
            add_rows(target, k * chunk, chunk, sources)

        def to_x(k):
            go(remote(x_sum.at[piece(k), :], x_buf.at[piece(k), :], send_x.at[k], recv_x.at[k], dev_x))

        def to_y(k):
            go(remote(y_sum.at[piece(k), :], y_buf.at[piece(k), :], send_y.at[k], recv_y.at[k], dev_y))

        def diagonal(k):
            chip(d_sum, D, k)
            source = d_sum.at[piece(k), :]
            if k < half:
                go(remote(source, x_diag.at[piece(k), :], send_x.at[n + k], recv_x.at[n + k], dev_x))
            else:
                to = y_diag.at[piece(k - half), :]
                go(remote(source, to, send_y.at[half + k], recv_y.at[half + k], dev_y))

        def direct(k):
            chip(x_sum, X, k)
            to_x(k)
            chip(y_sum, Y, half + k)
            to_y(half + k)

        def relayed(k):
            landed(y_diag.at[piece(k), :], recv_y.at[n + k], dev_y)
            chip(x_sum, X, half + k, (y_diag, middle_row))
            to_x(half + k)
            landed(x_diag.at[piece(k), :], recv_x.at[n + k], dev_x)
            chip(y_sum, Y, k, (x_diag, 0))
            to_y(k)

        def own(k):
            landed(x_buf.at[piece(k), :], recv_x.at[k], dev_x)
            landed(y_buf.at[piece(k), :], recv_y.at[k], dev_y)
            chip(out_ref, O, k, (x_buf, 0), (y_buf, 0))

        def last():
            for copy in sent:
                copy.wait_send()

        def makes(b):
            if product is None:
                return []
            return [functools.partial(made_for_core, b), functools.partial(make, mine[b])]

        middle = [functools.partial(diagonal, k) for k in orders[D]]
        middle += makes(X) + makes(Y)
        middle += [functools.partial(direct, k) for k in range(half)]
        middle += makes(O)
        middle += [functools.partial(relayed, k) for k in range(half)]
        middle += [functools.partial(own, k) for k in range(n)]
        return first, middle, last

    def low_vmem(*shape):
        return pltpu.VMEM(shape, jnp.bfloat16)

    whole, part = low_vmem(rows, columns), low_vmem(rows // 2, columns)
    link = DMA((n + half,))
    core = DMA((4 * n,))
    made = [] if product is None else [low_vmem(RANKS, rows, columns)]
    return Part(
        [(terms, VMEM)] if product is None else [(left, VMEM), (right, VMEM)],
        [(jax.ShapeDtypeStruct((rows, columns), jnp.float32), VMEM)],
        [low_vmem(4, rows, columns), whole, whole, part, part, whole, whole, whole]
        + [core, core, link, link, link, link]
        + made,
        steps,
        plane="near",
    )


def swap_part(blocks):
    def steps(ins, outs, scratch):
        (in_ref,), (out_ref,) = ins, outs
        send, recv, local = scratch
        own = slot(*corner())
        keep = pltpu.make_async_copy(in_ref.at[own], out_ref.at[own], local)
        peers = plane_peers()
        sent = []

        def first():
            keep.start()
            for i, (there, other) in enumerate(peers):
                copy = remote(in_ref.at[other], out_ref.at[own], send.at[i], recv.at[i], there)
                copy.start()
                sent.append(copy)

        def last():
            for i, (there, other) in enumerate(peers):
                landed(out_ref.at[other], recv.at[i], there)
            for copy in sent:
                copy.wait_send()
            keep.wait()

        return first, [], last

    n = len(OTHERS)
    return Part(
        [(blocks, VMEM)],
        [(jax.ShapeDtypeStruct(blocks.shape, blocks.dtype), ANYWHERE)],
        [DMA((n,)), DMA((n,)), DMA(())],
        steps,
        plane="all",
    )


def halves_part(term, owners):
    rows = term.shape[0] // owners
    half = owners // CORNERS

    def steps(ins, outs, scratch):
        (in_ref,), (out_ref,) = ins, outs
        send, recv, local = scratch
        y = lax.axis_index("y")
        dev_y = neighbours()[1]

        def rows_of(i, side):
            return in_ref.at[pl.ds(pl.multiple_of((i * CORNERS + side) * rows, rows), rows), :]

        def keep(i):
            return pltpu.make_async_copy(rows_of(i, y), out_ref.at[y * half + i], local.at[i])

        def give(i):
            return remote(rows_of(i, 1 - y), out_ref.at[y * half + i], send.at[i], recv.at[i], dev_y)

        def first():
            for i in range(half):
                keep(i).start()
                give(i).start()

        def last():
            for i in range(half):
                landed(out_ref.at[(1 - y) * half + i], recv.at[i], dev_y)
                give(i).wait_send()
                keep(i).wait()

        return first, [], last

    return Part(
        [(term, VMEM)],
        [(jax.ShapeDtypeStruct((owners, rows, term.shape[1]), term.dtype), VMEM)],
        [DMA((half,)), DMA((half,)), DMA((half,))],
        steps,
        plane="near",
    )


def line_gather_part(block, pieces=4):
    rows = block.shape[0] // pieces

    def steps(ins, outs, scratch):
        (in_ref,), (out_ref,) = ins, outs
        up_send, up_recv, down_send, down_recv, local = scratch
        z = lax.axis_index("z")
        keep = pltpu.make_async_copy(in_ref, out_ref.at[z], local)

        def at(block, k):
            return out_ref.at[block, pl.ds(k * rows, rows), :]

        def up(t, k, source=None):
            s = at(z - t, k) if source is None else source
            i = t * pieces + k
            return remote(s, at(z - t, k), up_send.at[i], up_recv.at[i], {"z": z + 1})

        def down(t, k, source=None):
            s = at(z + t, k) if source is None else source
            i = t * pieces + k
            return remote(s, at(z + t, k), down_send.at[i], down_recv.at[i], {"z": z - 1})

        def first():
            keep.start()
            for k in range(pieces):
                mine = in_ref.at[pl.ds(k * rows, rows), :]

                @pl.when(z < PLANES - 1)
                def _():
                    up(0, k, mine).start()

                @pl.when(z > 0)
                def _():
                    down(0, k, mine).start()

        def arrive(t, k):
            i = t * pieces + k
            on = t + 1 < PLANES - 1

            @pl.when(z - 1 - t >= 0)
            def _():
                landed(at(z - 1 - t, k), up_recv.at[i], {"z": z - 1})
                if on:

                    @pl.when(z < PLANES - 1)
                    def _():
                        up(t + 1, k).start()

            @pl.when(z + 1 + t < PLANES)
            def _():
                landed(at(z + 1 + t, k), down_recv.at[i], {"z": z + 1})
                if on:

                    @pl.when(z > 0)
                    def _():
                        down(t + 1, k).start()

        def last():
            for t in range(PLANES - 1):
                for k in range(pieces):

                    @pl.when((z < PLANES - 1) & (z - t >= 0))
                    def _():
                        up(t, k).wait_send()

                    @pl.when((z > 0) & (z + t < PLANES))
                    def _():
                        down(t, k).wait_send()

            keep.wait()

        middle = [
            functools.partial(arrive, t, k) for t in range(PLANES - 1) for k in range(pieces)
        ]
        return first, middle, last

    sems = DMA(((PLANES - 1) * pieces,))
    return Part(
        [(block, VMEM)],
        [(jax.ShapeDtypeStruct((PLANES,) + block.shape, block.dtype), ANYWHERE)],
        [sems, sems, sems, sems, DMA(())],
        steps,
        line=True,
    )


def line_scatter_part(terms, pieces=4, kind=jnp.float32):
    line, all_rows, columns = terms.shape
    rows = all_rows // pieces
    step = 32

    def steps(ins, outs, scratch):
        (in_ref,), (out_ref,) = ins, outs
        up_buf, down_buf, up_stage, down_stage, up_send, up_recv, down_send, down_recv = scratch
        z = lax.axis_index("z")
        f32 = jnp.float32

        def cut(k):
            return pl.ds(k * rows, rows)

        def send_up(source, d, k):
            i = (d - 1) * pieces + k
            return remote(source, up_buf.at[d - 1, cut(k), :], up_send.at[i], up_recv.at[i], {"z": z + 1})

        def send_down(source, d, k):
            i = (d - 1) * pieces + k
            to = down_buf.at[d - 1, cut(k), :]
            return remote(source, to, down_send.at[i], down_recv.at[i], {"z": z - 1})

        def first():
            for d in range(line - 1, 0, -1):
                for k in range(pieces):

                    @pl.when(z == 0)
                    def _():
                        send_up(in_ref.at[d, cut(k), :], d, k).start()

                    @pl.when(z == line - 1)
                    def _():
                        send_down(in_ref.at[line - 1 - d, cut(k), :], d, k).start()

        def pass_on(d, k):
            @pl.when(z + d < line)
            def _():
                if d + 1 < line:

                    @pl.when(z > 0)
                    def _():
                        landed(up_buf.at[d, cut(k), :], up_recv.at[d * pieces + k], {"z": z - 1})
                        sources = [(in_ref.at[z + d], 0), (up_buf.at[d], 0)]
                        add_rows(up_stage.at[d - 1], k * rows, rows, sources, step)
                        send_up(up_stage.at[d - 1, cut(k), :], d, k).start()

            @pl.when(z - d >= 0)
            def _():
                if d + 1 < line:

                    @pl.when(z < line - 1)
                    def _():
                        landed(down_buf.at[d, cut(k), :], down_recv.at[d * pieces + k], {"z": z + 1})
                        sources = [(in_ref.at[z - d], 0), (down_buf.at[d], 0)]
                        add_rows(down_stage.at[d - 1], k * rows, rows, sources, step)
                        send_down(down_stage.at[d - 1, cut(k), :], d, k).start()

        def own(k):
            @pl.when(z > 0)
            def _():
                landed(up_buf.at[0, cut(k), :], up_recv.at[k], {"z": z - 1})

            @pl.when(z < line - 1)
            def _():
                landed(down_buf.at[0, cut(k), :], down_recv.at[k], {"z": z + 1})

            mine, below, above = (in_ref.at[z], 0), (up_buf.at[0], 0), (down_buf.at[0], 0)

            @pl.when(z == 0)
            def _():
                add_rows(out_ref, k * rows, rows, [mine, above], step)

            @pl.when(z == line - 1)
            def _():
                add_rows(out_ref, k * rows, rows, [mine, below], step)

            @pl.when((z > 0) & (z < line - 1))
            def _():
                add_rows(out_ref, k * rows, rows, [mine, below, above], step)

        def last():
            for d in range(line - 1, 0, -1):
                for k in range(pieces):

                    @pl.when(z + d < line)
                    def _():
                        send_up(up_stage.at[d - 1, cut(k), :], d, k).wait_send()

                    @pl.when(z - d >= 0)
                    def _():
                        send_down(down_stage.at[d - 1, cut(k), :], d, k).wait_send()

        middle = [
            functools.partial(pass_on, d, k) for d in range(line - 2, 0, -1) for k in range(pieces)
        ]
        middle += [functools.partial(own, k) for k in range(pieces)]
        return first, middle, last

    sems = DMA(((line - 1) * pieces,))
    buffer = pltpu.VMEM((line - 1, all_rows, columns), jnp.bfloat16)
    return Part(
        [(terms, VMEM)],
        [(jax.ShapeDtypeStruct((all_rows, columns), kind), VMEM)],
        [buffer, buffer, buffer, buffer, sems, sems, sems, sems],
        steps,
        line=True,
    )


def columns_part(blocks):
    ranks, rows, columns = blocks.shape

    def steps(ins, outs, scratch):
        (in_ref,), (out_ref,) = ins, outs
        send, recv, up_send, up_recv, down_send, down_recv, local = scratch
        x, c, y = corner()
        z = lax.axis_index("z")
        own = slot(x, c, y)
        peers = plane_peers()
        spots = [(x * CORNERS + c, y)]
        spots += [(flip(x, dx) * CORNERS + flip(c, dc), flip(y, dy)) for dx, dc, dy in OTHERS]

        def at(i, plane):
            return out_ref.at[spots[i][0], plane, spots[i][1]]

        keep = pltpu.make_async_copy(in_ref.at[own], at(0, z), local)
        sent = []

        def up(t, i, source=None):
            s = at(i, z - t) if source is None else source
            n = t * RANKS + i
            return remote(s, at(i, z - t), up_send.at[n], up_recv.at[n], {"z": z + 1})

        def down(t, i, source=None):
            s = at(i, z + t) if source is None else source
            n = t * RANKS + i
            return remote(s, at(i, z + t), down_send.at[n], down_recv.at[n], {"z": z - 1})

        def begin(i, source=None):
            @pl.when(z < PLANES - 1)
            def _():
                up(0, i, source).start()

            @pl.when(z > 0)
            def _():
                down(0, i, source).start()

        def first():
            keep.start()
            for i, (there, other) in enumerate(peers):
                copy = remote(in_ref.at[other], at(0, z), send.at[i], recv.at[i], there)
                copy.start()
                sent.append(copy)
            begin(0, in_ref.at[own])

        def swapped(i):
            landed(at(i, z), recv.at[i - 1], peers[i - 1][0])
            begin(i)

        def arrive(t, i):
            n = t * RANKS + i
            on = t + 1 < PLANES - 1

            @pl.when(z - 1 - t >= 0)
            def _():
                landed(at(i, z - 1 - t), up_recv.at[n], {"z": z - 1})
                if on:

                    @pl.when(z < PLANES - 1)
                    def _():
                        up(t + 1, i).start()

            @pl.when(z + 1 + t < PLANES)
            def _():
                landed(at(i, z + 1 + t), down_recv.at[n], {"z": z + 1})
                if on:

                    @pl.when(z > 0)
                    def _():
                        down(t + 1, i).start()

        def last():
            for copy in sent:
                copy.wait_send()
            for t in range(PLANES - 1):
                for i in range(RANKS):

                    @pl.when((z < PLANES - 1) & (z - t >= 0))
                    def _():
                        up(t, i).wait_send()

                    @pl.when((z > 0) & (z + t < PLANES))
                    def _():
                        down(t, i).wait_send()

            keep.wait()

        middle = [functools.partial(swapped, i) for i in range(1, RANKS)]
        middle += [
            functools.partial(arrive, t, i) for t in range(PLANES - 1) for i in range(RANKS)
        ]
        return first, middle, last

    n = len(OTHERS)
    sems = DMA(((PLANES - 1) * RANKS,))
    shape = (CORNERS**2, PLANES, CORNERS, rows, columns)
    return Part(
        [(blocks, VMEM)],
        [(jax.ShapeDtypeStruct(shape, blocks.dtype), ANYWHERE)],
        [DMA((n,)), DMA((n,)), sems, sems, sems, sems, DMA(())],
        steps,
        plane="all",
        line=True,
    )


def tiles_part(tile):
    def steps(ins, outs, scratch):
        (in_ref,), (out_ref,) = ins, outs
        send, recv, up_send, up_recv, down_send, down_recv, local = scratch
        z = lax.axis_index("z")
        own = slot(*corner())
        peers = plane_peers()
        keep = pltpu.make_async_copy(in_ref, out_ref.at[z, own], local)

        def give(i):
            return remote(in_ref, out_ref.at[z, own], send.at[i], recv.at[i], peers[i][0])

        def up(t):
            to = out_ref.at[z - t]
            return remote(to, to, up_send.at[t], up_recv.at[t], {"z": z + 1})

        def down(t):
            to = out_ref.at[z + t]
            return remote(to, to, down_send.at[t], down_recv.at[t], {"z": z - 1})

        def first():
            keep.start()
            for i in range(len(peers)):
                give(i).start()

        def swapped():
            for i, (there, other) in enumerate(peers):
                landed(out_ref.at[z, other], recv.at[i], there)
            keep.wait()

            @pl.when(z < PLANES - 1)
            def _():
                up(0).start()

            @pl.when(z > 0)
            def _():
                down(0).start()

        def arrive(t):
            on = t + 1 < PLANES - 1

            @pl.when(z - 1 - t >= 0)
            def _():
                landed(out_ref.at[z - 1 - t], up_recv.at[t], {"z": z - 1})
                if on:

                    @pl.when(z < PLANES - 1)
                    def _():
                        up(t + 1).start()

            @pl.when(z + 1 + t < PLANES)
            def _():
                landed(out_ref.at[z + 1 + t], down_recv.at[t], {"z": z + 1})
                if on:

                    @pl.when(z > 0)
                    def _():
                        down(t + 1).start()

        def last():
            for i in range(len(peers)):
                give(i).wait_send()
            for t in range(PLANES - 1):

                @pl.when((z < PLANES - 1) & (z - t >= 0))
                def _():
                    up(t).wait_send()

                @pl.when((z > 0) & (z + t < PLANES))
                def _():
                    down(t).wait_send()

        middle = [swapped] + [functools.partial(arrive, t) for t in range(PLANES - 1)]
        return first, middle, last

    n = len(OTHERS)
    line = DMA((PLANES - 1,))
    return Part(
        [(tile, VMEM)],
        [(jax.ShapeDtypeStruct((PLANES, RANKS) + tile.shape, tile.dtype), VMEM)],
        [DMA((n,)), DMA((n,)), line, line, line, line, DMA(())],
        steps,
        plane="all",
        line=True,
    )


def marks_part(marks):
    def steps(ins, outs, scratch):
        (in_ref,), (out_ref,) = ins, outs
        send, recv, local = scratch
        x, c, _ = corner()
        keep = pltpu.make_async_copy(in_ref, out_ref.at[x * CORNERS + c], local)
        near = []
        for i, (dx, dc) in enumerate([(0, 1), (1, 0), (1, 1)]):
            px, pc = flip(x, dx), flip(c, dc)
            near.append((i, {"x": px, "core": pc}, px * CORNERS + pc))

        def give(i, there):
            return remote(in_ref, out_ref.at[x * CORNERS + c], send.at[i], recv.at[i], there)

        def first():
            keep.start()
            for i, there, _ in near:
                give(i, there).start()

        def last():
            for i, there, theirs in near:
                landed(out_ref.at[theirs], recv.at[i], there)
                give(i, there).wait_send()
            keep.wait()

        return first, [], last

    return Part(
        [(marks, VMEM)],
        [(jax.ShapeDtypeStruct((CORNERS**2,) + marks.shape, marks.dtype), VMEM)],
        [DMA((3,)), DMA((3,)), DMA(())],
        steps,
        plane="all",
    )


def root_mean_scale(values, gains):
    return values * lax.rsqrt(jnp.mean(values * values, axis=-1, keepdims=True) + 1e-06) * gains


def rope_tables(positions):
    half = HEAD_SIZE // 2
    steps_half = jnp.arange(half).astype(jnp.float32)
    inverse = jnp.power(1000000.0, steps_half * (-2.0 / HEAD_SIZE))
    angles = positions.astype(jnp.float32)[:, None] * inverse[None, :]
    cosine, sine = jnp.cos(angles), jnp.sin(angles)
    return jnp.concatenate([cosine, cosine], axis=-1), jnp.concatenate([-sine, sine], axis=-1)


def matrix_product(left, right):
    return jnp.dot(left, right, preferred_element_type=jnp.float32)


def contract_last(left, right):
    return lax.dot_general(
        left, right, (((1,), (1,)), ((), ())), preferred_element_type=jnp.float32
    )


def contract_first(left, right):
    return lax.dot_general(
        left, right, (((0,), (0,)), ((), ())), preferred_element_type=jnp.float32
    )


def low(values):
    return values.astype(jnp.bfloat16)

def turn(values, cosine, sine):
    return values * cosine + pltpu.roll(values, HEAD_SIZE // 2, 1) * sine


def turn_back(grads, cosine, sine):
    return grads * cosine + pltpu.roll(grads * sine, HEAD_SIZE // 2, 1)


def unit_scale(values):
    return lax.rsqrt(jnp.mean(values * values, axis=-1, keepdims=True) + 1e-06)


def norm_back(raw, gain, grads):
    scale = unit_scale(raw)
    unit = raw * scale
    inner = grads * gain
    d_raw = scale * (inner - unit * jnp.mean(inner * unit, axis=-1, keepdims=True))
    return d_raw, grads * unit


def head(index):
    return slice(index * HEAD_SIZE, (index + 1) * HEAD_SIZE)


def dot(left, right):
    return jnp.dot(left, right, preferred_element_type=jnp.float32)


def dot_rows(left, right):
    return lax.dot_general(
        left, right, (((1,), (1,)), ((), ())), preferred_element_type=jnp.float32
    )


def prepare_kernel(
    x_ref, gain_ref, w_ref, cos_ref, sin_ref, qg_ref, kg_ref, x_out, q_ref, kv_ref, raw_ref, gate_ref
):
    hidden = x_ref[...].astype(jnp.float32)
    x_out[...] = low(hidden * unit_scale(hidden) * gain_ref[...])
    raw = dot(x_out[...], w_ref[...])
    cosine, sine = cos_ref[...], sin_ref[...]

    def prepare(values, gain):
        return low(turn(values * unit_scale(values) * gain, cosine, sine))

    for h in range(REPEAT):
        q_ref[:, head(h)] = prepare(raw[:, head(h)], qg_ref[...])
    kv_ref[:, head(0)] = prepare(raw[:, head(REPEAT)], kg_ref[...])
    kv_ref[:, head(1)] = low(raw[:, head(REPEAT + 1)])
    raw_ref[...] = raw[:, : (REPEAT + 1) * HEAD_SIZE]
    gate_ref[...] = raw[:, (REPEAT + 2) * HEAD_SIZE :]


def rows_spec(rows, columns):
    return pl.BlockSpec((rows, columns), lambda i: (i, 0))


def fixed_spec(*shape):
    return pl.BlockSpec(shape, lambda i: (0,) * len(shape))


def kernel_params(vmem):
    return pltpu.CompilerParams(vmem_limit_bytes=vmem << 20)


def prepare_attention(hidden, gain_attn, w_attn, cosine, sine, gain_query, gain_key):
    tokens, width = hidden.shape
    columns = w_attn.shape[1]
    q_columns = REPEAT * HEAD_SIZE
    rows = tokens // RANKS
    shape = jax.ShapeDtypeStruct
    return pl.pallas_call(
        prepare_kernel,
        grid=(RANKS,),
        out_shape=[
            shape((tokens, width), jnp.bfloat16),
            shape((tokens, q_columns), jnp.bfloat16),
            shape((tokens, 2 * HEAD_SIZE), jnp.bfloat16),
            shape((tokens, q_columns + HEAD_SIZE), jnp.float32),
            shape((tokens, q_columns), jnp.float32),
        ],
        in_specs=[
            rows_spec(rows, width),
            fixed_spec(1, width),
            fixed_spec(width, columns),
            rows_spec(rows, HEAD_SIZE),
            rows_spec(rows, HEAD_SIZE),
            fixed_spec(1, HEAD_SIZE),
            fixed_spec(1, HEAD_SIZE),
        ],
        out_specs=[
            rows_spec(rows, width),
            rows_spec(rows, q_columns),
            rows_spec(rows, 2 * HEAD_SIZE),
            rows_spec(rows, q_columns + HEAD_SIZE),
            rows_spec(rows, q_columns),
        ],
        compiler_params=kernel_params(60),
        cost_estimate=expected(12),
    )(hidden, gain_attn[None], w_attn, cosine, sine, gain_query[None], gain_key[None])


EXPONENT = math.log2(math.e) / math.sqrt(HEAD_SIZE)


def allowed_keys(own_ref, keys_ref, z, window):
    seq, pos = own_ref[0, :, 0:1], own_ref[0, :, 1:2]
    key_seq = keys_ref[0, 0:1, z * window : (z + 1) * window]
    key_pos = keys_ref[0, 1:2, z * window : (z + 1) * window]
    return (key_pos <= pos) & ((key_seq == 0) | (key_seq == seq))


def attend_kernel(q_ref, kv_ref, gate_ref, own_ref, keys_ref, wo_ref, terms_ref, att_ref, log_ref, gated_ref):
    planes, window = kv_ref.shape[0], kv_ref.shape[1]
    totals = [None] * REPEAT
    ones = jnp.ones((window, HEAD_SIZE), jnp.bfloat16)
    for z in range(planes):
        allowed = allowed_keys(own_ref, keys_ref, z, window)
        keys = kv_ref[z, :, head(0)]
        values = jnp.concatenate([kv_ref[z, :, head(1)], ones], axis=1)
        for h in range(REPEAT):
            scores = dot_rows(q_ref[:, head(h)], keys) * EXPONENT
            exponent = low(jnp.where(allowed, jnp.exp2(scores), 0.0))
            part = dot(exponent, values)
            totals[h] = part if totals[h] is None else totals[h] + part
    for h in range(REPEAT):
        weight = totals[h][:, head(1)]
        attended = totals[h][:, head(0)] / weight
        att_ref[:, head(h)] = attended
        log_ref[:, head(h)] = jnp.log2(weight)
        gated_ref[:, head(h)] = low(attended * jax.nn.sigmoid(gate_ref[:, head(h)]))
    terms_ref[...] = low(dot(gated_ref[...], wo_ref[...]))


def group_specs(window):
    return [
        pl.BlockSpec((PLANES, window, 2 * HEAD_SIZE), lambda i: (0, i, 0)),
        pl.BlockSpec((1, window, 2), lambda i: (i, 0, 0)),
        pl.BlockSpec((1, 2, PLANES * window), lambda i: (i, 0, 0)),
    ]


def attend(query, pair, gate, own, keys, w_out):
    tokens, q_columns = query.shape
    groups = own.shape[0]
    window = tokens // groups
    width = w_out.shape[1]
    kv, mine, marks = group_specs(window)
    shape = jax.ShapeDtypeStruct
    columns = rows_spec(window, q_columns)
    return pl.pallas_call(
        attend_kernel,
        grid=(groups,),
        out_shape=[
            shape((tokens, width), jnp.bfloat16),
            shape((tokens, q_columns), jnp.float32),
            shape((tokens, q_columns), jnp.float32),
            shape((tokens, q_columns), jnp.bfloat16),
        ],
        in_specs=[columns, kv, columns, mine, marks, fixed_spec(q_columns, width)],
        out_specs=[rows_spec(window, width), columns, columns, columns],
        compiler_params=kernel_params(48),
        cost_estimate=expected(18),
    )(query, pair, gate, own, keys, w_out)


def attend_back_kernel(
    branch_ref, wo_ref, q_ref, kv_ref, gate_ref, own_ref, keys_ref, att_ref, log_ref, raw_ref,
    cos_ref, sin_ref, qg_ref, gated_ref, out_ref, dkv_ref, gain_ref, term_ref, term_sum,
):
    planes, window = kv_ref.shape[0], kv_ref.shape[1]
    scale = 1.0 / math.sqrt(HEAD_SIZE)
    turned = jnp.transpose(gated_ref[...])

    @pl.when(pl.program_id(0) == 0)
    def _():
        term_sum[...] = dot(turned, branch_ref[...])

    @pl.when(pl.program_id(0) > 0)
    def _():
        term_sum[...] += dot(turned, branch_ref[...])

    @pl.when(pl.program_id(0) == pl.num_programs(0) - 1)
    def _():
        term_ref[...] = low(term_sum[...])

    d_gated = dot_rows(branch_ref[...], wo_ref[...])
    gate = jax.nn.sigmoid(gate_ref[...])
    attended = att_ref[...]
    d_attended = low(d_gated * gate)
    out_ref[:, (REPEAT + 2) * HEAD_SIZE :] = low(d_gated * attended * gate * (1.0 - gate))
    product = d_attended.astype(jnp.float32) * attended
    delta = [jnp.sum(product[:, head(h)], axis=-1, keepdims=True) for h in range(REPEAT)]
    turned_q = [jnp.transpose(q_ref[:, head(h)]) for h in range(REPEAT)]
    turned_d = [jnp.transpose(d_attended[:, head(h)]) for h in range(REPEAT)]
    d_query = [None] * REPEAT
    for z in range(planes):
        allowed = allowed_keys(own_ref, keys_ref, z, window)
        keys, values = kv_ref[z, :, head(0)], kv_ref[z, :, head(1)]
        d_keys, d_values = None, None
        for h in range(REPEAT):
            scores = dot_rows(q_ref[:, head(h)], keys) * EXPONENT - log_ref[:, h * HEAD_SIZE : h * HEAD_SIZE + 1]
            probs = jnp.where(allowed, jnp.exp2(scores), 0.0)
            d_probs = dot_rows(d_attended[:, head(h)], values)
            d_scores = low(probs * (d_probs - delta[h]))
            part = dot(d_scores, keys)
            d_query[h] = part if d_query[h] is None else d_query[h] + part
            part = dot(turned_q[h], d_scores)
            d_keys = part if d_keys is None else d_keys + part
            part = dot(turned_d[h], low(probs))
            d_values = part if d_values is None else d_values + part
        dkv_ref[z, :, head(0)] = low(jnp.transpose(d_keys * scale))
        dkv_ref[z, :, head(1)] = low(jnp.transpose(d_values))
    cosine, sine = cos_ref[...], sin_ref[...]
    total = jnp.zeros((1, HEAD_SIZE), jnp.float32)
    for h in range(REPEAT):
        grads = turn_back(d_query[h] * scale, cosine, sine)
        d_raw, by_row = norm_back(raw_ref[:, head(h)], qg_ref[...], grads)
        out_ref[:, head(h)] = low(d_raw)
        total += jnp.sum(by_row, axis=0, keepdims=True)
    gain_ref[0] = jnp.broadcast_to(total, gain_ref.shape[1:])


def attend_back(
    branch, w_out, query, pair, gate, own, keys, attended, log, raw, cosine, sine, gain, gated
):
    tokens, q_columns = query.shape
    groups = own.shape[0]
    window = tokens // groups
    width = w_out.shape[1]
    kv, mine, marks = group_specs(window)
    shape = jax.ShapeDtypeStruct
    columns = rows_spec(window, q_columns)
    table = rows_spec(window, HEAD_SIZE)
    return pl.pallas_call(
        attend_back_kernel,
        grid=(groups,),
        out_shape=[
            shape((tokens, 2 * q_columns + 2 * HEAD_SIZE), jnp.bfloat16),
            shape(pair.shape, jnp.bfloat16),
            shape((groups, 8, HEAD_SIZE), jnp.float32),
            shape((q_columns, width), jnp.bfloat16),
        ],
        in_specs=[
            rows_spec(window, width), fixed_spec(q_columns, width), columns, kv, columns, mine, marks,
            columns, columns, rows_spec(window, raw.shape[1]), table, table, fixed_spec(1, HEAD_SIZE), columns,
        ],
        out_specs=[
            rows_spec(window, 2 * q_columns + 2 * HEAD_SIZE), kv, pl.BlockSpec((1, 8, HEAD_SIZE), lambda i: (i, 0, 0)),
            fixed_spec(q_columns, width),
        ],
        scratch_shapes=[pltpu.VMEM((q_columns, width), jnp.float32)],
        compiler_params=kernel_params(56),
        cost_estimate=expected(35),
    )(branch, w_out, query, pair, gate, own, keys, attended, log, raw, cosine, sine, gain[None], gated)


def finish_kernel(dkv_ref, raw_ref, cos_ref, sin_ref, kg_ref, partial_ref, out_ref, gain_ref):
    grads = turn_back(dkv_ref[:, head(0)], cos_ref[...], sin_ref[...])
    d_raw, by_row = norm_back(raw_ref[...], kg_ref[...], grads)
    out_ref[:, head(0)] = low(d_raw)
    out_ref[:, head(1)] = low(dkv_ref[:, head(1)])
    gain_ref[0] = jnp.broadcast_to(jnp.sum(by_row, axis=0, keepdims=True), gain_ref.shape[1:])


def finish_attention(d_pair, raw, cosine, sine, gain, partial, steps=4):
    tokens = d_pair.shape[0]
    rows = tokens // steps
    table = rows_spec(rows, HEAD_SIZE)
    shape = jax.ShapeDtypeStruct
    return pl.pallas_call(
        finish_kernel,
        grid=(steps,),
        out_shape=[shape(partial.shape, partial.dtype), shape((steps, 8, HEAD_SIZE), jnp.float32)],
        in_specs=[
            rows_spec(rows, 2 * HEAD_SIZE),
            pl.BlockSpec((rows, HEAD_SIZE), lambda i: (i, REPEAT)),
            table,
            table,
            fixed_spec(1, HEAD_SIZE),
            ANYWHERE,
        ],
        out_specs=[
            pl.BlockSpec((rows, 2 * HEAD_SIZE), lambda i: (i, REPEAT // 2)),
            pl.BlockSpec((1, 8, HEAD_SIZE), lambda i: (i, 0, 0)),
        ],
        input_output_aliases={5: 0},
        compiler_params=kernel_params(60),
        cost_estimate=expected(4),
    )(d_pair, raw, cosine, sine, gain[None], partial)


def split_part(gate, up, pieces):
    rows, every = gate.shape
    units = every // RANKS
    piece = units // pieces

    def steps(ins, outs, scratch):
        (out_ref,) = outs

        def some(corner_at):
            for y in range(CORNERS):
                for at, ref in ((0, ins[0]), (units, ins[1])):
                    starts = [((corner_at * pieces + d) * CORNERS + y) * piece for d in range(pieces)]
                    parts = [ref[:, start : start + piece] for start in starts]
                    out_ref[corner_at * CORNERS + y, :, at : at + units] = jnp.concatenate(parts, axis=1)

        return (lambda: None), [functools.partial(some, i) for i in range(CORNERS**2)], (lambda: None)

    return Part(
        [(gate, VMEM), (up, VMEM)],
        [(jax.ShapeDtypeStruct((RANKS, rows, 2 * units), gate.dtype), VMEM)],
        [],
        steps,
    )


def join_part(blocks, pieces):
    ranks, rows, width = blocks.shape
    units = width // 2
    piece = units // pieces

    def steps(ins, outs, scratch):
        (in_ref,) = ins

        def some(corner_at):
            for at, ref in ((0, outs[0]), (units, outs[1])):
                parts = []
                for d in range(pieces):
                    for y in range(CORNERS):
                        here = slice(at + d * piece, at + (d + 1) * piece)
                        parts.append(in_ref[corner_at * CORNERS + y, :, here])
                wide = CORNERS * units
                ref[:, corner_at * wide : (corner_at + 1) * wide] = jnp.concatenate(parts, axis=1)

        return (lambda: None), [functools.partial(some, i) for i in range(CORNERS**2)], (lambda: None)

    out = (jax.ShapeDtypeStruct((rows, ranks * units), blocks.dtype), VMEM)
    return Part([(blocks, VMEM)], [out, out], [], steps)


def norm_rows_kernel(x_ref, gain_ref, grads_ref, more_ref, out_ref, term_ref):
    values = x_ref[...].astype(jnp.float32)
    d_values, by_row = norm_back(values, gain_ref[...], grads_ref[...])
    out_ref[...] = more_ref[...].astype(jnp.float32) + d_values

    @pl.when(pl.program_id(0) == 0)
    def _():
        term_ref[...] = jnp.zeros_like(term_ref)

    term_ref[...] += jnp.sum(by_row.reshape(-1, *term_ref.shape), axis=0)


def norm_rows_back(values, gain, grads, more, steps=4):
    rows, width = values.shape
    some = rows_spec(rows // steps, width)
    d_values, term = pl.pallas_call(
        norm_rows_kernel,
        grid=(steps,),
        out_shape=[jax.ShapeDtypeStruct(values.shape, jnp.float32), jax.ShapeDtypeStruct((8, width), jnp.float32)],
        in_specs=[some, fixed_spec(1, width), some, some],
        out_specs=[some, fixed_spec(8, width)],
        compiler_params=kernel_params(60),
        cost_estimate=expected(3),
    )(values, gain[None], grads, more)
    return d_values, jnp.sum(term, axis=0)


def widen_kernel(count, in_ref, *refs):
    weights, refs = refs[:count], refs[count:]
    others = (len(refs) - count - 1) // 2
    low_refs, refs = refs[:others], refs[others:]
    out_refs, along_ref, wide_refs = refs[:count], refs[count], refs[count + 1 :]
    along = jnp.zeros(along_ref.shape, jnp.float32)
    for rank in range(RANKS):
        start = 0
        for weight_ref, ref in zip(weights, out_refs):
            width = ref.shape[1] // RANKS
            place = slice(rank * width, (rank + 1) * width)
            value = in_ref[rank, :, start : start + width].astype(jnp.float32)
            ref[:, place] = value
            product = value * weight_ref[:, place].astype(jnp.float32)
            along += sum(product[:, head(h)] for h in range(width // HEAD_SIZE))
            start += width
    along_ref[...] = jnp.broadcast_to(jnp.sum(along, axis=1, keepdims=True), along_ref.shape)
    for ref, wide in zip(low_refs, wide_refs):
        wide[...] = ref[...].astype(jnp.float32)


def widen_columns(parts, widths, weights, others):
    ranks, rows, columns = parts.shape
    shape = jax.ShapeDtypeStruct
    out_shape = [shape((rows, ranks * w), jnp.float32) for w in widths]
    out_shape += [shape((rows, HEAD_SIZE), jnp.float32)]
    out_shape += [shape(o.shape, jnp.float32) for o in others]
    return pl.pallas_call(
        functools.partial(widen_kernel, len(widths)),
        out_shape=out_shape,
        in_specs=[VMEM] * (1 + len(weights) + len(others)),
        out_specs=[VMEM] * len(out_shape),
        compiler_params=kernel_params(32),
        cost_estimate=expected(4),
    )(parts, *weights, *others)


def make_shards(cells):
    data_total = cells * PLANES

    def blocks(terms):
        return low(terms).reshape(RANKS, -1, terms.shape[1])

    def gather_tokens(rows):
        return run([gather_part(rows)], 0)[0]

    def scatter_tokens(terms):
        return run([scatter_part(blocks(terms))], 1, 40)[0]

    def split_columns(weight):
        return weight.reshape(weight.shape[0], RANKS, -1)

    def send_columns(pieces):
        return jnp.transpose(jnp.concatenate(pieces, axis=-1), (1, 0, 2))

    def join_cells(rows):
        if cells > 1:
            rows = lax.all_gather(rows, "cell", axis=0, tiled=False)
            rows = jnp.transpose(rows, (1, 0, 2, 3, 4, 5))
        return rows.reshape(-1, rows.shape[-1])

    def gather_columns(mine):
        rows, columns = mine.shape[1:]
        every = lax.all_gather(mine, DATA, axis=0, tiled=False)
        every = every.reshape(data_total, CORNERS**2, CORNERS, rows, columns)
        return jnp.transpose(every, (1, 0, 2, 3, 4)).reshape(-1, columns)

    def sum_columns(term):
        rows = term.shape[0] // (RANKS * data_total)
        split = low(term).reshape(CORNERS**2, data_total, CORNERS, rows, -1)
        split = jnp.transpose(split, (1, 0, 2, 3, 4)).reshape(data_total * RANKS, rows, -1)
        return lax.psum_scatter(split, DATA, scatter_dimension=0, tiled=True)

    inner = CORNERS * data_total
    to_rank = []
    for source in range(inner):
        rank_y, place = divmod(source, data_total)
        to_rank.append((source, place * CORNERS + rank_y))
    INNER = ("cell", "z", "y")

    def shards(
        hidden_in,
        query_weight,
        key_matrix,
        value_matrix,
        gate_weight,
        out_weight,
        norm_attn,
        query_gain,
        key_gain,
        norm_ffn,
        ffn_gate,
        ffn_up,
        ffn_down,
        cotangent,
        sequence_numbers,
        positions,
    ):
        rows = hidden_in.shape[0]
        tokens = rows * RANKS
        groups = CORNERS**2
        window = GROUP_TOKENS // PLANES

        sizes = [norm_attn.shape[0], norm_ffn.shape[0], query_gain.shape[0], key_gain.shape[0]]
        cuts = [0]
        for size in sizes:
            cuts.append(cuts[-1] + size)
        tile = (8, HEAD_SIZE)
        pad = tile[0] * tile[1] - cuts[-1]
        own_gains = jnp.concatenate([norm_attn, norm_ffn, query_gain, key_gain]).astype(jnp.float32)
        own_gains = jnp.pad(own_gains, (0, pad)).reshape(tile)
        plane = lax.axis_index("z")
        group_start = lax.axis_index("cell") * GROUP_TOKENS
        marks = jnp.concatenate(
            [
                lax.dynamic_slice_in_dim(sequence_numbers, group_start, GROUP_TOKENS),
                lax.dynamic_slice_in_dim(positions, group_start, GROUP_TOKENS),
            ]
        ).reshape(-1, HEAD_SIZE)
        attn_columns = send_columns(
            [
                split_columns(query_weight),
                split_columns(key_matrix),
                split_columns(value_matrix),
                split_columns(gate_weight),
            ]
        )
        gains, attn_rows, hidden_all, marks, ffn_columns = run(
            [
                tiles_part(own_gains),
                columns_part(attn_columns),
                between(gather_part(hidden_in), 0.22, 0.8),
                marks_part(marks),
                split_part(ffn_gate, ffn_up, data_total),
            ],
            2,
            micros=70,
        )
        attn_rows, out_rows, down_rows = lax.optimization_barrier(
            (attn_rows, lax.ppermute(out_weight, INNER, to_rank), ffn_down)
        )
        w_attn = join_cells(attn_rows)
        gains = gains.reshape(PLANES, CORNERS**2, CORNERS, -1)
        gains = jnp.transpose(gains, (1, 0, 2, 3)).reshape(CORNERS**2, PLANES * CORNERS, -1)
        if cells > 1:
            gains = lax.all_gather(gains, "cell", axis=1, tiled=False)
        gains = gains.reshape(RANKS * data_total, -1)
        gain_attn, gain_ffn, gain_query, gain_key = (
            gains[:, a:b].reshape(-1) for a, b in zip(cuts[:-1], cuts[1:])
        )
        w_out = lax.all_gather(out_rows, DATA, axis=0, tiled=True)
        w_down = lax.all_gather(down_rows, DATA, axis=0, tiled=True)

        marks = marks.reshape(groups, 2, GROUP_TOKENS)
        own_marks = lax.dynamic_slice_in_dim(marks, plane * window, window, axis=2)
        cosine, sine = rope_tables(own_marks[:, 1].reshape(tokens))
        own_marks = jnp.transpose(own_marks, (0, 2, 1))

        hidden = hidden_in.astype(jnp.float32)
        normed_input, query_low, pair, raw, gate_raw = prepare_attention(
            hidden_all, gain_attn, w_attn, cosine, sine, gain_query, gain_key
        )
        pair, cotangent_all, ffn_columns = run(
            [line_gather_part(pair), gather_part(cotangent), swap_part(ffn_columns)], 3, micros=75
        )
        w_ffn = gather_columns(ffn_columns)
        out_terms, attended, log_weight, gated_low = attend(
            query_low, pair, gate_raw, own_marks, marks, w_out
        )
        out_terms = out_terms.reshape(RANKS, rows, -1)
        middle = hidden + run([scatter_part(out_terms)], 1, 40)[0]

        normed_two = gather_tokens(low(root_mean_scale(middle, gain_ffn)))
        both = matrix_product(normed_two, w_ffn)
        units = both.shape[1] // 2
        gate_ffn, up_ffn = both[:, :units], both[:, units:]
        ffn_sig = jax.nn.sigmoid(gate_ffn)
        mixed_low = low(gate_ffn * ffn_sig * up_ffn)

        down_term = low(contract_first(mixed_low, cotangent_all))
        down_term, cotangent_all = lax.optimization_barrier((down_term, cotangent_all))
        grad_down = lax.psum_scatter(down_term, DATA, scatter_dimension=0, tiled=True)
        d_mixed = contract_last(cotangent_all, w_down)
        d_up_low = low(d_mixed * gate_ffn * ffn_sig)
        d_gate_ffn_low = low(d_mixed * up_ffn * ffn_sig * (1.0 + gate_ffn * (1.0 - ffn_sig)))
        d_both = jnp.concatenate([d_gate_ffn_low, d_up_low], axis=-1)
        both_term = low(contract_first(normed_two, d_both))
        both_term, d_both = lax.optimization_barrier((both_term, d_both))
        grad_both = sum_columns(both_term)
        (d_normed_two,) = run([scatter_part(product=(d_both, w_ffn), transposed=True)], 6, 48, 45)
        d_middle, grad_norm_two_term = norm_rows_back(middle, gain_ffn, d_normed_two, cotangent)

        branch_all = gather_tokens(low(d_middle))
        branch_all, grad_down = lax.optimization_barrier((branch_all, grad_down))
        d_partial, d_pair, query_gain_terms, out_term = attend_back(
            branch_all, w_out, query_low, pair, gate_raw, own_marks, marks,
            attended, log_weight, raw, cosine, sine, gain_query, gated_low,
        )
        d_pair, result, grad_both, out_term = run(
            [
                line_scatter_part(d_pair),
                scatter_part(product=(mixed_low, w_down)),
                swap_part(grad_both),
                halves_part(out_term, data_total),
            ],
            5,
            58,
            75,
        )
        grad_out = lax.psum_scatter(
            out_term.reshape(-1, out_term.shape[-1]), DATA, scatter_dimension=0, tiled=True
        )
        output = low(middle + result)
        d_raw, key_gain_terms = finish_attention(
            d_pair, raw, cosine, sine, gain_key, d_partial
        )
        grad_query_gain_term = jnp.sum(query_gain_terms[:, 0], axis=0)
        grad_key_gain_term = jnp.sum(key_gain_terms[:, 0], axis=0)
        a = REPEAT * HEAD_SIZE
        b, c = a + HEAD_SIZE, a + 2 * HEAD_SIZE
        attn_term = low(contract_first(normed_input, d_raw))
        attn_term, d_raw = lax.optimization_barrier((attn_term, d_raw))
        split = attn_term.reshape(CORNERS**2, cells, PLANES, CORNERS, -1, attn_term.shape[1])
        split = jnp.transpose(split, (2, 1, 0, 3, 4, 5)).reshape(PLANES, -1, attn_term.shape[1])
        small = jnp.concatenate(
            [
                t.reshape(RANKS * data_total, -1)
                for t in (grad_norm_two_term, grad_query_gain_term, grad_key_gain_term)
            ],
            axis=-1,
        )
        spare = tile[0] * tile[1] - small.shape[1]
        small = low(jnp.pad(small, ((0, 0), (0, spare))))
        small = small.reshape((CORNERS**2, cells, PLANES, CORNERS) + tile)
        small = jnp.transpose(small, (2, 1, 0, 3, 4, 5)).reshape(PLANES, -1, HEAD_SIZE)
        small, grad_attn, d_normed, grad_gate, grad_up = run(
            [
                line_scatter_part(small, pieces=1),
                line_scatter_part(split, kind=jnp.bfloat16),
                scatter_part(product=(d_raw, w_attn), transposed=True),
                join_part(grad_both, data_total),
            ],
            7,
            58,
            60,
        )
        if cells > 1:
            grad_attn = lax.psum_scatter(grad_attn, "cell", scatter_dimension=0, tiled=True)
            small = lax.psum_scatter(small, "cell", scatter_dimension=0, tiled=True)
        grad_attn = grad_attn.reshape(RANKS, -1, attn_term.shape[1])
        grad_attn, small = run(
            [swap_part(grad_attn), swap_part(small.reshape((RANKS,) + tile))], 4, micros=14
        )
        (
            grad_query, grad_key, grad_value, grad_gatew, along, grad_gate, grad_up, grad_down, grad_out
        ) = widen_columns(
            grad_attn,
            (a, b - a, c - b, a),
            (query_weight, key_matrix, value_matrix, gate_weight),
            (grad_gate, grad_up, grad_down, grad_out),
        )
        grad_norm_attn = along[:, 0] / norm_attn.astype(jnp.float32)
        input_grad = norm_rows_back(hidden_in, gain_attn, d_normed, d_middle)[0]
        small = jnp.sum(small, axis=0).reshape(-1)
        ends = [size - cuts[1] for size in cuts]
        grad_norm_ffn, grad_query_gain, grad_key_gain = (
            small[s:e] for s, e in zip(ends[1:-1], ends[2:])
        )
        return (
            output,
            input_grad,
            grad_query,
            grad_key,
            grad_value,
            grad_gatew,
            grad_out,
            grad_norm_attn,
            grad_query_gain,
            grad_key_gain,
            grad_norm_ffn,
            grad_gate,
            grad_up,
            grad_down,
        )

    return shards


def solution(mesh):
    cells = mesh.shape["fsdp"] // (PLANES * CORNERS)
    split = Mesh(
        mesh.devices.reshape(CORNERS, CORNERS, cells, PLANES, CORNERS),
        ALL,
    )
    rows, flat, group = P(ALL, None), P(ALL), P(("x", "core"))
    return jax.shard_map(
        make_shards(cells),
        mesh=split,
        in_specs=(rows,) * 6 + (flat,) * 4 + (rows,) * 4 + (group,) * 2,
        out_specs=(rows,) * 7 + (flat,) * 4 + (rows,) * 3,
        check_vma=False,
    )
```

```python
import functools
import math

import jax
import jax.numpy as jnp
from jax import lax
from jax.experimental import pallas as pl
from jax.experimental.pallas import tpu as pltpu
from jax.sharding import Mesh
from jax.sharding import PartitionSpec as P

QUERY_HEADS = 16
KEY_VALUE_HEADS = 8
HEAD_SIZE = 128
REPEAT = QUERY_HEADS // KEY_VALUE_HEADS
GROUP_TOKENS = 2048
CORNERS = 2
PLANES = 4
ALL = ("x", "core", "cell", "z", "y")
TENSOR = ("x", "core", "y")
DATA = ("cell", "z")
RANKS = CORNERS**3
CHUNKS = 4
MESH_ID = pl.DeviceIdType.MESH
OTHERS = [(dx, dc, dy) for dx in (0, 1) for dc in (0, 1) for dy in (0, 1) if dx + dc + dy]
DMA = pltpu.SemaphoreType.DMA
VMEM = pl.BlockSpec(memory_space=pltpu.VMEM)
ANYWHERE = pl.BlockSpec(memory_space=pl.ANY)


def remote(source, target, send, receive, device):
    return pltpu.make_async_remote_copy(
        src_ref=source,
        dst_ref=target,
        send_sem=send,
        recv_sem=receive,
        device_id=device,
        device_id_type=MESH_ID,
    )


def landed(ref, sem, device):
    remote(ref, ref, sem, sem, device).wait_recv()


def corner():
    return lax.axis_index("x"), lax.axis_index("core"), lax.axis_index("y")


def slot(x, c, y):
    return (x * CORNERS + c) * CORNERS + y


def flip(value, bit):
    return 1 - value if bit else value


def neighbours():
    x, c, y = corner()
    return {"x": 1 - x}, {"y": 1 - y}, {"core": 1 - c}


def plane_peers():
    x, c, y = corner()
    peers = []
    for dx, dc, dy in OTHERS:
        px, pc, py = flip(x, dx), flip(c, dc), flip(y, dy)
        peers.append(({"x": px, "core": pc, "y": py}, slot(px, pc, py)))
    return peers


def greet(plane, line):
    barrier = pltpu.get_barrier_semaphore()
    near = {"near": neighbours(), "all": [p for p, _ in plane_peers()], None: []}[plane]
    for device in near:
        pl.semaphore_signal(barrier, inc=1, device_id=device, device_id_type=MESH_ID)
    if not line:
        pl.semaphore_wait(barrier, len(near))
        return
    z = lax.axis_index("z")

    @pl.when(z > 0)
    def _():
        pl.semaphore_signal(barrier, inc=1, device_id={"z": z - 1}, device_id_type=MESH_ID)

    @pl.when(z < PLANES - 1)
    def _():
        pl.semaphore_signal(barrier, inc=1, device_id={"z": z + 1}, device_id_type=MESH_ID)

    edge = (z == 0) | (z == PLANES - 1)

    @pl.when(edge)
    def _():
        pl.semaphore_wait(barrier, len(near) + 1)

    @pl.when(jnp.logical_not(edge))
    def _():
        pl.semaphore_wait(barrier, len(near) + 2)


class Part:
    def __init__(self, inputs, outs, scratch, steps, plane=None, line=False):
        self.begin, self.end = 0.0, 1.0
        self.inputs = inputs
        self.outs = outs
        self.scratch = scratch
        self.steps = steps
        self.plane, self.line = plane, line


def run_kernel(parts, *refs):
    refs = list(refs)

    def take(counts):
        groups = []
        for count in counts:
            groups.append(refs[:count])
            del refs[:count]
        return groups

    ins = take([len(p.inputs) for p in parts])
    outs = take([len(p.outs) for p in parts])
    scratch = take([len(p.scratch) for p in parts])
    ranks = [None, "near", "all"]
    plane = ranks[max(ranks.index(p.plane) for p in parts)]
    greet(plane, any(p.line for p in parts))
    plans = [p.steps(i, o, s) for p, i, o, s in zip(parts, ins, outs, scratch)]
    ordered = []
    for p, (first, middle, _) in zip(parts, plans):
        ordered.append((p.begin - 1.0 if p.begin == 0 else p.begin, first))
        for n, step in enumerate(middle):
            ordered.append((p.begin + (p.end - p.begin) * (n + 0.5) / len(middle), step))
    for _, step in sorted(ordered, key=lambda pair: pair[0]):
        step()
    for _, _, last in plans:
        last()


def expected(micros):
    return pl.CostEstimate(flops=0, bytes_accessed=int(micros * 3.5e6), transcendentals=0)


def run(parts, collective_id, vmem=None, micros=40):
    inputs = [pair for p in parts for pair in p.inputs]
    outs = [pair for p in parts for pair in p.outs]
    return pl.pallas_call(
        functools.partial(run_kernel, parts),
        out_shape=[shape for shape, _ in outs],
        in_specs=[spec for _, spec in inputs],
        out_specs=[spec for _, spec in outs],
        scratch_shapes=[s for p in parts for s in p.scratch],
        compiler_params=pltpu.CompilerParams(
            collective_id=collective_id,
            has_side_effects=True,
            vmem_limit_bytes=None if vmem is None else vmem << 20,
        ),
        cost_estimate=expected(micros),
    )(*[array for array, _ in inputs])


def between(part, begin, end):
    part.begin, part.end = begin, end
    return part


def gather_part(block):
    rows, columns = block.shape
    n, half = CHUNKS, CHUNKS // 2
    chunk = rows // n

    def steps(ins, outs, scratch):
        (in_ref,), (out_ref,) = ins, outs
        send_x, send_y, send_c, recv_x, recv_y, recv_c, local = scratch
        x, c, y = corner()
        dev_x, dev_y, dev_c = neighbours()

        def at(index, k):
            start = pl.multiple_of(index * rows + k * chunk, chunk)
            return out_ref.at[pl.ds(start, chunk), :]

        own, beside_x, beside_y = slot(x, c, y), slot(1 - x, c, y), slot(x, c, 1 - y)
        across = slot(1 - x, c, 1 - y)
        mirror = [
            slot(x, 1 - c, y),
            slot(1 - x, 1 - c, y),
            slot(x, 1 - c, 1 - y),
            slot(1 - x, 1 - c, 1 - y),
        ]
        start = pl.multiple_of(own * rows, rows)
        keep = pltpu.make_async_copy(in_ref, out_ref.at[pl.ds(start, rows), :], local)
        sent = []

        def go(copy):
            copy.start()
            sent.append(copy)

        def share(index, k, b):
            go(remote(at(index, k), at(index, k), send_c.at[b * n + k], recv_c.at[b * n + k], dev_c))

        order_x = list(range(n))
        order_y = order_x[half:] + order_x[:half]

        def first():
            keep.start()

            def mine(k):
                return in_ref.at[pl.ds(k * chunk, chunk), :]

            for k, j in zip(order_x, order_y):
                go(remote(mine(k), at(own, k), send_x.at[k], recv_x.at[k], dev_x))
                go(remote(mine(j), at(own, j), send_y.at[j], recv_y.at[j], dev_y))
            for k in range(n):
                go(remote(mine(k), at(own, k), send_c.at[k], recv_c.at[k], dev_c))

        def straight(k, j):
            landed(at(beside_x, k), recv_x.at[k], dev_x)
            if k < half:
                to = at(beside_x, k)
                go(remote(to, to, send_y.at[n + k], recv_y.at[n + k], dev_y))
            share(beside_x, k, 1)
            landed(at(beside_y, j), recv_y.at[j], dev_y)
            if j >= half:
                to = at(beside_y, j)
                go(remote(to, to, send_x.at[half + j], recv_x.at[half + j], dev_x))
            share(beside_y, j, 2)

        def diagonal(k):
            landed(at(across, k), recv_y.at[n + k], dev_y)
            share(across, k, 3)
            landed(at(across, half + k), recv_x.at[n + k], dev_x)
            share(across, half + k, 3)

        def last():
            for b in range(4):
                for k in range(n):
                    landed(at(mirror[b], k), recv_c.at[b * n + k], dev_c)
            for copy in sent:
                copy.wait_send()
            keep.wait()

        middle = [functools.partial(straight, k, j) for k, j in zip(order_x, order_y)]
        middle += [functools.partial(diagonal, k) for k in range(half)]
        return first, middle, last

    link = DMA((n + half,))
    core = DMA((4 * n,))
    return Part(
        [(block, VMEM)],
        [(jax.ShapeDtypeStruct((RANKS * rows, columns), block.dtype), ANYWHERE)],
        [link, link, core, link, link, core, DMA(())],
        steps,
        plane="near",
    )


def add_rows(target, start, count, sources, step=16):
    def body(i, carry):
        r = pl.multiple_of(start + i * step, step)
        total = None
        for ref, shift in sources:
            value = ref[pl.ds(r - shift if shift else r, step), :].astype(jnp.float32)
            total = value if total is None else total + value
        target[pl.ds(r, step), :] = total.astype(target.dtype)
        return carry

    lax.fori_loop(0, count // step, body, 0)


def scatter_part(terms=None, product=None, transposed=False, tile=512, more=None):
    if product is None:
        ranks, rows, columns = terms.shape
    else:
        left, right = product
        rows, columns = left.shape[0] // RANKS, right.shape[0 if transposed else 1]
    n, half = CHUNKS, CHUNKS // 2
    chunk = rows // n
    middle_row = half * chunk

    def steps(ins, outs, scratch):
        (out_ref,) = outs
        extra = [] if more is None else [(ins[-1], 0)]
        ins = ins if more is None else ins[:-1]
        if product is None:
            (part_ref,) = ins
        else:
            left_ref, right_ref = ins
            part_ref, scratch = scratch[-1], scratch[:-1]
        core_buf, x_buf, y_buf, x_diag, y_diag, d_sum, x_sum, y_sum = scratch[:8]
        send_c, recv_c, send_x, recv_x, send_y, recv_y = scratch[8:]
        x, c, y = corner()
        dev_x, dev_y, dev_c = neighbours()
        D, X, Y, O = range(4)
        place = [(1 - x, 1 - y), (1 - x, y), (x, 1 - y), (x, y)]
        mine = [slot(px, c, py) for px, py in place]
        theirs = [slot(px, 1 - c, py) for px, py in place]
        orders = {D: [], X: list(range(n)), O: list(range(n))}
        for k in range(half):
            orders[D] += [k, half + k]
        orders[Y] = orders[X][half:] + orders[X][:half]
        sent = []

        def go(copy):
            copy.start()
            sent.append(copy)

        def piece(k):
            return pl.ds(k * chunk, chunk)

        def make(index):
            def body(j, carry):
                at = pl.ds(pl.multiple_of(j * tile, tile), tile)
                some = left_ref[pl.ds(pl.multiple_of(index * rows, rows), rows), :]
                if transposed:
                    value = dot_rows(some, right_ref[at, :])
                else:
                    value = dot(some, right_ref[:, at])
                part_ref[index, :, at] = low(value)
                return carry

            lax.fori_loop(0, columns // tile, body, 0)

        def to_core(b):
            for k in orders[b]:
                source = part_ref.at[theirs[b], piece(k), :]
                i = b * n + k
                go(remote(source, core_buf.at[b, piece(k), :], send_c.at[i], recv_c.at[i], dev_c))

        def made_for_core(b):
            make(theirs[b])
            to_core(b)

        def first():
            if product is None:
                for b in (D, X, Y, O):
                    to_core(b)
            else:
                made_for_core(D)
                make(mine[D])

        def chip(target, b, k, *more):
            landed(core_buf.at[b, piece(k), :], recv_c.at[b * n + k], dev_c)
            sources = [(part_ref.at[mine[b]], 0), (core_buf.at[b], 0), *more]
            add_rows(target, k * chunk, chunk, sources)

        def to_x(k):
            go(remote(x_sum.at[piece(k), :], x_buf.at[piece(k), :], send_x.at[k], recv_x.at[k], dev_x))

        def to_y(k):
            go(remote(y_sum.at[piece(k), :], y_buf.at[piece(k), :], send_y.at[k], recv_y.at[k], dev_y))

        def diagonal(k):
            chip(d_sum, D, k)
            source = d_sum.at[piece(k), :]
            if k < half:
                go(remote(source, x_diag.at[piece(k), :], send_x.at[n + k], recv_x.at[n + k], dev_x))
            else:
                to = y_diag.at[piece(k - half), :]
                go(remote(source, to, send_y.at[half + k], recv_y.at[half + k], dev_y))

        def direct(k):
            chip(x_sum, X, k)
            to_x(k)
            chip(y_sum, Y, half + k)
            to_y(half + k)

        def relayed(k):
            landed(y_diag.at[piece(k), :], recv_y.at[n + k], dev_y)
            chip(x_sum, X, half + k, (y_diag, middle_row))
            to_x(half + k)
            landed(x_diag.at[piece(k), :], recv_x.at[n + k], dev_x)
            chip(y_sum, Y, k, (x_diag, 0))
            to_y(k)

        def own(k):
            landed(x_buf.at[piece(k), :], recv_x.at[k], dev_x)
            landed(y_buf.at[piece(k), :], recv_y.at[k], dev_y)
            chip(out_ref, O, k, (x_buf, 0), (y_buf, 0), *extra)

        def last():
            for copy in sent:
                copy.wait_send()

        def makes(b):
            if product is None:
                return []
            return [functools.partial(made_for_core, b), functools.partial(make, mine[b])]

        middle = [functools.partial(diagonal, k) for k in orders[D]]
        middle += makes(X) + makes(Y)
        middle += [functools.partial(direct, k) for k in range(half)]
        middle += makes(O)
        middle += [functools.partial(relayed, k) for k in range(half)]
        middle += [functools.partial(own, k) for k in range(n)]
        return first, middle, last

    def low_vmem(*shape):
        return pltpu.VMEM(shape, jnp.bfloat16)

    whole, part = low_vmem(rows, columns), low_vmem(rows // 2, columns)
    link = DMA((n + half,))
    core = DMA((4 * n,))
    made = [] if product is None else [low_vmem(RANKS, rows, columns)]
    return Part(
        ([(terms, VMEM)] if product is None else [(left, VMEM), (right, VMEM)])
        + ([] if more is None else [(more, VMEM)]),
        [(jax.ShapeDtypeStruct((rows, columns), jnp.float32 if more is None else jnp.bfloat16), VMEM)],
        [low_vmem(4, rows, columns), whole, whole, part, part, whole, whole, whole]
        + [core, core, link, link, link, link]
        + made,
        steps,
        plane="near",
    )


def swap_part(blocks):
    def steps(ins, outs, scratch):
        (in_ref,), (out_ref,) = ins, outs
        send, recv, local = scratch
        own = slot(*corner())
        keep = pltpu.make_async_copy(in_ref.at[own], out_ref.at[own], local)
        peers = plane_peers()
        sent = []

        def first():
            keep.start()
            for i, (there, other) in enumerate(peers):
                copy = remote(in_ref.at[other], out_ref.at[own], send.at[i], recv.at[i], there)
                copy.start()
                sent.append(copy)

        def last():
            for i, (there, other) in enumerate(peers):
                landed(out_ref.at[other], recv.at[i], there)
            for copy in sent:
                copy.wait_send()
            keep.wait()

        return first, [], last

    n = len(OTHERS)
    return Part(
        [(blocks, VMEM)],
        [(jax.ShapeDtypeStruct(blocks.shape, blocks.dtype), ANYWHERE)],
        [DMA((n,)), DMA((n,)), DMA(())],
        steps,
        plane="all",
    )


def halves_part(term, owners):
    rows = term.shape[0] // owners
    half = owners // CORNERS

    def steps(ins, outs, scratch):
        (in_ref,), (out_ref,) = ins, outs
        send, recv, local = scratch
        y = lax.axis_index("y")
        dev_y = neighbours()[1]

        def rows_of(i, side):
            return in_ref.at[pl.ds(pl.multiple_of((i * CORNERS + side) * rows, rows), rows), :]

        def keep(i):
            return pltpu.make_async_copy(rows_of(i, y), out_ref.at[y * half + i], local.at[i])

        def give(i):
            return remote(rows_of(i, 1 - y), out_ref.at[y * half + i], send.at[i], recv.at[i], dev_y)

        def first():
            for i in range(half):
                keep(i).start()
                give(i).start()

        def last():
            for i in range(half):
                landed(out_ref.at[(1 - y) * half + i], recv.at[i], dev_y)
                give(i).wait_send()
                keep(i).wait()

        return first, [], last

    return Part(
        [(term, VMEM)],
        [(jax.ShapeDtypeStruct((owners, rows, term.shape[1]), term.dtype), VMEM)],
        [DMA((half,)), DMA((half,)), DMA((half,))],
        steps,
        plane="near",
    )


def line_gather_part(block, pieces=4):
    rows = block.shape[0] // pieces

    def steps(ins, outs, scratch):
        (in_ref,), (out_ref,) = ins, outs
        up_send, up_recv, down_send, down_recv, local = scratch
        z = lax.axis_index("z")
        keep = pltpu.make_async_copy(in_ref, out_ref.at[z], local)

        def at(block, k):
            return out_ref.at[block, pl.ds(k * rows, rows), :]

        def up(t, k, source=None):
            s = at(z - t, k) if source is None else source
            i = t * pieces + k
            return remote(s, at(z - t, k), up_send.at[i], up_recv.at[i], {"z": z + 1})

        def down(t, k, source=None):
            s = at(z + t, k) if source is None else source
            i = t * pieces + k
            return remote(s, at(z + t, k), down_send.at[i], down_recv.at[i], {"z": z - 1})

        def first():
            keep.start()
            for k in range(pieces):
                mine = in_ref.at[pl.ds(k * rows, rows), :]

                @pl.when(z < PLANES - 1)
                def _():
                    up(0, k, mine).start()

                @pl.when(z > 0)
                def _():
                    down(0, k, mine).start()

        def arrive(t, k):
            i = t * pieces + k
            on = t + 1 < PLANES - 1

            @pl.when(z - 1 - t >= 0)
            def _():
                landed(at(z - 1 - t, k), up_recv.at[i], {"z": z - 1})
                if on:

                    @pl.when(z < PLANES - 1)
                    def _():
                        up(t + 1, k).start()

            @pl.when(z + 1 + t < PLANES)
            def _():
                landed(at(z + 1 + t, k), down_recv.at[i], {"z": z + 1})
                if on:

                    @pl.when(z > 0)
                    def _():
                        down(t + 1, k).start()

        def last():
            for t in range(PLANES - 1):
                for k in range(pieces):

                    @pl.when((z < PLANES - 1) & (z - t >= 0))
                    def _():
                        up(t, k).wait_send()

                    @pl.when((z > 0) & (z + t < PLANES))
                    def _():
                        down(t, k).wait_send()

            keep.wait()

        middle = [
            functools.partial(arrive, t, k) for t in range(PLANES - 1) for k in range(pieces)
        ]
        return first, middle, last

    sems = DMA(((PLANES - 1) * pieces,))
    return Part(
        [(block, VMEM)],
        [(jax.ShapeDtypeStruct((PLANES,) + block.shape, block.dtype), ANYWHERE)],
        [sems, sems, sems, sems, DMA(())],
        steps,
        line=True,
    )


def line_scatter_part(terms, pieces=4, kind=jnp.float32):
    line, all_rows, columns = terms.shape
    rows = all_rows // pieces
    step = 32

    def steps(ins, outs, scratch):
        (in_ref,), (out_ref,) = ins, outs
        up_buf, down_buf, up_stage, down_stage, up_send, up_recv, down_send, down_recv = scratch
        z = lax.axis_index("z")
        f32 = jnp.float32

        def cut(k):
            return pl.ds(k * rows, rows)

        def send_up(source, d, k):
            i = (d - 1) * pieces + k
            return remote(source, up_buf.at[d - 1, cut(k), :], up_send.at[i], up_recv.at[i], {"z": z + 1})

        def send_down(source, d, k):
            i = (d - 1) * pieces + k
            to = down_buf.at[d - 1, cut(k), :]
            return remote(source, to, down_send.at[i], down_recv.at[i], {"z": z - 1})

        def first():
            for d in range(line - 1, 0, -1):
                for k in range(pieces):

                    @pl.when(z == 0)
                    def _():
                        send_up(in_ref.at[d, cut(k), :], d, k).start()

                    @pl.when(z == line - 1)
                    def _():
                        send_down(in_ref.at[line - 1 - d, cut(k), :], d, k).start()

        def pass_on(d, k):
            @pl.when(z + d < line)
            def _():
                if d + 1 < line:

                    @pl.when(z > 0)
                    def _():
                        landed(up_buf.at[d, cut(k), :], up_recv.at[d * pieces + k], {"z": z - 1})
                        sources = [(in_ref.at[z + d], 0), (up_buf.at[d], 0)]
                        add_rows(up_stage.at[d - 1], k * rows, rows, sources, step)
                        send_up(up_stage.at[d - 1, cut(k), :], d, k).start()

            @pl.when(z - d >= 0)
            def _():
                if d + 1 < line:

                    @pl.when(z < line - 1)
                    def _():
                        landed(down_buf.at[d, cut(k), :], down_recv.at[d * pieces + k], {"z": z + 1})
                        sources = [(in_ref.at[z - d], 0), (down_buf.at[d], 0)]
                        add_rows(down_stage.at[d - 1], k * rows, rows, sources, step)
                        send_down(down_stage.at[d - 1, cut(k), :], d, k).start()

        def own(k):
            @pl.when(z > 0)
            def _():
                landed(up_buf.at[0, cut(k), :], up_recv.at[k], {"z": z - 1})

            @pl.when(z < line - 1)
            def _():
                landed(down_buf.at[0, cut(k), :], down_recv.at[k], {"z": z + 1})

            mine, below, above = (in_ref.at[z], 0), (up_buf.at[0], 0), (down_buf.at[0], 0)

            @pl.when(z == 0)
            def _():
                add_rows(out_ref, k * rows, rows, [mine, above], step)

            @pl.when(z == line - 1)
            def _():
                add_rows(out_ref, k * rows, rows, [mine, below], step)

            @pl.when((z > 0) & (z < line - 1))
            def _():
                add_rows(out_ref, k * rows, rows, [mine, below, above], step)

        def last():
            for d in range(line - 1, 0, -1):
                for k in range(pieces):

                    @pl.when(z + d < line)
                    def _():
                        send_up(up_stage.at[d - 1, cut(k), :], d, k).wait_send()

                    @pl.when(z - d >= 0)
                    def _():
                        send_down(down_stage.at[d - 1, cut(k), :], d, k).wait_send()

        middle = [
            functools.partial(pass_on, d, k) for d in range(line - 2, 0, -1) for k in range(pieces)
        ]
        middle += [functools.partial(own, k) for k in range(pieces)]
        return first, middle, last

    sems = DMA(((line - 1) * pieces,))
    buffer = pltpu.VMEM((line - 1, all_rows, columns), jnp.bfloat16)
    return Part(
        [(terms, VMEM)],
        [(jax.ShapeDtypeStruct((all_rows, columns), kind), VMEM)],
        [buffer, buffer, buffer, buffer, sems, sems, sems, sems],
        steps,
        line=True,
    )


def columns_part(weights):
    rows = weights[0].shape[0]
    widths = [w.shape[1] // RANKS for w in weights]
    ends = [sum(widths[: n + 1]) for n in range(len(widths))]
    many = len(weights)

    def steps(ins, outs, scratch):
        (out_ref,) = outs
        send, recv, up_send, up_recv, down_send, down_recv, local = scratch
        x, c, y = corner()
        z = lax.axis_index("z")
        own = slot(x, c, y)
        peers = plane_peers()
        spots = [(x * CORNERS + c, y)]
        spots += [(flip(x, dx) * CORNERS + flip(c, dc), flip(y, dy)) for dx, dc, dy in OTHERS]

        def at(i, plane):
            return out_ref.at[spots[i][0], plane, spots[i][1]]

        def cut(n, index):
            return ins[n].at[:, pl.ds(pl.multiple_of(index * widths[n], widths[n]), widths[n])]

        def place(i, n):
            return at(i, z).at[:, pl.ds(ends[n] - widths[n], widths[n])]

        keeps = [pltpu.make_async_copy(cut(n, own), place(0, n), local.at[n]) for n in range(many)]
        sent = []

        def up(t, i, source=None):
            s = at(i, z - t) if source is None else source
            n = t * RANKS + i
            return remote(s, at(i, z - t), up_send.at[n], up_recv.at[n], {"z": z + 1})

        def down(t, i, source=None):
            s = at(i, z + t) if source is None else source
            n = t * RANKS + i
            return remote(s, at(i, z + t), down_send.at[n], down_recv.at[n], {"z": z - 1})

        def begin(i, source=None):
            @pl.when(z < PLANES - 1)
            def _():
                up(0, i, source).start()

            @pl.when(z > 0)
            def _():
                down(0, i, source).start()

        def first():
            for keep in keeps:
                keep.start()
            for i, (there, other) in enumerate(peers):
                for n in range(many):
                    m = i * many + n
                    copy = remote(cut(n, other), place(0, n), send.at[m], recv.at[m], there)
                    copy.start()
                    sent.append(copy)
            for keep in keeps:
                keep.wait()
            begin(0)

        def swapped(i):
            for n in range(many):
                landed(place(i, n), recv.at[(i - 1) * many + n], peers[i - 1][0])
            begin(i)

        def arrive(t, i):
            n = t * RANKS + i
            on = t + 1 < PLANES - 1

            @pl.when(z - 1 - t >= 0)
            def _():
                landed(at(i, z - 1 - t), up_recv.at[n], {"z": z - 1})
                if on:

                    @pl.when(z < PLANES - 1)
                    def _():
                        up(t + 1, i).start()

            @pl.when(z + 1 + t < PLANES)
            def _():
                landed(at(i, z + 1 + t), down_recv.at[n], {"z": z + 1})
                if on:

                    @pl.when(z > 0)
                    def _():
                        down(t + 1, i).start()

        def last():
            for copy in sent:
                copy.wait_send()
            for t in range(PLANES - 1):
                for i in range(RANKS):

                    @pl.when((z < PLANES - 1) & (z - t >= 0))
                    def _():
                        up(t, i).wait_send()

                    @pl.when((z > 0) & (z + t < PLANES))
                    def _():
                        down(t, i).wait_send()

        middle = [functools.partial(swapped, i) for i in range(1, RANKS)]
        middle += [
            functools.partial(arrive, t, i) for t in range(PLANES - 1) for i in range(RANKS)
        ]
        return first, middle, last

    n = len(OTHERS) * many
    sems = DMA(((PLANES - 1) * RANKS,))
    shape = (CORNERS**2, PLANES, CORNERS, rows, ends[-1])
    return Part(
        [(w, VMEM) for w in weights],
        [(jax.ShapeDtypeStruct(shape, weights[0].dtype), ANYWHERE)],
        [DMA((n,)), DMA((n,)), sems, sems, sems, sems, DMA((many,))],
        steps,
        plane="all",
        line=True,
    )


def tiles_part(tile):
    def steps(ins, outs, scratch):
        (in_ref,), (out_ref,) = ins, outs
        send, recv, up_send, up_recv, down_send, down_recv, local = scratch
        z = lax.axis_index("z")
        own = slot(*corner())
        peers = plane_peers()
        keep = pltpu.make_async_copy(in_ref, out_ref.at[z, own], local)

        def give(i):
            return remote(in_ref, out_ref.at[z, own], send.at[i], recv.at[i], peers[i][0])

        def up(t):
            to = out_ref.at[z - t]
            return remote(to, to, up_send.at[t], up_recv.at[t], {"z": z + 1})

        def down(t):
            to = out_ref.at[z + t]
            return remote(to, to, down_send.at[t], down_recv.at[t], {"z": z - 1})

        def first():
            keep.start()
            for i in range(len(peers)):
                give(i).start()

        def swapped():
            for i, (there, other) in enumerate(peers):
                landed(out_ref.at[z, other], recv.at[i], there)
            keep.wait()

            @pl.when(z < PLANES - 1)
            def _():
                up(0).start()

            @pl.when(z > 0)
            def _():
                down(0).start()

        def arrive(t):
            on = t + 1 < PLANES - 1

            @pl.when(z - 1 - t >= 0)
            def _():
                landed(out_ref.at[z - 1 - t], up_recv.at[t], {"z": z - 1})
                if on:

                    @pl.when(z < PLANES - 1)
                    def _():
                        up(t + 1).start()

            @pl.when(z + 1 + t < PLANES)
            def _():
                landed(out_ref.at[z + 1 + t], down_recv.at[t], {"z": z + 1})
                if on:

                    @pl.when(z > 0)
                    def _():
                        down(t + 1).start()

        def last():
            for i in range(len(peers)):
                give(i).wait_send()
            for t in range(PLANES - 1):

                @pl.when((z < PLANES - 1) & (z - t >= 0))
                def _():
                    up(t).wait_send()

                @pl.when((z > 0) & (z + t < PLANES))
                def _():
                    down(t).wait_send()

        middle = [swapped] + [functools.partial(arrive, t) for t in range(PLANES - 1)]
        return first, middle, last

    n = len(OTHERS)
    line = DMA((PLANES - 1,))
    return Part(
        [(tile, VMEM)],
        [(jax.ShapeDtypeStruct((PLANES, RANKS) + tile.shape, tile.dtype), VMEM)],
        [DMA((n,)), DMA((n,)), line, line, line, line, DMA(())],
        steps,
        plane="all",
        line=True,
    )


def marks_part(marks):
    def steps(ins, outs, scratch):
        (in_ref,), (out_ref,) = ins, outs
        send, recv, local = scratch
        x, c, _ = corner()
        keep = pltpu.make_async_copy(in_ref, out_ref.at[x * CORNERS + c], local)
        near = []
        for i, (dx, dc) in enumerate([(0, 1), (1, 0), (1, 1)]):
            px, pc = flip(x, dx), flip(c, dc)
            near.append((i, {"x": px, "core": pc}, px * CORNERS + pc))

        def give(i, there):
            return remote(in_ref, out_ref.at[x * CORNERS + c], send.at[i], recv.at[i], there)

        def first():
            keep.start()
            for i, there, _ in near:
                give(i, there).start()

        def last():
            for i, there, theirs in near:
                landed(out_ref.at[theirs], recv.at[i], there)
                give(i, there).wait_send()
            keep.wait()

        return first, [], last

    return Part(
        [(marks, VMEM)],
        [(jax.ShapeDtypeStruct((CORNERS**2,) + marks.shape, marks.dtype), VMEM)],
        [DMA((3,)), DMA((3,)), DMA(())],
        steps,
        plane="all",
    )


def root_mean_scale(values, gains):
    return values * lax.rsqrt(jnp.mean(values * values, axis=-1, keepdims=True) + 1e-06) * gains


def rope_tables(positions):
    half = HEAD_SIZE // 2
    steps_half = jnp.arange(half).astype(jnp.float32)
    inverse = jnp.power(1000000.0, steps_half * (-2.0 / HEAD_SIZE))
    angles = positions.astype(jnp.float32)[:, None] * inverse[None, :]
    cosine, sine = jnp.cos(angles), jnp.sin(angles)
    return jnp.concatenate([cosine, cosine], axis=-1), jnp.concatenate([-sine, sine], axis=-1)


def matrix_product(left, right):
    return jnp.dot(left, right, preferred_element_type=jnp.float32)


def contract_last(left, right):
    return lax.dot_general(
        left, right, (((1,), (1,)), ((), ())), preferred_element_type=jnp.float32
    )


def contract_first(left, right):
    return lax.dot_general(
        left, right, (((0,), (0,)), ((), ())), preferred_element_type=jnp.float32
    )


def low(values):
    return values.astype(jnp.bfloat16)

def turn(values, cosine, sine):
    return values * cosine + pltpu.roll(values, HEAD_SIZE // 2, 1) * sine


def turn_back(grads, cosine, sine):
    return grads * cosine + pltpu.roll(grads * sine, HEAD_SIZE // 2, 1)


def unit_scale(values):
    return lax.rsqrt(jnp.mean(values * values, axis=-1, keepdims=True) + 1e-06)


def norm_back(raw, gain, grads):
    scale = unit_scale(raw)
    unit = raw * scale
    inner = grads * gain
    d_raw = scale * (inner - unit * jnp.mean(inner * unit, axis=-1, keepdims=True))
    return d_raw, grads * unit


def head(index):
    return slice(index * HEAD_SIZE, (index + 1) * HEAD_SIZE)


def dot(left, right):
    return jnp.dot(left, right, preferred_element_type=jnp.float32)


def dot_rows(left, right):
    return lax.dot_general(
        left, right, (((1,), (1,)), ((), ())), preferred_element_type=jnp.float32
    )


def prepare_kernel(
    x_ref, gain_ref, w_ref, cos_ref, sin_ref, qg_ref, kg_ref, x_out, q_ref, kv_ref, raw_ref, gate_ref
):
    hidden = x_ref[...].astype(jnp.float32)
    x_out[...] = low(hidden * unit_scale(hidden) * gain_ref[...])
    raw = dot(x_out[...], w_ref[...])
    cosine, sine = cos_ref[...], sin_ref[...]

    def prepare(values, gain):
        return low(turn(values * unit_scale(values) * gain, cosine, sine))

    for h in range(REPEAT):
        q_ref[:, head(h)] = prepare(raw[:, head(h)], qg_ref[...])
    kv_ref[:, head(0)] = prepare(raw[:, head(REPEAT)], kg_ref[...])
    kv_ref[:, head(1)] = low(raw[:, head(REPEAT + 1)])
    raw_ref[...] = raw[:, : (REPEAT + 1) * HEAD_SIZE]
    gate_ref[...] = raw[:, (REPEAT + 2) * HEAD_SIZE :]


def table_specs(rows):
    return [
        pl.BlockSpec((rows, HEAD_SIZE), lambda i: (i, 0)),
        pl.BlockSpec((rows, HEAD_SIZE), lambda i: (i, 1)),
    ]


def rows_spec(rows, columns):
    return pl.BlockSpec((rows, columns), lambda i: (i, 0))


def fixed_spec(*shape):
    return pl.BlockSpec(shape, lambda i: (0,) * len(shape))


def kernel_params(vmem):
    return pltpu.CompilerParams(vmem_limit_bytes=vmem << 20)


def prepare_attention(hidden, gain_attn, w_attn, table, gain_query, gain_key):
    tokens, width = hidden.shape
    columns = w_attn.shape[1]
    q_columns = REPEAT * HEAD_SIZE
    rows = tokens // RANKS
    shape = jax.ShapeDtypeStruct
    return pl.pallas_call(
        prepare_kernel,
        grid=(RANKS,),
        out_shape=[
            shape((tokens, width), jnp.bfloat16),
            shape((tokens, q_columns), jnp.bfloat16),
            shape((tokens, 2 * HEAD_SIZE), jnp.bfloat16),
            shape((tokens, q_columns + HEAD_SIZE), jnp.float32),
            shape((tokens, q_columns), jnp.float32),
        ],
        in_specs=[
            rows_spec(rows, width),
            fixed_spec(1, width),
            fixed_spec(width, columns),
            *table_specs(rows),
            fixed_spec(1, HEAD_SIZE),
            fixed_spec(1, HEAD_SIZE),
        ],
        out_specs=[
            rows_spec(rows, width),
            rows_spec(rows, q_columns),
            rows_spec(rows, 2 * HEAD_SIZE),
            rows_spec(rows, q_columns + HEAD_SIZE),
            rows_spec(rows, q_columns),
        ],
        compiler_params=kernel_params(60),
        cost_estimate=expected(12),
    )(hidden, gain_attn[None], w_attn, table, table, gain_query[None], gain_key[None])


EXPONENT = math.log2(math.e) / math.sqrt(HEAD_SIZE)


def allowed_keys(own_ref, keys_ref, z, window):
    seq, pos = own_ref[0, :, 0:1], own_ref[0, :, 1:2]
    key_seq = keys_ref[0, 0:1, z * window : (z + 1) * window]
    key_pos = keys_ref[0, 1:2, z * window : (z + 1) * window]
    return (key_pos <= pos) & ((key_seq == 0) | (key_seq == seq))


def attend_kernel(q_ref, kv_ref, gate_ref, own_ref, keys_ref, wo_ref, terms_ref, att_ref, log_ref, gated_ref):
    planes, window = kv_ref.shape[0], kv_ref.shape[1]
    totals = [None] * REPEAT
    ones = jnp.ones((window, HEAD_SIZE), jnp.bfloat16)
    for z in range(planes):
        allowed = allowed_keys(own_ref, keys_ref, z, window)
        keys = kv_ref[z, :, head(0)]
        values = jnp.concatenate([kv_ref[z, :, head(1)], ones], axis=1)
        for h in range(REPEAT):
            scores = dot_rows(q_ref[:, head(h)], keys) * EXPONENT
            exponent = low(jnp.where(allowed, jnp.exp2(scores), 0.0))
            part = dot(exponent, values)
            totals[h] = part if totals[h] is None else totals[h] + part
    for h in range(REPEAT):
        weight = totals[h][:, head(1)]
        attended = totals[h][:, head(0)] / weight
        att_ref[:, head(h)] = attended
        log_ref[:, head(h)] = jnp.log2(weight)
        gated_ref[:, head(h)] = low(attended * jax.nn.sigmoid(gate_ref[:, head(h)]))
    terms_ref[...] = low(dot(gated_ref[...], wo_ref[...]))


def group_specs(window):
    return [
        pl.BlockSpec((PLANES, window, 2 * HEAD_SIZE), lambda i: (0, i, 0)),
        pl.BlockSpec((1, window, 2), lambda i: (i, 0, 0)),
        pl.BlockSpec((1, 2, PLANES * window), lambda i: (i, 0, 0)),
    ]


def attend(query, pair, gate, own, keys, w_out):
    tokens, q_columns = query.shape
    groups = own.shape[0]
    window = tokens // groups
    width = w_out.shape[1]
    kv, mine, marks = group_specs(window)
    shape = jax.ShapeDtypeStruct
    columns = rows_spec(window, q_columns)
    return pl.pallas_call(
        attend_kernel,
        grid=(groups,),
        out_shape=[
            shape((tokens, width), jnp.bfloat16),
            shape((tokens, q_columns), jnp.float32),
            shape((tokens, q_columns), jnp.float32),
            shape((tokens, q_columns), jnp.bfloat16),
        ],
        in_specs=[columns, kv, columns, mine, marks, fixed_spec(q_columns, width)],
        out_specs=[rows_spec(window, width), columns, columns, columns],
        compiler_params=kernel_params(48),
        cost_estimate=expected(18),
    )(query, pair, gate, own, keys, w_out)


def attend_back_kernel(
    branch_ref, wo_ref, q_ref, kv_ref, gate_ref, own_ref, keys_ref, att_ref, log_ref, raw_ref,
    cos_ref, sin_ref, qg_ref, gated_ref, out_ref, dkv_ref, gain_ref, term_ref, term_sum,
):
    planes, window = kv_ref.shape[0], kv_ref.shape[1]
    scale = 1.0 / math.sqrt(HEAD_SIZE)
    turned = jnp.transpose(gated_ref[...])

    @pl.when(pl.program_id(0) == 0)
    def _():
        term_sum[...] = dot(turned, branch_ref[...])

    @pl.when(pl.program_id(0) > 0)
    def _():
        term_sum[...] += dot(turned, branch_ref[...])

    @pl.when(pl.program_id(0) == pl.num_programs(0) - 1)
    def _():
        term_ref[...] = low(term_sum[...])

    d_gated = dot_rows(branch_ref[...], wo_ref[...])
    gate = jax.nn.sigmoid(gate_ref[...])
    attended = att_ref[...]
    d_attended = low(d_gated * gate)
    out_ref[:, (REPEAT + 2) * HEAD_SIZE :] = low(d_gated * attended * gate * (1.0 - gate))
    product = d_attended.astype(jnp.float32) * attended
    delta = [jnp.sum(product[:, head(h)], axis=-1, keepdims=True) for h in range(REPEAT)]
    turned_q = [jnp.transpose(q_ref[:, head(h)]) for h in range(REPEAT)]
    turned_d = [jnp.transpose(d_attended[:, head(h)]) for h in range(REPEAT)]
    d_query = [None] * REPEAT
    for z in range(planes):
        allowed = allowed_keys(own_ref, keys_ref, z, window)
        keys, values = kv_ref[z, :, head(0)], kv_ref[z, :, head(1)]
        d_keys, d_values = None, None
        for h in range(REPEAT):
            scores = dot_rows(q_ref[:, head(h)], keys) * EXPONENT - log_ref[:, h * HEAD_SIZE : h * HEAD_SIZE + 1]
            probs = jnp.where(allowed, jnp.exp2(scores), 0.0)
            d_probs = dot_rows(d_attended[:, head(h)], values)
            d_scores = low(probs * (d_probs - delta[h]))
            part = dot(d_scores, keys)
            d_query[h] = part if d_query[h] is None else d_query[h] + part
            part = dot(turned_q[h], d_scores)
            d_keys = part if d_keys is None else d_keys + part
            part = dot(turned_d[h], low(probs))
            d_values = part if d_values is None else d_values + part
        dkv_ref[z, :, head(0)] = low(jnp.transpose(d_keys * scale))
        dkv_ref[z, :, head(1)] = low(jnp.transpose(d_values))
    cosine, sine = cos_ref[...], sin_ref[...]
    total = jnp.zeros((1, HEAD_SIZE), jnp.float32)
    for h in range(REPEAT):
        grads = turn_back(d_query[h] * scale, cosine, sine)
        d_raw, by_row = norm_back(raw_ref[:, head(h)], qg_ref[...], grads)
        out_ref[:, head(h)] = low(d_raw)
        total += jnp.sum(by_row, axis=0, keepdims=True)
    gain_ref[0] = jnp.broadcast_to(total, gain_ref.shape[1:])


def attend_back(
    branch, w_out, query, pair, gate, own, keys, attended, log, raw, table, gain, gated
):
    tokens, q_columns = query.shape
    groups = own.shape[0]
    window = tokens // groups
    width = w_out.shape[1]
    kv, mine, marks = group_specs(window)
    shape = jax.ShapeDtypeStruct
    columns = rows_spec(window, q_columns)
    return pl.pallas_call(
        attend_back_kernel,
        grid=(groups,),
        out_shape=[
            shape((tokens, 2 * q_columns + 2 * HEAD_SIZE), jnp.bfloat16),
            shape(pair.shape, jnp.bfloat16),
            shape((groups, 8, HEAD_SIZE), jnp.float32),
            shape((q_columns, width), jnp.bfloat16),
        ],
        in_specs=[
            rows_spec(window, width), fixed_spec(q_columns, width), columns, kv, columns, mine, marks,
            columns, columns, rows_spec(window, raw.shape[1]), *table_specs(window), fixed_spec(1, HEAD_SIZE), columns,
        ],
        out_specs=[
            rows_spec(window, 2 * q_columns + 2 * HEAD_SIZE), kv, pl.BlockSpec((1, 8, HEAD_SIZE), lambda i: (i, 0, 0)),
            fixed_spec(q_columns, width),
        ],
        scratch_shapes=[pltpu.VMEM((q_columns, width), jnp.float32)],
        compiler_params=kernel_params(56),
        cost_estimate=expected(35),
    )(branch, w_out, query, pair, gate, own, keys, attended, log, raw, table, table, gain[None], gated)


def finish_kernel(dkv_ref, raw_ref, cos_ref, sin_ref, kg_ref, partial_ref, out_ref, gain_ref):
    grads = turn_back(dkv_ref[:, head(0)], cos_ref[...], sin_ref[...])
    d_raw, by_row = norm_back(raw_ref[...], kg_ref[...], grads)
    out_ref[:, head(0)] = low(d_raw)
    out_ref[:, head(1)] = low(dkv_ref[:, head(1)])
    gain_ref[0] = jnp.broadcast_to(jnp.sum(by_row, axis=0, keepdims=True), gain_ref.shape[1:])


def finish_attention(d_pair, raw, table, gain, partial, steps=4):
    tokens = d_pair.shape[0]
    rows = tokens // steps
    shape = jax.ShapeDtypeStruct
    return pl.pallas_call(
        finish_kernel,
        grid=(steps,),
        out_shape=[shape(partial.shape, partial.dtype), shape((steps, 8, HEAD_SIZE), jnp.float32)],
        in_specs=[
            rows_spec(rows, 2 * HEAD_SIZE),
            pl.BlockSpec((rows, HEAD_SIZE), lambda i: (i, REPEAT)),
            *table_specs(rows),
            fixed_spec(1, HEAD_SIZE),
            ANYWHERE,
        ],
        out_specs=[
            pl.BlockSpec((rows, 2 * HEAD_SIZE), lambda i: (i, REPEAT // 2)),
            pl.BlockSpec((1, 8, HEAD_SIZE), lambda i: (i, 0, 0)),
        ],
        input_output_aliases={5: 0},
        compiler_params=kernel_params(60),
        cost_estimate=expected(4),
    )(d_pair, raw, table, table, gain[None], partial)


def split_part(gate, up, pieces):
    rows, every = gate.shape
    units = every // RANKS
    piece = units // pieces

    def steps(ins, outs, scratch):
        (out_ref,) = outs

        def some(corner_at):
            for y in range(CORNERS):
                for at, ref in ((0, ins[0]), (units, ins[1])):
                    starts = [((corner_at * pieces + d) * CORNERS + y) * piece for d in range(pieces)]
                    parts = [ref[:, start : start + piece] for start in starts]
                    out_ref[corner_at * CORNERS + y, :, at : at + units] = jnp.concatenate(parts, axis=1)

        return (lambda: None), [functools.partial(some, i) for i in range(CORNERS**2)], (lambda: None)

    return Part(
        [(gate, VMEM), (up, VMEM)],
        [(jax.ShapeDtypeStruct((RANKS, rows, 2 * units), gate.dtype), VMEM)],
        [],
        steps,
    )


def join_part(blocks, pieces):
    ranks, rows, width = blocks.shape
    units = width // 2
    piece = units // pieces

    def steps(ins, outs, scratch):
        (in_ref,) = ins

        def some(corner_at):
            for at, ref in ((0, outs[0]), (units, outs[1])):
                parts = []
                for d in range(pieces):
                    for y in range(CORNERS):
                        here = slice(at + d * piece, at + (d + 1) * piece)
                        parts.append(in_ref[corner_at * CORNERS + y, :, here])
                wide = CORNERS * units
                ref[:, corner_at * wide : (corner_at + 1) * wide] = jnp.concatenate(parts, axis=1)

        return (lambda: None), [functools.partial(some, i) for i in range(CORNERS**2)], (lambda: None)

    out = (jax.ShapeDtypeStruct((rows, ranks * units), blocks.dtype), VMEM)
    return Part([(blocks, VMEM)], [out, out], [], steps)


def norm_rows_kernel(x_ref, gain_ref, grads_ref, more_ref, out_ref, term_ref):
    values = x_ref[...].astype(jnp.float32)
    d_values, by_row = norm_back(values, gain_ref[...], grads_ref[...])
    out_ref[...] = more_ref[...].astype(jnp.float32) + d_values

    @pl.when(pl.program_id(0) == 0)
    def _():
        term_ref[...] = jnp.zeros_like(term_ref)

    term_ref[...] += jnp.sum(by_row.reshape(-1, *term_ref.shape), axis=0)


def norm_rows_back(values, gain, grads, more, steps=4):
    rows, width = values.shape
    some = rows_spec(rows // steps, width)
    d_values, term = pl.pallas_call(
        norm_rows_kernel,
        grid=(steps,),
        out_shape=[jax.ShapeDtypeStruct(values.shape, jnp.float32), jax.ShapeDtypeStruct((8, width), jnp.float32)],
        in_specs=[some, fixed_spec(1, width), some, some],
        out_specs=[some, fixed_spec(8, width)],
        compiler_params=kernel_params(60),
        cost_estimate=expected(3),
    )(values, gain[None], grads, more)
    return d_values, jnp.sum(term, axis=0)


def widen_kernel(count, in_ref, small_ref, *refs):
    weights, refs = refs[:count], refs[count:]
    others = (len(refs) - count - 2) // 2
    low_refs, refs = refs[:others], refs[others:]
    out_refs, along_ref, total_ref, wide_refs = refs[:count], refs[count], refs[count + 1], refs[count + 2 :]
    along = jnp.zeros(along_ref.shape, jnp.float32)
    for rank in range(RANKS):
        start = 0
        for weight_ref, ref in zip(weights, out_refs):
            width = ref.shape[1] // RANKS
            place = slice(rank * width, (rank + 1) * width)
            value = in_ref[rank, :, start : start + width].astype(jnp.float32)
            ref[:, place] = value
            product = value * weight_ref[:, place].astype(jnp.float32)
            along += sum(product[:, head(h)] for h in range(width // HEAD_SIZE))
            start += width
    along_ref[...] = jnp.broadcast_to(jnp.sum(along, axis=1, keepdims=True), along_ref.shape)
    total_ref[...] = jnp.sum(small_ref[...], axis=0)
    for ref, wide in zip(low_refs, wide_refs):
        wide[...] = ref[...].astype(wide.dtype)


def widen_columns(parts, small, widths, weights, others):
    ranks, rows, columns = parts.shape
    shape = jax.ShapeDtypeStruct
    out_shape = [shape((rows, ranks * w), jnp.float32) for w in widths]
    out_shape += [shape((rows, HEAD_SIZE), jnp.float32), shape(small.shape[1:], jnp.float32)]
    out_shape += [shape(o.shape, kind) for o, kind in others]
    return pl.pallas_call(
        functools.partial(widen_kernel, len(widths)),
        out_shape=out_shape,
        in_specs=[VMEM] * (2 + len(weights) + len(others)),
        out_specs=[VMEM] * len(out_shape),
        compiler_params=kernel_params(32),
        cost_estimate=expected(4),
    )(parts, small, *weights, *[o for o, _ in others])


def make_shards(cells):
    data_total = cells * PLANES

    def blocks(terms):
        return low(terms).reshape(RANKS, -1, terms.shape[1])

    def gather_tokens(rows):
        return run([gather_part(rows)], 0)[0]

    def scatter_tokens(terms):
        return run([scatter_part(blocks(terms))], 1, 40)[0]

    def join_cells(rows):
        if cells > 1:
            rows = lax.all_gather(rows, "cell", axis=0, tiled=False)
            rows = jnp.transpose(rows, (1, 0, 2, 3, 4, 5))
        return rows.reshape(-1, rows.shape[-1])

    def gather_columns(mine):
        rows, columns = mine.shape[1:]
        every = lax.all_gather(mine, DATA, axis=0, tiled=False)
        every = every.reshape(data_total, CORNERS**2, CORNERS, rows, columns)
        return jnp.transpose(every, (1, 0, 2, 3, 4)).reshape(-1, columns)

    def sum_columns(term):
        rows = term.shape[0] // (RANKS * data_total)
        split = low(term).reshape(CORNERS**2, data_total, CORNERS, rows, -1)
        split = jnp.transpose(split, (1, 0, 2, 3, 4)).reshape(data_total * RANKS, rows, -1)
        return lax.psum_scatter(split, DATA, scatter_dimension=0, tiled=True)

    inner = CORNERS * data_total
    to_rank = []
    for source in range(inner):
        rank_y, place = divmod(source, data_total)
        to_rank.append((source, place * CORNERS + rank_y))
    INNER = ("cell", "z", "y")

    def shards(
        hidden_in,
        query_weight,
        key_matrix,
        value_matrix,
        gate_weight,
        out_weight,
        norm_attn,
        query_gain,
        key_gain,
        norm_ffn,
        ffn_gate,
        ffn_up,
        ffn_down,
        cotangent,
        sequence_numbers,
        positions,
    ):
        rows = hidden_in.shape[0]
        tokens = rows * RANKS
        groups = CORNERS**2
        window = GROUP_TOKENS // PLANES

        sizes = [norm_attn.shape[0], norm_ffn.shape[0], query_gain.shape[0], key_gain.shape[0]]
        cuts = [0]
        for size in sizes:
            cuts.append(cuts[-1] + size)
        tile = (8, HEAD_SIZE)
        pad = tile[0] * tile[1] - cuts[-1]
        own_gains = jnp.concatenate([norm_attn, norm_ffn, query_gain, key_gain]).astype(jnp.float32)
        own_gains = jnp.pad(own_gains, (0, pad)).reshape(tile)
        plane = lax.axis_index("z")
        group_start = lax.axis_index("cell") * GROUP_TOKENS
        own_start = group_start + (plane * CORNERS + lax.axis_index("y")) * rows
        own_table = jnp.concatenate(
            rope_tables(lax.dynamic_slice_in_dim(positions, own_start, rows)), axis=-1
        )
        marks = [
            lax.dynamic_slice_in_dim(m, group_start, GROUP_TOKENS).reshape(-1, HEAD_SIZE)
            for m in (sequence_numbers, positions)
        ]
        gains, attn_rows, table, hidden_all, all_seq, all_pos, ffn_columns = run(
            [
                tiles_part(own_gains),
                columns_part([query_weight, key_matrix, value_matrix, gate_weight]),
                between(gather_part(own_table), 0.22, 0.7),
                between(gather_part(hidden_in), 0.22, 0.8),
                *map(marks_part, marks),
                split_part(ffn_gate, ffn_up, data_total),
            ],
            2,
            micros=70,
        )
        attn_rows, out_rows, down_rows = lax.optimization_barrier(
            (attn_rows, lax.ppermute(out_weight, INNER, to_rank), ffn_down)
        )
        w_attn = join_cells(attn_rows)
        gains = gains.reshape(PLANES, CORNERS**2, CORNERS, -1)
        gains = jnp.transpose(gains, (1, 0, 2, 3)).reshape(CORNERS**2, PLANES * CORNERS, -1)
        if cells > 1:
            gains = lax.all_gather(gains, "cell", axis=1, tiled=False)
        gains = gains.reshape(RANKS * data_total, -1)
        gain_attn, gain_ffn, gain_query, gain_key = (
            gains[:, a:b].reshape(-1) for a, b in zip(cuts[:-1], cuts[1:])
        )
        w_out = lax.all_gather(out_rows, DATA, axis=0, tiled=True)
        w_down = lax.all_gather(down_rows, DATA, axis=0, tiled=True)

        marks = jnp.stack([m.reshape(groups, GROUP_TOKENS) for m in (all_seq, all_pos)], axis=1)
        own_marks = lax.dynamic_slice_in_dim(marks, plane * window, window, axis=2)
        own_marks = jnp.transpose(own_marks, (0, 2, 1))

        hidden = hidden_in.astype(jnp.float32)
        normed_input, query_low, pair, raw, gate_raw = prepare_attention(
            hidden_all, gain_attn, w_attn, table, gain_query, gain_key
        )
        pair, cotangent_all, ffn_columns = run(
            [line_gather_part(pair), gather_part(cotangent), swap_part(ffn_columns)], 3, micros=75
        )
        w_ffn = gather_columns(ffn_columns)
        out_terms, attended, log_weight, gated_low = attend(
            query_low, pair, gate_raw, own_marks, marks, w_out
        )
        out_terms = out_terms.reshape(RANKS, rows, -1)
        middle = hidden + run([scatter_part(out_terms)], 1, 40)[0]

        normed_two = gather_tokens(low(root_mean_scale(middle, gain_ffn)))
        both = matrix_product(normed_two, w_ffn)
        units = both.shape[1] // 2
        gate_ffn, up_ffn = both[:, :units], both[:, units:]
        ffn_sig = jax.nn.sigmoid(gate_ffn)
        mixed_low = low(gate_ffn * ffn_sig * up_ffn)

        down_term = low(contract_first(mixed_low, cotangent_all))
        down_term, cotangent_all = lax.optimization_barrier((down_term, cotangent_all))
        grad_down = lax.psum_scatter(down_term, DATA, scatter_dimension=0, tiled=True)
        d_mixed = contract_last(cotangent_all, w_down)
        d_up_low = low(d_mixed * gate_ffn * ffn_sig)
        d_gate_ffn_low = low(d_mixed * up_ffn * ffn_sig * (1.0 + gate_ffn * (1.0 - ffn_sig)))
        d_both = jnp.concatenate([d_gate_ffn_low, d_up_low], axis=-1)
        both_term = low(contract_first(normed_two, d_both))
        both_term, d_both = lax.optimization_barrier((both_term, d_both))
        grad_both = sum_columns(both_term)
        (d_normed_two,) = run([scatter_part(product=(d_both, w_ffn), transposed=True)], 6, 48, 45)
        d_middle, grad_norm_two_term = norm_rows_back(middle, gain_ffn, d_normed_two, cotangent)

        branch_all = gather_tokens(low(d_middle))
        branch_all, grad_down = lax.optimization_barrier((branch_all, grad_down))
        d_partial, d_pair, query_gain_terms, out_term = attend_back(
            branch_all, w_out, query_low, pair, gate_raw, own_marks, marks,
            attended, log_weight, raw, table, gain_query, gated_low,
        )
        d_pair, output, grad_both, out_term = run(
            [
                line_scatter_part(d_pair),
                scatter_part(product=(mixed_low, w_down), more=middle),
                swap_part(grad_both),
                halves_part(out_term, data_total),
            ],
            5,
            58,
            75,
        )
        grad_out = lax.psum_scatter(
            out_term.reshape(-1, out_term.shape[-1]), DATA, scatter_dimension=0, tiled=True
        )
        d_raw, key_gain_terms = finish_attention(
            d_pair, raw, table, gain_key, d_partial
        )
        grad_query_gain_term = jnp.sum(query_gain_terms[:, 0], axis=0)
        grad_key_gain_term = jnp.sum(key_gain_terms[:, 0], axis=0)
        a = REPEAT * HEAD_SIZE
        b, c = a + HEAD_SIZE, a + 2 * HEAD_SIZE
        attn_term = low(contract_first(normed_input, d_raw))
        attn_term, d_raw = lax.optimization_barrier((attn_term, d_raw))
        split = attn_term.reshape(CORNERS**2, cells, PLANES, CORNERS, -1, attn_term.shape[1])
        split = jnp.transpose(split, (2, 1, 0, 3, 4, 5)).reshape(PLANES, -1, attn_term.shape[1])
        small = jnp.concatenate(
            [
                t.reshape(RANKS * data_total, -1)
                for t in (grad_norm_two_term, grad_query_gain_term, grad_key_gain_term)
            ],
            axis=-1,
        )
        spare = tile[0] * tile[1] - small.shape[1]
        small = low(jnp.pad(small, ((0, 0), (0, spare))))
        small = small.reshape((CORNERS**2, cells, PLANES, CORNERS) + tile)
        small = jnp.transpose(small, (2, 1, 0, 3, 4, 5)).reshape(PLANES, -1, HEAD_SIZE)
        small, grad_attn, d_normed, grad_gate, grad_up = run(
            [
                line_scatter_part(small, pieces=1),
                line_scatter_part(split, kind=jnp.bfloat16),
                scatter_part(product=(d_raw, w_attn), transposed=True),
                join_part(grad_both, data_total),
            ],
            7,
            58,
            60,
        )
        if cells > 1:
            grad_attn = lax.psum_scatter(grad_attn, "cell", scatter_dimension=0, tiled=True)
            small = lax.psum_scatter(small, "cell", scatter_dimension=0, tiled=True)
        grad_attn = grad_attn.reshape(RANKS, -1, attn_term.shape[1])
        grad_attn, small = run(
            [swap_part(grad_attn), swap_part(small.reshape((RANKS,) + tile))], 4, micros=14
        )
        wide = [(g, jnp.float32) for g in (grad_gate, grad_up, grad_down, grad_out)]
        (
            grad_query, grad_key, grad_value, grad_gatew, along, small,
            grad_gate, grad_up, grad_down, grad_out, output,
        ) = widen_columns(
            grad_attn,
            small,
            (a, b - a, c - b, a),
            (query_weight, key_matrix, value_matrix, gate_weight),
            wide + [(output, output.dtype)],
        )
        grad_norm_attn = along[:, 0] / norm_attn.astype(jnp.float32)
        input_grad = norm_rows_back(hidden_in, gain_attn, d_normed, d_middle)[0]
        small = small.reshape(-1)
        ends = [size - cuts[1] for size in cuts]
        grad_norm_ffn, grad_query_gain, grad_key_gain = (
            small[s:e] for s, e in zip(ends[1:-1], ends[2:])
        )
        return (
            output,
            input_grad,
            grad_query,
            grad_key,
            grad_value,
            grad_gatew,
            grad_out,
            grad_norm_attn,
            grad_query_gain,
            grad_key_gain,
            grad_norm_ffn,
            grad_gate,
            grad_up,
            grad_down,
        )

    return shards


def solution(mesh):
    cells = mesh.shape["fsdp"] // (PLANES * CORNERS)
    split = Mesh(
        mesh.devices.reshape(CORNERS, CORNERS, cells, PLANES, CORNERS),
        ALL,
    )
    rows, flat, group = P(ALL, None), P(ALL), P(("x", "core"))
    return jax.shard_map(
        make_shards(cells),
        mesh=split,
        in_specs=(rows,) * 6 + (flat,) * 4 + (rows,) * 4 + (group,) * 2,
        out_specs=(rows,) * 7 + (flat,) * 4 + (rows,) * 3,
        check_vma=False,
    )
```

```python
import functools
import math

import jax
import jax.numpy as jnp
from jax import lax
from jax.experimental import pallas as pl
from jax.experimental.pallas import tpu as pltpu
from jax.sharding import Mesh
from jax.sharding import PartitionSpec as P

QUERY_HEADS = 16
KEY_VALUE_HEADS = 8
HEAD_SIZE = 128
REPEAT = QUERY_HEADS // KEY_VALUE_HEADS
GROUP_TOKENS = 2048
CORNERS = 2
PLANES = 4
ALL = ("x", "core", "cell", "z", "y")
TENSOR = ("x", "core", "y")
DATA = ("cell", "z")
RANKS = CORNERS**3
CHUNKS = 4
MESH_ID = pl.DeviceIdType.MESH
OTHERS = [(dx, dc, dy) for dx in (0, 1) for dc in (0, 1) for dy in (0, 1) if dx + dc + dy]
DMA = pltpu.SemaphoreType.DMA
VMEM = pl.BlockSpec(memory_space=pltpu.VMEM)
ANYWHERE = pl.BlockSpec(memory_space=pl.ANY)


def remote(source, target, send, receive, device):
    return pltpu.make_async_remote_copy(
        src_ref=source,
        dst_ref=target,
        send_sem=send,
        recv_sem=receive,
        device_id=device,
        device_id_type=MESH_ID,
    )


def landed(ref, sem, device):
    remote(ref, ref, sem, sem, device).wait_recv()


def corner():
    return lax.axis_index("x"), lax.axis_index("core"), lax.axis_index("y")


def slot(x, c, y):
    return (x * CORNERS + c) * CORNERS + y


def flip(value, bit):
    return 1 - value if bit else value


def neighbours():
    x, c, y = corner()
    return {"x": 1 - x}, {"y": 1 - y}, {"core": 1 - c}


def plane_peers():
    x, c, y = corner()
    peers = []
    for dx, dc, dy in OTHERS:
        px, pc, py = flip(x, dx), flip(c, dc), flip(y, dy)
        peers.append(({"x": px, "core": pc, "y": py}, slot(px, pc, py)))
    return peers


def greet(plane, line):
    barrier = pltpu.get_barrier_semaphore()
    near = {"near": neighbours(), "all": [p for p, _ in plane_peers()], None: []}[plane]
    for device in near:
        pl.semaphore_signal(barrier, inc=1, device_id=device, device_id_type=MESH_ID)
    if not line:
        pl.semaphore_wait(barrier, len(near))
        return
    z = lax.axis_index("z")

    @pl.when(z > 0)
    def _():
        pl.semaphore_signal(barrier, inc=1, device_id={"z": z - 1}, device_id_type=MESH_ID)

    @pl.when(z < PLANES - 1)
    def _():
        pl.semaphore_signal(barrier, inc=1, device_id={"z": z + 1}, device_id_type=MESH_ID)

    edge = (z == 0) | (z == PLANES - 1)

    @pl.when(edge)
    def _():
        pl.semaphore_wait(barrier, len(near) + 1)

    @pl.when(jnp.logical_not(edge))
    def _():
        pl.semaphore_wait(barrier, len(near) + 2)


class Part:
    def __init__(self, inputs, outs, scratch, steps, plane=None, line=False):
        self.begin, self.end = 0.0, 1.0
        self.inputs = inputs
        self.outs = outs
        self.scratch = scratch
        self.steps = steps
        self.plane, self.line = plane, line


def run_kernel(parts, *refs):
    refs = list(refs)

    def take(counts):
        groups = []
        for count in counts:
            groups.append(refs[:count])
            del refs[:count]
        return groups

    ins = take([len(p.inputs) for p in parts])
    outs = take([len(p.outs) for p in parts])
    scratch = take([len(p.scratch) for p in parts])
    ranks = [None, "near", "all"]
    plane = ranks[max(ranks.index(p.plane) for p in parts)]
    greet(plane, any(p.line for p in parts))
    plans = [p.steps(i, o, s) for p, i, o, s in zip(parts, ins, outs, scratch)]
    ordered = []
    for p, (first, middle, _) in zip(parts, plans):
        ordered.append((p.begin - 1.0 if p.begin == 0 else p.begin, first))
        for n, step in enumerate(middle):
            ordered.append((p.begin + (p.end - p.begin) * (n + 0.5) / len(middle), step))
    for _, step in sorted(ordered, key=lambda pair: pair[0]):
        step()
    for _, _, last in plans:
        last()


def expected(micros):
    return pl.CostEstimate(flops=0, bytes_accessed=int(micros * 3.5e6), transcendentals=0)


def run(parts, collective_id, vmem=None, micros=40):
    inputs = [pair for p in parts for pair in p.inputs]
    outs = [pair for p in parts for pair in p.outs]
    return pl.pallas_call(
        functools.partial(run_kernel, parts),
        out_shape=[shape for shape, _ in outs],
        in_specs=[spec for _, spec in inputs],
        out_specs=[spec for _, spec in outs],
        scratch_shapes=[s for p in parts for s in p.scratch],
        compiler_params=pltpu.CompilerParams(
            collective_id=collective_id,
            has_side_effects=True,
            vmem_limit_bytes=None if vmem is None else vmem << 20,
        ),
        cost_estimate=expected(micros),
    )(*[array for array, _ in inputs])


def between(part, begin, end):
    part.begin, part.end = begin, end
    return part


def gather_part(block):
    rows, columns = block.shape
    n, half = CHUNKS, CHUNKS // 2
    chunk = rows // n

    def steps(ins, outs, scratch):
        (in_ref,), (out_ref,) = ins, outs
        send_x, send_y, send_c, recv_x, recv_y, recv_c, local = scratch
        x, c, y = corner()
        dev_x, dev_y, dev_c = neighbours()

        def at(index, k):
            start = pl.multiple_of(index * rows + k * chunk, chunk)
            return out_ref.at[pl.ds(start, chunk), :]

        own, beside_x, beside_y = slot(x, c, y), slot(1 - x, c, y), slot(x, c, 1 - y)
        across = slot(1 - x, c, 1 - y)
        mirror = [
            slot(x, 1 - c, y),
            slot(1 - x, 1 - c, y),
            slot(x, 1 - c, 1 - y),
            slot(1 - x, 1 - c, 1 - y),
        ]
        start = pl.multiple_of(own * rows, rows)
        keep = pltpu.make_async_copy(in_ref, out_ref.at[pl.ds(start, rows), :], local)
        sent = []

        def go(copy):
            copy.start()
            sent.append(copy)

        def share(index, k, b):
            go(remote(at(index, k), at(index, k), send_c.at[b * n + k], recv_c.at[b * n + k], dev_c))

        order_x = list(range(n))
        order_y = order_x[half:] + order_x[:half]

        def first():
            keep.start()

            def mine(k):
                return in_ref.at[pl.ds(k * chunk, chunk), :]

            for k, j in zip(order_x, order_y):
                go(remote(mine(k), at(own, k), send_x.at[k], recv_x.at[k], dev_x))
                go(remote(mine(j), at(own, j), send_y.at[j], recv_y.at[j], dev_y))
            for k in range(n):
                go(remote(mine(k), at(own, k), send_c.at[k], recv_c.at[k], dev_c))

        def straight(k, j):
            landed(at(beside_x, k), recv_x.at[k], dev_x)
            if k < half:
                to = at(beside_x, k)
                go(remote(to, to, send_y.at[n + k], recv_y.at[n + k], dev_y))
            share(beside_x, k, 1)
            landed(at(beside_y, j), recv_y.at[j], dev_y)
            if j >= half:
                to = at(beside_y, j)
                go(remote(to, to, send_x.at[half + j], recv_x.at[half + j], dev_x))
            share(beside_y, j, 2)

        def diagonal(k):
            landed(at(across, k), recv_y.at[n + k], dev_y)
            share(across, k, 3)
            landed(at(across, half + k), recv_x.at[n + k], dev_x)
            share(across, half + k, 3)

        def last():
            for b in range(4):
                for k in range(n):
                    landed(at(mirror[b], k), recv_c.at[b * n + k], dev_c)
            for copy in sent:
                copy.wait_send()
            keep.wait()

        middle = [functools.partial(straight, k, j) for k, j in zip(order_x, order_y)]
        middle += [functools.partial(diagonal, k) for k in range(half)]
        return first, middle, last

    link = DMA((n + half,))
    core = DMA((4 * n,))
    return Part(
        [(block, VMEM)],
        [(jax.ShapeDtypeStruct((RANKS * rows, columns), block.dtype), ANYWHERE)],
        [link, link, core, link, link, core, DMA(())],
        steps,
        plane="near",
    )


def add_rows(target, start, count, sources, step=16):
    def body(i, carry):
        r = pl.multiple_of(start + i * step, step)
        total = None
        for ref, shift in sources:
            value = ref[pl.ds(r - shift if shift else r, step), :].astype(jnp.float32)
            total = value if total is None else total + value
        target[pl.ds(r, step), :] = total.astype(target.dtype)
        return carry

    lax.fori_loop(0, count // step, body, 0)


def scatter_part(terms=None, product=None, transposed=False, tile=512, more=None):
    if product is None:
        ranks, rows, columns = terms.shape
    else:
        left, right = product
        rows, columns = left.shape[0] // RANKS, right.shape[0 if transposed else 1]
    n, half = CHUNKS, CHUNKS // 2
    chunk = rows // n
    middle_row = half * chunk

    def steps(ins, outs, scratch):
        (out_ref,) = outs
        extra = [] if more is None else [(ins[-1], 0)]
        ins = ins if more is None else ins[:-1]
        if product is None:
            (part_ref,) = ins
        else:
            left_ref, right_ref = ins
            part_ref, scratch = scratch[-1], scratch[:-1]
        core_buf, x_buf, y_buf, x_diag, y_diag, d_sum, x_sum, y_sum = scratch[:8]
        send_c, recv_c, send_x, recv_x, send_y, recv_y = scratch[8:]
        x, c, y = corner()
        dev_x, dev_y, dev_c = neighbours()
        D, X, Y, O = range(4)
        place = [(1 - x, 1 - y), (1 - x, y), (x, 1 - y), (x, y)]
        mine = [slot(px, c, py) for px, py in place]
        theirs = [slot(px, 1 - c, py) for px, py in place]
        orders = {D: [], X: list(range(n)), O: list(range(n))}
        for k in range(half):
            orders[D] += [k, half + k]
        orders[Y] = orders[X][half:] + orders[X][:half]
        sent = []

        def go(copy):
            copy.start()
            sent.append(copy)

        def piece(k):
            return pl.ds(k * chunk, chunk)

        def make(index):
            def body(j, carry):
                at = pl.ds(pl.multiple_of(j * tile, tile), tile)
                some = left_ref[pl.ds(pl.multiple_of(index * rows, rows), rows), :]
                if transposed:
                    value = dot_rows(some, right_ref[at, :])
                else:
                    value = dot(some, right_ref[:, at])
                part_ref[index, :, at] = low(value)
                return carry

            lax.fori_loop(0, columns // tile, body, 0)

        def to_core(b):
            for k in orders[b]:
                source = part_ref.at[theirs[b], piece(k), :]
                i = b * n + k
                go(remote(source, core_buf.at[b, piece(k), :], send_c.at[i], recv_c.at[i], dev_c))

        def made_for_core(b):
            make(theirs[b])
            to_core(b)

        def first():
            if product is None:
                for b in (D, X, Y, O):
                    to_core(b)
            else:
                made_for_core(D)
                make(mine[D])

        def chip(target, b, k, *more):
            landed(core_buf.at[b, piece(k), :], recv_c.at[b * n + k], dev_c)
            sources = [(part_ref.at[mine[b]], 0), (core_buf.at[b], 0), *more]
            add_rows(target, k * chunk, chunk, sources)

        def to_x(k):
            go(remote(x_sum.at[piece(k), :], x_buf.at[piece(k), :], send_x.at[k], recv_x.at[k], dev_x))

        def to_y(k):
            go(remote(y_sum.at[piece(k), :], y_buf.at[piece(k), :], send_y.at[k], recv_y.at[k], dev_y))

        def diagonal(k):
            chip(d_sum, D, k)
            source = d_sum.at[piece(k), :]
            if k < half:
                go(remote(source, x_diag.at[piece(k), :], send_x.at[n + k], recv_x.at[n + k], dev_x))
            else:
                to = y_diag.at[piece(k - half), :]
                go(remote(source, to, send_y.at[half + k], recv_y.at[half + k], dev_y))

        def direct(k):
            chip(x_sum, X, k)
            to_x(k)
            chip(y_sum, Y, half + k)
            to_y(half + k)

        def relayed(k):
            landed(y_diag.at[piece(k), :], recv_y.at[n + k], dev_y)
            chip(x_sum, X, half + k, (y_diag, middle_row))
            to_x(half + k)
            landed(x_diag.at[piece(k), :], recv_x.at[n + k], dev_x)
            chip(y_sum, Y, k, (x_diag, 0))
            to_y(k)

        def own(k):
            landed(x_buf.at[piece(k), :], recv_x.at[k], dev_x)
            landed(y_buf.at[piece(k), :], recv_y.at[k], dev_y)
            chip(out_ref, O, k, (x_buf, 0), (y_buf, 0), *extra)

        def last():
            for copy in sent:
                copy.wait_send()

        def makes(b):
            if product is None:
                return []
            return [functools.partial(made_for_core, b), functools.partial(make, mine[b])]

        middle = [functools.partial(diagonal, k) for k in orders[D]]
        middle += makes(X) + makes(Y)
        middle += [functools.partial(direct, k) for k in range(half)]
        middle += makes(O)
        middle += [functools.partial(relayed, k) for k in range(half)]
        middle += [functools.partial(own, k) for k in range(n)]
        return first, middle, last

    def low_vmem(*shape):
        return pltpu.VMEM(shape, jnp.bfloat16)

    whole, part = low_vmem(rows, columns), low_vmem(rows // 2, columns)
    link = DMA((n + half,))
    core = DMA((4 * n,))
    made = [] if product is None else [low_vmem(RANKS, rows, columns)]
    return Part(
        ([(terms, VMEM)] if product is None else [(left, VMEM), (right, VMEM)])
        + ([] if more is None else [(more, VMEM)]),
        [(jax.ShapeDtypeStruct((rows, columns), jnp.float32 if more is None else jnp.bfloat16), VMEM)],
        [low_vmem(4, rows, columns), whole, whole, part, part, whole, whole, whole]
        + [core, core, link, link, link, link]
        + made,
        steps,
        plane="near",
    )


def swap_part(blocks):
    def steps(ins, outs, scratch):
        (in_ref,), (out_ref,) = ins, outs
        send, recv, local = scratch
        own = slot(*corner())
        keep = pltpu.make_async_copy(in_ref.at[own], out_ref.at[own], local)
        peers = plane_peers()
        sent = []

        def first():
            keep.start()
            for i, (there, other) in enumerate(peers):
                copy = remote(in_ref.at[other], out_ref.at[own], send.at[i], recv.at[i], there)
                copy.start()
                sent.append(copy)

        def last():
            for i, (there, other) in enumerate(peers):
                landed(out_ref.at[other], recv.at[i], there)
            for copy in sent:
                copy.wait_send()
            keep.wait()

        return first, [], last

    n = len(OTHERS)
    return Part(
        [(blocks, VMEM)],
        [(jax.ShapeDtypeStruct(blocks.shape, blocks.dtype), ANYWHERE)],
        [DMA((n,)), DMA((n,)), DMA(())],
        steps,
        plane="all",
    )


def halves_part(term, owners):
    rows = term.shape[0] // owners
    half = owners // CORNERS

    def steps(ins, outs, scratch):
        (in_ref,), (out_ref,) = ins, outs
        send, recv, local = scratch
        y = lax.axis_index("y")
        dev_y = neighbours()[1]

        def rows_of(i, side):
            return in_ref.at[pl.ds(pl.multiple_of((i * CORNERS + side) * rows, rows), rows), :]

        def keep(i):
            return pltpu.make_async_copy(rows_of(i, y), out_ref.at[y * half + i], local.at[i])

        def give(i):
            return remote(rows_of(i, 1 - y), out_ref.at[y * half + i], send.at[i], recv.at[i], dev_y)

        def first():
            for i in range(half):
                keep(i).start()
                give(i).start()

        def last():
            for i in range(half):
                landed(out_ref.at[(1 - y) * half + i], recv.at[i], dev_y)
                give(i).wait_send()
                keep(i).wait()

        return first, [], last

    return Part(
        [(term, VMEM)],
        [(jax.ShapeDtypeStruct((owners, rows, term.shape[1]), term.dtype), VMEM)],
        [DMA((half,)), DMA((half,)), DMA((half,))],
        steps,
        plane="near",
    )


def line_gather_part(block, pieces=4):
    rows = block.shape[0] // pieces

    def steps(ins, outs, scratch):
        (in_ref,), (out_ref,) = ins, outs
        up_send, up_recv, down_send, down_recv, local = scratch
        z = lax.axis_index("z")
        keep = pltpu.make_async_copy(in_ref, out_ref.at[z], local)

        def at(block, k):
            return out_ref.at[block, pl.ds(k * rows, rows), :]

        def up(t, k, source=None):
            s = at(z - t, k) if source is None else source
            i = t * pieces + k
            return remote(s, at(z - t, k), up_send.at[i], up_recv.at[i], {"z": z + 1})

        def down(t, k, source=None):
            s = at(z + t, k) if source is None else source
            i = t * pieces + k
            return remote(s, at(z + t, k), down_send.at[i], down_recv.at[i], {"z": z - 1})

        def first():
            keep.start()
            for k in range(pieces):
                mine = in_ref.at[pl.ds(k * rows, rows), :]

                @pl.when(z < PLANES - 1)
                def _():
                    up(0, k, mine).start()

                @pl.when(z > 0)
                def _():
                    down(0, k, mine).start()

        def arrive(t, k):
            i = t * pieces + k
            on = t + 1 < PLANES - 1

            @pl.when(z - 1 - t >= 0)
            def _():
                landed(at(z - 1 - t, k), up_recv.at[i], {"z": z - 1})
                if on:

                    @pl.when(z < PLANES - 1)
                    def _():
                        up(t + 1, k).start()

            @pl.when(z + 1 + t < PLANES)
            def _():
                landed(at(z + 1 + t, k), down_recv.at[i], {"z": z + 1})
                if on:

                    @pl.when(z > 0)
                    def _():
                        down(t + 1, k).start()

        def last():
            for t in range(PLANES - 1):
                for k in range(pieces):

                    @pl.when((z < PLANES - 1) & (z - t >= 0))
                    def _():
                        up(t, k).wait_send()

                    @pl.when((z > 0) & (z + t < PLANES))
                    def _():
                        down(t, k).wait_send()

            keep.wait()

        middle = [
            functools.partial(arrive, t, k) for t in range(PLANES - 1) for k in range(pieces)
        ]
        return first, middle, last

    sems = DMA(((PLANES - 1) * pieces,))
    return Part(
        [(block, VMEM)],
        [(jax.ShapeDtypeStruct((PLANES,) + block.shape, block.dtype), ANYWHERE)],
        [sems, sems, sems, sems, DMA(())],
        steps,
        line=True,
    )


def line_scatter_part(terms, pieces=4, kind=jnp.float32):
    line, all_rows, columns = terms.shape
    rows = all_rows // pieces
    step = 32

    def steps(ins, outs, scratch):
        (in_ref,), (out_ref,) = ins, outs
        up_buf, down_buf, up_stage, down_stage, up_send, up_recv, down_send, down_recv = scratch
        z = lax.axis_index("z")
        f32 = jnp.float32

        def cut(k):
            return pl.ds(k * rows, rows)

        def send_up(source, d, k):
            i = (d - 1) * pieces + k
            return remote(source, up_buf.at[d - 1, cut(k), :], up_send.at[i], up_recv.at[i], {"z": z + 1})

        def send_down(source, d, k):
            i = (d - 1) * pieces + k
            to = down_buf.at[d - 1, cut(k), :]
            return remote(source, to, down_send.at[i], down_recv.at[i], {"z": z - 1})

        def first():
            for d in range(line - 1, 0, -1):
                for k in range(pieces):

                    @pl.when(z == 0)
                    def _():
                        send_up(in_ref.at[d, cut(k), :], d, k).start()

                    @pl.when(z == line - 1)
                    def _():
                        send_down(in_ref.at[line - 1 - d, cut(k), :], d, k).start()

        def pass_on(d, k):
            @pl.when(z + d < line)
            def _():
                if d + 1 < line:

                    @pl.when(z > 0)
                    def _():
                        landed(up_buf.at[d, cut(k), :], up_recv.at[d * pieces + k], {"z": z - 1})
                        sources = [(in_ref.at[z + d], 0), (up_buf.at[d], 0)]
                        add_rows(up_stage.at[d - 1], k * rows, rows, sources, step)
                        send_up(up_stage.at[d - 1, cut(k), :], d, k).start()

            @pl.when(z - d >= 0)
            def _():
                if d + 1 < line:

                    @pl.when(z < line - 1)
                    def _():
                        landed(down_buf.at[d, cut(k), :], down_recv.at[d * pieces + k], {"z": z + 1})
                        sources = [(in_ref.at[z - d], 0), (down_buf.at[d], 0)]
                        add_rows(down_stage.at[d - 1], k * rows, rows, sources, step)
                        send_down(down_stage.at[d - 1, cut(k), :], d, k).start()

        def own(k):
            @pl.when(z > 0)
            def _():
                landed(up_buf.at[0, cut(k), :], up_recv.at[k], {"z": z - 1})

            @pl.when(z < line - 1)
            def _():
                landed(down_buf.at[0, cut(k), :], down_recv.at[k], {"z": z + 1})

            mine, below, above = (in_ref.at[z], 0), (up_buf.at[0], 0), (down_buf.at[0], 0)

            @pl.when(z == 0)
            def _():
                add_rows(out_ref, k * rows, rows, [mine, above], step)

            @pl.when(z == line - 1)
            def _():
                add_rows(out_ref, k * rows, rows, [mine, below], step)

            @pl.when((z > 0) & (z < line - 1))
            def _():
                add_rows(out_ref, k * rows, rows, [mine, below, above], step)

        def last():
            for d in range(line - 1, 0, -1):
                for k in range(pieces):

                    @pl.when(z + d < line)
                    def _():
                        send_up(up_stage.at[d - 1, cut(k), :], d, k).wait_send()

                    @pl.when(z - d >= 0)
                    def _():
                        send_down(down_stage.at[d - 1, cut(k), :], d, k).wait_send()

        middle = [
            functools.partial(pass_on, d, k) for d in range(line - 2, 0, -1) for k in range(pieces)
        ]
        middle += [functools.partial(own, k) for k in range(pieces)]
        return first, middle, last

    sems = DMA(((line - 1) * pieces,))
    buffer = pltpu.VMEM((line - 1, all_rows, columns), jnp.bfloat16)
    return Part(
        [(terms, VMEM)],
        [(jax.ShapeDtypeStruct((all_rows, columns), kind), VMEM)],
        [buffer, buffer, buffer, buffer, sems, sems, sems, sems],
        steps,
        line=True,
    )


def columns_part(weights):
    rows = weights[0].shape[0]
    widths = [w.shape[1] // RANKS for w in weights]
    ends = [sum(widths[: n + 1]) for n in range(len(widths))]
    many = len(weights)

    def steps(ins, outs, scratch):
        (out_ref,) = outs
        send, recv, up_send, up_recv, down_send, down_recv, local = scratch
        x, c, y = corner()
        z = lax.axis_index("z")
        own = slot(x, c, y)
        peers = plane_peers()
        spots = [(x * CORNERS + c, y)]
        spots += [(flip(x, dx) * CORNERS + flip(c, dc), flip(y, dy)) for dx, dc, dy in OTHERS]

        def at(i, plane):
            return out_ref.at[spots[i][0], plane, spots[i][1]]

        def cut(n, index):
            return ins[n].at[:, pl.ds(pl.multiple_of(index * widths[n], widths[n]), widths[n])]

        def place(i, n):
            return at(i, z).at[:, pl.ds(ends[n] - widths[n], widths[n])]

        keeps = [pltpu.make_async_copy(cut(n, own), place(0, n), local.at[n]) for n in range(many)]
        sent = []

        def up(t, i, source=None):
            s = at(i, z - t) if source is None else source
            n = t * RANKS + i
            return remote(s, at(i, z - t), up_send.at[n], up_recv.at[n], {"z": z + 1})

        def down(t, i, source=None):
            s = at(i, z + t) if source is None else source
            n = t * RANKS + i
            return remote(s, at(i, z + t), down_send.at[n], down_recv.at[n], {"z": z - 1})

        def begin(i, source=None):
            @pl.when(z < PLANES - 1)
            def _():
                up(0, i, source).start()

            @pl.when(z > 0)
            def _():
                down(0, i, source).start()

        def first():
            for keep in keeps:
                keep.start()
            for i, (there, other) in enumerate(peers):
                for n in range(many):
                    m = i * many + n
                    copy = remote(cut(n, other), place(0, n), send.at[m], recv.at[m], there)
                    copy.start()
                    sent.append(copy)
            for keep in keeps:
                keep.wait()
            begin(0)

        def swapped(i):
            for n in range(many):
                landed(place(i, n), recv.at[(i - 1) * many + n], peers[i - 1][0])
            begin(i)

        def arrive(t, i):
            n = t * RANKS + i
            on = t + 1 < PLANES - 1

            @pl.when(z - 1 - t >= 0)
            def _():
                landed(at(i, z - 1 - t), up_recv.at[n], {"z": z - 1})
                if on:

                    @pl.when(z < PLANES - 1)
                    def _():
                        up(t + 1, i).start()

            @pl.when(z + 1 + t < PLANES)
            def _():
                landed(at(i, z + 1 + t), down_recv.at[n], {"z": z + 1})
                if on:

                    @pl.when(z > 0)
                    def _():
                        down(t + 1, i).start()

        def last():
            for copy in sent:
                copy.wait_send()
            for t in range(PLANES - 1):
                for i in range(RANKS):

                    @pl.when((z < PLANES - 1) & (z - t >= 0))
                    def _():
                        up(t, i).wait_send()

                    @pl.when((z > 0) & (z + t < PLANES))
                    def _():
                        down(t, i).wait_send()

        middle = [functools.partial(swapped, i) for i in range(1, RANKS)]
        middle += [
            functools.partial(arrive, t, i) for t in range(PLANES - 1) for i in range(RANKS)
        ]
        return first, middle, last

    n = len(OTHERS) * many
    sems = DMA(((PLANES - 1) * RANKS,))
    shape = (CORNERS**2, PLANES, CORNERS, rows, ends[-1])
    return Part(
        [(w, VMEM) for w in weights],
        [(jax.ShapeDtypeStruct(shape, weights[0].dtype), ANYWHERE)],
        [DMA((n,)), DMA((n,)), sems, sems, sems, sems, DMA((many,))],
        steps,
        plane="all",
        line=True,
    )


def tiles_part(tile):
    def steps(ins, outs, scratch):
        (in_ref,), (out_ref,) = ins, outs
        send, recv, up_send, up_recv, down_send, down_recv, local = scratch
        z = lax.axis_index("z")
        own = slot(*corner())
        peers = plane_peers()
        keep = pltpu.make_async_copy(in_ref, out_ref.at[z, own], local)

        def give(i):
            return remote(in_ref, out_ref.at[z, own], send.at[i], recv.at[i], peers[i][0])

        def up(t):
            to = out_ref.at[z - t]
            return remote(to, to, up_send.at[t], up_recv.at[t], {"z": z + 1})

        def down(t):
            to = out_ref.at[z + t]
            return remote(to, to, down_send.at[t], down_recv.at[t], {"z": z - 1})

        def first():
            keep.start()
            for i in range(len(peers)):
                give(i).start()

        def swapped():
            for i, (there, other) in enumerate(peers):
                landed(out_ref.at[z, other], recv.at[i], there)
            keep.wait()

            @pl.when(z < PLANES - 1)
            def _():
                up(0).start()

            @pl.when(z > 0)
            def _():
                down(0).start()

        def arrive(t):
            on = t + 1 < PLANES - 1

            @pl.when(z - 1 - t >= 0)
            def _():
                landed(out_ref.at[z - 1 - t], up_recv.at[t], {"z": z - 1})
                if on:

                    @pl.when(z < PLANES - 1)
                    def _():
                        up(t + 1).start()

            @pl.when(z + 1 + t < PLANES)
            def _():
                landed(out_ref.at[z + 1 + t], down_recv.at[t], {"z": z + 1})
                if on:

                    @pl.when(z > 0)
                    def _():
                        down(t + 1).start()

        def last():
            for i in range(len(peers)):
                give(i).wait_send()
            for t in range(PLANES - 1):

                @pl.when((z < PLANES - 1) & (z - t >= 0))
                def _():
                    up(t).wait_send()

                @pl.when((z > 0) & (z + t < PLANES))
                def _():
                    down(t).wait_send()

        middle = [swapped] + [functools.partial(arrive, t) for t in range(PLANES - 1)]
        return first, middle, last

    n = len(OTHERS)
    line = DMA((PLANES - 1,))
    return Part(
        [(tile, VMEM)],
        [(jax.ShapeDtypeStruct((PLANES, RANKS) + tile.shape, tile.dtype), VMEM)],
        [DMA((n,)), DMA((n,)), line, line, line, line, DMA(())],
        steps,
        plane="all",
        line=True,
    )


def marks_part(marks):
    def steps(ins, outs, scratch):
        (in_ref,), (out_ref,) = ins, outs
        send, recv, local = scratch
        x, c, _ = corner()
        keep = pltpu.make_async_copy(in_ref, out_ref.at[x * CORNERS + c], local)
        near = []
        for i, (dx, dc) in enumerate([(0, 1), (1, 0), (1, 1)]):
            px, pc = flip(x, dx), flip(c, dc)
            near.append((i, {"x": px, "core": pc}, px * CORNERS + pc))

        def give(i, there):
            return remote(in_ref, out_ref.at[x * CORNERS + c], send.at[i], recv.at[i], there)

        def first():
            keep.start()
            for i, there, _ in near:
                give(i, there).start()

        def last():
            for i, there, theirs in near:
                landed(out_ref.at[theirs], recv.at[i], there)
                give(i, there).wait_send()
            keep.wait()

        return first, [], last

    return Part(
        [(marks, VMEM)],
        [(jax.ShapeDtypeStruct((CORNERS**2,) + marks.shape, marks.dtype), VMEM)],
        [DMA((3,)), DMA((3,)), DMA(())],
        steps,
        plane="all",
    )


def root_mean_scale(values, gains):
    return values * lax.rsqrt(jnp.mean(values * values, axis=-1, keepdims=True) + 1e-06) * gains


def rope_tables(positions):
    half = HEAD_SIZE // 2
    steps_half = jnp.arange(half).astype(jnp.float32)
    inverse = jnp.power(1000000.0, steps_half * (-2.0 / HEAD_SIZE))
    angles = positions.astype(jnp.float32)[:, None] * inverse[None, :]
    cosine, sine = jnp.cos(angles), jnp.sin(angles)
    return jnp.concatenate([cosine, cosine], axis=-1), jnp.concatenate([-sine, sine], axis=-1)


def matrix_product(left, right):
    return jnp.dot(left, right, preferred_element_type=jnp.float32)


def contract_last(left, right):
    return lax.dot_general(
        left, right, (((1,), (1,)), ((), ())), preferred_element_type=jnp.float32
    )


def contract_first(left, right):
    return lax.dot_general(
        left, right, (((0,), (0,)), ((), ())), preferred_element_type=jnp.float32
    )


def low(values):
    return values.astype(jnp.bfloat16)

def turn(values, cosine, sine):
    return values * cosine + pltpu.roll(values, HEAD_SIZE // 2, 1) * sine


def turn_back(grads, cosine, sine):
    return grads * cosine + pltpu.roll(grads * sine, HEAD_SIZE // 2, 1)


def unit_scale(values):
    return lax.rsqrt(jnp.mean(values * values, axis=-1, keepdims=True) + 1e-06)


def norm_back(raw, gain, grads):
    scale = unit_scale(raw)
    unit = raw * scale
    inner = grads * gain
    d_raw = scale * (inner - unit * jnp.mean(inner * unit, axis=-1, keepdims=True))
    return d_raw, grads * unit


def head(index):
    return slice(index * HEAD_SIZE, (index + 1) * HEAD_SIZE)


def dot(left, right):
    return jnp.dot(left, right, preferred_element_type=jnp.float32)


def dot_rows(left, right):
    return lax.dot_general(
        left, right, (((1,), (1,)), ((), ())), preferred_element_type=jnp.float32
    )


def prepare_kernel(
    x_ref, gain_ref, w_ref, cos_ref, sin_ref, qg_ref, kg_ref, x_out, q_ref, kv_ref, raw_ref, gate_ref
):
    hidden = x_ref[...].astype(jnp.float32)
    x_out[...] = low(hidden * unit_scale(hidden) * gain_ref[...])
    raw = dot(x_out[...], w_ref[...])
    cosine, sine = cos_ref[...], sin_ref[...]

    def prepare(values, gain):
        return low(turn(values * unit_scale(values) * gain, cosine, sine))

    for h in range(REPEAT):
        q_ref[:, head(h)] = prepare(raw[:, head(h)], qg_ref[...])
    kv_ref[:, head(0)] = prepare(raw[:, head(REPEAT)], kg_ref[...])
    kv_ref[:, head(1)] = low(raw[:, head(REPEAT + 1)])
    raw_ref[...] = raw[:, : (REPEAT + 1) * HEAD_SIZE]
    gate_ref[...] = raw[:, (REPEAT + 2) * HEAD_SIZE :]


def table_specs(rows):
    return [
        pl.BlockSpec((rows, HEAD_SIZE), lambda i: (i, 0)),
        pl.BlockSpec((rows, HEAD_SIZE), lambda i: (i, 1)),
    ]


def rows_spec(rows, columns):
    return pl.BlockSpec((rows, columns), lambda i: (i, 0))


def fixed_spec(*shape):
    return pl.BlockSpec(shape, lambda i: (0,) * len(shape))


def kernel_params(vmem):
    return pltpu.CompilerParams(vmem_limit_bytes=vmem << 20)


def prepare_attention(hidden, gain_attn, w_attn, table, gain_query, gain_key):
    tokens, width = hidden.shape
    columns = w_attn.shape[1]
    q_columns = REPEAT * HEAD_SIZE
    steps = RANKS // 2
    rows = tokens // steps
    shape = jax.ShapeDtypeStruct
    return pl.pallas_call(
        prepare_kernel,
        grid=(steps,),
        out_shape=[
            shape((tokens, width), jnp.bfloat16),
            shape((tokens, q_columns), jnp.bfloat16),
            shape((tokens, 2 * HEAD_SIZE), jnp.bfloat16),
            shape((tokens, q_columns + HEAD_SIZE), jnp.float32),
            shape((tokens, q_columns), jnp.float32),
        ],
        in_specs=[
            rows_spec(rows, width),
            fixed_spec(1, width),
            fixed_spec(width, columns),
            *table_specs(rows),
            fixed_spec(1, HEAD_SIZE),
            fixed_spec(1, HEAD_SIZE),
        ],
        out_specs=[
            rows_spec(rows, width),
            rows_spec(rows, q_columns),
            rows_spec(rows, 2 * HEAD_SIZE),
            rows_spec(rows, q_columns + HEAD_SIZE),
            rows_spec(rows, q_columns),
        ],
        compiler_params=kernel_params(60),
        cost_estimate=expected(12),
    )(hidden, gain_attn[None], w_attn, table, table, gain_query[None], gain_key[None])


EXPONENT = math.log2(math.e) / math.sqrt(HEAD_SIZE)


def allowed_keys(own_ref, keys_ref, z, window):
    seq, pos = own_ref[0, :, 0:1], own_ref[0, :, 1:2]
    key_seq = keys_ref[0, 0:1, z * window : (z + 1) * window]
    key_pos = keys_ref[0, 1:2, z * window : (z + 1) * window]
    return (key_pos <= pos) & ((key_seq == 0) | (key_seq == seq))


def attend_kernel(q_ref, kv_ref, gate_ref, own_ref, keys_ref, wo_ref, terms_ref, att_ref, log_ref, gated_ref):
    planes, window = kv_ref.shape[0], kv_ref.shape[1]
    totals = [None] * REPEAT
    ones = jnp.ones((window, HEAD_SIZE), jnp.bfloat16)
    for z in range(planes):
        allowed = allowed_keys(own_ref, keys_ref, z, window)
        keys = kv_ref[z, :, head(0)]
        values = jnp.concatenate([kv_ref[z, :, head(1)], ones], axis=1)
        for h in range(REPEAT):
            scores = dot_rows(q_ref[:, head(h)], keys) * EXPONENT
            exponent = low(jnp.where(allowed, jnp.exp2(scores), 0.0))
            part = dot(exponent, values)
            totals[h] = part if totals[h] is None else totals[h] + part
    for h in range(REPEAT):
        weight = totals[h][:, head(1)]
        attended = totals[h][:, head(0)] / weight
        att_ref[:, head(h)] = attended
        log_ref[:, head(h)] = jnp.log2(weight)
        gated_ref[:, head(h)] = low(attended * jax.nn.sigmoid(gate_ref[:, head(h)]))
    terms_ref[...] = low(dot(gated_ref[...], wo_ref[...]))


def group_specs(window):
    return [
        pl.BlockSpec((PLANES, window, 2 * HEAD_SIZE), lambda i: (0, i, 0)),
        pl.BlockSpec((1, window, 2), lambda i: (i, 0, 0)),
        pl.BlockSpec((1, 2, PLANES * window), lambda i: (i, 0, 0)),
    ]


def attend(query, pair, gate, own, keys, w_out):
    tokens, q_columns = query.shape
    groups = own.shape[0]
    window = tokens // groups
    width = w_out.shape[1]
    kv, mine, marks = group_specs(window)
    shape = jax.ShapeDtypeStruct
    columns = rows_spec(window, q_columns)
    return pl.pallas_call(
        attend_kernel,
        grid=(groups,),
        out_shape=[
            shape((tokens, width), jnp.bfloat16),
            shape((tokens, q_columns), jnp.float32),
            shape((tokens, q_columns), jnp.float32),
            shape((tokens, q_columns), jnp.bfloat16),
        ],
        in_specs=[columns, kv, columns, mine, marks, fixed_spec(q_columns, width)],
        out_specs=[rows_spec(window, width), columns, columns, columns],
        compiler_params=kernel_params(48),
        cost_estimate=expected(18),
    )(query, pair, gate, own, keys, w_out)


def attend_back_kernel(
    branch_ref, wo_ref, q_ref, kv_ref, gate_ref, own_ref, keys_ref, att_ref, log_ref, raw_ref,
    cos_ref, sin_ref, qg_ref, gated_ref, out_ref, dkv_ref, gain_ref, term_ref, term_sum,
):
    planes, window = kv_ref.shape[0], kv_ref.shape[1]
    scale = 1.0 / math.sqrt(HEAD_SIZE)
    turned = jnp.transpose(gated_ref[...])

    @pl.when(pl.program_id(0) == 0)
    def _():
        term_sum[...] = dot(turned, branch_ref[...])

    @pl.when(pl.program_id(0) > 0)
    def _():
        term_sum[...] += dot(turned, branch_ref[...])

    @pl.when(pl.program_id(0) == pl.num_programs(0) - 1)
    def _():
        term_ref[...] = low(term_sum[...])

    d_gated = dot_rows(branch_ref[...], wo_ref[...])
    gate = jax.nn.sigmoid(gate_ref[...])
    attended = att_ref[...]
    d_attended = low(d_gated * gate)
    out_ref[:, (REPEAT + 2) * HEAD_SIZE :] = low(d_gated * attended * gate * (1.0 - gate))
    product = d_attended.astype(jnp.float32) * attended
    delta = [jnp.sum(product[:, head(h)], axis=-1, keepdims=True) for h in range(REPEAT)]
    turned_q = [jnp.transpose(q_ref[:, head(h)]) for h in range(REPEAT)]
    turned_d = [jnp.transpose(d_attended[:, head(h)]) for h in range(REPEAT)]
    d_query = [None] * REPEAT
    for z in range(planes):
        allowed = allowed_keys(own_ref, keys_ref, z, window)
        keys, values = kv_ref[z, :, head(0)], kv_ref[z, :, head(1)]
        d_keys, d_values = None, None
        for h in range(REPEAT):
            scores = dot_rows(q_ref[:, head(h)], keys) * EXPONENT - log_ref[:, h * HEAD_SIZE : h * HEAD_SIZE + 1]
            probs = jnp.where(allowed, jnp.exp2(scores), 0.0)
            d_probs = dot_rows(d_attended[:, head(h)], values)
            d_scores = low(probs * (d_probs - delta[h]))
            part = dot(d_scores, keys)
            d_query[h] = part if d_query[h] is None else d_query[h] + part
            part = dot(turned_q[h], d_scores)
            d_keys = part if d_keys is None else d_keys + part
            part = dot(turned_d[h], low(probs))
            d_values = part if d_values is None else d_values + part
        dkv_ref[z, :, head(0)] = low(jnp.transpose(d_keys * scale))
        dkv_ref[z, :, head(1)] = low(jnp.transpose(d_values))
    cosine, sine = cos_ref[...], sin_ref[...]
    total = jnp.zeros((1, HEAD_SIZE), jnp.float32)
    for h in range(REPEAT):
        grads = turn_back(d_query[h] * scale, cosine, sine)
        d_raw, by_row = norm_back(raw_ref[:, head(h)], qg_ref[...], grads)
        out_ref[:, head(h)] = low(d_raw)
        total += jnp.sum(by_row, axis=0, keepdims=True)
    gain_ref[0] = jnp.broadcast_to(total, gain_ref.shape[1:])


def attend_back(
    branch, w_out, query, pair, gate, own, keys, attended, log, raw, table, gain, gated
):
    tokens, q_columns = query.shape
    groups = own.shape[0]
    window = tokens // groups
    width = w_out.shape[1]
    kv, mine, marks = group_specs(window)
    shape = jax.ShapeDtypeStruct
    columns = rows_spec(window, q_columns)
    return pl.pallas_call(
        attend_back_kernel,
        grid=(groups,),
        out_shape=[
            shape((tokens, 2 * q_columns + 2 * HEAD_SIZE), jnp.bfloat16),
            shape(pair.shape, jnp.bfloat16),
            shape((groups, 8, HEAD_SIZE), jnp.float32),
            shape((q_columns, width), jnp.bfloat16),
        ],
        in_specs=[
            rows_spec(window, width), fixed_spec(q_columns, width), columns, kv, columns, mine, marks,
            columns, columns, rows_spec(window, raw.shape[1]), *table_specs(window), fixed_spec(1, HEAD_SIZE), columns,
        ],
        out_specs=[
            rows_spec(window, 2 * q_columns + 2 * HEAD_SIZE), kv, pl.BlockSpec((1, 8, HEAD_SIZE), lambda i: (i, 0, 0)),
            fixed_spec(q_columns, width),
        ],
        scratch_shapes=[pltpu.VMEM((q_columns, width), jnp.float32)],
        compiler_params=kernel_params(56),
        cost_estimate=expected(35),
    )(branch, w_out, query, pair, gate, own, keys, attended, log, raw, table, table, gain[None], gated)


def finish_kernel(dkv_ref, raw_ref, cos_ref, sin_ref, kg_ref, partial_ref, out_ref, gain_ref):
    grads = turn_back(dkv_ref[:, head(0)], cos_ref[...], sin_ref[...])
    d_raw, by_row = norm_back(raw_ref[...], kg_ref[...], grads)
    out_ref[:, head(0)] = low(d_raw)
    out_ref[:, head(1)] = low(dkv_ref[:, head(1)])
    gain_ref[0] = jnp.broadcast_to(jnp.sum(by_row, axis=0, keepdims=True), gain_ref.shape[1:])


def finish_attention(d_pair, raw, table, gain, partial, steps=4):
    tokens = d_pair.shape[0]
    rows = tokens // steps
    shape = jax.ShapeDtypeStruct
    return pl.pallas_call(
        finish_kernel,
        grid=(steps,),
        out_shape=[shape(partial.shape, partial.dtype), shape((steps, 8, HEAD_SIZE), jnp.float32)],
        in_specs=[
            rows_spec(rows, 2 * HEAD_SIZE),
            pl.BlockSpec((rows, HEAD_SIZE), lambda i: (i, REPEAT)),
            *table_specs(rows),
            fixed_spec(1, HEAD_SIZE),
            ANYWHERE,
        ],
        out_specs=[
            pl.BlockSpec((rows, 2 * HEAD_SIZE), lambda i: (i, REPEAT // 2)),
            pl.BlockSpec((1, 8, HEAD_SIZE), lambda i: (i, 0, 0)),
        ],
        input_output_aliases={5: 0},
        compiler_params=kernel_params(60),
        cost_estimate=expected(4),
    )(d_pair, raw, table, table, gain[None], partial)


def split_part(gate, up, pieces):
    rows, every = gate.shape
    units = every // RANKS
    piece = units // pieces

    def steps(ins, outs, scratch):
        (out_ref,) = outs

        def some(corner_at):
            for y in range(CORNERS):
                for at, ref in ((0, ins[0]), (units, ins[1])):
                    starts = [((corner_at * pieces + d) * CORNERS + y) * piece for d in range(pieces)]
                    parts = [ref[:, start : start + piece] for start in starts]
                    out_ref[corner_at * CORNERS + y, :, at : at + units] = jnp.concatenate(parts, axis=1)

        return (lambda: None), [functools.partial(some, i) for i in range(CORNERS**2)], (lambda: None)

    return Part(
        [(gate, VMEM), (up, VMEM)],
        [(jax.ShapeDtypeStruct((RANKS, rows, 2 * units), gate.dtype), VMEM)],
        [],
        steps,
    )


def join_part(blocks, pieces):
    ranks, rows, width = blocks.shape
    units = width // 2
    piece = units // pieces

    def steps(ins, outs, scratch):
        (in_ref,) = ins

        def some(corner_at):
            for at, ref in ((0, outs[0]), (units, outs[1])):
                parts = []
                for d in range(pieces):
                    for y in range(CORNERS):
                        here = slice(at + d * piece, at + (d + 1) * piece)
                        parts.append(in_ref[corner_at * CORNERS + y, :, here])
                wide = CORNERS * units
                ref[:, corner_at * wide : (corner_at + 1) * wide] = jnp.concatenate(parts, axis=1)

        return (lambda: None), [functools.partial(some, i) for i in range(CORNERS**2)], (lambda: None)

    out = (jax.ShapeDtypeStruct((rows, ranks * units), blocks.dtype), VMEM)
    return Part([(blocks, VMEM)], [out, out], [], steps)


def norm_rows_kernel(x_ref, gain_ref, grads_ref, more_ref, out_ref, term_ref):
    values = x_ref[...].astype(jnp.float32)
    d_values, by_row = norm_back(values, gain_ref[...], grads_ref[...])
    out_ref[...] = more_ref[...].astype(jnp.float32) + d_values

    @pl.when(pl.program_id(0) == 0)
    def _():
        term_ref[...] = jnp.zeros_like(term_ref)

    term_ref[...] += jnp.sum(by_row.reshape(-1, *term_ref.shape), axis=0)


def norm_rows_back(values, gain, grads, more, steps=4):
    rows, width = values.shape
    some = rows_spec(rows // steps, width)
    d_values, term = pl.pallas_call(
        norm_rows_kernel,
        grid=(steps,),
        out_shape=[jax.ShapeDtypeStruct(values.shape, jnp.float32), jax.ShapeDtypeStruct((8, width), jnp.float32)],
        in_specs=[some, fixed_spec(1, width), some, some],
        out_specs=[some, fixed_spec(8, width)],
        compiler_params=kernel_params(60),
        cost_estimate=expected(3),
    )(values, gain[None], grads, more)
    return d_values, jnp.sum(term, axis=0)


def widen_kernel(count, in_ref, small_ref, *refs):
    weights, refs = refs[:count], refs[count:]
    others = (len(refs) - count - 2) // 2
    low_refs, refs = refs[:others], refs[others:]
    out_refs, along_ref, total_ref, wide_refs = refs[:count], refs[count], refs[count + 1], refs[count + 2 :]
    along = jnp.zeros(along_ref.shape, jnp.float32)
    for rank in range(RANKS):
        start = 0
        for weight_ref, ref in zip(weights, out_refs):
            width = ref.shape[1] // RANKS
            place = slice(rank * width, (rank + 1) * width)
            value = in_ref[rank, :, start : start + width].astype(jnp.float32)
            ref[:, place] = value
            product = value * weight_ref[:, place].astype(jnp.float32)
            along += sum(product[:, head(h)] for h in range(width // HEAD_SIZE))
            start += width
    along_ref[...] = jnp.broadcast_to(jnp.sum(along, axis=1, keepdims=True), along_ref.shape)
    total_ref[...] = jnp.sum(small_ref[...], axis=0)
    for ref, wide in zip(low_refs, wide_refs):
        wide[...] = ref[...].astype(wide.dtype)


def widen_columns(parts, small, widths, weights, others):
    ranks, rows, columns = parts.shape
    shape = jax.ShapeDtypeStruct
    out_shape = [shape((rows, ranks * w), jnp.float32) for w in widths]
    out_shape += [shape((rows, HEAD_SIZE), jnp.float32), shape(small.shape[1:], jnp.float32)]
    out_shape += [shape(o.shape, kind) for o, kind in others]
    return pl.pallas_call(
        functools.partial(widen_kernel, len(widths)),
        out_shape=out_shape,
        in_specs=[VMEM] * (2 + len(weights) + len(others)),
        out_specs=[VMEM] * len(out_shape),
        compiler_params=kernel_params(32),
        cost_estimate=expected(4),
    )(parts, small, *weights, *[o for o, _ in others])


def make_shards(cells):
    data_total = cells * PLANES

    def blocks(terms):
        return low(terms).reshape(RANKS, -1, terms.shape[1])

    def gather_tokens(rows):
        return run([gather_part(rows)], 0)[0]

    def scatter_tokens(terms):
        return run([scatter_part(blocks(terms))], 1, 40)[0]

    def join_cells(rows):
        if cells > 1:
            rows = lax.all_gather(rows, "cell", axis=0, tiled=False)
            rows = jnp.transpose(rows, (1, 0, 2, 3, 4, 5))
        return rows.reshape(-1, rows.shape[-1])

    def gather_columns(mine):
        rows, columns = mine.shape[1:]
        every = lax.all_gather(mine, DATA, axis=0, tiled=False)
        every = every.reshape(data_total, CORNERS**2, CORNERS, rows, columns)
        return jnp.transpose(every, (1, 0, 2, 3, 4)).reshape(-1, columns)

    def sum_columns(term):
        rows = term.shape[0] // (RANKS * data_total)
        split = low(term).reshape(CORNERS**2, data_total, CORNERS, rows, -1)
        split = jnp.transpose(split, (1, 0, 2, 3, 4)).reshape(data_total * RANKS, rows, -1)
        return lax.psum_scatter(split, DATA, scatter_dimension=0, tiled=True)

    inner = CORNERS * data_total
    to_rank = []
    for source in range(inner):
        rank_y, place = divmod(source, data_total)
        to_rank.append((source, place * CORNERS + rank_y))
    INNER = ("cell", "z", "y")

    def shards(
        hidden_in,
        query_weight,
        key_matrix,
        value_matrix,
        gate_weight,
        out_weight,
        norm_attn,
        query_gain,
        key_gain,
        norm_ffn,
        ffn_gate,
        ffn_up,
        ffn_down,
        cotangent,
        sequence_numbers,
        positions,
    ):
        rows = hidden_in.shape[0]
        tokens = rows * RANKS
        groups = CORNERS**2
        window = GROUP_TOKENS // PLANES

        sizes = [norm_attn.shape[0], norm_ffn.shape[0], query_gain.shape[0], key_gain.shape[0]]
        cuts = [0]
        for size in sizes:
            cuts.append(cuts[-1] + size)
        tile = (8, HEAD_SIZE)
        pad = tile[0] * tile[1] - cuts[-1]
        own_gains = jnp.concatenate([norm_attn, norm_ffn, query_gain, key_gain]).astype(jnp.float32)
        own_gains = jnp.pad(own_gains, (0, pad)).reshape(tile)
        plane = lax.axis_index("z")
        group_start = lax.axis_index("cell") * GROUP_TOKENS
        own_start = group_start + (plane * CORNERS + lax.axis_index("y")) * rows
        own_table = jnp.concatenate(
            rope_tables(lax.dynamic_slice_in_dim(positions, own_start, rows)), axis=-1
        )
        marks = [
            lax.dynamic_slice_in_dim(m, group_start, GROUP_TOKENS).reshape(-1, HEAD_SIZE)
            for m in (sequence_numbers, positions)
        ]
        gains, attn_rows, table, hidden_all, all_seq, all_pos, ffn_columns = run(
            [
                between(tiles_part(own_gains), 0.0, 0.6),
                columns_part([query_weight, key_matrix, value_matrix, gate_weight]),
                between(gather_part(own_table), 0.22, 0.7),
                between(gather_part(hidden_in), 0.22, 0.8),
                *map(marks_part, marks),
                split_part(ffn_gate, ffn_up, data_total),
            ],
            2,
            micros=70,
        )
        attn_rows, out_rows, down_rows = lax.optimization_barrier(
            (attn_rows, lax.ppermute(out_weight, INNER, to_rank), ffn_down)
        )
        w_attn = join_cells(attn_rows)
        gains = gains.reshape(PLANES, CORNERS**2, CORNERS, -1)
        gains = jnp.transpose(gains, (1, 0, 2, 3)).reshape(CORNERS**2, PLANES * CORNERS, -1)
        if cells > 1:
            gains = lax.all_gather(gains, "cell", axis=1, tiled=False)
        gains = gains.reshape(RANKS * data_total, -1)
        gain_attn, gain_ffn, gain_query, gain_key = (
            gains[:, a:b].reshape(-1) for a, b in zip(cuts[:-1], cuts[1:])
        )
        w_out = lax.all_gather(out_rows, DATA, axis=0, tiled=True)
        w_down = lax.all_gather(down_rows, DATA, axis=0, tiled=True)

        marks = jnp.stack([m.reshape(groups, GROUP_TOKENS) for m in (all_seq, all_pos)], axis=1)
        own_marks = lax.dynamic_slice_in_dim(marks, plane * window, window, axis=2)
        own_marks = jnp.transpose(own_marks, (0, 2, 1))

        hidden = hidden_in.astype(jnp.float32)
        normed_input, query_low, pair, raw, gate_raw = prepare_attention(
            hidden_all, gain_attn, w_attn, table, gain_query, gain_key
        )
        pair, cotangent_all, ffn_columns = run(
            [line_gather_part(pair), gather_part(cotangent), swap_part(ffn_columns)], 3, micros=75
        )
        w_ffn = gather_columns(ffn_columns)
        out_terms, attended, log_weight, gated_low = attend(
            query_low, pair, gate_raw, own_marks, marks, w_out
        )
        out_terms = out_terms.reshape(RANKS, rows, -1)
        middle = hidden + run([scatter_part(out_terms)], 1, 40)[0]

        normed_two = gather_tokens(low(root_mean_scale(middle, gain_ffn)))
        both = matrix_product(normed_two, w_ffn)
        units = both.shape[1] // 2
        gate_ffn, up_ffn = both[:, :units], both[:, units:]
        ffn_sig = jax.nn.sigmoid(gate_ffn)
        mixed_low = low(gate_ffn * ffn_sig * up_ffn)

        down_term = low(contract_first(mixed_low, cotangent_all))
        down_term, cotangent_all = lax.optimization_barrier((down_term, cotangent_all))
        grad_down = lax.psum_scatter(down_term, DATA, scatter_dimension=0, tiled=True)
        d_mixed = contract_last(cotangent_all, w_down)
        d_up_low = low(d_mixed * gate_ffn * ffn_sig)
        d_gate_ffn_low = low(d_mixed * up_ffn * ffn_sig * (1.0 + gate_ffn * (1.0 - ffn_sig)))
        d_both = jnp.concatenate([d_gate_ffn_low, d_up_low], axis=-1)
        both_term = low(contract_first(normed_two, d_both))
        both_term, d_both = lax.optimization_barrier((both_term, d_both))
        grad_both = sum_columns(both_term)
        (d_normed_two,) = run([scatter_part(product=(d_both, w_ffn), transposed=True)], 6, 48, 45)
        d_middle, grad_norm_two_term = norm_rows_back(middle, gain_ffn, d_normed_two, cotangent)

        branch_all = gather_tokens(low(d_middle))
        branch_all, grad_down = lax.optimization_barrier((branch_all, grad_down))
        d_partial, d_pair, query_gain_terms, out_term = attend_back(
            branch_all, w_out, query_low, pair, gate_raw, own_marks, marks,
            attended, log_weight, raw, table, gain_query, gated_low,
        )
        d_pair, output, grad_both, out_term = run(
            [
                line_scatter_part(d_pair),
                scatter_part(product=(mixed_low, w_down), more=middle),
                swap_part(grad_both),
                halves_part(out_term, data_total),
            ],
            5,
            58,
            75,
        )
        grad_out = lax.psum_scatter(
            out_term.reshape(-1, out_term.shape[-1]), DATA, scatter_dimension=0, tiled=True
        )
        d_raw, key_gain_terms = finish_attention(
            d_pair, raw, table, gain_key, d_partial
        )
        grad_query_gain_term = jnp.sum(query_gain_terms[:, 0], axis=0)
        grad_key_gain_term = jnp.sum(key_gain_terms[:, 0], axis=0)
        a = REPEAT * HEAD_SIZE
        b, c = a + HEAD_SIZE, a + 2 * HEAD_SIZE
        attn_term = low(contract_first(normed_input, d_raw))
        attn_term, d_raw = lax.optimization_barrier((attn_term, d_raw))
        split = attn_term.reshape(CORNERS**2, cells, PLANES, CORNERS, -1, attn_term.shape[1])
        split = jnp.transpose(split, (2, 1, 0, 3, 4, 5)).reshape(PLANES, -1, attn_term.shape[1])
        small = jnp.concatenate(
            [
                t.reshape(RANKS * data_total, -1)
                for t in (grad_norm_two_term, grad_query_gain_term, grad_key_gain_term)
            ],
            axis=-1,
        )
        spare = tile[0] * tile[1] - small.shape[1]
        small = low(jnp.pad(small, ((0, 0), (0, spare))))
        small = small.reshape((CORNERS**2, cells, PLANES, CORNERS) + tile)
        small = jnp.transpose(small, (2, 1, 0, 3, 4, 5)).reshape(PLANES, -1, HEAD_SIZE)
        small, grad_attn, d_normed, grad_gate, grad_up = run(
            [
                line_scatter_part(small, pieces=1),
                line_scatter_part(split, kind=jnp.bfloat16),
                scatter_part(product=(d_raw, w_attn), transposed=True),
                join_part(grad_both, data_total),
            ],
            7,
            58,
            60,
        )
        if cells > 1:
            grad_attn = lax.psum_scatter(grad_attn, "cell", scatter_dimension=0, tiled=True)
            small = lax.psum_scatter(small, "cell", scatter_dimension=0, tiled=True)
        grad_attn = grad_attn.reshape(RANKS, -1, attn_term.shape[1])
        grad_attn, small = run(
            [swap_part(grad_attn), swap_part(small.reshape((RANKS,) + tile))], 4, micros=14
        )
        wide = [(g, jnp.float32) for g in (grad_gate, grad_up, grad_down, grad_out)]
        (
            grad_query, grad_key, grad_value, grad_gatew, along, small,
            grad_gate, grad_up, grad_down, grad_out, output,
        ) = widen_columns(
            grad_attn,
            small,
            (a, b - a, c - b, a),
            (query_weight, key_matrix, value_matrix, gate_weight),
            wide + [(output, output.dtype)],
        )
        grad_norm_attn = along[:, 0] / norm_attn.astype(jnp.float32)
        input_grad = norm_rows_back(hidden_in, gain_attn, d_normed, d_middle)[0]
        small = small.reshape(-1)
        ends = [size - cuts[1] for size in cuts]
        grad_norm_ffn, grad_query_gain, grad_key_gain = (
            small[s:e] for s, e in zip(ends[1:-1], ends[2:])
        )
        return (
            output,
            input_grad,
            grad_query,
            grad_key,
            grad_value,
            grad_gatew,
            grad_out,
            grad_norm_attn,
            grad_query_gain,
            grad_key_gain,
            grad_norm_ffn,
            grad_gate,
            grad_up,
            grad_down,
        )

    return shards


def solution(mesh):
    cells = mesh.shape["fsdp"] // (PLANES * CORNERS)
    split = Mesh(
        mesh.devices.reshape(CORNERS, CORNERS, cells, PLANES, CORNERS),
        ALL,
    )
    rows, flat, group = P(ALL, None), P(ALL), P(("x", "core"))
    return jax.shard_map(
        make_shards(cells),
        mesh=split,
        in_specs=(rows,) * 6 + (flat,) * 4 + (rows,) * 4 + (group,) * 2,
        out_specs=(rows,) * 7 + (flat,) * 4 + (rows,) * 3,
        check_vma=False,
    )
```
